32 devices in a mesh: shard: 2 (over y), context: 4 (over x, core), tensor: 4 (over z).
Axes of the slice: x: 2, y: 2, z: 4, core: 2. Of those that a mesh axis runs over, the one named last changes fastest.
Arguments:
- inputs: float32 [8, 2048, 1024], P('shard', ('context', 'tensor')), may hold values from -6 to 6
- teacher: float32 [8, 2048, 1024], P('shard', ('context', 'tensor')), may hold values from -6 to 6
- segments: int32 [8, 2048], P('shard', ('context', 'tensor')), may hold values from 0 to 35, as said below
- pad_mask: int32 [8, 2048], P('shard', ('context', 'tensor')), may hold values from 0 to 1, as said below
- query_weight: float32 [1024, 1024], P(('shard', 'context'), 'tensor'), may hold values from -0.1875 to 0.1875
- key_weight: float32 [1024, 1024], P(('shard', 'context'), 'tensor'), may hold values from -0.1875 to 0.1875
- value_weight: float32 [1024, 1024], P(('shard', 'context'), 'tensor'), may hold values from -0.1875 to 0.1875
- output_weight: float32 [1024, 1024], P('tensor', ('shard', 'context')), may hold values from -0.1875 to 0.1875
- up_weight: float32 [1024, 4096], P(('shard', 'context'), 'tensor'), may hold values from -0.1875 to 0.1875
- down_weight: float32 [4096, 1024], P('tensor', ('shard', 'context')), may hold values from -0.09375 to 0.09375
- first_gain: float32 [1024], replicated, may hold values from 0.5 to 1.5
- first_shift: float32 [1024], replicated, may hold values from -1.75 to 1.75
- query_shift: float32 [1024], replicated, may hold values from -1.75 to 1.75
- value_shift: float32 [1024], replicated, may hold values from -1.75 to 1.75
- mixed_gain: float32 [1024], replicated, may hold values from 0.5 to 1.5
- mixed_shift: float32 [1024], replicated, may hold values from -1.75 to 1.75
- output_shift: float32 [1024], replicated, may hold values from -1.75 to 1.75
- second_gain: float32 [1024], replicated, may hold values from 0.5 to 1.5
- second_shift: float32 [1024], replicated, may hold values from -1.75 to 1.75
- up_shift: float32 [4096], replicated, may hold values from -1.75 to 1.75
- hidden_gain: float32 [4096], replicated, may hold values from 0.5 to 1.5
- hidden_shift: float32 [4096], replicated, may hold values from -1.75 to 1.75
- down_shift: float32 [1024], replicated, may hold values from -1.75 to 1.75
Outputs:
- result: float32 [8, 2048, 1024], P('shard', ('context', 'tensor'))
- loss_value: float32 [], replicated
- input_grad: float32 [8, 2048, 1024], P('shard', ('context', 'tensor'))
- query_grad: float32 [1024, 1024], P(('shard', 'context'), 'tensor')
- key_grad: float32 [1024, 1024], P(('shard', 'context'), 'tensor')
- value_grad: float32 [1024, 1024], P(('shard', 'context'), 'tensor')
- output_grad: float32 [1024, 1024], P('tensor', ('shard', 'context'))
- up_grad: float32 [1024, 4096], P(('shard', 'context'), 'tensor')
- down_grad: float32 [4096, 1024], P('tensor', ('shard', 'context'))
- first_gain_grad: float32 [1024], replicated
- first_shift_grad: float32 [1024], replicated
- query_shift_grad: float32 [1024], replicated
- value_shift_grad: float32 [1024], replicated
- mixed_gain_grad: float32 [1024], replicated
- mixed_shift_grad: float32 [1024], replicated
- output_shift_grad: float32 [1024], replicated
- second_gain_grad: float32 [1024], replicated
- second_shift_grad: float32 [1024], replicated
- up_shift_grad: float32 [4096], replicated
- hidden_gain_grad: float32 [4096], replicated
- hidden_shift_grad: float32 [4096], replicated
- down_shift_grad: float32 [1024], replicated
The draws below stay inside these ranges and needn't reach their ends.
Inputs may be any that keep to these rules, and one draw needn't show every extreme that they name: `segments`: within a sequence the id never falls; each id below 35 is one document of at most 800 tokens, the first document of every sequence has exactly 800 tokens, and the id 2048 // 60 + 1 marks the padding, a nonempty tail of every sequence of at most a quarter of it. `pad_mask`: 0 exactly on the padding tail that segments marks.
All inputs are finite; a program needn't handle non-finite values.
Results may differ from the reference program's by a relative error of at most 0.014.
Values may be sent and summed in bfloat16 or wider, within the bound.
A program may use at most 192 MiB of HBM per device.

```python
import jax
import jax.numpy as jnp
from jax import lax

D = 1024
HEADS = 16
HEAD_DIM = 64
FF = 4096
SEQ_LEN = 2048
DOC_MIN = 60
DOC_MAX = 800
NSEQ = 8


def token_layout(key):
    doc_count = SEQ_LEN // DOC_MIN + 1
    length_key, pad_key = jax.random.split(jax.random.fold_in(key, 11))
    lengths = jax.random.randint(length_key, (NSEQ, doc_count), DOC_MIN, DOC_MAX + 1)
    lengths = lengths.at[:, 0].set(DOC_MAX)
    bounds = jnp.cumsum(lengths, axis=1)
    position = jnp.arange(SEQ_LEN, dtype=jnp.int32)
    doc_ids = jnp.sum((bounds[:, None, :] <= position[None, :, None]).astype(jnp.int32), axis=2)
    padding = jax.random.randint(pad_key, (NSEQ, 1), 1, SEQ_LEN // 4 + 1)
    is_pad = position[None, :] >= SEQ_LEN - padding
    doc_ids = jnp.where(is_pad, doc_count, doc_ids)
    return (doc_ids.astype(jnp.int32), jnp.where(is_pad, 0, 1).astype(jnp.int32))


def draw_segments(key, part):
    return token_layout(key)[0]


def draw_pad_mask(key, part):
    return token_layout(key)[1]


def shard_levels(rng, dims, shards, smallest, top_value):
    gain = 1.0
    for axis_at, shards_of in shards:
        steps = jax.random.uniform(jax.random.fold_in(jax.random.fold_in(rng, 6), axis_at), (shards_of,), jnp.float32, smallest / len(shards), top_value / len(shards))
        gain = gain * jnp.repeat(jnp.exp(steps), dims[axis_at] // shards_of).reshape((-1,) + (1,) * (len(dims) - 1 - axis_at))
    return gain


def gaussian(key, extent, scale, bound, pieces=(), kind=jnp.bfloat16):
    result = scale * jax.random.normal(key, extent, jnp.float32)
    if pieces:
        result = result * shard_levels(key, extent, pieces, -0.22, 0.18)
    return jnp.clip(result, -bound, bound).astype(kind)


def setup_inputs(seed: int = 0) -> dict:
    splits = jax.random.split(jax.random.key(seed), 24)
    return {
        "inputs": gaussian(splits[0], (NSEQ, SEQ_LEN, D), 1.0, 6.0, ((0, 2), (1, 16)), jnp.float32),
        "teacher": gaussian(splits[1], (NSEQ, SEQ_LEN, D), 1.0, 6.0, ((0, 2), (1, 16)), jnp.float32),
        "segments": draw_segments(jax.random.fold_in(splits[23], 71), 0),
        "pad_mask": draw_pad_mask(jax.random.fold_in(splits[23], 71), 0),
        "query_weight": gaussian(splits[4], (D, D), D ** -0.5, 0.1875, ((0, 8), (1, 4)), jnp.float32),
        "key_weight": gaussian(splits[5], (D, D), D ** -0.5, 0.1875, ((0, 8), (1, 4)), jnp.float32),
        "value_weight": gaussian(splits[6], (D, D), D ** -0.5, 0.1875, ((0, 8), (1, 4)), jnp.float32),
        "output_weight": gaussian(splits[7], (D, D), D ** -0.5, 0.1875, ((0, 4), (1, 8)), jnp.float32),
        "up_weight": gaussian(splits[8], (D, FF), D ** -0.5, 0.1875, ((0, 8), (1, 4)), jnp.float32),
        "down_weight": gaussian(splits[9], (FF, D), FF ** -0.5, 0.09375, ((0, 4), (1, 8)), jnp.float32),
        "first_gain": jnp.clip(1.0 + 0.1 * jax.random.normal(splits[10], (D,), jnp.float32), 0.5, 1.5),
        "first_shift": gaussian(splits[11], (D,), 0.3, 1.75, (), jnp.float32),
        "query_shift": gaussian(splits[12], (D,), 0.3, 1.75, (), jnp.float32),
        "value_shift": gaussian(splits[13], (D,), 0.3, 1.75, (), jnp.float32),
        "mixed_gain": jnp.clip(1.0 + 0.1 * jax.random.normal(splits[14], (D,), jnp.float32), 0.5, 1.5),
        "mixed_shift": gaussian(splits[15], (D,), 0.3, 1.75, (), jnp.float32),
        "output_shift": gaussian(splits[16], (D,), 0.3, 1.75, (), jnp.float32),
        "second_gain": jnp.clip(1.0 + 0.1 * jax.random.normal(splits[17], (D,), jnp.float32), 0.5, 1.5),
        "second_shift": gaussian(splits[18], (D,), 0.3, 1.75, (), jnp.float32),
        "up_shift": gaussian(splits[19], (FF,), 0.3, 1.75, (), jnp.float32),
        "hidden_gain": jnp.clip(1.0 + 0.1 * jax.random.normal(splits[20], (FF,), jnp.float32), 0.5, 1.5),
        "hidden_shift": gaussian(splits[21], (FF,), 0.3, 1.75, (), jnp.float32),
        "down_shift": gaussian(splits[22], (D,), 0.3, 1.75, (), jnp.float32),
    }


@jax.custom_vjp
def low(v):
    return lax.optimization_barrier(v.astype(jnp.bfloat16)).astype(jnp.float32)

@jax.custom_vjp
def low_back(v):
    return v

def low_keep(v):
    return (low(v), None)

def low_pass(kept, grad):
    return (grad,)

def back_keep(v):
    return (v, None)

def back_low(kept, grad):
    return (low(grad),)
low.defvjp(low_keep, low_pass)
low_back.defvjp(back_keep, back_low)

def matmul(left, right):
    return jnp.dot(left, right, precision=lax.Precision.HIGHEST)

def layer_norm(values, norm_gain, norm_bias):
    center = lax.optimization_barrier(jnp.mean(values, axis=-1, keepdims=True))
    spread = lax.optimization_barrier(jnp.mean(values * values, axis=-1, keepdims=True)) - center * center
    return (values - center) * lax.rsqrt(spread + 1e-05) * norm_gain + norm_bias

def attention(queries, key_rows, value_rows, segment):
    same_doc = segment[:, None] == segment[None, :]

    def one_head(head_block):
        head_query, head_keys, head_values = head_block
        scores = low_back(matmul(head_query, head_keys.T) * HEAD_DIM ** (-0.5))
        scores = jnp.where(same_doc, scores, -1e+30)
        row_top = lax.optimization_barrier(jnp.max(scores, axis=1, keepdims=True))
        exponent = jnp.exp(scores - row_top)
        attend_weights = exponent / lax.optimization_barrier(jnp.sum(exponent, axis=1, keepdims=True))
        return matmul(low(attend_weights), head_values)

    def split_heads(values):
        return values.reshape(SEQ_LEN, HEADS, HEAD_DIM).transpose(1, 0, 2)
    head_out = lax.map(jax.checkpoint(one_head), (split_heads(queries), split_heads(key_rows), split_heads(value_rows)))
    return head_out.transpose(1, 0, 2).reshape(SEQ_LEN, HEADS * HEAD_DIM)

def forward(params, inputs, segment):
    query_weight, key_weight, value_weight, output_weight, up_weight, down_weight, first_gain, first_shift, query_shift, value_shift, mixed_gain, mixed_shift, output_shift, second_gain, second_shift, up_shift, hidden_gain, hidden_shift, down_shift = params
    normed = low(layer_norm(inputs, first_gain, first_shift))
    queries = low_back(low(matmul(normed, low(query_weight)) + query_shift))
    key_rows = low_back(low(matmul(normed, low(key_weight))))
    value_rows = low_back(low(matmul(normed, low(value_weight)) + value_shift))
    mixed_rows = low_back(attention(queries, key_rows, value_rows, segment))
    inner_rows = low(layer_norm(mixed_rows, mixed_gain, mixed_shift))
    middle = inputs + low_back(matmul(inner_rows, low(output_weight)) + output_shift)
    normed_two = low(layer_norm(middle, second_gain, second_shift))
    hidden_pre = low_back(matmul(normed_two, low(up_weight)) + up_shift)
    hidden = low(layer_norm(jax.nn.gelu(hidden_pre, approximate=True), hidden_gain, hidden_shift))
    return middle + low_back(matmul(hidden, low(down_weight)) + down_shift)

def reference(inputs, teacher, segments, pad_mask, query_weight, key_weight, value_weight, output_weight, up_weight, down_weight, first_gain, first_shift, query_shift, value_shift, mixed_gain, mixed_shift, output_shift, second_gain, second_shift, up_shift, hidden_gain, hidden_shift, down_shift):
    params = (query_weight, key_weight, value_weight, output_weight, up_weight, down_weight, first_gain, first_shift, query_shift, value_shift, mixed_gain, mixed_shift, output_shift, second_gain, second_shift, up_shift, hidden_gain, hidden_shift, down_shift)
    valid_rows = pad_mask.astype(jnp.float32)
    valid_count = jnp.sum(valid_rows)
    cotangent = 0.5 * NSEQ * SEQ_LEN / valid_count

    def scan_step(carried, sequence_item):
        totals, loss_sum = carried
        sequence_rows, target, segment, keep_rows = sequence_item

        def forward_loss(weights, rows_in):
            layer_out = forward(weights, rows_in, segment)
            errors = layer_out - target
            return (layer_out, jnp.sum(keep_rows[:, None] * errors * errors))
        (layer_out, loss_part), pullback = jax.vjp(forward_loss, params, sequence_rows)
        grad_parts, row_grad = pullback((jnp.zeros_like(layer_out), cotangent))
        totals = jax.tree.map(lambda first_term, second_term: first_term + second_term, totals, grad_parts)
        return ((totals, loss_sum + loss_part), (layer_out, row_grad))
    grad_zeros = jax.tree.map(jnp.zeros_like, params)
    (grad_parts, loss_sum), (outputs, input_grad) = lax.scan(scan_step, (grad_zeros, jnp.zeros((), jnp.float32)), (inputs, teacher, segments, valid_rows))
    return (outputs, loss_sum / valid_count, input_grad, grad_parts[0], grad_parts[1], grad_parts[2], grad_parts[3], grad_parts[4], grad_parts[5], grad_parts[6], grad_parts[7], grad_parts[8], grad_parts[9], grad_parts[10], grad_parts[11], grad_parts[12], grad_parts[13], grad_parts[14], grad_parts[15], grad_parts[16], grad_parts[17], grad_parts[18])
```

```python
import functools

import jax
import jax.numpy as jnp
from jax import lax
from jax.experimental import pallas as pl
from jax.experimental.pallas import tpu as pltpu
from jax.sharding import PartitionSpec as P

NEG=-1e30
def _dot(a,b,ca,cb):
    return lax.dot_general(a,b,(((ca,),(cb,)),((),())),preferred_element_type=jnp.float32)

def half_masks(rows):
    lane=lax.broadcasted_iota(jnp.int32,(rows,128),1)
    return lane<64

def fwd_kernel(lo_ref,hi_ref,q_ref,k_ref,v_ref,col_ref,row_ref,o_ref,lse_ref,acc_ref,m_ref,l_ref):
    s=pl.program_id(0); i=pl.program_id(1)
    bq=acc_ref.shape[1]; bk=row_ref.shape[-1]; n=k_ref.shape[2]; per=bk//n
    left=half_masks(bq)
    q=q_ref[...].reshape(bq,128)*jnp.bfloat16(0.125)
    zero=jnp.zeros_like(q)
    qs=(jnp.where(left,q,zero),jnp.where(left,zero,q))
    col=col_ref[0]
    for h in range(2):
        acc_ref[h]=jnp.zeros((bq,128),jnp.float32)
        m_ref[h]=jnp.full((bq,128),NEG,jnp.float32)
        l_ref[h]=jnp.zeros((bq,128),jnp.float32)
    def step(j,_):
        k=k_ref[pl.ds(j*per,per),0].reshape(bk,128)
        v=v_ref[pl.ds(j*per,per),0].reshape(bk,128)
        same=col==row_ref[0,j]
        for h in range(2):
            sc=jnp.where(same,_dot(qs[h],k,1,1),NEG)
            old=m_ref[h]
            top=jnp.maximum(old,jnp.max(sc,axis=1,keepdims=True))
            e=jnp.exp(sc-jnp.concatenate([top]*(bk//128),axis=1))
            a=jnp.exp(old-top)
            l_ref[h]=l_ref[h]*a+jnp.sum(e,axis=1,keepdims=True)
            m_ref[h]=top
            acc_ref[h]=acc_ref[h]*a+_dot(e.astype(jnp.bfloat16),v,1,0)
        return 0
    lax.fori_loop(lo_ref[s,i],hi_ref[s,i],step,0)
    o=jnp.where(left,acc_ref[0]/l_ref[0],acc_ref[1]/l_ref[1])
    o_ref[...]=o.astype(jnp.bfloat16).reshape(o_ref.shape)
    lse=jnp.where(left,m_ref[0]+jnp.log(l_ref[0]),m_ref[1]+jnp.log(l_ref[1]))
    lse_ref[...]=lse.reshape(lse_ref.shape)

def bounds(ids,bq,bk):
    L=ids.shape[1]
    first=ids[:,::bq]; last=ids[:,bq-1::bq]
    start=jnp.sum((ids[:,None,:]<first[:,:,None]).astype(jnp.int32),axis=2)
    end=jnp.sum((ids[:,None,:]<=last[:,:,None]).astype(jnp.int32),axis=2)
    return start//bk,(end+bk-1)//bk

def attend_fwd(q,k,v,ids,bq=256,bk=256):
    G,spg,n,_=q.shape; L=G*n
    lo,hi=bounds(ids,bq,bk)
    nq=L//bq
    col=ids[:,:,None]; row=ids.reshape(spg,L//bk,1,bk)
    qspec=pl.BlockSpec((bq//n,1,n,128),lambda s,i,*_:(i,s,0,0))
    kspec=pl.BlockSpec((G,1,n,128),lambda s,i,*_:(0,s,0,0))
    return pl.pallas_call(fwd_kernel,
        grid_spec=pltpu.PrefetchScalarGridSpec(num_scalar_prefetch=2,grid=(spg,nq),
            in_specs=[qspec,kspec,kspec,pl.BlockSpec((1,bq,1),lambda s,i,*_:(s,i,0)),pl.BlockSpec((1,L//bk,1,bk),lambda s,i,*_:(s,0,0,0))],
            out_specs=[qspec,qspec],
            scratch_shapes=[pltpu.VMEM((2,bq,128),jnp.float32)]*3),
        out_shape=[jax.ShapeDtypeStruct(q.shape,jnp.bfloat16),jax.ShapeDtypeStruct(q.shape,jnp.float32)],
        compiler_params=pltpu.CompilerParams(dimension_semantics=("arbitrary","arbitrary"),vmem_limit_bytes=48<<20),
        cost_estimate=pl.CostEstimate(flops=1000,bytes_accessed=1000,transcendentals=0),
        name="attend_fwd")(lo,hi,q,k,v,col,row)

def bwd_kernel(lo_ref,hi_ref,q_ref,k_ref,v_ref,g_ref,o_ref,lse_ref,col_ref,row_ref,dq_ref,dk_ref,dv_ref,dqa,dka,dva):
    s=pl.program_id(0); i=pl.program_id(1)
    bq=dqa.shape[1]; bk=bq; n=k_ref.shape[2]; per=bk//n
    @pl.when(i==0)
    def _():
        dka[...]=jnp.zeros_like(dka); dva[...]=jnp.zeros_like(dva)
    left=half_masks(bq)
    q=q_ref[...].reshape(bq,128)*jnp.bfloat16(0.125)
    g=g_ref[...].reshape(bq,128)
    zero=jnp.zeros_like(q)
    qs=(jnp.where(left,q,zero),jnp.where(left,zero,q))
    gs=(jnp.where(left,g,zero),jnp.where(left,zero,g))
    lse_t=lse_ref[...].reshape(bq,128).T
    d_t=(g.astype(jnp.float32)*o_ref[...].reshape(bq,128).astype(jnp.float32)).T
    lses=(lse_t[0:1],lse_t[64:65])
    ds=(jnp.sum(d_t[:64],axis=0,keepdims=True),jnp.sum(d_t[64:],axis=0,keepdims=True))
    ids_q=row_ref[0,i]
    dqa[...]=jnp.zeros_like(dqa)
    def step(j,_):
        k=k_ref[pl.ds(j*per,per),0].reshape(bk,128)
        v=v_ref[pl.ds(j*per,per),0].reshape(bk,128)
        rows=pl.ds(pl.multiple_of(j*bk,bk),bk)
        same=col_ref[0,rows,:]==ids_q
        dk=dka[rows,:]; dv=dva[rows,:]
        for h in range(2):
            st=_dot(k,qs[h],1,1)
            p=jnp.exp(jnp.where(same,st,NEG)-lses[h])
            dp=_dot(v,gs[h],1,1)
            d=(p*(dp-ds[h])).astype(jnp.bfloat16)
            dv=dv+_dot(p.astype(jnp.bfloat16),gs[h],1,0)
            dk=dk+_dot(d,qs[h],1,0)
            dqa[h]+=_dot(d,k,0,0)
        dka[rows,:]=dk; dva[rows,:]=dv
        return 0
    lax.fori_loop(lo_ref[s,i],hi_ref[s,i],step,0)
    dq_ref[...]=(jnp.where(left,dqa[0],dqa[1])*0.125).astype(jnp.bfloat16).reshape(dq_ref.shape)
    @pl.when(i==pl.num_programs(1)-1)
    def _():
        dk_ref[...]=dka[...].astype(jnp.bfloat16).reshape(dk_ref.shape)
        dv_ref[...]=dva[...].astype(jnp.bfloat16).reshape(dv_ref.shape)

def attend_bwd(q,k,v,g,o,lse,ids,bq=256):
    bk=bq
    G,spg,n,_=q.shape; L=G*n
    lo,hi=bounds(ids,bq,bk)
    nq=L//bq
    col=ids[:,:,None]; row=ids.reshape(spg,L//bk,1,bk)
    qspec=pl.BlockSpec((bq//n,1,n,128),lambda s,i,*_:(i,s,0,0))
    kspec=pl.BlockSpec((G,1,n,128),lambda s,i,*_:(0,s,0,0))
    out=jax.ShapeDtypeStruct(q.shape,jnp.bfloat16)
    return pl.pallas_call(bwd_kernel,
        grid_spec=pltpu.PrefetchScalarGridSpec(num_scalar_prefetch=2,grid=(spg,nq),
            in_specs=[qspec,kspec,kspec,qspec,qspec,qspec,pl.BlockSpec((1,L,1),lambda s,i,*_:(s,0,0)),pl.BlockSpec((1,L//bk,1,bk),lambda s,i,*_:(s,0,0,0))],
            out_specs=[qspec,kspec,kspec],
            scratch_shapes=[pltpu.VMEM((2,bq,128),jnp.float32)]+[pltpu.VMEM((L,128),jnp.float32)]*2),
        out_shape=[out]*3,
        compiler_params=pltpu.CompilerParams(dimension_semantics=("arbitrary","arbitrary"),vmem_limit_bytes=48<<20),
        cost_estimate=pl.CostEstimate(flops=1000,bytes_accessed=1000,transcendentals=0),
        name="attend_bwd")(lo,hi,q,k,v,g,o,lse,col,row)

EPS=1e-5
ALL=("tensor","shard","context")
PAIR=128

def norm_parts(v):
    m=jnp.mean(v,axis=-1,keepdims=True)
    s=jnp.mean(v*v,axis=-1,keepdims=True)-m*m
    r=lax.rsqrt(s+EPS)
    return (v-m)*r,r

def norm_back(e,h,r,gain):
    t=e*gain
    return r*(t-jnp.mean(t,axis=-1,keepdims=True)-h*jnp.mean(t*h,axis=-1,keepdims=True))

def low(v):
    return v.astype(jnp.bfloat16)

def mm(spec,a,b):
    return jnp.einsum(spec,a,b,preferred_element_type=jnp.float32)


MESH_ID=pl.DeviceIdType.MESH

class Place:
    def __init__(self,S,C,T):
        self.CC=2 if C%2==0 else 1
        self.size={"t":T,"s":S,"x":C//self.CC,"c":self.CC}
        c=lax.axis_index("context")
        self.at={"t":lax.axis_index("tensor"),"s":lax.axis_index("shard"),"x":c//self.CC,"c":lax.rem(c,self.CC)}
        self.group=c*T+self.at["t"]
        self.T=T; self.G=C*T
    def peers(self,axis):
        m=self.size[axis]
        for d in range(1,m):
            other=lax.rem(self.at[axis]+d,m)
            if axis=="t": yield d-1,other,{"tensor":other}
            elif axis=="s": yield d-1,other,{"shard":other}
            elif axis=="x": yield d-1,other,{"context":other*self.CC+self.at["c"]}
            else: yield d-1,other,{"context":self.at["x"]*self.CC+other}
    def group_peers(self):
        for d in range(1,self.G):
            other=lax.rem(self.group+d,self.G)
            yield d-1,other,{"context":other//self.T,"tensor":lax.rem(other,self.T)}

def slots(size,order):
    base,total={},0
    for a in order:
        base[a]=total; total+=size[a]-1
    return base,total

def greet(place):
    barrier=pltpu.get_barrier_semaphore()
    count=0
    for _,_,dev in place.group_peers():
        pl.semaphore_signal(barrier,inc=1,device_id=dev,device_id_type=MESH_ID); count+=1
    for _,_,dev in place.peers("s"):
        pl.semaphore_signal(barrier,inc=1,device_id=dev,device_id_type=MESH_ID); count+=1
    pl.semaphore_wait(barrier,count)

def remote(src,dst,send,recv,dev):
    return pltpu.make_async_remote_copy(src_ref=src,dst_ref=dst,send_sem=send,recv_sem=recv,device_id=dev,device_id_type=MESH_ID)

def project_kernel(S,C,T,x_ref,gain_ref,shift_ref,wq_ref,wk_ref,wv_ref,bias_ref,ids_ref,
                   low_ref,rows_ref,wide_ref,allids_ref,
                   wbuf,obuf,idbuf,ag_send,ag_recv,a_send,a_recv,i_send,i_recv,local):
    place=Place(S,C,T)
    R,D=low_ref.shape
    G,spg,n=rows_ref.shape[1:4]
    HP=D//PAIR; SG=G//HP
    cols=wbuf.shape[-1]; hpt=cols//PAIR
    me=place.group
    order="tsxc"
    base,total=slots(place.size,order)
    own=[place.at[a] for a in order]
    for w,ref in enumerate((wq_ref,wk_ref,wv_ref)):
        wbuf[w,own[0],own[1],own[2],own[3]]=ref[...].astype(jnp.bfloat16)
    greet(place)
    stages={2:"tsxc",1:"txsc",0:"tsxc"}
    sent=[]
    copies={}
    def start(w,r):
        done=stages[w][:r]; axis=stages[w][r]
        idx=tuple(slice(None) if a in done else place.at[a] for a in order)
        copies[w,r]=[]
        for k,_,dev in place.peers(axis):
            c=remote(wbuf.at[(w,)+idx],wbuf.at[(w,)+idx],ag_send.at[w,base[axis]+k],ag_recv.at[w,base[axis]+k],dev)
            c.start(); copies[w,r].append(c); sent.append(c)
    def arrive(w,r):
        for c in copies[w,r]: c.wait_recv()
    for w in (2,1,0): start(w,0)
    ids_own=pltpu.make_async_copy(ids_ref,idbuf.at[place.at["s"]],local.at[0]); ids_own.start()
    id_first=[]
    for k,_,dev in place.peers("s"):
        c=remote(ids_ref,idbuf.at[place.at["s"]],i_send.at[k],i_recv.at[k],dev); c.start(); id_first.append(c); sent.append(c)
    step=min(64,R)
    def norm(i,_):
        rows=pl.ds(pl.multiple_of(i*step,step),step)
        h,_r=norm_parts(x_ref[rows,:])
        low_ref[rows,:]=(h*gain_ref[...]+shift_ref[...]).astype(jnp.bfloat16)
        return 0
    lax.fori_loop(0,R//step,norm,0)
    def spread_ids():
        ids_own.wait()
        for c in id_first: c.wait_recv()
        out=[]
        mine=pltpu.make_async_copy(idbuf,allids_ref.at[me],local.at[1]); mine.start(); out.append(mine)
        for k,_,dev in place.group_peers():
            c=remote(idbuf,allids_ref.at[me],i_send.at[S-1+k],i_recv.at[S-1+k],dev); c.start(); sent.append(c); out.append(c)
        return out
    late=[]
    def compute(w):
        def one(t,_):
            y=_dot(low_ref[...],wbuf[w,t].reshape(D,cols),1,0)+bias_ref[w,t]
            y=y.astype(jnp.bfloat16)
            for g in range(SG):
                for j in range(hpt):
                    obuf[w,g*HP+t*hpt+j]=y[g*spg*n:(g+1)*spg*n,j*PAIR:(j+1)*PAIR].reshape(spg,n,PAIR)
            return 0
        lax.fori_loop(0,T,one,0)
        mine=pltpu.make_async_copy(obuf.at[w,me],rows_ref.at[w,me],local.at[2+w]); mine.start(); late.append(mine)
        for k,other,dev in place.group_peers():
            c=remote(obuf.at[w,other],rows_ref.at[w,me],a_send.at[w,k],a_recv.at[w,k],dev)
            c.start(); sent.append(c); late.append(c)
        keep=pltpu.make_async_copy(wbuf.at[w],wide_ref.at[w],local.at[5+w]); keep.start(); late.append(keep)
    arrive(2,0); start(2,1)
    arrive(1,0); start(1,1)
    ids_out=spread_ids()
    arrive(2,1); start(2,2)
    arrive(1,1); start(1,2)
    arrive(0,0); start(0,1)
    arrive(2,2); start(2,3)
    arrive(2,3); compute(2)
    arrive(1,2); start(1,3)
    arrive(0,1); start(0,2)
    arrive(1,3); compute(1)
    arrive(0,2); start(0,3)
    arrive(0,3); compute(0)
    for c in late+ids_out:
        if any(c is o for o in sent): c.wait_recv()
        else: c.wait()
    for c in sent: c.wait_send()

def project(S,C,T,x,gain,shift,wq,wk,wv,bias,ids,ns,n):
    R,D=x.shape
    G=C*T; HP=D//PAIR; spg=ns*HP//G
    DR,cols=wq.shape
    CC=2 if C%2==0 else 1
    piece=(3,T,S,C//CC,CC,DR,cols)
    _,total=slots({"t":T,"s":S,"x":C//CC,"c":CC},"tsxc")
    vm=pl.BlockSpec(memory_space=pltpu.VMEM); anyspec=pl.BlockSpec(memory_space=pl.ANY)
    dma=pltpu.SemaphoreType.DMA
    return pl.pallas_call(functools.partial(project_kernel,S,C,T),
        in_specs=[vm]*8,
        out_specs=[vm,anyspec,anyspec,anyspec],
        out_shape=[jax.ShapeDtypeStruct((R,D),jnp.bfloat16),jax.ShapeDtypeStruct((3,G,spg,n,PAIR),jnp.bfloat16),
                   jax.ShapeDtypeStruct(piece,jnp.bfloat16),jax.ShapeDtypeStruct((G,S,1,ns*n),jnp.int32)],
        scratch_shapes=[pltpu.VMEM(piece,jnp.bfloat16),pltpu.VMEM((3,G,spg,n,PAIR),jnp.bfloat16),pltpu.VMEM((S,1,ns*n),jnp.int32),
                        dma((3,total)),dma((3,total)),dma((3,G-1)),dma((3,G-1)),dma((S-1+G-1,)),dma((S-1+G-1,)),dma((8,))],
        compiler_params=pltpu.CompilerParams(collective_id=0,has_side_effects=True,vmem_limit_bytes=40<<20),
        name="project")(x,gain,shift,wq,wk,wv,bias,ids)


def shards(inputs,teacher,segments,pad_mask,query_weight,key_weight,value_weight,output_weight,up_weight,down_weight,
           first_gain,first_shift,query_shift,value_shift,mixed_gain,mixed_shift,output_shift,second_gain,second_shift,
           up_shift,hidden_gain,hidden_shift,down_shift):
    S,C,T=lax.axis_size("shard"),lax.axis_size("context"),lax.axis_size("tensor")
    G=C*T
    ns,n,D=inputs.shape
    R=ns*n
    HP=D//PAIR
    SG=G//HP
    spg=ns//SG
    token_total=S*C*T*R
    me_s=lax.axis_index("shard")
    me_g=lax.axis_index("context")*T+lax.axis_index("tensor")
    w2=jnp.concatenate([low(output_weight.T),low(up_weight),low(down_weight.T)],axis=1)
    c1=query_weight.shape[1]; c2=output_weight.shape[0]; cf=up_weight.shape[1]
    F=cf*T
    W2=lax.all_gather(w2,ALL,axis=0,tiled=True)
    W2=W2.reshape(T,D,c2+2*cf)
    Wo,Wu,Wd=W2[:,:,:c2],W2[:,:,c2:c2+cf],W2[:,:,c2+cf:]
    x=inputs.reshape(R,D)
    zeros=jnp.zeros_like(query_shift)
    bias=jnp.stack([query_shift,zeros,value_shift]).reshape(3,T,1,c1)
    first_low,qkv,wide,ids_all=project(S,C,T,x,first_gain[None],first_shift[None],query_weight,key_weight,value_weight,bias,
                                       segments.reshape(1,R),ns,n)
    W1=wide.reshape(3,T,D,c1)
    ids_all=ids_all.reshape(G,S,ns,n)
    valid_count=jnp.sum((ids_all!=(2048//60+1)).astype(jnp.float32))
    ids_mine=lax.dynamic_index_in_dim(ids_all,me_s,1,keepdims=False)
    ids_mine=lax.dynamic_slice_in_dim(ids_mine,(me_g//HP)*spg,spg,1).transpose(1,0,2).reshape(spg,G*n)
    first_normal,first_inverse=norm_parts(x)
    def out_rows(a,lead):
        a=a.reshape(SG,spg,n,HP,lead,PAIR).transpose(0,3,4,1,2,5).reshape(G,lead,spg,n,PAIR)
        return lax.all_to_all(a,("context","tensor"),0,0,tiled=True)
    def in_rows(a,lead):
        a=lax.all_to_all(a,("context","tensor"),0,0,tiled=True)
        return a.reshape(SG,HP,lead,spg,n,PAIR).transpose(2,0,3,4,1,5).reshape(lead,R,D)
    q,k,v=qkv[0],qkv[1],qkv[2]
    o,lse=attend_fwd(q,k,v,ids_mine)
    mixed=in_rows(o[:,None],1)[0].astype(jnp.float32)
    mixed_normal,mixed_inverse=norm_parts(mixed)
    inner_low=low(mixed_normal*mixed_gain+mixed_shift)
    middle=x+(mm("nte,tde->nd",inner_low.reshape(R,T,c2),Wo)+output_shift)
    second_normal,second_inverse=norm_parts(middle)
    second_low=low(second_normal*second_gain+second_shift)
    unit=(mm("nd,tdf->ntf",second_low,Wu)).reshape(R,F)+up_shift
    act,pull=jax.vjp(lambda a: jax.nn.gelu(a,approximate=True),unit)
    hidden_normal,hidden_inverse=norm_parts(act)
    hidden_low=low(hidden_normal*hidden_gain+hidden_shift)
    result=middle+(mm("ntf,tdf->nd",hidden_low.reshape(R,T,cf),Wd)+down_shift)
    keep=pad_mask.reshape(R,1).astype(jnp.float32)
    errors=result-teacher.reshape(R,D)
    loss_part=jnp.sum(keep*errors*errors)
    out_grad=keep*errors*(token_total/valid_count)
    out_low=low(out_grad)
    down_shift_grad=jnp.sum(out_low.astype(jnp.float32),axis=0)
    d_down=low(mm("nd,ntf->tdf",out_low,hidden_low.reshape(R,T,cf)))
    hidden_grad=mm("nd,tdf->ntf",out_low,Wd).reshape(R,F)
    hidden_gain_grad=jnp.sum(hidden_grad*hidden_normal,axis=0)
    hidden_shift_grad=jnp.sum(hidden_grad,axis=0)
    unit_low=low(pull(norm_back(hidden_grad,hidden_normal,hidden_inverse,hidden_gain))[0])
    up_shift_grad=jnp.sum(unit_low.astype(jnp.float32),axis=0)
    d_up=low(mm("nd,ntf->tdf",second_low,unit_low.reshape(R,T,cf)))
    second_grad=mm("ntf,tdf->nd",unit_low.reshape(R,T,cf),Wu)
    middle_grad=out_grad+norm_back(second_grad,second_normal,second_inverse,second_gain)
    second_gain_grad=jnp.sum(second_grad*second_normal,axis=0)
    second_shift_grad=jnp.sum(second_grad,axis=0)
    middle_low=low(middle_grad)
    output_shift_grad=jnp.sum(middle_low.astype(jnp.float32),axis=0)
    d_out=low(mm("nd,nte->tde",middle_low,inner_low.reshape(R,T,c2)))
    inner_grad=mm("nd,tde->nte",middle_low,Wo).reshape(R,D)
    mixed_gain_grad=jnp.sum(inner_grad*mixed_normal,axis=0)
    mixed_shift_grad=jnp.sum(inner_grad,axis=0)
    mixed_low=low(norm_back(inner_grad,mixed_normal,mixed_inverse,mixed_gain))
    g=out_rows(mixed_low.reshape(R,HP,1,PAIR),1)[:,0]
    dW2=jnp.concatenate([d_out,d_up,d_down],axis=2)
    g,dW2=lax.optimization_barrier((g,dW2))
    dw2=lax.psum_scatter(dW2.reshape(T*D,c2+2*cf),ALL,scatter_dimension=0,tiled=True)
    dq,dk,dv=attend_bwd(q,k,v,g,o,lse,ids_mine)
    dqkv=in_rows(jnp.stack([dq,dk,dv],axis=1),3)
    sums=jnp.sum(dqkv.astype(jnp.float32),axis=1)
    dcat=dqkv.reshape(3,R,T,c1)
    dW1=low(mm("nd,wnte->tdwe",first_low,dcat)).reshape(T,D,3*c1)
    dW1,dw2=lax.optimization_barrier((dW1,dw2))
    dw1=lax.psum_scatter(dW1.reshape(T*D,3*c1),ALL,scatter_dimension=0,tiled=True)
    first_grad=mm("wnte,wtde->nd",dcat,W1)
    input_grad=middle_grad+norm_back(first_grad,first_normal,first_inverse,first_gain)
    first_gain_grad=jnp.sum(first_grad*first_normal,axis=0)
    first_shift_grad=jnp.sum(first_grad,axis=0)
    loss,*vectors=lax.psum((loss_part,first_gain_grad,first_shift_grad,sums[0],sums[2],mixed_gain_grad,mixed_shift_grad,output_shift_grad,
                     second_gain_grad,second_shift_grad,up_shift_grad,hidden_gain_grad,hidden_shift_grad,down_shift_grad),
                    ("shard","context","tensor"))
    dw1=dw1.astype(jnp.float32); dw2=dw2.astype(jnp.float32)
    return (result.reshape(ns,n,D),loss/valid_count,input_grad.reshape(ns,n,D),
            dw1[:,:c1],dw1[:,c1:2*c1],dw1[:,2*c1:],dw2[:,:c2].T,dw2[:,c2:c2+cf],dw2[:,c2+cf:].T)+tuple(vectors)


def solution(mesh):
    rows=P("shard",("context","tensor"),None)
    ids=P("shard",("context","tensor"))
    wide=P(("shard","context"),"tensor")
    tall=P("tensor",("shard","context"))
    weights=(wide,wide,wide,tall,wide,tall)
    return jax.shard_map(shards,mesh=mesh,in_specs=(rows,rows,ids,ids)+weights+(P(),)*13,
                         out_specs=(rows,P(),rows)+weights+(P(),)*13,check_vma=False)
```

```python
import functools

import jax
import jax.numpy as jnp
from jax import lax
from jax.experimental import pallas as pl
from jax.experimental.pallas import tpu as pltpu
from jax.sharding import PartitionSpec as P


NEG=-1e30
def _dot(a,b,ca,cb):
    return lax.dot_general(a,b,(((ca,),(cb,)),((),())),preferred_element_type=jnp.float32)

def half_masks(rows):
    lane=lax.broadcasted_iota(jnp.int32,(rows,128),1)
    return lane<64

def fwd_kernel(lo_ref,hi_ref,q_ref,k_ref,v_ref,col_ref,row_ref,o_ref,lse_ref,acc_ref,m_ref,l_ref):
    s=pl.program_id(0); i=pl.program_id(1)
    bq=acc_ref.shape[1]; bk=row_ref.shape[-1]; n=k_ref.shape[2]; per=bk//n
    left=half_masks(bq)
    q=q_ref[...].reshape(bq,128)*jnp.bfloat16(0.125)
    zero=jnp.zeros_like(q)
    qs=(jnp.where(left,q,zero),jnp.where(left,zero,q))
    col=col_ref[0]
    for h in range(2):
        acc_ref[h]=jnp.zeros((bq,128),jnp.float32)
        m_ref[h]=jnp.full((bq,128),NEG,jnp.float32)
        l_ref[h]=jnp.zeros((bq,128),jnp.float32)
    def step(j,_):
        k=k_ref[pl.ds(j*per,per),0].reshape(bk,128)
        v=v_ref[pl.ds(j*per,per),0].reshape(bk,128)
        same=col==row_ref[0,j]
        for h in range(2):
            sc=jnp.where(same,_dot(qs[h],k,1,1),NEG)
            old=m_ref[h]
            top=jnp.maximum(old,jnp.max(sc,axis=1,keepdims=True))
            e=jnp.exp(sc-jnp.concatenate([top]*(bk//128),axis=1))
            a=jnp.exp(old-top)
            l_ref[h]=l_ref[h]*a+jnp.sum(e,axis=1,keepdims=True)
            m_ref[h]=top
            acc_ref[h]=acc_ref[h]*a+_dot(e.astype(jnp.bfloat16),v,1,0)
        return 0
    lax.fori_loop(lo_ref[s,i],hi_ref[s,i],step,0)
    o=jnp.where(left,acc_ref[0]/l_ref[0],acc_ref[1]/l_ref[1])
    o_ref[...]=o.astype(jnp.bfloat16).reshape(o_ref.shape)
    lse=jnp.where(left,m_ref[0]+jnp.log(l_ref[0]),m_ref[1]+jnp.log(l_ref[1]))
    lse_ref[...]=lse.reshape(lse_ref.shape)

def bounds(ids,bq,bk):
    L=ids.shape[1]
    first=ids[:,::bq]; last=ids[:,bq-1::bq]
    start=jnp.sum((ids[:,None,:]<first[:,:,None]).astype(jnp.int32),axis=2)
    end=jnp.sum((ids[:,None,:]<=last[:,:,None]).astype(jnp.int32),axis=2)
    return start//bk,(end+bk-1)//bk

def attend_fwd(q,k,v,ids,bq=256,bk=256):
    G,spg,n,_=q.shape; L=G*n
    lo,hi=bounds(ids,bq,bk)
    nq=L//bq
    col=ids[:,:,None]; row=ids.reshape(spg,L//bk,1,bk)
    qspec=pl.BlockSpec((bq//n,1,n,128),lambda s,i,*_:(i,s,0,0))
    kspec=pl.BlockSpec((G,1,n,128),lambda s,i,*_:(0,s,0,0))
    return pl.pallas_call(fwd_kernel,
        grid_spec=pltpu.PrefetchScalarGridSpec(num_scalar_prefetch=2,grid=(spg,nq),
            in_specs=[qspec,kspec,kspec,pl.BlockSpec((1,bq,1),lambda s,i,*_:(s,i,0)),pl.BlockSpec((1,L//bk,1,bk),lambda s,i,*_:(s,0,0,0))],
            out_specs=[qspec,qspec],
            scratch_shapes=[pltpu.VMEM((2,bq,128),jnp.float32)]*3),
        out_shape=[jax.ShapeDtypeStruct(q.shape,jnp.bfloat16),jax.ShapeDtypeStruct(q.shape,jnp.float32)],
        compiler_params=pltpu.CompilerParams(dimension_semantics=("arbitrary","arbitrary"),vmem_limit_bytes=48<<20),
        cost_estimate=pl.CostEstimate(flops=1000,bytes_accessed=1000,transcendentals=0),
        name="attend_fwd")(lo,hi,q,k,v,col,row)

def bwd_kernel(lo_ref,hi_ref,q_ref,k_ref,v_ref,g_ref,o_ref,lse_ref,col_ref,row_ref,dq_ref,dk_ref,dv_ref,dqa,dka,dva):
    s=pl.program_id(0); i=pl.program_id(1)
    bq=dqa.shape[1]; bk=bq; n=k_ref.shape[2]; per=bk//n
    @pl.when(i==0)
    def _():
        dka[...]=jnp.zeros_like(dka); dva[...]=jnp.zeros_like(dva)
    left=half_masks(bq)
    q=q_ref[...].reshape(bq,128)*jnp.bfloat16(0.125)
    g=g_ref[...].reshape(bq,128)
    zero=jnp.zeros_like(q)
    qs=(jnp.where(left,q,zero),jnp.where(left,zero,q))
    gs=(jnp.where(left,g,zero),jnp.where(left,zero,g))
    lse_t=lse_ref[...].reshape(bq,128).T
    d_t=(g.astype(jnp.float32)*o_ref[...].reshape(bq,128).astype(jnp.float32)).T
    lses=(lse_t[0:1],lse_t[64:65])
    ds=(jnp.sum(d_t[:64],axis=0,keepdims=True),jnp.sum(d_t[64:],axis=0,keepdims=True))
    ids_q=row_ref[0,i]
    dqa[...]=jnp.zeros_like(dqa)
    def step(j,_):
        k=k_ref[pl.ds(j*per,per),0].reshape(bk,128)
        v=v_ref[pl.ds(j*per,per),0].reshape(bk,128)
        rows=pl.ds(pl.multiple_of(j*bk,bk),bk)
        same=col_ref[0,rows,:]==ids_q
        dk=dka[rows,:]; dv=dva[rows,:]
        for h in range(2):
            st=_dot(k,qs[h],1,1)
            p=jnp.exp(jnp.where(same,st,NEG)-lses[h])
            dp=_dot(v,gs[h],1,1)
            d=(p*(dp-ds[h])).astype(jnp.bfloat16)
            dv=dv+_dot(p.astype(jnp.bfloat16),gs[h],1,0)
            dk=dk+_dot(d,qs[h],1,0)
            dqa[h]+=_dot(d,k,0,0)
        dka[rows,:]=dk; dva[rows,:]=dv
        return 0
    lax.fori_loop(lo_ref[s,i],hi_ref[s,i],step,0)
    dq_ref[...]=(jnp.where(left,dqa[0],dqa[1])*0.125).astype(jnp.bfloat16).reshape(dq_ref.shape)
    @pl.when(i==pl.num_programs(1)-1)
    def _():
        dk_ref[...]=dka[...].astype(jnp.bfloat16).reshape(dk_ref.shape)
        dv_ref[...]=dva[...].astype(jnp.bfloat16).reshape(dv_ref.shape)

def attend_bwd(q,k,v,g,o,lse,ids,bq=256):
    bk=bq
    G,spg,n,_=q.shape; L=G*n
    lo,hi=bounds(ids,bq,bk)
    nq=L//bq
    col=ids[:,:,None]; row=ids.reshape(spg,L//bk,1,bk)
    qspec=pl.BlockSpec((bq//n,1,n,128),lambda s,i,*_:(i,s,0,0))
    kspec=pl.BlockSpec((G,1,n,128),lambda s,i,*_:(0,s,0,0))
    out=jax.ShapeDtypeStruct(q.shape,jnp.bfloat16)
    return pl.pallas_call(bwd_kernel,
        grid_spec=pltpu.PrefetchScalarGridSpec(num_scalar_prefetch=2,grid=(spg,nq),
            in_specs=[qspec,kspec,kspec,qspec,qspec,qspec,pl.BlockSpec((1,L,1),lambda s,i,*_:(s,0,0)),pl.BlockSpec((1,L//bk,1,bk),lambda s,i,*_:(s,0,0,0))],
            out_specs=[qspec,kspec,kspec],
            scratch_shapes=[pltpu.VMEM((2,bq,128),jnp.float32)]+[pltpu.VMEM((L,128),jnp.float32)]*2),
        out_shape=[out]*3,
        compiler_params=pltpu.CompilerParams(dimension_semantics=("arbitrary","arbitrary"),vmem_limit_bytes=48<<20),
        cost_estimate=pl.CostEstimate(flops=1000,bytes_accessed=1000,transcendentals=0),
        name="attend_bwd")(lo,hi,q,k,v,g,o,lse,col,row)


EPS=1e-5
PAIR=128

def norm_parts(v):
    m=jnp.mean(v,axis=-1,keepdims=True)
    s=jnp.mean(v*v,axis=-1,keepdims=True)-m*m
    r=lax.rsqrt(s+EPS)
    return (v-m)*r,r

def norm_back(e,h,r,gain):
    t=e*gain
    return r*(t-jnp.mean(t,axis=-1,keepdims=True)-h*jnp.mean(t*h,axis=-1,keepdims=True))


MESH_ID=pl.DeviceIdType.MESH

class Place:
    def __init__(self,S,C,T):
        self.CC=2 if C%2==0 else 1
        self.size={"t":T,"s":S,"x":C//self.CC,"c":self.CC}
        c=lax.axis_index("context")
        self.at={"t":lax.axis_index("tensor"),"s":lax.axis_index("shard"),"x":c//self.CC,"c":lax.rem(c,self.CC)}
        self.group=c*T+self.at["t"]
        self.T=T; self.G=C*T
    def peers(self,axis):
        m=self.size[axis]
        for d in range(1,m):
            other=lax.rem(self.at[axis]+d,m)
            if axis=="t": yield d-1,other,{"tensor":other}
            elif axis=="s": yield d-1,other,{"shard":other}
            elif axis=="x": yield d-1,other,{"context":other*self.CC+self.at["c"]}
            else: yield d-1,other,{"context":self.at["x"]*self.CC+other}
    def group_peers(self):
        for d in range(1,self.G):
            other=lax.rem(self.group+d,self.G)
            yield d-1,other,{"context":other//self.T,"tensor":lax.rem(other,self.T)}

def slots(size,order):
    base,total={},0
    for a in order:
        base[a]=total; total+=size[a]-1
    return base,total

def greet(place):
    barrier=pltpu.get_barrier_semaphore()
    count=0
    for _,_,dev in place.group_peers():
        pl.semaphore_signal(barrier,inc=1,device_id=dev,device_id_type=MESH_ID); count+=1
    for _,_,dev in place.peers("s"):
        pl.semaphore_signal(barrier,inc=1,device_id=dev,device_id_type=MESH_ID); count+=1
    pl.semaphore_wait(barrier,count)

def remote(src,dst,send,recv,dev):
    return pltpu.make_async_remote_copy(src_ref=src,dst_ref=dst,send_sem=send,recv_sem=recv,device_id=dev,device_id_type=MESH_ID)

def project_kernel(S,C,T,x_ref,gain_ref,shift_ref,wq_ref,wk_ref,wv_ref,bias_ref,ids_ref,wo_ref,wu_ref,wd_ref,
                   low_ref,rows_ref,wide_ref,allids_ref,pa_ref,pb_ref,
                   zbuf,z_send,z_recv,p_send,p_recv,wbuf,obuf,idbuf,ag_send,ag_recv,a_send,a_recv,i_send,i_recv,local):
    place=Place(S,C,T)
    R,D=low_ref.shape
    G,spg,n=rows_ref.shape[1:4]
    HP=D//PAIR; SG=G//HP
    cols=wbuf.shape[-1]; hpt=cols//PAIR
    me=place.group
    order="tsxc"
    base,total=slots(place.size,order)
    own=[place.at[a] for a in order]
    for w,ref in enumerate((wq_ref,wk_ref,wv_ref)):
        wbuf[w,own[0],own[1],own[2],own[3]]=ref[...].astype(jnp.bfloat16)
    t0=place.at["t"]
    HR,c2=zbuf.shape[-2:]
    c0=wo_ref.shape[0]; cf=wu_ref.shape[1]
    zbuf[t0,:,:,0:c0]=wo_ref[...].T.astype(jnp.bfloat16).reshape(2,HR,c0)
    zbuf[t0,:,:,c0:c0+cf]=wu_ref[...].astype(jnp.bfloat16).reshape(2,HR,cf)
    zbuf[t0,:,:,c0+cf:]=wd_ref[...].T.astype(jnp.bfloat16).reshape(2,HR,cf)
    def hop(way,h,piece):
        to=t0+1 if way==0 else t0-1
        return remote(zbuf.at[piece],zbuf.at[piece],z_send.at[way,h-1],z_recv.at[way,h-1],{"tensor":lax.rem(to+T,T)})
    def line_start():
        @pl.when(t0<T-1)
        def _(): hop(0,1,t0).start()
        @pl.when(t0>0)
        def _(): hop(1,1,t0).start()
    def line_pass(h):
        @pl.when(t0>=h)
        def _():
            hop(0,h,lax.rem(t0-h+T,T)).wait_recv()
            @pl.when(t0<T-1)
            def _(): hop(0,h+1,lax.rem(t0-h+T,T)).start()
        @pl.when(t0+h<=T-1)
        def _():
            hop(1,h,lax.rem(t0+h,T)).wait_recv()
            @pl.when(t0>0)
            def _(): hop(1,h+1,lax.rem(t0+h,T)).start()
    def line_end():
        for h in range(1,T):
            @pl.when((t0<T-1)&(t0>=h-1))
            def _(): hop(0,h,lax.rem(t0-h+1+T,T)).wait_send()
            @pl.when((t0>0)&(t0+h-1<=T-1))
            def _(): hop(1,h,lax.rem(t0+h-1,T)).wait_send()
    def plane():
        a=pltpu.make_async_copy(zbuf.at[:,0],pa_ref.at[place.at["x"]],local.at[8]); a.start()
        b=pltpu.make_async_copy(zbuf.at[:,1],pb_ref.at[place.at["s"]],local.at[9]); b.start()
        out=[a,b]
        for k,_,dev in place.peers("x"):
            c=remote(zbuf.at[:,0],pa_ref.at[place.at["x"]],p_send.at[0,k],p_recv.at[0,k],dev); c.start(); sent.append(c); out.append(c)
        for k,_,dev in place.peers("s"):
            c=remote(zbuf.at[:,1],pb_ref.at[place.at["s"]],p_send.at[1,k],p_recv.at[1,k],dev); c.start(); sent.append(c); out.append(c)
        return out
    greet(place)
    stages={2:"tsxc",1:"txsc",0:"tsxc"}
    sent=[]
    copies={}
    def start(w,r):
        done=stages[w][:r]; axis=stages[w][r]
        idx=tuple(slice(None) if a in done else place.at[a] for a in order)
        copies[w,r]=[]
        for k,_,dev in place.peers(axis):
            c=remote(wbuf.at[(w,)+idx],wbuf.at[(w,)+idx],ag_send.at[w,base[axis]+k],ag_recv.at[w,base[axis]+k],dev)
            c.start(); copies[w,r].append(c); sent.append(c)
    def arrive(w,r):
        for c in copies[w,r]: c.wait_recv()
    for w in (2,1,0): start(w,0)
    line_start()
    ids_own=pltpu.make_async_copy(ids_ref,idbuf.at[place.at["s"]],local.at[0]); ids_own.start()
    id_first=[]
    for k,_,dev in place.peers("s"):
        c=remote(ids_ref,idbuf.at[place.at["s"]],i_send.at[k],i_recv.at[k],dev); c.start(); id_first.append(c); sent.append(c)
    step=min(64,R)
    def norm(i,_):
        rows=pl.ds(pl.multiple_of(i*step,step),step)
        h,_r=norm_parts(x_ref[rows,:])
        low_ref[rows,:]=(h*gain_ref[...]+shift_ref[...]).astype(jnp.bfloat16)
        return 0
    lax.fori_loop(0,R//step,norm,0)
    def spread_ids():
        ids_own.wait()
        for c in id_first: c.wait_recv()
        out=[]
        mine=pltpu.make_async_copy(idbuf,allids_ref.at[me],local.at[1]); mine.start(); out.append(mine)
        for k,_,dev in place.group_peers():
            c=remote(idbuf,allids_ref.at[me],i_send.at[S-1+k],i_recv.at[S-1+k],dev); c.start(); sent.append(c); out.append(c)
        return out
    late=[]
    def compute(w):
        def one(t,_):
            y=_dot(low_ref[...],wbuf[w,t].reshape(D,cols),1,0)+bias_ref[w,t]
            y=y.astype(jnp.bfloat16)
            for g in range(SG):
                for j in range(hpt):
                    obuf[w,g*HP+t*hpt+j]=y[g*spg*n:(g+1)*spg*n,j*PAIR:(j+1)*PAIR].reshape(spg,n,PAIR)
            return 0
        lax.fori_loop(0,T,one,0)
        mine=pltpu.make_async_copy(obuf.at[w,me],rows_ref.at[w,me],local.at[2+w]); mine.start(); late.append(mine)
        for k,other,dev in place.group_peers():
            c=remote(obuf.at[w,other],rows_ref.at[w,me],a_send.at[w,k],a_recv.at[w,k],dev)
            c.start(); sent.append(c); late.append(c)
        keep=pltpu.make_async_copy(wbuf.at[w],wide_ref.at[w],local.at[5+w]); keep.start(); late.append(keep)
    arrive(2,0); start(2,1)
    arrive(1,0); start(1,1)
    ids_out=spread_ids()
    arrive(2,1); start(2,2)
    arrive(1,1); start(1,2)
    arrive(0,0); start(0,1)
    arrive(2,2); start(2,3)
    line_pass(1)
    arrive(2,3); compute(2)
    arrive(1,2); start(1,3)
    arrive(0,1); start(0,2)
    arrive(1,3); compute(1)
    if T>2: line_pass(2)
    arrive(0,2); start(0,3)
    arrive(0,3); compute(0)
    for h in range(3,T): line_pass(h)
    ids_out=ids_out+plane()
    for c in late+ids_out:
        if any(c is o for o in sent): c.wait_recv()
        else: c.wait()
    for c in sent: c.wait_send()
    line_end()

def project(S,C,T,x,gain,shift,wq,wk,wv,bias,ids,wo,wu,wd,ns,n):
    R,D=x.shape
    G=C*T; HP=D//PAIR; spg=ns*HP//G
    DR,cols=wq.shape
    CC=2 if C%2==0 else 1
    piece=(3,T,S,C//CC,CC,DR,cols)
    HR=DR//2; width=wo.shape[0]+2*wu.shape[1]; most=max(S,C//CC)-1
    _,total=slots({"t":T,"s":S,"x":C//CC,"c":CC},"tsxc")
    vm=pl.BlockSpec(memory_space=pltpu.VMEM); anyspec=pl.BlockSpec(memory_space=pl.ANY)
    dma=pltpu.SemaphoreType.DMA
    return pl.pallas_call(functools.partial(project_kernel,S,C,T),
        in_specs=[vm]*11,
        out_specs=[vm]+[anyspec]*5,
        out_shape=[jax.ShapeDtypeStruct((R,D),jnp.bfloat16),jax.ShapeDtypeStruct((3,G,spg,n,PAIR),jnp.bfloat16),
                   jax.ShapeDtypeStruct(piece,jnp.bfloat16),jax.ShapeDtypeStruct((G,S,1,ns*n),jnp.int32),
                   jax.ShapeDtypeStruct((C//CC,T,HR,width),jnp.bfloat16),jax.ShapeDtypeStruct((S,T,HR,width),jnp.bfloat16)],
        scratch_shapes=[pltpu.VMEM((T,2,HR,width),jnp.bfloat16),dma((2,T-1)),dma((2,T-1)),dma((2,most)),dma((2,most)),pltpu.VMEM(piece,jnp.bfloat16),pltpu.VMEM((3,G,spg,n,PAIR),jnp.bfloat16),pltpu.VMEM((S,1,ns*n),jnp.int32),
                        dma((3,total)),dma((3,total)),dma((3,G-1)),dma((3,G-1)),dma((S-1+G-1,)),dma((S-1+G-1,)),dma((10,))],
        compiler_params=pltpu.CompilerParams(collective_id=0,has_side_effects=True,vmem_limit_bytes=40<<20),
        name="project")(x,gain,shift,wq,wk,wv,bias,ids,wo,wu,wd)


def feed_kernel(S,C,T,NC,*refs):
    place=Place(S,C,T)
    CX=place.size["x"]; CC=place.CC
    o_ref=refs[0]; wa_refs=refs[1:1+S]; wb_refs=refs[1+S:1+S+CX]
    (x_ref,teach_ref,keep_ref,scale_ref,vec_ref,wide_ref)=refs[1+S+CX:7+S+CX]
    (res_ref,mg_ref,g_ref,inner_ref,second_ref,out_ref,midl_ref,hid_ref,unl_ref,sum_ref)=refs[7+S+CX:17+S+CX]
    (w2,rbuf,mix,inner,second,outl,midl,hid,unl,act,dact,tt,acc,middle,og,s1,s2,res,mg,gout,vacc,wacc,
     w_local,w_send,w_recv,a_send,a_recv,misc,o_sem,s1b,s2b)=refs[17+S+CX:]
    R,D=x_ref.shape
    G,spg,n=o_ref.shape[:3]
    HP=D//PAIR; SG=G//HP
    HR=w2.shape[-2]
    F=hid.shape[1]; cf=F//T; c2=D//T
    B=R//2; gpb=SG//2 if SG>1 else 1
    f32=jnp.float32; b16=jnp.bfloat16
    me=place.group
    s0,x0,c0=place.at["s"],place.at["x"],place.at["c"]
    DS=D//S
    ranges=((0,c2),(c2,c2+cf),(c2+cf,c2+2*cf))
    def pieces(r):
        lo,hi=ranges[r]
        out=[]
        for d in range(S):
            src=lax.rem(s0+S-d,S)
            for i in range(CX):
                out.append((wa_refs[d].at[i,:,:,lo:hi],w2.at[:,src,i,c0,0,:,lo:hi]))
        for d in range(CX):
            src=lax.rem(x0+CX-d,CX)
            for i in range(S):
                out.append((wb_refs[d].at[i,:,:,lo:hi],w2.at[:,i,src,c0,1,:,lo:hi]))
        return out
    local=[[pltpu.make_async_copy(a,b,w_local.at[r,i]) for i,(a,b) in enumerate(pieces(r))] for r in range(3)]
    for r in range(3):
        for c in local[r]: c.start()
    barrier=pltpu.get_barrier_semaphore()
    count=0
    for _,_,dev in place.group_peers():
        pl.semaphore_signal(barrier,inc=1,device_id=dev,device_id_type=MESH_ID); count+=1
    pl.semaphore_wait(barrier,count)
    own=pltpu.make_async_copy(o_ref.at[me],rbuf.at[me],misc.at[0]); own.start()
    rows_in=[remote(o_ref.at[other],rbuf.at[me],a_send.at[k],a_recv.at[k],dev) for k,other,dev in place.group_peers()]
    for c in rows_in: c.start()
    far=[[remote(a,b,w_send.at[r,k,i],w_recv.at[r,k,i],dev) for k,_,dev in place.peers("c") for i,(a,b) in enumerate(pieces(r))] for r in range(3)]
    for r in range(3):
        for c in far[r]: c.start()
    def weights(r):
        for c in local[r]: c.wait()
        for c in far[r]: c.wait_recv()
    sum_ref[...]=jnp.zeros_like(sum_ref)
    vacc[...]=jnp.zeros_like(vacc); wacc[...]=jnp.zeros_like(wacc)
    own.wait()
    for c in rows_in: c.wait_recv()
    def vec(i): return vec_ref[i:i+1,:]
    MIXG,MIXS,OUTS,SECG,SECS,DOWNS=range(6)
    sub=min(32,B)
    def each(fn):
        def body(i,_):
            fn(pl.ds(pl.multiple_of(i*sub,sub),sub),i)
            return 0
        lax.fori_loop(0,B//sub,body,0)
    def fold(a):
        return jnp.sum(a.reshape(sub//8,8,a.shape[1]),axis=0)
    def lanes(a):
        v=a[:,:PAIR]
        for j in range(1,a.shape[1]//PAIR): v=v+a[:,j*PAIR:(j+1)*PAIR]
        return v
    def flat(t,lo,hi,s=None):
        if s is None: return w2[t,:,:,:,:,:,lo:hi].reshape(D,hi-lo)
        return w2[t,s,:,:,:,:,lo:hi].reshape(DS,hi-lo)
    weights(0)
    def block(b):
        r0=b*B
        def rows(i): return pl.ds(pl.multiple_of(r0+i*sub,sub),sub)
        whole=pl.ds(pl.multiple_of(r0,B),B)
        for gg in range(gpb):
            for h in range(HP):
                mix[gg*spg*n:(gg+1)*spg*n,h*PAIR:(h+1)*PAIR]=rbuf[(b*gpb+gg)*HP+h].reshape(spg*n,PAIR)
        def f1(q,i):
            h,_=norm_parts(mix[q,:].astype(f32))
            inner[rows(i),:]=(h*vec(MIXG)+vec(MIXS)).astype(b16)
        each(f1)
        acc[...]=jnp.zeros_like(acc)
        def att(t,_):
            a=inner[whole,pl.ds(pl.multiple_of(t*c2,128),c2)]
            for s in range(S):
                acc[:,s*DS:(s+1)*DS]+=_dot(a,flat(t,0,c2,s),1,1)
            return 0
        lax.fori_loop(0,T,att,0)
        def f2(q,i):
            m=x_ref[rows(i),:]+(acc[q,:]+vec(OUTS))
            middle[q,:]=m
            h,_=norm_parts(m)
            second[rows(i),:]=(h*vec(SECG)+vec(SECS)).astype(b16)
        each(f2)
        if b==0: weights(1)
        s1[...]=jnp.zeros_like(s1); s2[...]=jnp.zeros_like(s2)
        def up(t,_):
            a=second[whole,:]
            for j in range(NC):
                w=cf//NC
                act[t,:,j*w:(j+1)*w]=_dot(a,flat(t,c2+j*w,c2+(j+1)*w),1,0)
            def e(q,i):
                u=act[t,q,:]+wide_ref[t,0:1,:]
                u2=u*u
                th=jnp.tanh(0.7978845608028654*u*(1.0+0.044715*u2))
                half=0.5+0.5*th
                a=u*half
                act[t,q,:]=a
                dact[t,q,:]=half+(0.5*0.7978845608028654)*u*(1.0-th*th)*(1.0+(3*0.044715)*u2)
                s1[q,:]+=lanes(a); s2[q,:]+=lanes(a*a)
            each(e)
            return 0
        lax.fori_loop(0,T,up,0)
        def f3(q,i):
            m=jnp.sum(s1[q,:],axis=1,keepdims=True)/F
            v=jnp.sum(s2[q,:],axis=1,keepdims=True)/F-m*m
            s1[q,:]=jnp.broadcast_to(m,(sub,PAIR)); s2[q,:]=jnp.broadcast_to(lax.rsqrt(v+EPS),(sub,PAIR))
        each(f3)
        if b==0: weights(2)
        acc[...]=jnp.zeros_like(acc)
        def down(t,_):
            fcols=pl.ds(pl.multiple_of(t*cf,128),cf)
            def e(q,i):
                h=(act[t,q,:]-s1[q,0:1])*s2[q,0:1]
                act[t,q,:]=h
                hid[rows(i),fcols]=(h*wide_ref[t,1:2,:]+wide_ref[t,2:3,:]).astype(b16)
            each(e)
            a=hid[whole,fcols]
            for s in range(S):
                acc[:,s*DS:(s+1)*DS]+=_dot(a,flat(t,c2+cf,c2+2*cf,s),1,1)
            return 0
        lax.fori_loop(0,T,down,0)
        def f4(q,i):
            r=middle[q,:]+(acc[q,:]+vec(DOWNS))
            res[rows(i),:]=r
            err=r-teach_ref[rows(i),:]
            k=keep_ref[rows(i),:]
            e=k*err
            vacc[6]+=fold(e*err)
            g=e*scale_ref[0:1,0:1]
            og[q,:]=g
            low_=g.astype(b16)
            outl[rows(i),:]=low_
            vacc[5]+=fold(low_.astype(f32))
        each(f4)
        def back1(t,_):
            a=outl[whole,:]
            for j in range(NC):
                w=cf//NC
                tt[t,:,j*w:(j+1)*w]=_dot(a,flat(t,c2+cf+j*w,c2+cf+(j+1)*w),1,0)
            def e(q,i):
                g=tt[t,q,:]; h=act[t,q,:]
                wacc[0,t]+=fold(g*h); wacc[1,t]+=fold(g)
                v=g*wide_ref[t,1:2,:]
                tt[t,q,:]=v
                s1b[q,:]+=lanes(v); s2b[q,:]+=lanes(v*h)
            each(e)
            return 0
        s1b[...]=jnp.zeros_like(s1b); s2b[...]=jnp.zeros_like(s2b)
        lax.fori_loop(0,T,back1,0)
        def f5(q,i):
            s1b[q,:]=jnp.broadcast_to(jnp.sum(s1b[q,:],axis=1,keepdims=True)/F,(sub,PAIR))
            s2b[q,:]=jnp.broadcast_to(jnp.sum(s2b[q,:],axis=1,keepdims=True)/F,(sub,PAIR))
        each(f5)
        acc[...]=jnp.zeros_like(acc)
        def back2(t,_):
            fcols=pl.ds(pl.multiple_of(t*cf,128),cf)
            def e(q,i):
                ag=s2[q,0:1]*(tt[t,q,:]-s1b[q,0:1]-act[t,q,:]*s2b[q,0:1])
                ul=(ag*dact[t,q,:]).astype(b16)
                unl[rows(i),fcols]=ul
                wacc[2,t]+=fold(ul.astype(f32))
            each(e)
            a=unl[whole,fcols]
            for s in range(S):
                acc[:,s*DS:(s+1)*DS]+=_dot(a,flat(t,c2,c2+cf,s),1,1)
            return 0
        lax.fori_loop(0,T,back2,0)
        def f6(q,i):
            h,r=norm_parts(middle[q,:])
            e=acc[q,:]
            vacc[3]+=fold(e*h); vacc[4]+=fold(e)
            m=og[q,:]+norm_back(e,h,r,vec(SECG))
            mg[rows(i),:]=m
            ml=m.astype(b16)
            midl[rows(i),:]=ml
            vacc[2]+=fold(ml.astype(f32))
        each(f6)
        def back3(t,_):
            acc[:,pl.ds(pl.multiple_of(t*c2,128),c2)]=_dot(midl[whole,:],flat(t,0,c2),1,0)
            return 0
        lax.fori_loop(0,T,back3,0)
        def f7(q,i):
            h,r=norm_parts(mix[q,:].astype(f32))
            e=acc[q,:]
            vacc[0]+=fold(e*h); vacc[1]+=fold(e)
            mix[q,:]=norm_back(e,h,r,vec(MIXG)).astype(b16)
        each(f7)
        for gg in range(gpb):
            for h in range(HP):
                gout[(b*gpb+gg)*HP+h]=mix[gg*spg*n:(gg+1)*spg*n,h*PAIR:(h+1)*PAIR].reshape(spg,n,PAIR)
        copies=[pltpu.make_async_copy(src.at[whole],dst.at[whole],o_sem.at[b,i]) for i,(src,dst) in enumerate(
            ((res,res_ref),(mg,mg_ref),(inner,inner_ref),(second,second_ref),(outl,out_ref),(midl,midl_ref),(hid,hid_ref),(unl,unl_ref)))]
        gs=pl.ds(b*gpb*HP,gpb*HP)
        copies.append(pltpu.make_async_copy(gout.at[gs],g_ref.at[gs],o_sem.at[b,8]))
        for c in copies: c.start()
        return copies
    done=[]
    for b in range(2): done+=block(b)
    for i in range(7):
        sum_ref[i:i+1,:]=jnp.sum(vacc[i],axis=0,keepdims=True)
    for i in range(3):
        for t in range(T):
            at=(i*F+t*cf)
            sum_ref[7+at//D:8+at//D,at%D:at%D+cf]=jnp.sum(wacc[i,t],axis=0,keepdims=True)
    for c in done: c.wait()
    for c in rows_in: c.wait_send()
    for r in range(3):
        for c in far[r]: c.wait_send()

def feed(S,C,T,o,wa,wb,x,teacher,keep,scale,vecs,wides):
    R,D=x.shape
    G,spg,n=o.shape[:3]
    CC=2 if C%2==0 else 1
    CX=C//CC
    HR,c2=wa[0].shape[-2:]
    cf=wides.shape[-1]; F=cf*T; B=R//2
    b16,f32=jnp.bfloat16,jnp.float32
    vm=pl.BlockSpec(memory_space=pltpu.VMEM); anyspec=pl.BlockSpec(memory_space=pl.ANY)
    dma=pltpu.SemaphoreType.DMA
    V=lambda shape,dt=b16: pltpu.VMEM(shape,dt)
    NP=2*S*CX; NCC=max(CC-1,1)
    sums=7+3*F//D; sums+=-sums%8
    sds=jax.ShapeDtypeStruct
    return pl.pallas_call(functools.partial(feed_kernel,S,C,T,max(cf//512,1)),
        in_specs=[anyspec]*(1+S+CX)+[vm]*6,
        out_specs=[anyspec]*9+[vm],
        out_shape=[sds((R,D),f32),sds((R,D),f32),sds(o.shape,b16)]+[sds((R,D),b16)]*4+[sds((R,F),b16)]*2+[sds((sums,D),f32)],
        scratch_shapes=[V((T,S,CX,CC,2,HR,c2)),V(o.shape),V((B,D)),V((R,D)),V((R,D)),V((R,D)),V((R,D)),V((R,F)),V((R,F)),
                        V((T,B,cf),f32),V((T,B,cf),f32),V((T,B,cf),f32),V((B,D),f32),V((B,D),f32),V((B,D),f32),V((B,PAIR),f32),V((B,PAIR),f32),
                        V((R,D),f32),V((R,D),f32),V(o.shape),V((7,8,D),f32),V((3,T,8,cf),f32),
                        dma((3,NP)),dma((3,NCC,NP)),dma((3,NCC,NP)),dma((G-1,)),dma((G-1,)),dma((1,)),dma((2,9)),V((B,PAIR),f32),V((B,PAIR),f32)],
        compiler_params=pltpu.CompilerParams(collective_id=3,has_side_effects=True,vmem_limit_bytes=63<<20),
        name="feed")(o,*wa,*wb,x,teacher,keep,scale,vecs,wides)


def weight_grads_kernel(S,C,T,out_ref,second_ref,middle_ref,inner_ref,unit_ref,hidden_ref,g_ref,*rest):
    CX0=C//(2 if C%2==0 else 1)
    pa_refs,pb_refs=rest[:S],rest[S:S+CX0]
    gin_ref,own,got,send,recv,local,a_send,a_recv,a_local=rest[S+CX0:]
    place=Place(S,C,T)
    R,D=out_ref.shape
    CX=place.size["x"]; CC=place.CC
    HR,width=own.shape[-2:]
    c2=inner_ref.shape[1]//T; cf=unit_ref.shape[1]//T
    cc=place.at["c"]
    barrier=pltpu.get_barrier_semaphore()
    others=list(place.peers("c"))
    count=0
    for _,_,dev in place.group_peers():
        pl.semaphore_signal(barrier,inc=1,device_id=dev,device_id_type=MESH_ID); count+=1
    pl.semaphore_wait(barrier,count)
    me=place.group
    mine=pltpu.make_async_copy(g_ref.at[me],gin_ref.at[me],a_local.at[0]); mine.start()
    rows_in=[remote(g_ref.at[other],gin_ref.at[me],a_send.at[k],a_recv.at[k],dev) for k,other,dev in place.group_peers()]
    for c in rows_in: c.start()
    plan=[(middle_ref,inner_ref,0,c2,c2),(second_ref,unit_ref,c2,cf,min(cf,512)),(out_ref,hidden_ref,c2+cf,cf,min(cf,512))]
    def swap(t):
        return [remote(own.at[t,:,:,other],got.at[t,k],send.at[t,k],recv.at[t,k],dev) for k,other,dev in others]
    def outs(t):
        a=[pltpu.make_async_copy(got.at[t,0,lax.rem(place.at["s"]+d,S),:,0],pa_refs[d].at[t],local.at[t,d]) for d in range(S)]
        b=[pltpu.make_async_copy(got.at[t,0,:,lax.rem(place.at["x"]+d,CX),1],pb_refs[d].at[t],local.at[t,S+d]) for d in range(CX)]
        return a+b
    def settle(t):
        for c in swap(t): c.wait_recv()
        for s in range(S):
            for x in range(CX):
                total=own[t,s,x,cc].astype(jnp.float32)
                for k,_,_ in others:
                    total=total+got[t,k,s,x].astype(jnp.float32)
                got[t,0,s,x]=total.astype(jnp.bfloat16)
        for c in outs(t): c.start()
    def one(t,_):
        for left,right,base,cols,chunk in plan:
            for j in range(cols//chunk):
                y=_dot(left[...],right[:,pl.ds(pl.multiple_of(t*cols+j*chunk,128),chunk)],0,0)
                own[t,:,:,:,:,:,base+j*chunk:base+(j+1)*chunk]=y.astype(jnp.bfloat16).reshape(S,CX,CC,2,HR,chunk)
        for c in swap(t): c.start()
        @pl.when(t>0)
        def _(): settle(t-1)
        return 0
    lax.fori_loop(0,T,one,0)
    settle(T-1)
    def finish(t,_):
        for c in swap(t): c.wait_send()
        for c in outs(t): c.wait()
        return 0
    lax.fori_loop(0,T,finish,0)
    mine.wait()
    for c in rows_in: c.wait()

def weight_grads(S,C,T,out_low,second_low,middle_low,inner_low,unit_low,hidden_low,g):
    R,D=out_low.shape
    CC=2 if C%2==0 else 1
    CX=C//CC; HR=D//(S*C*2); width=(D+2*unit_low.shape[1])//T
    vm=pl.BlockSpec(memory_space=pltpu.VMEM); anyspec=pl.BlockSpec(memory_space=pl.ANY)
    dma=pltpu.SemaphoreType.DMA
    return pl.pallas_call(functools.partial(weight_grads_kernel,S,C,T),
        in_specs=[vm]*6+[anyspec],out_specs=[anyspec]*(S+CX+1),
        out_shape=[jax.ShapeDtypeStruct((T,CX,HR,width),jnp.bfloat16)]*S+[jax.ShapeDtypeStruct((T,S,HR,width),jnp.bfloat16)]*CX+[jax.ShapeDtypeStruct(g.shape,jnp.bfloat16)],
        scratch_shapes=[pltpu.VMEM((T,S,CX,CC,2,HR,width),jnp.bfloat16),pltpu.VMEM((T,max(CC-1,1),S,CX,2,HR,width),jnp.bfloat16),
                        dma((T,max(CC-1,1))),dma((T,max(CC-1,1))),dma((T,S+CX)),dma((C*T-1,)),dma((C*T-1,)),dma((1,))],
        compiler_params=pltpu.CompilerParams(collective_id=1,has_side_effects=True,vmem_limit_bytes=60<<20),
        name="weight_grads")(out_low,second_low,middle_low,inner_low,unit_low,hidden_low,g)


def finish_kernel(S,C,T,dq_ref,dk_ref,dv_ref,low_ref,wide_ref,x_ref,mg_ref,gain_ref,early_ref,*rest):
    CX0=C//(2 if C%2==0 else 1)
    ra_refs,rb_refs=rest[:S],rest[S:S+CX0]
    finish_body(S,C,T,dq_ref,dk_ref,dv_ref,low_ref,wide_ref,x_ref,mg_ref,gain_ref,early_ref,ra_refs,rb_refs,*rest[S+CX0:])

def finish_body(S,C,T,dq_ref,dk_ref,dv_ref,low_ref,wide_ref,x_ref,mg_ref,gain_ref,early_ref,ra_refs,rb_refs,
                  grad_ref,d1_ref,d2_ref,late_ref,all_ref,
                  rbuf,wbuf,acc,gbuf,rc,ra2,rb2,ra3,rb3,zin,zrec,
                  xa,xb,ya,yb,za,zb,zra,zrb,
                  ev,ev_c,ev_s,ev_x,ev_t,lv,lv_c,lv_s,lv_x,lv_t,
                  a_send,a_recv,w_send,w_recv,g_send,g_recv,v_send,v_recv,local):
    place=Place(S,C,T)
    R,D=low_ref.shape
    G,spg,n=dq_ref.shape[:3]
    HP=D//PAIR; SG=G//HP
    cols=wbuf.shape[-1]; hpt=cols//PAIR
    DR=wbuf.shape[-2]
    CX=place.size["x"]; CC=place.CC; TH=T//2
    t0,s0,x0,c0=place.at["t"],place.at["s"],place.at["x"],place.at["c"]
    me=place.group
    f32=jnp.float32; b16=jnp.bfloat16
    sent=[]
    def go(copies):
        for c in copies: c.start()
        sent.extend(copies)
        return copies
    def land(copies):
        for c in copies: c.wait_recv()
    loads=[pltpu.make_async_copy(wide_ref,wbuf,local.at[6])]
    loads+=[pltpu.make_async_copy(ref,xa.at[i],local.at[7+i]) for i,ref in enumerate(ra_refs)]
    loads+=[pltpu.make_async_copy(ref,xb.at[i],local.at[7+S+i]) for i,ref in enumerate(rb_refs)]
    for c in loads: c.start()
    greet(place)
    rows_in=[None]*3
    mine=[None]*3
    for w,ref in ((2,dv_ref),(1,dk_ref),(0,dq_ref)):
        mine[w]=pltpu.make_async_copy(ref.at[me],rbuf.at[w,me],local.at[3+w]); mine[w].start()
        rows_in[w]=go([remote(ref.at[other],rbuf.at[w,me],a_send.at[w,k],a_recv.at[w,k],dev) for k,other,dev in place.group_peers()])

    base,total=slots(place.size,"csxt")
    def vec_start(which,axis,cur,rec):
        rec[place.at[axis]]=cur[...]
        return go([remote(cur,rec.at[place.at[axis]],v_send.at[which,base[axis]+k],v_recv.at[which,base[axis]+k],dev) for k,_,dev in place.peers(axis)])
    def vec_end(copies,cur,rec,axis):
        land(copies)
        for c in copies: c.wait_send()
        total=rec[0]
        for i in range(1,place.size[axis]): total=total+rec[i]
        cur[...]=total
    ev[...]=early_ref[...]
    e_c=vec_start(0,"c",ev,ev_c)

    for c in loads[1:]: c.wait()
    def add_a(t,_):
        v=xa[0,t].astype(f32)
        for i in range(1,S): v=v+xa[i,t].astype(f32)
        ya[t]=v.astype(b16)
        return 0
    lax.fori_loop(0,T,add_a,0)
    big_a=go([remote(ya.at[:,other],za.at[k],w_send.at[0,k],w_recv.at[0,k],dev) for k,other,dev in place.peers("x")])
    def add_b(t,_):
        v=xb[0,t].astype(f32)
        for i in range(1,CX): v=v+xb[i,t].astype(f32)
        yb[t]=v.astype(b16)
        return 0
    lax.fori_loop(0,T,add_b,0)
    big_b=go([remote(yb.at[:,other],zb.at[k],w_send.at[1,k],w_recv.at[1,k],dev) for k,other,dev in place.peers("s")])
    vec_end(e_c,ev,ev_c,"c"); e_s=vec_start(0,"s",ev,ev_s)
    loads[0].wait()

    lv[...]=jnp.zeros_like(lv)
    def compute(w,first):
        mine[w].wait(); land(rows_in[w])
        def one(t,_):
            d=jnp.concatenate([jnp.concatenate([rbuf[w,g*HP+t*hpt+j].reshape(spg*n,PAIR) for j in range(hpt)],axis=1) for g in range(SG)],axis=0)
            y=_dot(low_ref[...],d,0,0)
            gbuf[w,t]=y.astype(b16).reshape(S,CX,CC,DR,cols)
            z=_dot(d,wbuf[w,t].reshape(D,cols),1,1)
            if first:
                @pl.when(t==0)
                def _(): acc[...]=z
                @pl.when(t>0)
                def _(): acc[...]+=z
            else:
                acc[...]+=z
            if w!=1:
                lv[2+w//2:3+w//2,pl.ds(pl.multiple_of(t*cols,128),cols)]=jnp.sum(d.astype(f32),axis=0,keepdims=True)
            return 0
        lax.fori_loop(0,T,one,0)
        return go([remote(gbuf.at[w,:,:,:,other],rc.at[w,k],g_send.at[w,0,k],g_recv.at[w,0,k],dev) for k,other,dev in place.peers("c")])
    def after_core(w,copies):
        land(copies)
        for t in range(T):
            v=gbuf[w,t,:,:,c0].astype(f32)
            for k in range(CC-1): v=v+rc[w,k,t].astype(f32)
            rc[w,0,t]=v.astype(b16)
        a=go([remote(rc.at[w,0,0:TH,other],ra2.at[w,k],g_send.at[w,1,k],g_recv.at[w,1,k],dev) for k,other,dev in place.peers("s")])
        b=go([remote(rc.at[w,0,TH:T,:,other],rb2.at[w,k],g_send.at[w,2,k],g_recv.at[w,2,k],dev) for k,other,dev in place.peers("x")])
        return a,b
    def after_second(w,pair):
        land(pair[0])
        v=rc[w,0,0:TH,s0].astype(f32)
        for k in range(S-1): v=v+ra2[w,k].astype(f32)
        ra2[w,0]=v.astype(b16)
        a=go([remote(ra2.at[w,0,:,other],ra3.at[w,k],g_send.at[w,3,k],g_recv.at[w,3,k],dev) for k,other,dev in place.peers("x")])
        land(pair[1])
        v=rc[w,0,TH:T,:,x0].astype(f32)
        for k in range(CX-1): v=v+rb2[w,k].astype(f32)
        rb2[w,0]=v.astype(b16)
        b=go([remote(rb2.at[w,0,:,other],rb3.at[w,k],g_send.at[w,4,k],g_recv.at[w,4,k],dev) for k,other,dev in place.peers("s")])
        return a,b
    def after_third(w,pair):
        land(pair[0])
        v=ra2[w,0,:,x0].astype(f32)
        for k in range(CX-1): v=v+ra3[w,k].astype(f32)
        zin[w,0:TH]=v.astype(b16)
        land(pair[1])
        v=rb2[w,0,:,s0].astype(f32)
        for k in range(S-1): v=v+rb3[w,k].astype(f32)
        zin[w,TH:T]=v.astype(b16)
        return go([remote(zin.at[w,other],zrec.at[w,k],g_send.at[w,5,k],g_recv.at[w,5,k],dev) for k,other,dev in place.peers("t")])
    def after_last(w,copies):
        land(copies)
        v=zin[w,t0].astype(f32)
        for k in range(T-1): v=v+zrec[w,k].astype(f32)
        d1_ref[w]=v
    core_v=compute(2,True)
    vec_end(e_s,ev,ev_s,"s"); e_x=vec_start(0,"x",ev,ev_x)
    two_v=after_core(2,core_v)
    core_k=compute(1,False)
    vec_end(e_x,ev,ev_x,"x"); e_t=vec_start(0,"t",ev,ev_t)
    three_v=after_second(2,two_v)
    two_k=after_core(1,core_k)
    core_q=compute(0,False)
    land(big_a)
    def add_a2(t,_):
        v=ya[t,x0].astype(f32)
        for k in range(CX-1): v=v+za[k,t].astype(f32)
        za[0,t]=v.astype(b16)
        return 0
    lax.fori_loop(0,T,add_a2,0)
    last_a=go([remote(za.at[0,other],zra.at[k],w_send.at[2,k],w_recv.at[2,k],dev) for k,other,dev in place.peers("t")])
    two_q=after_core(0,core_q)
    land(big_b)
    def add_b2(t,_):
        v=yb[t,s0].astype(f32)
        for k in range(S-1): v=v+zb[k,t].astype(f32)
        zb[0,t]=v.astype(b16)
        return 0
    lax.fori_loop(0,T,add_b2,0)
    last_b=go([remote(zb.at[0,other],zrb.at[k],w_send.at[3,k],w_recv.at[3,k],dev) for k,other,dev in place.peers("t")])
    z_v=after_third(2,three_v)
    three_k=after_second(1,two_k)
    step=min(64,R)
    def back(i,carry):
        rows=pl.ds(pl.multiple_of(i*step,step),step)
        h,r=norm_parts(x_ref[rows,:])
        e=acc[rows,:]
        grad_ref[rows,:]=mg_ref[rows,:]+norm_back(e,h,r,gain_ref[...])
        return carry[0]+jnp.sum(e*h,axis=0,keepdims=True),carry[1]+jnp.sum(e,axis=0,keepdims=True)
    zero=jnp.zeros((1,D),f32)
    ga,sa=lax.fori_loop(0,R//step,back,(zero,zero))
    lv[0:1,:]=ga; lv[1:2,:]=sa
    l_c=vec_start(1,"c",lv,lv_c)
    three_q=after_second(0,two_q)
    z_k=after_third(1,three_k)
    vec_end(l_c,lv,lv_c,"c"); l_s=vec_start(1,"s",lv,lv_s)
    vec_end(e_t,ev,ev_t,"t"); all_ref[...]=ev[...]
    after_last(2,z_v)
    z_q=after_third(0,three_q)
    vec_end(l_s,lv,lv_s,"s"); l_x=vec_start(1,"x",lv,lv_x)
    land(last_a)
    v=za[0,t0].astype(f32)
    for k in range(T-1): v=v+zra[k].astype(f32)
    d2_ref[0]=v
    vec_end(l_x,lv,lv_x,"x"); l_t=vec_start(1,"t",lv,lv_t)
    land(last_b)
    v=zb[0,t0].astype(f32)
    for k in range(T-1): v=v+zrb[k].astype(f32)
    d2_ref[1]=v
    after_last(1,z_k)
    after_last(0,z_q)
    vec_end(l_t,lv,lv_t,"t"); late_ref[...]=lv[...]
    vec_copies=[id(c) for group in (e_c,e_s,e_x,e_t,l_c,l_s,l_x,l_t) for c in group]
    for c in sent:
        if id(c) not in vec_copies: c.wait_send()

def finish(S,C,T,dq,dk,dv,first_low,wide,ra,rb,x,middle_grad,gain,early):
    R,D=x.shape
    G,spg,n=dq.shape[:3]
    CC=2 if C%2==0 else 1
    CX=C//CC; TH=T//2
    DR,cols=wide.shape[-2:]
    HR,c2=ra[0].shape[-2:]
    b16,f32=jnp.bfloat16,jnp.float32
    vm=pl.BlockSpec(memory_space=pltpu.VMEM); anyspec=pl.BlockSpec(memory_space=pl.ANY)
    dma=pltpu.SemaphoreType.DMA
    size={"t":T,"s":S,"x":CX,"c":CC}
    _,total=slots(size,"csxt")
    most=max(T,S,CX,CC)-1
    NE=early.shape[0]; NL=8
    V=lambda shape,dt=b16: pltpu.VMEM(shape,dt)
    scratch=[V((3,G,spg,n,PAIR)),V(wide.shape),V((R,D),f32),V((3,T,S,CX,CC,DR,cols)),V((3,max(CC-1,1),T,S,CX,DR,cols)),
             V((3,max(S-1,1),TH,CX,DR,cols)),V((3,max(CX-1,1),TH,S,DR,cols)),V((3,max(CX-1,1),TH,DR,cols)),V((3,max(S-1,1),TH,DR,cols)),
             V((3,T,DR,cols)),V((3,T-1,DR,cols)),
             V((S,)+ra[0].shape),V((CX,)+rb[0].shape),V((T,CX,HR,c2)),V((T,S,HR,c2)),V((max(CX-1,1),T,HR,c2)),V((max(S-1,1),T,HR,c2)),V((T-1,HR,c2)),V((T-1,HR,c2)),
             V((NE,D),f32)]+[V((size[a],NE,D),f32) for a in "csxt"]+[V((NL,D),f32)]+[V((size[a],NL,D),f32) for a in "csxt"]+[
             dma((3,G-1)),dma((3,G-1)),dma((4,most)),dma((4,most)),dma((3,6,most)),dma((3,6,most)),dma((2,total)),dma((2,total)),dma((7+S+CX,))]
    return pl.pallas_call(functools.partial(finish_kernel,S,C,T),
        in_specs=[anyspec]*3+[vm,anyspec]+[vm]*4+[anyspec]*(S+CX),
        out_specs=[vm]*5,
        out_shape=[jax.ShapeDtypeStruct((R,D),f32),jax.ShapeDtypeStruct((3,DR,cols),f32),jax.ShapeDtypeStruct((2,HR,c2),f32),
                   jax.ShapeDtypeStruct((NL,D),f32),jax.ShapeDtypeStruct((NE,D),f32)],
        scratch_shapes=scratch,
        compiler_params=pltpu.CompilerParams(collective_id=2,has_side_effects=True,vmem_limit_bytes=62<<20),
        name="finish")(dq,dk,dv,first_low,wide,x,middle_grad,gain,early,*ra,*rb)


def shards(inputs,teacher,segments,pad_mask,query_weight,key_weight,value_weight,output_weight,up_weight,down_weight,
           first_gain,first_shift,query_shift,value_shift,mixed_gain,mixed_shift,output_shift,second_gain,second_shift,
           up_shift,hidden_gain,hidden_shift,down_shift):
    S,C,T=lax.axis_size("shard"),lax.axis_size("context"),lax.axis_size("tensor")
    CC=2 if C%2==0 else 1
    CX=C//CC
    G=C*T
    ns,n,D=inputs.shape
    R=ns*n
    HP=D//PAIR
    SG=G//HP
    spg=ns//SG
    token_total=S*C*T*R
    me_s=lax.axis_index("shard")
    me_g=lax.axis_index("context")*T+lax.axis_index("tensor")
    c1=query_weight.shape[1]; c2=output_weight.shape[0]; cf=up_weight.shape[1]
    F=cf*T
    x=inputs.reshape(R,D)
    zeros=jnp.zeros_like(query_shift)
    bias=jnp.stack([query_shift,zeros,value_shift]).reshape(3,T,1,c1)
    first_low,qkv,wide,ids_all,pa,pb=project(S,C,T,x,first_gain[None],first_shift[None],query_weight,key_weight,value_weight,bias,
                                             segments.reshape(1,R),output_weight,up_weight,down_weight,ns,n)
    def over_shard(a,d):
        return lax.ppermute(a,"shard",[(i,(i+d)%S) for i in range(S)]) if d else a
    def over_x(a,d):
        return lax.ppermute(a,"context",[(i*CC+j,((i+d)%CX)*CC+j) for i in range(CX) for j in range(CC)]) if d else a
    wa=[over_shard(pa,d) for d in range(S)]
    wb=[over_x(pb,d) for d in range(CX)]
    ids_all=ids_all.reshape(G,S,ns,n)
    valid_count=jnp.sum((ids_all!=(2048//60+1)).astype(jnp.float32))
    ids_mine=lax.dynamic_index_in_dim(ids_all,me_s,1,keepdims=False)
    ids_mine=lax.dynamic_slice_in_dim(ids_mine,(me_g//HP)*spg,spg,1).transpose(1,0,2).reshape(spg,G*n)
    q,k,v=qkv[0],qkv[1],qkv[2]
    o,lse=attend_fwd(q,k,v,ids_mine)
    keep=pad_mask.reshape(R,1).astype(jnp.float32)
    scale=jnp.full((1,PAIR),token_total/valid_count)
    vecs=jnp.stack([mixed_gain,mixed_shift,output_shift,second_gain,second_shift,down_shift,down_shift,down_shift])
    wides=jnp.stack([up_shift.reshape(T,cf),hidden_gain.reshape(T,cf),hidden_shift.reshape(T,cf)],axis=1)
    result,middle_grad,g,inner_low,second_low,out_low,middle_low,hidden_low,unit_low,early=feed(
        S,C,T,o,wa,wb,x,teacher.reshape(R,D),keep,scale,vecs,wides)
    *outs,g=weight_grads(S,C,T,out_low,second_low,middle_low,inner_low,unit_low,hidden_low,g)
    ra=[over_shard(outs[d],d) for d in range(S)]
    rb=[over_x(outs[S+d],d) for d in range(CX)]
    dq,dk,dv=attend_bwd(q,k,v,g,o,lse,ids_mine)
    input_grad,dw1,dw2,late,early=finish(S,C,T,dq,dk,dv,first_low,wide,ra,rb,x,middle_grad,first_gain[None],early)
    dw2=dw2.reshape(-1,dw2.shape[-1])
    B=F//D
    vectors=(late[0],late[1],late[2],late[3],early[0],early[1],early[2],early[3],early[4],early[7+2*B:7+3*B].reshape(F),
             early[7:7+B].reshape(F),early[7+B:7+2*B].reshape(F),early[5])
    loss=jnp.sum(early[6])
    return (result.reshape(ns,n,D),loss/valid_count,input_grad.reshape(ns,n,D),
            dw1[0],dw1[1],dw1[2],dw2[:,:c2].T,dw2[:,c2:c2+cf],dw2[:,c2+cf:].T)+vectors


def solution(mesh):
    rows=P("shard",("context","tensor"),None)
    ids=P("shard",("context","tensor"))
    wide=P(("shard","context"),"tensor")
    tall=P("tensor",("shard","context"))
    weights=(wide,wide,wide,tall,wide,tall)
    return jax.shard_map(shards,mesh=mesh,in_specs=(rows,rows,ids,ids)+weights+(P(),)*13,
                         out_specs=(rows,P(),rows)+weights+(P(),)*13,check_vma=False)
```

```python
import functools

import jax
import jax.numpy as jnp
from jax import lax
from jax.experimental import pallas as pl
from jax.experimental.pallas import tpu as pltpu
from jax.sharding import PartitionSpec as P


NEG=-1e30
def _dot(a,b,ca,cb):
    return lax.dot_general(a,b,(((ca,),(cb,)),((),())),preferred_element_type=jnp.float32)

def half_masks(rows):
    lane=lax.broadcasted_iota(jnp.int32,(rows,128),1)
    return lane<64

def fwd_kernel(lo_ref,hi_ref,q_ref,k_ref,v_ref,col_ref,row_ref,o_ref,lse_ref,acc_ref,m_ref,l_ref):
    i=pl.program_id(0)
    bq=acc_ref.shape[1]; bk=row_ref.shape[-1]; n=k_ref.shape[2]; per=bk//n
    left=half_masks(bq)
    q=q_ref[...].reshape(bq,128)*jnp.bfloat16(0.125)
    zero=jnp.zeros_like(q)
    qs=(jnp.where(left,q,zero),jnp.where(left,zero,q))
    col=col_ref[...]
    for h in range(2):
        acc_ref[h]=jnp.zeros((bq,128),jnp.float32)
        m_ref[h]=jnp.full((bq,128),NEG,jnp.float32)
        l_ref[h]=jnp.zeros((bq,128),jnp.float32)
    def step(j,_):
        k=k_ref[pl.ds(j*per,per),0].reshape(bk,128)
        v=v_ref[pl.ds(j*per,per),0].reshape(bk,128)
        same=col==row_ref[j]
        for h in range(2):
            sc=jnp.where(same,_dot(qs[h],k,1,1),NEG)
            old=m_ref[h]
            top=jnp.maximum(old,jnp.max(sc,axis=1,keepdims=True))
            e=jnp.exp(sc-jnp.concatenate([top]*(bk//128),axis=1))
            a=jnp.exp(old-top)
            l_ref[h]=l_ref[h]*a+jnp.sum(e,axis=1,keepdims=True)
            m_ref[h]=top
            acc_ref[h]=acc_ref[h]*a+_dot(e.astype(jnp.bfloat16),v,1,0)
        return 0
    lax.fori_loop(lo_ref[i],hi_ref[i],step,0)
    o=jnp.where(left,acc_ref[0]/l_ref[0],acc_ref[1]/l_ref[1])
    o_ref[...]=o.astype(jnp.bfloat16).reshape(o_ref.shape)
    lse=jnp.where(left,m_ref[0]+jnp.log(l_ref[0]),m_ref[1]+jnp.log(l_ref[1]))
    lse_ref[...]=lse.reshape(lse_ref.shape)

def bounds(ids,bq,bk):
    first=ids[::bq]; last=ids[bq-1::bq]
    start=jnp.sum((ids[None,:]<first[:,None]).astype(jnp.int32),axis=1)
    end=jnp.sum((ids[None,:]<=last[:,None]).astype(jnp.int32),axis=1)
    return start//bk,(end+bk-1)//bk

def attend_fwd(qkv,ids,col,edges,bq=256,bk=256):
    G,_,n,_=qkv.shape; L=G*n
    row=ids.reshape(L//bk,1,bk)
    part=lambda w: pl.BlockSpec((G,1,n,128),lambda i,*_: (0,w,0,0))
    ospec=pl.BlockSpec((bq//n,n,128),lambda i,*_:(i,0,0))
    return pl.pallas_call(fwd_kernel,
        grid_spec=pltpu.PrefetchScalarGridSpec(num_scalar_prefetch=2,grid=(L//bq,),
            in_specs=[pl.BlockSpec((bq//n,1,n,128),lambda i,*_:(i,0,0,0)),part(1),part(2),pl.BlockSpec((bq,1),lambda i,*_:(i,0)),
                      pl.BlockSpec((L//bk,1,bk),lambda i,*_:(0,0,0))],
            out_specs=[ospec,ospec],
            scratch_shapes=[pltpu.VMEM((2,bq,128),jnp.float32)]*3),
        out_shape=[jax.ShapeDtypeStruct((G,n,128),jnp.bfloat16),jax.ShapeDtypeStruct((G,n,128),jnp.float32)],
        compiler_params=pltpu.CompilerParams(dimension_semantics=("arbitrary",),vmem_limit_bytes=48<<20),
        cost_estimate=pl.CostEstimate(flops=4*L*1024*128*2,bytes_accessed=8*L*256,transcendentals=2*L*1024),
        name="attend_fwd")(*edges,qkv,qkv,qkv,col,row)

def bwd_kernel(lo_ref,hi_ref,q_ref,k_ref,v_ref,g_ref,o_ref,lse_ref,col_ref,row_ref,d_ref,dqa,dka,dva):
    i=pl.program_id(0)
    bq=dqa.shape[1]; bk=bq; n=k_ref.shape[2]; per=bk//n
    @pl.when(i==0)
    def _():
        dka[...]=jnp.zeros_like(dka); dva[...]=jnp.zeros_like(dva)
    left=half_masks(bq)
    q=q_ref[...].reshape(bq,128)*jnp.bfloat16(0.125)
    g=g_ref[...].reshape(bq,128)
    zero=jnp.zeros_like(q)
    qs=(jnp.where(left,q,zero),jnp.where(left,zero,q))
    gs=(jnp.where(left,g,zero),jnp.where(left,zero,g))
    lse_t=lse_ref[...].reshape(bq,128).T
    d_t=(g.astype(jnp.float32)*o_ref[...].reshape(bq,128).astype(jnp.float32)).T
    lses=(lse_t[0:1],lse_t[64:65])
    ds=(jnp.sum(d_t[:64],axis=0,keepdims=True),jnp.sum(d_t[64:],axis=0,keepdims=True))
    ids_q=row_ref[i]
    dqa[...]=jnp.zeros_like(dqa)
    def step(j,_):
        k=k_ref[pl.ds(j*per,per),0].reshape(bk,128)
        v=v_ref[pl.ds(j*per,per),0].reshape(bk,128)
        rows=pl.ds(pl.multiple_of(j*bk,bk),bk)
        same=col_ref[rows,:]==ids_q
        dk=dka[rows,:]; dv=dva[rows,:]
        for h in range(2):
            st=_dot(k,qs[h],1,1)
            p=jnp.exp(jnp.where(same,st,NEG)-lses[h])
            dp=_dot(v,gs[h],1,1)
            d=(p*(dp-ds[h])).astype(jnp.bfloat16)
            dv=dv+_dot(p.astype(jnp.bfloat16),gs[h],1,0)
            dk=dk+_dot(d,qs[h],1,0)
            dqa[h]+=_dot(d,k,0,0)
        dka[rows,:]=dk; dva[rows,:]=dv
        return 0
    lax.fori_loop(lo_ref[i],hi_ref[i],step,0)
    d_ref[pl.ds(i*(bq//n),bq//n),0]=(jnp.where(left,dqa[0],dqa[1])*0.125).astype(jnp.bfloat16).reshape(bq//n,n,128)
    @pl.when(i==pl.num_programs(0)-1)
    def _():
        d_ref[:,1]=dka[...].astype(jnp.bfloat16).reshape(d_ref.shape[0],n,128)
        d_ref[:,2]=dva[...].astype(jnp.bfloat16).reshape(d_ref.shape[0],n,128)

def attend_bwd(qkv,g,o,lse,ids,col,edges,bq=256):
    bk=bq
    G,_,n,_=qkv.shape; L=G*n
    row=ids.reshape(L//bk,1,bk)
    part=lambda w: pl.BlockSpec((G,1,n,128),lambda i,*_: (0,w,0,0))
    ospec=pl.BlockSpec((bq//n,n,128),lambda i,*_:(i,0,0))
    return pl.pallas_call(bwd_kernel,
        grid_spec=pltpu.PrefetchScalarGridSpec(num_scalar_prefetch=2,grid=(L//bq,),
            in_specs=[pl.BlockSpec((bq//n,1,n,128),lambda i,*_:(i,0,0,0)),part(1),part(2),ospec,
                      ospec,ospec,pl.BlockSpec((L,1),lambda i,*_:(0,0)),pl.BlockSpec((L//bk,1,bk),lambda i,*_:(0,0,0))],
            out_specs=pl.BlockSpec((G,3,n,128),lambda i,*_:(0,0,0,0)),
            scratch_shapes=[pltpu.VMEM((2,bq,128),jnp.float32)]+[pltpu.VMEM((L,128),jnp.float32)]*2),
        out_shape=jax.ShapeDtypeStruct((G,3,n,128),jnp.bfloat16),
        compiler_params=pltpu.CompilerParams(dimension_semantics=("arbitrary",),vmem_limit_bytes=48<<20),
        cost_estimate=pl.CostEstimate(flops=1000000,bytes_accessed=1000000,transcendentals=0),
        name="attend_bwd")(*edges,qkv,qkv,qkv,g,o,lse,col,row)


EPS=1e-5
PAIR=128

def norm_parts(v):
    m=jnp.mean(v,axis=-1,keepdims=True)
    s=jnp.mean(v*v,axis=-1,keepdims=True)-m*m
    r=lax.rsqrt(s+EPS)
    return (v-m)*r,r

def norm_back(e,h,r,gain):
    t=e*gain
    return r*(t-jnp.mean(t,axis=-1,keepdims=True)-h*jnp.mean(t*h,axis=-1,keepdims=True))


MESH_ID=pl.DeviceIdType.MESH

class Place:
    def __init__(self,S,C,T):
        self.CC=2 if C%2==0 else 1
        self.size={"t":T,"s":S,"x":C//self.CC,"c":self.CC}
        c=lax.axis_index("context")
        self.at={"t":lax.axis_index("tensor"),"s":lax.axis_index("shard"),"x":c//self.CC,"c":lax.rem(c,self.CC)}
        self.group=c*T+self.at["t"]
        self.T=T; self.G=C*T
    def peers(self,axis):
        m=self.size[axis]
        for d in range(1,m):
            other=lax.rem(self.at[axis]+d,m)
            if axis=="t": yield d-1,other,{"tensor":other}
            elif axis=="s": yield d-1,other,{"shard":other}
            elif axis=="x": yield d-1,other,{"context":other*self.CC+self.at["c"]}
            else: yield d-1,other,{"context":self.at["x"]*self.CC+other}
    def group_peers(self):
        for d in range(1,self.G):
            other=lax.rem(self.group+d,self.G)
            yield d-1,other,{"context":other//self.T,"tensor":lax.rem(other,self.T)}

def slots(size,order):
    base,total={},0
    for a in order:
        base[a]=total; total+=size[a]-1
    return base,total

def greet(place):
    barrier=pltpu.get_barrier_semaphore()
    count=0
    for _,_,dev in place.group_peers():
        pl.semaphore_signal(barrier,inc=1,device_id=dev,device_id_type=MESH_ID); count+=1
    for _,_,dev in place.peers("s"):
        pl.semaphore_signal(barrier,inc=1,device_id=dev,device_id_type=MESH_ID); count+=1
    pl.semaphore_wait(barrier,count)

def remote(src,dst,send,recv,dev):
    return pltpu.make_async_remote_copy(src_ref=src,dst_ref=dst,send_sem=send,recv_sem=recv,device_id=dev,device_id_type=MESH_ID)

def project_kernel(S,C,T,x_ref,gain_ref,shift_ref,wq_ref,wk_ref,wv_ref,bias_ref,ids_ref,wo_ref,wu_ref,wd_ref,
                   low_ref,wide_ref,allids_ref,pa_ref,pb_ref,*rest):
    spg=len(rest)-15
    rows_refs=rest[:spg]
    project_body(S,C,T,x_ref,gain_ref,shift_ref,wq_ref,wk_ref,wv_ref,bias_ref,ids_ref,wo_ref,wu_ref,wd_ref,
                 low_ref,wide_ref,allids_ref,pa_ref,pb_ref,rows_refs,*rest[spg:])

def project_body(S,C,T,x_ref,gain_ref,shift_ref,wq_ref,wk_ref,wv_ref,bias_ref,ids_ref,wo_ref,wu_ref,wd_ref,
                   low_ref,wide_ref,allids_ref,pa_ref,pb_ref,rows_refs,
                   zbuf,z_send,z_recv,p_send,p_recv,wbuf,obuf,idbuf,ag_send,ag_recv,a_send,a_recv,i_send,i_recv,local):
    place=Place(S,C,T)
    R,D=low_ref.shape
    G,_,n=rows_refs[0].shape[:3]
    spg=len(rows_refs)
    HP=D//PAIR; SG=G//HP
    cols=wbuf.shape[-1]; hpt=cols//PAIR
    me=place.group
    order="tsxc"
    base,total=slots(place.size,order)
    own=[place.at[a] for a in order]
    for w,ref in enumerate((wq_ref,wk_ref,wv_ref)):
        wbuf[w,own[0],own[1],own[2],own[3]]=ref[...].astype(jnp.bfloat16)
    t0=place.at["t"]
    HR,c2=zbuf.shape[-2:]
    c0=wo_ref.shape[0]; cf=wu_ref.shape[1]
    zbuf[t0,:,:,0:c0]=wo_ref[...].T.astype(jnp.bfloat16).reshape(2,HR,c0)
    zbuf[t0,:,:,c0:c0+cf]=wu_ref[...].astype(jnp.bfloat16).reshape(2,HR,cf)
    zbuf[t0,:,:,c0+cf:]=wd_ref[...].T.astype(jnp.bfloat16).reshape(2,HR,cf)
    def hop(way,h,piece):
        to=t0+1 if way==0 else t0-1
        return remote(zbuf.at[piece],zbuf.at[piece],z_send.at[way,h-1],z_recv.at[way,h-1],{"tensor":lax.rem(to+T,T)})
    def line_start():
        @pl.when(t0<T-1)
        def _(): hop(0,1,t0).start()
        @pl.when(t0>0)
        def _(): hop(1,1,t0).start()
    def line_pass(h):
        @pl.when(t0>=h)
        def _():
            hop(0,h,lax.rem(t0-h+T,T)).wait_recv()
            @pl.when(t0<T-1)
            def _(): hop(0,h+1,lax.rem(t0-h+T,T)).start()
        @pl.when(t0+h<=T-1)
        def _():
            hop(1,h,lax.rem(t0+h,T)).wait_recv()
            @pl.when(t0>0)
            def _(): hop(1,h+1,lax.rem(t0+h,T)).start()
    def line_end():
        for h in range(1,T):
            @pl.when((t0<T-1)&(t0>=h-1))
            def _(): hop(0,h,lax.rem(t0-h+1+T,T)).wait_send()
            @pl.when((t0>0)&(t0+h-1<=T-1))
            def _(): hop(1,h,lax.rem(t0+h-1,T)).wait_send()
    def plane():
        a=pltpu.make_async_copy(zbuf.at[:,0],pa_ref.at[place.at["x"]],local.at[8]); a.start()
        b=pltpu.make_async_copy(zbuf.at[:,1],pb_ref.at[place.at["s"]],local.at[9]); b.start()
        out=[a,b]
        for k,_,dev in place.peers("x"):
            c=remote(zbuf.at[:,0],pa_ref.at[place.at["x"]],p_send.at[0,k],p_recv.at[0,k],dev); c.start(); sent.append(c); out.append(c)
        for k,_,dev in place.peers("s"):
            c=remote(zbuf.at[:,1],pb_ref.at[place.at["s"]],p_send.at[1,k],p_recv.at[1,k],dev); c.start(); sent.append(c); out.append(c)
        return out
    greet(place)
    stages={2:"tsxc",1:"txsc",0:"tsxc"}
    sent=[]
    copies={}
    def start(w,r):
        done=stages[w][:r]; axis=stages[w][r]
        idx=tuple(slice(None) if a in done else place.at[a] for a in order)
        copies[w,r]=[]
        for k,_,dev in place.peers(axis):
            c=remote(wbuf.at[(w,)+idx],wbuf.at[(w,)+idx],ag_send.at[w,base[axis]+k],ag_recv.at[w,base[axis]+k],dev)
            c.start(); copies[w,r].append(c); sent.append(c)
    def arrive(w,r):
        for c in copies[w,r]: c.wait_recv()
    for w in (2,1,0): start(w,0)
    line_start()
    ids_own=pltpu.make_async_copy(ids_ref,idbuf.at[place.at["s"]],local.at[0]); ids_own.start()
    id_first=[]
    for k,_,dev in place.peers("s"):
        c=remote(ids_ref,idbuf.at[place.at["s"]],i_send.at[k],i_recv.at[k],dev); c.start(); id_first.append(c); sent.append(c)
    step=min(64,R)
    def norm(i,_):
        rows=pl.ds(pl.multiple_of(i*step,step),step)
        h,_r=norm_parts(x_ref[rows,:])
        low_ref[rows,:]=(h*gain_ref[...]+shift_ref[...]).astype(jnp.bfloat16)
        return 0
    lax.fori_loop(0,R//step,norm,0)
    def spread_ids():
        ids_own.wait()
        for c in id_first: c.wait_recv()
        out=[]
        mine=pltpu.make_async_copy(idbuf,allids_ref.at[me],local.at[1]); mine.start(); out.append(mine)
        for k,_,dev in place.group_peers():
            c=remote(idbuf,allids_ref.at[me],i_send.at[S-1+k],i_recv.at[S-1+k],dev); c.start(); sent.append(c); out.append(c)
        return out
    late=[]
    def compute(w):
        def one(t,_):
            y=_dot(low_ref[...],wbuf[w,t].reshape(D,cols),1,0)+bias_ref[w,t]
            y=y.astype(jnp.bfloat16)
            for g in range(SG):
                for j in range(hpt):
                    obuf[w,g*HP+t*hpt+j]=y[g*spg*n:(g+1)*spg*n,j*PAIR:(j+1)*PAIR].reshape(spg,n,PAIR)
            return 0
        lax.fori_loop(0,T,one,0)
        mine=pltpu.make_async_copy(obuf.at[w,me,0],rows_refs[0].at[me,w],local.at[2+w]); mine.start(); late.append(mine)
        for k,other,dev in place.group_peers():
            c=remote(obuf.at[w,other,0],rows_refs[0].at[me,w],a_send.at[w,k],a_recv.at[w,k],dev)
            c.start(); sent.append(c); late.append(c)
        for i in range(1,spg):
            c=pltpu.make_async_copy(obuf.at[w,:,i],rows_refs[i].at[:,w],local.at[10+w*spg+i]); c.start(); late.append(c)
        keep=pltpu.make_async_copy(wbuf.at[w],wide_ref.at[w],local.at[5+w]); keep.start(); late.append(keep)
    arrive(2,0); start(2,1)
    arrive(1,0); start(1,1)
    ids_out=spread_ids()
    arrive(2,1); start(2,2)
    arrive(1,1); start(1,2)
    arrive(0,0); start(0,1)
    arrive(2,2); start(2,3)
    line_pass(1)
    arrive(2,3); compute(2)
    arrive(1,2); start(1,3)
    arrive(0,1); start(0,2)
    arrive(1,3); compute(1)
    if T>2: line_pass(2)
    arrive(0,2); start(0,3)
    arrive(0,3); compute(0)
    for h in range(3,T): line_pass(h)
    ids_out=ids_out+plane()
    for c in late+ids_out:
        if any(c is o for o in sent): c.wait_recv()
        else: c.wait()
    for c in sent: c.wait_send()
    line_end()

def project(S,C,T,x,gain,shift,wq,wk,wv,bias,ids,wo,wu,wd,ns,n):
    R,D=x.shape
    G=C*T; HP=D//PAIR; spg=ns*HP//G
    DR,cols=wq.shape
    CC=2 if C%2==0 else 1
    piece=(3,T,S,C//CC,CC,DR,cols)
    HR=DR//2; width=wo.shape[0]+2*wu.shape[1]; most=max(S,C//CC)-1
    _,total=slots({"t":T,"s":S,"x":C//CC,"c":CC},"tsxc")
    vm=pl.BlockSpec(memory_space=pltpu.VMEM); anyspec=pl.BlockSpec(memory_space=pl.ANY)
    dma=pltpu.SemaphoreType.DMA
    return pl.pallas_call(functools.partial(project_kernel,S,C,T),
        in_specs=[vm]*11,
        out_specs=[vm]+[anyspec]*(4+spg),
        out_shape=[jax.ShapeDtypeStruct((R,D),jnp.bfloat16),jax.ShapeDtypeStruct(piece,jnp.bfloat16),jax.ShapeDtypeStruct((G,S,1,ns*n),jnp.int32),
                   jax.ShapeDtypeStruct((C//CC,T,HR,width),jnp.bfloat16),jax.ShapeDtypeStruct((S,T,HR,width),jnp.bfloat16)]+
                  [jax.ShapeDtypeStruct((G,3,n,PAIR),jnp.bfloat16)]*spg,
        scratch_shapes=[pltpu.VMEM((T,2,HR,width),jnp.bfloat16),dma((2,T-1)),dma((2,T-1)),dma((2,most)),dma((2,most)),pltpu.VMEM(piece,jnp.bfloat16),pltpu.VMEM((3,G,spg,n,PAIR),jnp.bfloat16),pltpu.VMEM((S,1,ns*n),jnp.int32),
                        dma((3,total)),dma((3,total)),dma((3,G-1)),dma((3,G-1)),dma((S-1+G-1,)),dma((S-1+G-1,)),dma((10+3*spg,))],
        compiler_params=pltpu.CompilerParams(collective_id=0,has_side_effects=True,vmem_limit_bytes=40<<20),
        name="project")(x,gain,shift,wq,wk,wv,bias,ids,wo,wu,wd)


SUB=128

def feed_kernel(S,C,T,NC,NO,*refs):
    place=Place(S,C,T)
    CX=place.size["x"]; CC=place.CC
    spg=NO
    o_refs=refs[:spg]; o_ref=o_refs[-1]; refs=refs[spg-1:]
    wa_refs=refs[1:1+S]; wb_refs=refs[1+S:1+S+CX]
    (x_ref,teach_ref,keep_ref,scale_ref,vec_ref,wide_ref)=refs[1+S+CX:7+S+CX]
    (res_ref,mg_ref,inner_ref,second_ref,out_ref,midl_ref,hid_ref,unl_ref,sum_ref)=refs[7+S+CX:16+S+CX]
    g_refs=refs[16+S+CX:16+S+CX+spg]; refs=refs[spg-1:]
    (w2,rbuf,mix,inner,second,outl,midl,hid,unl,act,dact,tt,acc,middle,og,s1,s2,res,mg,gout,vacc,wacc,
     w_local,w_send,w_recv,a_send,a_recv,g_send,g_recv,misc,o_sem,s1b,s2b)=refs[17+S+CX:]
    R,D=x_ref.shape
    G,n=o_ref.shape[:2]
    HP=D//PAIR; SG=G//HP
    HR=w2.shape[-2]
    F=hid.shape[1]; cf=F//T; c2=D//T
    B=R//spg; sub=min(SUB,n)
    f32=jnp.float32; b16=jnp.bfloat16
    me=place.group
    s0,x0,c0=place.at["s"],place.at["x"],place.at["c"]
    DS=D//S
    ranges=((0,c2),(c2,c2+cf),(c2+cf,c2+2*cf))
    def pieces(r):
        lo,hi=ranges[r]
        out=[]
        for d in range(S):
            src=lax.rem(s0+S-d,S)
            for i in range(CX):
                out.append((wa_refs[d].at[i,:,:,lo:hi],w2.at[:,src,i,c0,0,:,lo:hi]))
        for d in range(CX):
            src=lax.rem(x0+CX-d,CX)
            for i in range(S):
                out.append((wb_refs[d].at[i,:,:,lo:hi],w2.at[:,i,src,c0,1,:,lo:hi]))
        return out
    local=[[pltpu.make_async_copy(a,b,w_local.at[r,i]) for i,(a,b) in enumerate(pieces(r))] for r in range(3)]
    for r in range(3):
        for c in local[r]: c.start()
    barrier=pltpu.get_barrier_semaphore()
    count=0
    for _,_,dev in place.group_peers():
        pl.semaphore_signal(barrier,inc=1,device_id=dev,device_id_type=MESH_ID); count+=1
    pl.semaphore_wait(barrier,count)
    own=[pltpu.make_async_copy(o_ref.at[me],rbuf.at[me,spg-1],misc.at[0])]
    own+=[pltpu.make_async_copy(o_refs[i],rbuf.at[:,i],misc.at[1+i]) for i in range(spg-1)]
    for c in own: c.start()
    rows_in=[remote(o_ref.at[other],rbuf.at[me,spg-1],a_send.at[k],a_recv.at[k],dev) for k,other,dev in place.group_peers()]
    for c in rows_in: c.start()
    far=[[remote(a,b,w_send.at[r,k,i],w_recv.at[r,k,i],dev) for k,_,dev in place.peers("c") for i,(a,b) in enumerate(pieces(r))] for r in range(3)]
    for r in range(3):
        for c in far[r]: c.start()
    def weights(r):
        for c in local[r]: c.wait()
        for c in far[r]: c.wait_recv()
    sum_ref[...]=jnp.zeros_like(sum_ref)
    vacc[...]=jnp.zeros_like(vacc); wacc[...]=jnp.zeros_like(wacc)
    def vec(i): return vec_ref[i:i+1,:]
    MIXG,MIXS,OUTS,SECG,SECS,DOWNS=range(6)
    def each(fn):
        def body(i,_):
            fn(pl.ds(pl.multiple_of(i*sub,sub),sub),i)
            return 0
        lax.fori_loop(0,B//sub,body,0)
    def fold(a):
        return jnp.sum(a.reshape(sub//8,8,a.shape[1]),axis=0)
    def lanes(a):
        v=a[:,:PAIR]
        for j in range(1,a.shape[1]//PAIR): v=v+a[:,j*PAIR:(j+1)*PAIR]
        return v
    def flat(t,lo,hi,s=None):
        if s is None: return w2[t,:,:,:,:,:,lo:hi].reshape(D,hi-lo)
        return w2[t,s,:,:,:,:,lo:hi].reshape(DS,hi-lo)
    weights(0)
    def block(b):
        r0=b*B
        def rows(i): return pl.ds(pl.multiple_of(r0+i*sub,sub),sub)
        def tokens(i): return pl.ds(pl.multiple_of(i//(n//sub)*(spg*n)+b*n+lax.rem(i,n//sub)*sub,sub),sub)
        whole=pl.ds(r0,B)
        if b<spg-1: own[1+b].wait()
        else:
            own[0].wait()
            for c in rows_in: c.wait_recv()
        for gg in range(SG):
            for h in range(HP):
                mix[gg*n:(gg+1)*n,h*PAIR:(h+1)*PAIR]=rbuf[gg*HP+h,b]
        def f1(q,i):
            h,_=norm_parts(mix[q,:].astype(f32))
            inner[rows(i),:]=(h*vec(MIXG)+vec(MIXS)).astype(b16)
        each(f1)
        acc[...]=jnp.zeros_like(acc)
        def att(t,_):
            a=inner[whole,pl.ds(pl.multiple_of(t*c2,128),c2)]
            for s in range(S):
                acc[:,s*DS:(s+1)*DS]+=_dot(a,flat(t,0,c2,s),1,1)
            return 0
        lax.fori_loop(0,T,att,0)
        def f2(q,i):
            m=x_ref[tokens(i),:]+(acc[q,:]+vec(OUTS))
            middle[q,:]=m
            h,_=norm_parts(m)
            second[rows(i),:]=(h*vec(SECG)+vec(SECS)).astype(b16)
        each(f2)
        if b==0: weights(1)
        s1[...]=jnp.zeros_like(s1); s2[...]=jnp.zeros_like(s2)
        def up(t,_):
            a=second[whole,:]
            for j in range(NC):
                w=cf//NC
                act[t,:,j*w:(j+1)*w]=_dot(a,flat(t,c2+j*w,c2+(j+1)*w),1,0)
            def e(q,i):
                u=act[t,q,:]+wide_ref[t,0:1,:]
                u2=u*u
                th=jnp.tanh(0.7978845608028654*u*(1.0+0.044715*u2))
                half=0.5+0.5*th
                a=u*half
                act[t,q,:]=a
                dact[t,q,:]=half+(0.5*0.7978845608028654)*u*(1.0-th*th)*(1.0+(3*0.044715)*u2)
                s1[q,:]+=lanes(a); s2[q,:]+=lanes(a*a)
            each(e)
            return 0
        lax.fori_loop(0,T,up,0)
        def f3(q,i):
            m=jnp.sum(s1[q,:],axis=1,keepdims=True)/F
            v=jnp.sum(s2[q,:],axis=1,keepdims=True)/F-m*m
            s1[q,:]=jnp.broadcast_to(m,(sub,PAIR)); s2[q,:]=jnp.broadcast_to(lax.rsqrt(v+EPS),(sub,PAIR))
        each(f3)
        if b==0: weights(2)
        acc[...]=jnp.zeros_like(acc)
        def down(t,_):
            fcols=pl.ds(pl.multiple_of(t*cf,128),cf)
            def e(q,i):
                h=(act[t,q,:]-s1[q,0:1])*s2[q,0:1]
                act[t,q,:]=h
                hid[rows(i),fcols]=(h*wide_ref[t,1:2,:]+wide_ref[t,2:3,:]).astype(b16)
            each(e)
            a=hid[whole,fcols]
            for s in range(S):
                acc[:,s*DS:(s+1)*DS]+=_dot(a,flat(t,c2+cf,c2+2*cf,s),1,1)
            return 0
        lax.fori_loop(0,T,down,0)
        def f4(q,i):
            r=middle[q,:]+(acc[q,:]+vec(DOWNS))
            res[tokens(i),:]=r
            err=r-teach_ref[tokens(i),:]
            k=keep_ref[tokens(i),:]
            e=k*err
            vacc[6]+=fold(e*err)
            g=e*scale_ref[0:1,0:1]
            og[q,:]=g
            low_=g.astype(b16)
            outl[rows(i),:]=low_
            vacc[5]+=fold(low_.astype(f32))
        each(f4)
        def back1(t,_):
            a=outl[whole,:]
            for j in range(NC):
                w=cf//NC
                tt[t,:,j*w:(j+1)*w]=_dot(a,flat(t,c2+cf+j*w,c2+cf+(j+1)*w),1,0)
            def e(q,i):
                g=tt[t,q,:]; h=act[t,q,:]
                wacc[0,t]+=fold(g*h); wacc[1,t]+=fold(g)
                v=g*wide_ref[t,1:2,:]
                tt[t,q,:]=v
                s1b[q,:]+=lanes(v); s2b[q,:]+=lanes(v*h)
            each(e)
            return 0
        s1b[...]=jnp.zeros_like(s1b); s2b[...]=jnp.zeros_like(s2b)
        lax.fori_loop(0,T,back1,0)
        def f5(q,i):
            s1b[q,:]=jnp.broadcast_to(jnp.sum(s1b[q,:],axis=1,keepdims=True)/F,(sub,PAIR))
            s2b[q,:]=jnp.broadcast_to(jnp.sum(s2b[q,:],axis=1,keepdims=True)/F,(sub,PAIR))
        each(f5)
        acc[...]=jnp.zeros_like(acc)
        def back2(t,_):
            fcols=pl.ds(pl.multiple_of(t*cf,128),cf)
            def e(q,i):
                ag=s2[q,0:1]*(tt[t,q,:]-s1b[q,0:1]-act[t,q,:]*s2b[q,0:1])
                ul=(ag*dact[t,q,:]).astype(b16)
                unl[rows(i),fcols]=ul
                wacc[2,t]+=fold(ul.astype(f32))
            each(e)
            a=unl[whole,fcols]
            for s in range(S):
                acc[:,s*DS:(s+1)*DS]+=_dot(a,flat(t,c2,c2+cf,s),1,1)
            return 0
        lax.fori_loop(0,T,back2,0)
        def f6(q,i):
            h,r=norm_parts(middle[q,:])
            e=acc[q,:]
            vacc[3]+=fold(e*h); vacc[4]+=fold(e)
            m=og[q,:]+norm_back(e,h,r,vec(SECG))
            mg[tokens(i),:]=m
            ml=m.astype(b16)
            midl[rows(i),:]=ml
            vacc[2]+=fold(ml.astype(f32))
        each(f6)
        def back3(t,_):
            acc[:,pl.ds(pl.multiple_of(t*c2,128),c2)]=_dot(midl[whole,:],flat(t,0,c2),1,0)
            return 0
        lax.fori_loop(0,T,back3,0)
        def f7(q,i):
            h,r=norm_parts(mix[q,:].astype(f32))
            e=acc[q,:]
            vacc[0]+=fold(e*h); vacc[1]+=fold(e)
            mix[q,:]=norm_back(e,h,r,vec(MIXG)).astype(b16)
        each(f7)
        for gg in range(SG):
            for h in range(HP):
                gout[b,gg*HP+h]=mix[gg*n:(gg+1)*n,h*PAIR:(h+1)*PAIR]
        copies=[pltpu.make_async_copy(src.at[whole],dst.at[whole],o_sem.at[b,i]) for i,(src,dst) in enumerate(
            ((inner,inner_ref),(second,second_ref),(outl,out_ref),(midl,midl_ref),(hid,hid_ref),(unl,unl_ref)))]
        for gg in range(SG):
            part=pl.ds(gg*spg*n+b*n,n)
            copies+=[pltpu.make_async_copy(src.at[part],dst.at[part],o_sem.at[b,6+2*gg+i]) for i,(src,dst) in enumerate(((res,res_ref),(mg,mg_ref)))]
        if b<spg-1:
            copies.append(pltpu.make_async_copy(gout.at[b,me],g_refs[b].at[me],o_sem.at[b,6+2*SG]))
            far_g=[remote(gout.at[b,other],g_refs[b].at[me],g_send.at[b,k],g_recv.at[b,k],dev) for k,other,dev in place.group_peers()]
            for c in far_g: c.start()
            g_out.extend(far_g)
        else:
            copies.append(pltpu.make_async_copy(gout.at[b],g_refs[b],o_sem.at[b,6+2*SG]))
        for c in copies: c.start()
        return copies
    g_out=[]
    done=[]
    for b in range(spg): done+=block(b)
    for i in range(7):
        sum_ref[i:i+1,:]=jnp.sum(vacc[i],axis=0,keepdims=True)
    for i in range(3):
        for t in range(T):
            at=(i*F+t*cf)
            sum_ref[7+at//D:8+at//D,at%D:at%D+cf]=jnp.sum(wacc[i,t],axis=0,keepdims=True)
    for c in done: c.wait()
    for c in g_out: c.wait()
    for c in rows_in: c.wait_send()
    for r in range(3):
        for c in far[r]: c.wait_send()

def feed(S,C,T,o,wa,wb,x,teacher,keep,scale,vecs,wides):
    R,D=x.shape
    spg=len(o)
    G,n=o[0].shape[:2]
    rows=(G,spg,n,PAIR)
    CC=2 if C%2==0 else 1
    CX=C//CC
    HR,c2=wa[0].shape[-2:]
    cf=wides.shape[-1]; F=cf*T; B=R//spg; SG=G//(D//PAIR)
    b16,f32=jnp.bfloat16,jnp.float32
    vm=pl.BlockSpec(memory_space=pltpu.VMEM); anyspec=pl.BlockSpec(memory_space=pl.ANY)
    dma=pltpu.SemaphoreType.DMA
    V=lambda shape,dt=b16: pltpu.VMEM(shape,dt)
    NP=2*S*CX; NCC=max(CC-1,1)
    sums=7+3*F//D; sums+=-sums%8
    sds=jax.ShapeDtypeStruct
    return pl.pallas_call(functools.partial(feed_kernel,S,C,T,max(cf//512,1),spg),
        in_specs=[anyspec]*(spg+S+CX)+[vm]*6,
        out_specs=[anyspec]*8+[vm]+[anyspec]*spg,
        out_shape=[sds((R,D),f32),sds((R,D),f32)]+[sds((R,D),b16)]*4+[sds((R,F),b16)]*2+[sds((sums,D),f32)]+[sds((G,n,PAIR),b16)]*spg,
        scratch_shapes=[V((T,S,CX,CC,2,HR,c2)),V(rows),V((B,D)),V((R,D)),V((R,D)),V((R,D)),V((R,D)),V((R,F)),V((R,F)),
                        V((T,B,cf),f32),V((T,B,cf),f32),V((T,B,cf),f32),V((B,D),f32),V((B,D),f32),V((B,D),f32),V((B,PAIR),f32),V((B,PAIR),f32),
                        V((R,D),f32),V((R,D),f32),V((spg,G,n,PAIR)),V((7,8,D),f32),V((3,T,8,cf),f32),
                        dma((3,NP)),dma((3,NCC,NP)),dma((3,NCC,NP)),dma((G-1,)),dma((G-1,)),dma((spg,G-1)),dma((spg,G-1)),dma((spg,)),dma((spg,7+2*SG)),V((B,PAIR),f32),V((B,PAIR),f32)],
        compiler_params=pltpu.CompilerParams(collective_id=3,has_side_effects=True,vmem_limit_bytes=63<<20),
        name="feed")(*o,*wa,*wb,x,teacher,keep,scale,vecs,wides)


def weight_grads_kernel(S,C,T,out_ref,second_ref,middle_ref,inner_ref,unit_ref,hidden_ref,g_ref,*rest):
    CX0=C//(2 if C%2==0 else 1)
    NA=1+2*(S-1); NB=1+2*(CX0-1); TH=T//2
    pa_refs,pb_refs=rest[:NA],rest[NA:NA+NB]
    gin_ref,own,got,send,recv,local,a_send,a_recv,a_local=rest[NA+NB:]
    place=Place(S,C,T)
    R,D=out_ref.shape
    CX=place.size["x"]; CC=place.CC
    HR,width=own.shape[-2:]
    c2=inner_ref.shape[1]//T; cf=unit_ref.shape[1]//T
    cc=place.at["c"]
    barrier=pltpu.get_barrier_semaphore()
    others=list(place.peers("c"))
    count=0
    for _,_,dev in place.group_peers():
        pl.semaphore_signal(barrier,inc=1,device_id=dev,device_id_type=MESH_ID); count+=1
    pl.semaphore_wait(barrier,count)
    me=place.group
    mine=pltpu.make_async_copy(g_ref.at[me],gin_ref.at[me],a_local.at[0]); mine.start()
    rows_in=[remote(g_ref.at[other],gin_ref.at[me],a_send.at[k],a_recv.at[k],dev) for k,other,dev in place.group_peers()]
    for c in rows_in: c.start()
    plan=[(middle_ref,inner_ref,0,c2,c2),(second_ref,unit_ref,c2,cf,min(cf,512)),(out_ref,hidden_ref,c2+cf,cf,min(cf,512))]
    def swap(t):
        return [remote(own.at[t,:,:,other],got.at[t,k],send.at[t,k],recv.at[t,k],dev) for k,other,dev in others]
    def outs(t,act):
        def go(src,ref,sem,cond=None):
            if cond is None: act(pltpu.make_async_copy(src,ref,sem))
            else:
                @pl.when(cond)
                def _(): act(pltpu.make_async_copy(src,ref,sem))
        for d in range(S):
            src=got.at[t,0,lax.rem(place.at["s"]+d,S),:,0]
            if d==0: go(src,pa_refs[0].at[t],local.at[t,0])
            else:
                go(src,pa_refs[2*d-1].at[lax.rem(t,TH)],local.at[t,d],t<TH)
                go(src,pa_refs[2*d].at[lax.rem(t,TH)],local.at[t,d],t>=TH)
        for d in range(CX):
            src=got.at[t,0,:,lax.rem(place.at["x"]+d,CX),1]
            if d==0: go(src,pb_refs[0].at[t],local.at[t,S])
            else:
                go(src,pb_refs[2*d-1].at[lax.rem(t,TH)],local.at[t,S+d],t<TH)
                go(src,pb_refs[2*d].at[lax.rem(t,TH)],local.at[t,S+d],t>=TH)
    def settle(t):
        for c in swap(t): c.wait_recv()
        for s in range(S):
            for x in range(CX):
                total=own[t,s,x,cc].astype(jnp.float32)
                for k,_,_ in others:
                    total=total+got[t,k,s,x].astype(jnp.float32)
                got[t,0,s,x]=total.astype(jnp.bfloat16)
        outs(t,lambda c: c.start())
    def one(t,_):
        for left,right,base,cols,chunk in plan:
            for j in range(cols//chunk):
                y=_dot(left[...],right[:,pl.ds(pl.multiple_of(t*cols+j*chunk,128),chunk)],0,0)
                own[t,:,:,:,:,:,base+j*chunk:base+(j+1)*chunk]=y.astype(jnp.bfloat16).reshape(S,CX,CC,2,HR,chunk)
        for c in swap(t): c.start()
        @pl.when(t>0)
        def _(): settle(t-1)
        return 0
    lax.fori_loop(0,T,one,0)
    settle(T-1)
    def finish(t,_):
        for c in swap(t): c.wait_send()
        outs(t,lambda c: c.wait())
        return 0
    lax.fori_loop(0,T,finish,0)
    mine.wait()
    for c in rows_in: c.wait()

def weight_grads(S,C,T,out_low,second_low,middle_low,inner_low,unit_low,hidden_low,g):
    R,D=out_low.shape
    CC=2 if C%2==0 else 1
    CX=C//CC; HR=D//(S*C*2); width=(D+2*unit_low.shape[1])//T
    vm=pl.BlockSpec(memory_space=pltpu.VMEM); anyspec=pl.BlockSpec(memory_space=pl.ANY)
    dma=pltpu.SemaphoreType.DMA
    return pl.pallas_call(functools.partial(weight_grads_kernel,S,C,T),
        in_specs=[vm]*6+[anyspec],out_specs=[anyspec]*(2*S+2*CX-1),
        out_shape=[jax.ShapeDtypeStruct((T,CX,HR,width),jnp.bfloat16)]+[jax.ShapeDtypeStruct((T//2,CX,HR,width),jnp.bfloat16)]*(2*S-2)+
                  [jax.ShapeDtypeStruct((T,S,HR,width),jnp.bfloat16)]+[jax.ShapeDtypeStruct((T//2,S,HR,width),jnp.bfloat16)]*(2*CX-2)+[jax.ShapeDtypeStruct(g.shape,jnp.bfloat16)],
        scratch_shapes=[pltpu.VMEM((T,S,CX,CC,2,HR,width),jnp.bfloat16),pltpu.VMEM((T,max(CC-1,1),S,CX,2,HR,width),jnp.bfloat16),
                        dma((T,max(CC-1,1))),dma((T,max(CC-1,1))),dma((T,S+CX)),dma((C*T-1,)),dma((C*T-1,)),dma((1,))],
        compiler_params=pltpu.CompilerParams(collective_id=1,has_side_effects=True,vmem_limit_bytes=60<<20),
        name="weight_grads")(out_low,second_low,middle_low,inner_low,unit_low,hidden_low,g)


def finish_kernel(S,C,T,NO,*refs):
    d_refs=refs[:NO]
    finish_split(S,C,T,d_refs,*refs[NO:])

def finish_split(S,C,T,d_refs,low_ref,wide_ref,x_ref,mg_ref,gain_ref,early_ref,*rest):
    CX0=C//(2 if C%2==0 else 1)
    NA=1+2*(S-1); NB=1+2*(CX0-1)
    ra_refs,rb_refs=rest[:NA],rest[NA:NA+NB]
    finish_body(S,C,T,d_refs,low_ref,wide_ref,x_ref,mg_ref,gain_ref,early_ref,ra_refs,rb_refs,*rest[NA+NB:])

def finish_body(S,C,T,d_refs,low_ref,wide_ref,x_ref,mg_ref,gain_ref,early_ref,ra_refs,rb_refs,
                  grad_ref,d1_ref,d2_ref,late_ref,all_ref,
                  rbuf,wbuf,acc,gbuf,rc,ra2,rb2,ra3,rb3,gz,gzr,bz,bzr,z_send,z_recv,
                  xa,xb,ya,yb,za,zb,
                  ev,ev_c,ev_s,ev_x,ev_t,lv,lv_c,lv_s,lv_x,lv_t,
                  a_send,a_recv,w_send,w_recv,g_send,g_recv,v_send,v_recv,local):
    gz,gzr,bz,bzr=[list(r) for r in (gz,gzr,bz,bzr)]
    place=Place(S,C,T)
    R,D=low_ref.shape
    G,_,n=d_refs[0].shape[:3]
    spg=len(d_refs)
    HP=D//PAIR; SG=G//HP
    cols=wbuf.shape[-1]; hpt=cols//PAIR
    DR=wbuf.shape[-2]
    CX=place.size["x"]; CC=place.CC; TH=T//2
    t0,s0,x0,c0=place.at["t"],place.at["s"],place.at["x"],place.at["c"]
    me=place.group
    f32=jnp.float32; b16=jnp.bfloat16
    sent=[]
    def go(copies):
        for c in copies: c.start()
        sent.extend(copies)
        return copies
    def land(copies):
        for c in copies: c.wait_recv()
    steps=[1<<k for k in range(T.bit_length()-1)]
    def bit(k): return lax.rem(t0//steps[k],2)
    def trade(k,which,bufs,recs):
        other=t0+steps[k]-2*steps[k]*bit(k)
        return go([remote(bufs[k].at[:,1-bit(k)],recs[k],z_send.at[which,k],z_recv.at[which,k],{"tensor":other})])
    def settle(k,copies,bufs,recs):
        land(copies)
        v=bufs[k][:,bit(k)].astype(f32)+recs[k][...].astype(f32)
        if k+1<len(steps): bufs[k+1][...]=v.astype(b16).reshape(bufs[k+1].shape)
        return v
    gzs=[[r.at[w] for r in gz] for w in range(3)]; gzrs=[[r.at[w] for r in gzr] for w in range(3)]
    loads=[pltpu.make_async_copy(wide_ref,wbuf,local.at[3*spg])]
    def arrivals(refs,buf,base):
        out=[pltpu.make_async_copy(refs[0],buf.at[0],local.at[base])]
        for i,ref in enumerate(refs[1:]):
            out.append(pltpu.make_async_copy(ref,buf.at[1+i//2,i%2*TH:i%2*TH+TH],local.at[base+1+i]))
        return out
    loads+=arrivals(ra_refs,xa,3*spg+1)
    loads+=arrivals(rb_refs,xb,3*spg+1+len(ra_refs))
    for c in loads: c.start()
    greet(place)
    rows_in=[None]*3
    mine=[None]*3
    last=d_refs[-1]
    for w in (2,1,0):
        mine[w]=[pltpu.make_async_copy(last.at[me,w],rbuf.at[w,me,spg-1],local.at[w*spg])]
        mine[w]+=[pltpu.make_async_copy(d_refs[i].at[:,w],rbuf.at[w,:,i],local.at[w*spg+1+i]) for i in range(spg-1)]
        for c in mine[w]: c.start()
        rows_in[w]=go([remote(last.at[other,w],rbuf.at[w,me,spg-1],a_send.at[w,k],a_recv.at[w,k],dev) for k,other,dev in place.group_peers()])

    base,total=slots(place.size,"csxt")
    def vec_start(which,axis,cur,rec):
        rec[place.at[axis]]=cur[...]
        return go([remote(cur,rec.at[place.at[axis]],v_send.at[which,base[axis]+k],v_recv.at[which,base[axis]+k],dev) for k,_,dev in place.peers(axis)])
    def vec_end(copies,cur,rec,axis):
        land(copies)
        for c in copies: c.wait_send()
        total=rec[0]
        for i in range(1,place.size[axis]): total=total+rec[i]
        cur[...]=total
    ev[...]=early_ref[...]
    e_c=vec_start(0,"c",ev,ev_c)

    for c in loads[1:]: c.wait()
    c2=xa.shape[-1]
    cuts=[0,c2//256*128,c2]
    def add_a(t,_):
        v=xa[0,t].astype(f32)
        for i in range(1,S): v=v+xa[i,t].astype(f32)
        ya[t]=v.astype(b16)
        return 0
    lax.fori_loop(0,T,add_a,0)
    def add_b(t,_):
        v=xb[0,t].astype(f32)
        for i in range(1,CX): v=v+xb[i,t].astype(f32)
        yb[t]=v.astype(b16)
        return 0
    lax.fori_loop(0,T,add_b,0)
    plane_a,plane_b=[],[]
    for h in range(2):
        lane=slice(cuts[h],cuts[h+1])
        plane_a.append(go([remote(ya.at[:,other,:,lane],za.at[k,:,:,lane],w_send.at[0,h,k],w_recv.at[0,h,k],dev) for k,other,dev in place.peers("x")]))
        plane_b.append(go([remote(yb.at[:,other,:,lane],zb.at[k,:,:,lane],w_send.at[1,h,k],w_recv.at[1,h,k],dev) for k,other,dev in place.peers("s")]))
    vec_end(e_c,ev,ev_c,"c"); e_s=vec_start(0,"s",ev,ev_s)
    loads[0].wait()

    lv[...]=jnp.zeros_like(lv)
    def compute(w,first):
        for c in mine[w]: c.wait()
        land(rows_in[w])
        def one(t,_):
            d=jnp.concatenate([jnp.concatenate([rbuf[w,g*HP+t*hpt+j].reshape(spg*n,PAIR) for j in range(hpt)],axis=1) for g in range(SG)],axis=0)
            y=_dot(low_ref[...],d,0,0)
            gbuf[w,t]=y.astype(b16).reshape(S,CX,CC,DR,cols)
            z=_dot(d,wbuf[w,t].reshape(D,cols),1,1)
            if first:
                @pl.when(t==0)
                def _(): acc[...]=z
                @pl.when(t>0)
                def _(): acc[...]+=z
            else:
                acc[...]+=z
            if w!=1:
                lv[2+w//2:3+w//2,pl.ds(pl.multiple_of(t*cols,128),cols)]=jnp.sum(d.astype(f32),axis=0,keepdims=True)
            return 0
        lax.fori_loop(0,T,one,0)
        return go([remote(gbuf.at[w,:,:,:,other],rc.at[w,k],g_send.at[w,0,k],g_recv.at[w,0,k],dev) for k,other,dev in place.peers("c")])
    def after_core(w,copies):
        land(copies)
        for t in range(T):
            v=gbuf[w,t,:,:,c0].astype(f32)
            for k in range(CC-1): v=v+rc[w,k,t].astype(f32)
            rc[w,0,t]=v.astype(b16)
        a=go([remote(rc.at[w,0,0:TH,other],ra2.at[w,k],g_send.at[w,1,k],g_recv.at[w,1,k],dev) for k,other,dev in place.peers("s")])
        b=go([remote(rc.at[w,0,TH:T,:,other],rb2.at[w,k],g_send.at[w,2,k],g_recv.at[w,2,k],dev) for k,other,dev in place.peers("x")])
        return a,b
    def after_second(w,pair):
        land(pair[0])
        v=rc[w,0,0:TH,s0].astype(f32)
        for k in range(S-1): v=v+ra2[w,k].astype(f32)
        ra2[w,0]=v.astype(b16)
        a=go([remote(ra2.at[w,0,:,other],ra3.at[w,k],g_send.at[w,3,k],g_recv.at[w,3,k],dev) for k,other,dev in place.peers("x")])
        land(pair[1])
        v=rc[w,0,TH:T,:,x0].astype(f32)
        for k in range(CX-1): v=v+rb2[w,k].astype(f32)
        rb2[w,0]=v.astype(b16)
        b=go([remote(rb2.at[w,0,:,other],rb3.at[w,k],g_send.at[w,4,k],g_recv.at[w,4,k],dev) for k,other,dev in place.peers("s")])
        return a,b
    def after_third(w,pair):
        land(pair[0])
        v=ra2[w,0,:,x0].astype(f32)
        for k in range(CX-1): v=v+ra3[w,k].astype(f32)
        gz[0][w,0:T//4]=v.astype(b16).reshape(T//4,2,DR,cols)
        land(pair[1])
        v=rb2[w,0,:,s0].astype(f32)
        for k in range(S-1): v=v+rb3[w,k].astype(f32)
        gz[0][w,T//4:T//2]=v.astype(b16).reshape(T//4,2,DR,cols)
        return trade(0,w,gzs[w],gzrs[w])
    def onward(k,w,copies):
        settle(k-1,copies,gzs[w],gzrs[w])
        return trade(k,w,gzs[w],gzrs[w])
    def big_trade(k,h):
        lane=slice(cuts[h],cuts[h+1])
        other=t0+steps[k]-2*steps[k]*bit(k)
        return go([remote(bz[k].at[i,:,1-bit(k),:,lane],bzr[k].at[i,:,:,lane],z_send.at[3+2*h+i,k],z_recv.at[3+2*h+i,k],{"tensor":other}) for i in range(2)])
    def big_settle(k,h,copies):
        lane=slice(cuts[h],cuts[h+1])
        land(copies)
        for i in range(2):
            v=bz[k][i,:,bit(k),:,lane].astype(f32)+bzr[k][i,:,:,lane].astype(f32)
            if k+1<len(steps): bz[k+1][i,:,:,:,lane]=v.astype(b16).reshape(bz[k+1].shape[1:4]+(v.shape[-1],))
            else: d2_ref[i,:,lane]=v[0]
    def big_onward(k,h,copies):
        big_settle(k-1,h,copies)
        return big_trade(k,h)
    def big_first(h):
        lane=slice(cuts[h],cuts[h+1])
        land(plane_a[h])
        def add_a2(j,_):
            v=ya[pl.ds(2*j,2),x0,:,lane].astype(f32)
            for k in range(CX-1): v=v+za[k,pl.ds(2*j,2),:,lane].astype(f32)
            bz[0][0,j,:,:,lane]=v.astype(b16)
            return 0
        lax.fori_loop(0,T//2,add_a2,0)
        land(plane_b[h])
        def add_b2(j,_):
            v=yb[pl.ds(2*j,2),s0,:,lane].astype(f32)
            for k in range(S-1): v=v+zb[k,pl.ds(2*j,2),:,lane].astype(f32)
            bz[0][1,j,:,:,lane]=v.astype(b16)
            return 0
        lax.fori_loop(0,T//2,add_b2,0)
        return big_trade(0,h)
    end=len(steps)
    core_v=compute(2,True)
    vec_end(e_s,ev,ev_s,"s"); e_x=vec_start(0,"x",ev,ev_x)
    two_v=after_core(2,core_v)
    core_k=compute(1,False)
    big=[big_first(0),None]
    three_v=after_second(2,two_v)
    two_k=after_core(1,core_k)
    vec_end(e_x,ev,ev_x,"x"); e_t=vec_start(0,"t",ev,ev_t)
    core_q=compute(0,False)
    big[1]=big_first(1)
    z_v=after_third(2,three_v)
    three_k=after_second(1,two_k)
    two_q=after_core(0,core_q)
    big[0]=big_onward(1,0,big[0])
    step=min(64,R)
    def back(i,carry):
        rows=pl.ds(pl.multiple_of(i*step,step),step)
        h,r=norm_parts(x_ref[rows,:])
        e=acc[rows,:]
        grad_ref[rows,:]=mg_ref[rows,:]+norm_back(e,h,r,gain_ref[...])
        return carry[0]+jnp.sum(e*h,axis=0,keepdims=True),carry[1]+jnp.sum(e,axis=0,keepdims=True)
    zero=jnp.zeros((1,D),f32)
    ga,sa=lax.fori_loop(0,R//step,back,(zero,zero))
    lv[0:1,:]=ga; lv[1:2,:]=sa
    l_c=vec_start(1,"c",lv,lv_c)
    three_q=after_second(0,two_q)
    z_k=after_third(1,three_k)
    z_v=onward(1,2,z_v)
    vec_end(l_c,lv,lv_c,"c"); l_s=vec_start(1,"s",lv,lv_s)
    z_q=after_third(0,three_q)
    big[1]=big_onward(1,1,big[1])
    z_k=onward(1,1,z_k)
    vec_end(l_s,lv,lv_s,"s"); l_x=vec_start(1,"x",lv,lv_x)
    vec_end(e_t,ev,ev_t,"t"); all_ref[...]=ev[...]
    z_q=onward(1,0,z_q)
    vec_end(l_x,lv,lv_x,"x"); l_t=vec_start(1,"t",lv,lv_t)
    for k in range(2,end):
        for h in range(2): big[h]=big_onward(k,h,big[h])
        z_v=onward(k,2,z_v); z_k=onward(k,1,z_k); z_q=onward(k,0,z_q)
    d1_ref[2]=settle(end-1,z_v,gzs[2],gzrs[2])[0]
    big_settle(end-1,0,big[0])
    d1_ref[1]=settle(end-1,z_k,gzs[1],gzrs[1])[0]
    d1_ref[0]=settle(end-1,z_q,gzs[0],gzrs[0])[0]
    big_settle(end-1,1,big[1])
    vec_end(l_t,lv,lv_t,"t"); late_ref[...]=lv[...]
    vec_copies=[id(c) for group in (e_c,e_s,e_x,e_t,l_c,l_s,l_x,l_t) for c in group]
    for c in sent:
        if id(c) not in vec_copies: c.wait_send()

def finish(S,C,T,ds,first_low,wide,ra,rb,x,middle_grad,gain,early):
    R,D=x.shape
    G,_,n=ds[0].shape[:3]
    spg=len(ds)
    CC=2 if C%2==0 else 1
    CX=C//CC; TH=T//2
    DR,cols=wide.shape[-2:]
    HR,c2=ra[0].shape[-2:]
    b16,f32=jnp.bfloat16,jnp.float32
    vm=pl.BlockSpec(memory_space=pltpu.VMEM); anyspec=pl.BlockSpec(memory_space=pl.ANY)
    dma=pltpu.SemaphoreType.DMA
    size={"t":T,"s":S,"x":CX,"c":CC}
    _,total=slots(size,"csxt")
    most=max(T,S,CX,CC)-1
    NE=early.shape[0]; NL=8
    V=lambda shape,dt=b16: pltpu.VMEM(shape,dt)
    halves=[T>>(k+1) for k in range(T.bit_length()-1)]
    scratch=[V((3,G,spg,n,PAIR)),V(wide.shape),V((R,D),f32),V((3,T,S,CX,CC,DR,cols)),V((3,max(CC-1,1),T,S,CX,DR,cols)),
             V((3,max(S-1,1),TH,CX,DR,cols)),V((3,max(CX-1,1),TH,S,DR,cols)),V((3,max(CX-1,1),TH,DR,cols)),V((3,max(S-1,1),TH,DR,cols)),
             [V((3,h,2,DR,cols)) for h in halves],[V((3,h,DR,cols)) for h in halves],
             [V((2,h,2,HR,c2)) for h in halves],[V((2,h,HR,c2)) for h in halves],
             dma((7,len(halves))),dma((7,len(halves))),
             V((S,)+ra[0].shape),V((CX,)+rb[0].shape),V((T,CX,HR,c2)),V((T,S,HR,c2)),V((max(CX-1,1),T,HR,c2)),V((max(S-1,1),T,HR,c2)),
             V((NE,D),f32)]+[V((size[a],NE,D),f32) for a in "csxt"]+[V((NL,D),f32)]+[V((size[a],NL,D),f32) for a in "csxt"]+[
             dma((3,G-1)),dma((3,G-1)),dma((2,2,most)),dma((2,2,most)),dma((3,6,most)),dma((3,6,most)),dma((2,total)),dma((2,total)),dma((3*spg+1+len(ra)+len(rb),))]
    return pl.pallas_call(functools.partial(finish_kernel,S,C,T,spg),
        in_specs=[anyspec]*spg+[vm,anyspec]+[vm]*4+[anyspec]*(len(ra)+len(rb)),
        out_specs=[vm]*5,
        out_shape=[jax.ShapeDtypeStruct((R,D),f32),jax.ShapeDtypeStruct((3,DR,cols),f32),jax.ShapeDtypeStruct((2,HR,c2),f32),
                   jax.ShapeDtypeStruct((NL,D),f32),jax.ShapeDtypeStruct((NE,D),f32)],
        scratch_shapes=scratch,
        compiler_params=pltpu.CompilerParams(collective_id=2,has_side_effects=True,vmem_limit_bytes=62<<20),
        name="finish")(*ds,first_low,wide,x,middle_grad,gain,early,*ra,*rb)


def shards(inputs,teacher,segments,pad_mask,query_weight,key_weight,value_weight,output_weight,up_weight,down_weight,
           first_gain,first_shift,query_shift,value_shift,mixed_gain,mixed_shift,output_shift,second_gain,second_shift,
           up_shift,hidden_gain,hidden_shift,down_shift):
    S,C,T=lax.axis_size("shard"),lax.axis_size("context"),lax.axis_size("tensor")
    CC=2 if C%2==0 else 1
    CX=C//CC
    G=C*T
    ns,n,D=inputs.shape
    R=ns*n
    HP=D//PAIR
    SG=G//HP
    spg=ns//SG
    token_total=S*C*T*R
    me_s=lax.axis_index("shard")
    me_g=lax.axis_index("context")*T+lax.axis_index("tensor")
    c1=query_weight.shape[1]; c2=output_weight.shape[0]; cf=up_weight.shape[1]
    F=cf*T
    x=inputs.reshape(R,D)
    zeros=jnp.zeros_like(query_shift)
    bias=jnp.stack([query_shift,zeros,value_shift]).reshape(3,T,1,c1)
    first_low,wide,ids_all,pa,pb,*rows_out=project(S,C,T,x,first_gain[None],first_shift[None],query_weight,key_weight,value_weight,bias,
                                             segments.reshape(1,R),output_weight,up_weight,down_weight,ns,n)
    def over_shard(a,d):
        return lax.ppermute(a,"shard",[(i,(i+d)%S) for i in range(S)]) if d else a
    def over_x(a,d):
        return lax.ppermute(a,"context",[(i*CC+j,((i+d)%CX)*CC+j) for i in range(CX) for j in range(CC)]) if d else a
    wa=[over_shard(pa,d) for d in range(S)]
    wb=[over_x(pb,d) for d in range(CX)]
    ids_all=ids_all.reshape(G,S,ns,n)
    valid_count=jnp.sum((ids_all!=(2048//60+1)).astype(jnp.float32))
    ids_mine=lax.dynamic_index_in_dim(ids_all,me_s,1,keepdims=False)
    ids_mine=lax.dynamic_slice_in_dim(ids_mine,(me_g//HP)*spg,spg,1).transpose(1,0,2).reshape(spg,G*n)
    edges=[bounds(ids_mine[i],256,256) for i in range(spg)]
    cols=[ids_mine[i][:,None] for i in range(spg)]
    def trade(a):
        return lax.all_to_all(a,("context","tensor"),0,0,tiled=True)
    qkv=[rows_out[0]]+[trade(a) for a in rows_out[1:]]
    mixed=[attend_fwd(qkv[i],ids_mine[i],cols[i],edges[i]) for i in range(spg)]
    arrived=[trade(mixed[i][0]) for i in range(spg-1)]+[mixed[-1][0]]
    keep=pad_mask.reshape(R,1).astype(jnp.float32)
    scale=jnp.full((1,PAIR),token_total/valid_count)
    vecs=jnp.stack([mixed_gain,mixed_shift,output_shift,second_gain,second_shift,down_shift,down_shift,down_shift])
    wides=jnp.stack([up_shift.reshape(T,cf),hidden_gain.reshape(T,cf),hidden_shift.reshape(T,cf)],axis=1)
    result,middle_grad,inner_low,second_low,out_low,middle_low,hidden_low,unit_low,early,*gs=feed(
        S,C,T,arrived,wa,wb,x,teacher.reshape(R,D),keep,scale,vecs,wides)
    *outs,last_g=weight_grads(S,C,T,out_low,second_low,middle_low,inner_low,unit_low,hidden_low,gs[-1])
    gs=list(lax.optimization_barrier(tuple(gs[:-1])+(last_g,)))
    NA=1+2*(S-1)
    hops=[over_shard(outs[1+i],1+i//2) for i in range(2*(S-1))],[over_x(outs[NA+1+i],1+i//2) for i in range(2*(CX-1))]
    ds=[attend_bwd(qkv[i],gs[i],mixed[i][0],mixed[i][1],ids_mine[i],cols[i],edges[i]) for i in range(spg)]
    if spg>1:
        ds[0],(first_a,first_b)=lax.optimization_barrier((ds[0],(hops[0][0::2],hops[1][0::2])))
        hops[0][0::2],hops[1][0::2]=first_a,first_b
    ra,rb=[outs[0]]+hops[0],[outs[NA]]+hops[1]
    ds=[trade(a) for a in ds[:-1]]+[ds[-1]]
    input_grad,dw1,dw2,late,early=finish(S,C,T,ds,first_low,wide,ra,rb,x,middle_grad,first_gain[None],early)
    dw2=dw2.reshape(-1,dw2.shape[-1])
    B=F//D
    vectors=(late[0],late[1],late[2],late[3],early[0],early[1],early[2],early[3],early[4],early[7+2*B:7+3*B].reshape(F),
             early[7:7+B].reshape(F),early[7+B:7+2*B].reshape(F),early[5])
    loss=jnp.sum(early[6])
    return (result.reshape(ns,n,D),loss/valid_count,input_grad.reshape(ns,n,D),
            dw1[0],dw1[1],dw1[2],dw2[:,:c2].T,dw2[:,c2:c2+cf],dw2[:,c2+cf:].T)+vectors


def solution(mesh):
    rows=P("shard",("context","tensor"),None)
    ids=P("shard",("context","tensor"))
    wide=P(("shard","context"),"tensor")
    tall=P("tensor",("shard","context"))
    weights=(wide,wide,wide,tall,wide,tall)
    return jax.shard_map(shards,mesh=mesh,in_specs=(rows,rows,ids,ids)+weights+(P(),)*13,
                         out_specs=(rows,P(),rows)+weights+(P(),)*13,check_vma=False)
```

```python
import functools

import jax
import jax.numpy as jnp
from jax import lax
from jax.experimental import pallas as pl
from jax.experimental.pallas import tpu as pltpu
from jax.sharding import PartitionSpec as P


NEG=-1e30
BLOCK=512
def _dot(a,b,ca,cb):
    return lax.dot_general(a,b,(((ca,),(cb,)),((),())),preferred_element_type=jnp.float32)

def half_masks(rows):
    lane=lax.broadcasted_iota(jnp.int32,(rows,128),1)
    return lane<64

def fwd_kernel(lo_ref,hi_ref,q_ref,k_ref,v_ref,col_ref,row_ref,o_ref,lse_ref,vt_ref,acc_ref,m_ref):
    i=pl.program_id(0)
    bq=acc_ref.shape[2]; bk=vt_ref.shape[3]; n=k_ref.shape[2]; per=bk//n
    upper=lax.broadcasted_iota(jnp.int32,(128,1),0)<64
    @pl.when(i==0)
    def _():
        def turn(j,_):
            vt=v_ref[pl.ds(j*per,per),0].reshape(bk,128).astype(jnp.float32).T
            vt_ref[0,j]=jnp.where(upper,vt,1.0).astype(jnp.bfloat16)
            vt_ref[1,j]=jnp.where(upper,1.0,vt).astype(jnp.bfloat16)
            return 0
        lax.fori_loop(0,vt_ref.shape[1],turn,0)
    left=half_masks(bq)
    q=q_ref[...].reshape(bq,128)*jnp.bfloat16(0.125)
    zero=jnp.zeros_like(q)
    qs=(jnp.where(left,q,zero),jnp.where(left,zero,q))
    ids_q=row_ref[i]
    acc_ref[...]=jnp.zeros_like(acc_ref)
    m_ref[...]=jnp.full_like(m_ref,NEG)
    def step(j,_):
        k=k_ref[pl.ds(j*per,per),0].reshape(bk,128)
        same=col_ref[pl.ds(pl.multiple_of(j*bk,bk),bk),:]==ids_q
        for h in range(2):
            sc=jnp.where(same,_dot(k,qs[h],1,1),NEG)
            old=m_ref[h:h+1,:]
            top=jnp.maximum(old,jnp.max(sc,axis=0,keepdims=True))
            e=jnp.exp(sc-top).astype(jnp.bfloat16)
            m_ref[h:h+1,:]=top
            acc_ref[h]=acc_ref[h]*jnp.exp(old-top)+_dot(vt_ref[h,j],e,1,0)
        return 0
    lax.fori_loop(lo_ref[i],hi_ref[i],step,0)
    t0=acc_ref[0,64:65,:]; t1=acc_ref[1,0:1,:]
    o=jnp.where(upper,acc_ref[0]/t0,acc_ref[1]/t1).T
    o_ref[...]=o.astype(jnp.bfloat16).reshape(o_ref.shape)
    lse_ref[0,0:1,:]=m_ref[0:1,:]+jnp.log(t0)
    lse_ref[0,1:2,:]=m_ref[1:2,:]+jnp.log(t1)

def bounds(ids,bq,bk):
    first=ids[::bq]; last=ids[bq-1::bq]
    start=jnp.sum((ids[None,:]<first[:,None]).astype(jnp.int32),axis=1)
    end=jnp.sum((ids[None,:]<=last[:,None]).astype(jnp.int32),axis=1)
    return start//bk,(end+bk-1)//bk

def attend_fwd(qkv,ids,col,edges,bq=BLOCK,bk=BLOCK):
    G,_,n,_=qkv.shape; L=G*n
    row=ids.reshape(L//bq,1,bq)
    part=lambda w: pl.BlockSpec((G,1,n,128),lambda i,*_: (0,w,0,0))
    ospec=pl.BlockSpec((bq//n,n,128),lambda i,*_:(i,0,0))
    return pl.pallas_call(fwd_kernel,
        grid_spec=pltpu.PrefetchScalarGridSpec(num_scalar_prefetch=2,grid=(L//bq,),
            in_specs=[pl.BlockSpec((bq//n,1,n,128),lambda i,*_:(i,0,0,0)),part(1),part(2),pl.BlockSpec((L,1),lambda i,*_:(0,0)),
                      pl.BlockSpec((L//bq,1,bq),lambda i,*_:(0,0,0))],
            out_specs=[ospec,pl.BlockSpec((1,2,bq),lambda i,*_:(i,0,0))],
            scratch_shapes=[pltpu.VMEM((2,L//bk,128,bk),jnp.bfloat16),pltpu.VMEM((2,128,bq),jnp.float32),pltpu.VMEM((2,bq),jnp.float32)]),
        out_shape=[jax.ShapeDtypeStruct((G,n,128),jnp.bfloat16),jax.ShapeDtypeStruct((L//bq,2,bq),jnp.float32)],
        compiler_params=pltpu.CompilerParams(dimension_semantics=("arbitrary",),vmem_limit_bytes=63<<20),
        cost_estimate=pl.CostEstimate(flops=4*L*1024*128*2,bytes_accessed=8*L*256,transcendentals=2*L*1024),
        name="attend_fwd")(*edges,qkv,qkv,qkv,col,row)

def bwd_kernel(lo_ref,hi_ref,q_ref,k_ref,v_ref,g_ref,o_ref,lse_ref,col_ref,row_ref,d_ref,dqa,dka,dva):
    i=pl.program_id(0)
    bq=dqa.shape[1]; bk=BLOCK; n=k_ref.shape[2]; per=bk//n
    @pl.when(i==0)
    def _():
        dka[...]=jnp.zeros_like(dka); dva[...]=jnp.zeros_like(dva)
    left=half_masks(bq)
    q=q_ref[...].reshape(bq,128)*jnp.bfloat16(0.125)
    g=g_ref[...].reshape(bq,128)
    zero=jnp.zeros_like(q)
    qs=(jnp.where(left,q,zero),jnp.where(left,zero,q))
    gs=(jnp.where(left,g,zero),jnp.where(left,zero,g))
    d_t=(g.astype(jnp.float32)*o_ref[...].reshape(bq,128).astype(jnp.float32)).T
    lses=(lse_ref[0,0:1,:],lse_ref[0,1:2,:])
    ds=(jnp.sum(d_t[:64],axis=0,keepdims=True),jnp.sum(d_t[64:],axis=0,keepdims=True))
    ids_q=row_ref[i]
    dqa[...]=jnp.zeros_like(dqa)
    def step(j,_):
        k=k_ref[pl.ds(j*per,per),0].reshape(bk,128)
        v=v_ref[pl.ds(j*per,per),0].reshape(bk,128)
        rows=pl.ds(pl.multiple_of(j*bk,bk),bk)
        same=col_ref[rows,:]==ids_q
        dk=dka[rows,:]; dv=dva[rows,:]
        for h in range(2):
            st=_dot(k,qs[h],1,1)
            p=jnp.exp(jnp.where(same,st,NEG)-lses[h])
            dp=_dot(v,gs[h],1,1)
            d=(p*(dp-ds[h])).astype(jnp.bfloat16)
            dv=dv+_dot(p.astype(jnp.bfloat16),gs[h],1,0)
            dk=dk+_dot(d,qs[h],1,0)
            dqa[h]+=_dot(d,k,0,0)
        dka[rows,:]=dk; dva[rows,:]=dv
        return 0
    lax.fori_loop(lo_ref[i],hi_ref[i],step,0)
    d_ref[pl.ds(i*(bq//n),bq//n),0]=(jnp.where(left,dqa[0],dqa[1])*0.125).astype(jnp.bfloat16).reshape(bq//n,n,128)
    @pl.when(i==pl.num_programs(0)-1)
    def _():
        d_ref[:,1]=dka[...].astype(jnp.bfloat16).reshape(d_ref.shape[0],n,128)
        d_ref[:,2]=dva[...].astype(jnp.bfloat16).reshape(d_ref.shape[0],n,128)

def attend_bwd(qkv,g,o,lse,ids,col,edges,bq=BLOCK):
    bk=BLOCK
    G,_,n,_=qkv.shape; L=G*n
    row=ids.reshape(L//bq,1,bq)
    part=lambda w: pl.BlockSpec((G,1,n,128),lambda i,*_: (0,w,0,0))
    ospec=pl.BlockSpec((bq//n,n,128),lambda i,*_:(i,0,0))
    return pl.pallas_call(bwd_kernel,
        grid_spec=pltpu.PrefetchScalarGridSpec(num_scalar_prefetch=2,grid=(L//bq,),
            in_specs=[pl.BlockSpec((bq//n,1,n,128),lambda i,*_:(i,0,0,0)),part(1),part(2),ospec,
                      ospec,pl.BlockSpec((1,2,bq),lambda i,*_:(i,0,0)),pl.BlockSpec((L,1),lambda i,*_:(0,0)),pl.BlockSpec((L//bq,1,bq),lambda i,*_:(0,0,0))],
            out_specs=pl.BlockSpec((G,3,n,128),lambda i,*_:(0,0,0,0)),
            scratch_shapes=[pltpu.VMEM((2,bq,128),jnp.float32)]+[pltpu.VMEM((L,128),jnp.float32)]*2),
        out_shape=jax.ShapeDtypeStruct((G,3,n,128),jnp.bfloat16),
        compiler_params=pltpu.CompilerParams(dimension_semantics=("arbitrary",),vmem_limit_bytes=63<<20),
        cost_estimate=pl.CostEstimate(flops=1000000,bytes_accessed=1000000,transcendentals=0),
        name="attend_bwd")(*edges,qkv,qkv,qkv,g,o,lse,col,row)


EPS=1e-5
PAIR=128

def norm_parts(v):
    m=jnp.mean(v,axis=-1,keepdims=True)
    s=jnp.mean(v*v,axis=-1,keepdims=True)-m*m
    r=lax.rsqrt(s+EPS)
    return (v-m)*r,r

def norm_back(e,h,r,gain):
    t=e*gain
    return r*(t-jnp.mean(t,axis=-1,keepdims=True)-h*jnp.mean(t*h,axis=-1,keepdims=True))


MESH_ID=pl.DeviceIdType.MESH

class Place:
    def __init__(self,S,C,T):
        self.CC=2 if C%2==0 else 1
        self.size={"t":T,"s":S,"x":C//self.CC,"c":self.CC}
        c=lax.axis_index("context")
        self.at={"t":lax.axis_index("tensor"),"s":lax.axis_index("shard"),"x":c//self.CC,"c":lax.rem(c,self.CC)}
        self.group=c*T+self.at["t"]
        self.T=T; self.G=C*T
    def peers(self,axis):
        m=self.size[axis]
        for d in range(1,m):
            other=lax.rem(self.at[axis]+d,m)
            if axis=="t": yield d-1,other,{"tensor":other}
            elif axis=="s": yield d-1,other,{"shard":other}
            elif axis=="x": yield d-1,other,{"context":other*self.CC+self.at["c"]}
            else: yield d-1,other,{"context":self.at["x"]*self.CC+other}
    def group_peers(self):
        for d in range(1,self.G):
            other=lax.rem(self.group+d,self.G)
            yield d-1,other,{"context":other//self.T,"tensor":lax.rem(other,self.T)}

def slots(size,order):
    base,total={},0
    for a in order:
        base[a]=total; total+=size[a]-1
    return base,total

def greet(place):
    barrier=pltpu.get_barrier_semaphore()
    count=0
    for _,_,dev in place.group_peers():
        pl.semaphore_signal(barrier,inc=1,device_id=dev,device_id_type=MESH_ID); count+=1
    for _,_,dev in place.peers("s"):
        pl.semaphore_signal(barrier,inc=1,device_id=dev,device_id_type=MESH_ID); count+=1
    pl.semaphore_wait(barrier,count)

class VectorSum:
    order="csxt"
    def __init__(self,place,cur,recs,send,recv):
        self.place,self.cur,self.send,self.recv=place,cur,send,recv
        self.recs=dict(zip(self.order,recs))
        self.base,_=slots(place.size,self.order)
    def copies(self,axis):
        at=self.place.at[axis]
        return [remote(self.cur,self.recs[axis].at[at],self.send.at[self.base[axis]+k],self.recv.at[self.base[axis]+k],dev)
                for k,_,dev in self.place.peers(axis)]
    def start(self,axis):
        self.recs[axis][self.place.at[axis]]=self.cur[...]
        for c in self.copies(axis): c.start()
    def end(self,axis):
        for c in self.copies(axis): c.wait()
        rec=self.recs[axis]
        total=rec[0]
        for i in range(1,self.place.size[axis]): total=total+rec[i]
        self.cur[...]=total

def vector_scratch(size,rows,D):
    _,total=slots(size,VectorSum.order)
    dma=pltpu.SemaphoreType.DMA
    return [pltpu.VMEM((rows,D),jnp.float32),[pltpu.VMEM((size[a],rows,D),jnp.float32) for a in VectorSum.order],dma((total,)),dma((total,))]

def remote(src,dst,send,recv,dev):
    return pltpu.make_async_remote_copy(src_ref=src,dst_ref=dst,send_sem=send,recv_sem=recv,device_id=dev,device_id_type=MESH_ID)

def fetch(sources,buffers,sem):
    copies=[pltpu.make_async_copy(a,b,sem.at[i]) for i,(a,b) in enumerate(zip(sources,buffers))]
    for c in copies: c.start()
    return copies

def project_kernel(S,C,T,x_ref,gain_ref,shift_ref,wq_ref,wk_ref,wv_ref,qs_ref,vs_ref,ids_ref,wo_ref,wu_ref,wd_ref,
                   low_ref,wide_ref,allids_ref,pa_ref,pb_ref,*rest):
    spg=len(rest)-17
    rows_refs=rest[:spg]
    *scratch,buffers,load=rest[spg:]
    loads=fetch((wq_ref,wk_ref,wv_ref,wo_ref,wu_ref,wd_ref,ids_ref,x_ref,gain_ref,shift_ref,qs_ref,vs_ref),buffers,load)
    wq_ref,wk_ref,wv_ref,wo_ref,wu_ref,wd_ref,ids_ref,x_ref,gain_ref,shift_ref,qs_ref,vs_ref=buffers
    project_body(S,C,T,loads,x_ref,gain_ref,shift_ref,wq_ref,wk_ref,wv_ref,(qs_ref,None,vs_ref),ids_ref,wo_ref,wu_ref,wd_ref,
                 low_ref,wide_ref,allids_ref,pa_ref,pb_ref,rows_refs,*scratch)

def project_body(S,C,T,loads,x_ref,gain_ref,shift_ref,wq_ref,wk_ref,wv_ref,bias_refs,ids_ref,wo_ref,wu_ref,wd_ref,
                   low_ref,wide_ref,allids_ref,pa_ref,pb_ref,rows_refs,
                   zbuf,z_send,z_recv,p_send,p_recv,wbuf,obuf,idbuf,ag_send,ag_recv,a_send,a_recv,i_send,i_recv,local):
    place=Place(S,C,T)
    R,D=low_ref.shape
    G,_,n=rows_refs[0].shape[:3]
    spg=len(rows_refs)
    HP=D//PAIR; SG=G//HP
    cols=wbuf.shape[-1]; hpt=cols//PAIR
    me=place.group
    order="tsxc"
    base,total=slots(place.size,order)
    own=[place.at[a] for a in order]
    for c in loads[:6]: c.wait()
    for w,ref in enumerate((wq_ref,wk_ref,wv_ref)):
        wbuf[w,own[0],own[1],own[2],own[3]]=ref[...].astype(jnp.bfloat16)
    t0=place.at["t"]
    HR,c2=zbuf.shape[-2:]
    c0=wo_ref.shape[0]; cf=wu_ref.shape[1]
    zbuf[t0,:,:,0:c0]=wo_ref[...].T.astype(jnp.bfloat16).reshape(2,HR,c0)
    zbuf[t0,:,:,c0:c0+cf]=wu_ref[...].astype(jnp.bfloat16).reshape(2,HR,cf)
    zbuf[t0,:,:,c0+cf:]=wd_ref[...].T.astype(jnp.bfloat16).reshape(2,HR,cf)
    cuts=[0,(c0+cf)//128*128,c0+2*cf]
    def hop(way,h,piece,j):
        to=t0+1 if way==0 else t0-1
        lane=slice(cuts[j],cuts[j+1])
        return remote(zbuf.at[piece,:,:,lane],zbuf.at[piece,:,:,lane],z_send.at[way,h-1,j],z_recv.at[way,h-1,j],{"tensor":lax.rem(to+T,T)})
    def line_start(j):
        @pl.when(t0<T-1)
        def _(): hop(0,1,t0,j).start()
        @pl.when(t0>0)
        def _(): hop(1,1,t0,j).start()
    def line_pass(h,j):
        @pl.when(t0>=h)
        def _():
            hop(0,h,lax.rem(t0-h+T,T),j).wait_recv()
            @pl.when(t0<T-1)
            def _(): hop(0,h+1,lax.rem(t0-h+T,T),j).start()
        @pl.when(t0+h<=T-1)
        def _():
            hop(1,h,lax.rem(t0+h,T),j).wait_recv()
            @pl.when(t0>0)
            def _(): hop(1,h+1,lax.rem(t0+h,T),j).start()
    def line_end():
        for j in range(2):
            for h in range(1,T):
                @pl.when((t0<T-1)&(t0>=h-1))
                def _(): hop(0,h,lax.rem(t0-h+1+T,T),j).wait_send()
                @pl.when((t0>0)&(t0+h-1<=T-1))
                def _(): hop(1,h,lax.rem(t0+h-1,T),j).wait_send()
    def plane(j):
        lane=slice(cuts[j],cuts[j+1])
        x0,s0=place.at["x"],place.at["s"]
        out=[pltpu.make_async_copy(zbuf.at[:,0,:,lane],pa_ref.at[x0,:,:,lane],local.at[8+2*j]),
             pltpu.make_async_copy(zbuf.at[:,1,:,lane],pb_ref.at[s0,:,:,lane],local.at[9+2*j])]
        for k,_,dev in place.peers("x"):
            c=remote(zbuf.at[:,0,:,lane],pa_ref.at[x0,:,:,lane],p_send.at[0,k,j],p_recv.at[0,k,j],dev); sent.append(c); out.append(c)
        for k,_,dev in place.peers("s"):
            c=remote(zbuf.at[:,1,:,lane],pb_ref.at[s0,:,:,lane],p_send.at[1,k,j],p_recv.at[1,k,j],dev); sent.append(c); out.append(c)
        for c in out: c.start()
        return out
    greet(place)
    stages={2:"tsxc",1:"txsc",0:"tsxc"}
    sent=[]
    copies={}
    def start(w,r):
        done=stages[w][:r]; axis=stages[w][r]
        idx=tuple(slice(None) if a in done else place.at[a] for a in order)
        copies[w,r]=[]
        for k,_,dev in place.peers(axis):
            c=remote(wbuf.at[(w,)+idx],wbuf.at[(w,)+idx],ag_send.at[w,base[axis]+k],ag_recv.at[w,base[axis]+k],dev)
            c.start(); copies[w,r].append(c); sent.append(c)
    def arrive(w,r):
        for c in copies[w,r]: c.wait_recv()
    for w in (2,1,0): start(w,0)
    line_start(0); line_start(1)
    loads[6].wait()
    ids_own=pltpu.make_async_copy(ids_ref,idbuf.at[place.at["s"]],local.at[0]); ids_own.start()
    id_first=[]
    for k,_,dev in place.peers("s"):
        c=remote(ids_ref,idbuf.at[place.at["s"]],i_send.at[k],i_recv.at[k],dev); c.start(); id_first.append(c); sent.append(c)
    for c in loads[7:]: c.wait()
    step=min(64,R)
    def norm(i,_):
        rows=pl.ds(pl.multiple_of(i*step,step),step)
        h,_r=norm_parts(x_ref[rows,:])
        low_ref[rows,:]=(h*gain_ref[...]+shift_ref[...]).astype(jnp.bfloat16)
        return 0
    lax.fori_loop(0,R//step,norm,0)
    def spread_ids():
        ids_own.wait()
        for c in id_first: c.wait_recv()
        out=[]
        mine=pltpu.make_async_copy(idbuf,allids_ref.at[me],local.at[1]); mine.start(); out.append(mine)
        for k,_,dev in place.group_peers():
            c=remote(idbuf,allids_ref.at[me],i_send.at[S-1+k],i_recv.at[S-1+k],dev); c.start(); sent.append(c); out.append(c)
        return out
    late=[]
    def compute(w):
        def one(t,_):
            y=_dot(low_ref[...],wbuf[w,t].reshape(D,cols),1,0)
            if bias_refs[w] is not None: y=y+bias_refs[w][:,pl.ds(pl.multiple_of(t*cols,128),cols)]
            y=y.astype(jnp.bfloat16)
            for g in range(SG):
                for j in range(hpt):
                    obuf[w,g*HP+t*hpt+j]=y[g*spg*n:(g+1)*spg*n,j*PAIR:(j+1)*PAIR].reshape(spg,n,PAIR)
            return 0
        lax.fori_loop(0,T,one,0)
        mine=pltpu.make_async_copy(obuf.at[w,me,0],rows_refs[0].at[me,w],local.at[2+w]); mine.start(); late.append(mine)
        for k,other,dev in place.group_peers():
            c=remote(obuf.at[w,other,0],rows_refs[0].at[me,w],a_send.at[w,k],a_recv.at[w,k],dev)
            c.start(); sent.append(c); late.append(c)
        for i in range(1,spg):
            c=pltpu.make_async_copy(obuf.at[w,:,i],rows_refs[i].at[:,w],local.at[12+w*spg+i]); c.start(); late.append(c)
        keep=pltpu.make_async_copy(wbuf.at[w],wide_ref.at[w],local.at[5+w]); keep.start(); late.append(keep)
    arrive(2,0); start(2,1)
    arrive(1,0); start(1,1)
    ids_out=spread_ids()
    arrive(2,1); start(2,2)
    arrive(0,0); start(0,1)
    arrive(1,1); start(1,2)
    line_pass(1,0)
    arrive(2,2); start(2,3)
    line_pass(1,1)
    arrive(2,3); compute(2)
    arrive(1,2); start(1,3)
    if T>2: line_pass(2,0)
    arrive(0,1); start(0,2)
    arrive(1,3); compute(1)
    if T>2: line_pass(2,1)
    for h in range(3,T): line_pass(h,0)
    ids_out=ids_out+plane(0)
    arrive(0,2); start(0,3)
    for h in range(3,T): line_pass(h,1)
    ids_out=ids_out+plane(1)
    arrive(0,3); compute(0)
    for c in late+ids_out:
        if any(c is o for o in sent): c.wait_recv()
        else: c.wait()
    for c in sent: c.wait_send()
    line_end()

def project(S,C,T,x,gain,shift,wq,wk,wv,qs,vs,ids,wo,wu,wd,ns,n):
    R,D=x.shape
    G=C*T; HP=D//PAIR; spg=ns*HP//G
    DR,cols=wq.shape
    CC=2 if C%2==0 else 1
    piece=(3,T,S,C//CC,CC,DR,cols)
    HR=DR//2; width=wo.shape[0]+2*wu.shape[1]; most=max(S,C//CC)-1
    _,total=slots({"t":T,"s":S,"x":C//CC,"c":CC},"tsxc")
    vm=pl.BlockSpec(memory_space=pltpu.VMEM); anyspec=pl.BlockSpec(memory_space=pl.ANY)
    dma=pltpu.SemaphoreType.DMA
    return pl.pallas_call(functools.partial(project_kernel,S,C,T),
        in_specs=[pl.BlockSpec(memory_space=pltpu.HBM)]*12,
        out_specs=[vm]+[anyspec]*(4+spg),
        out_shape=[jax.ShapeDtypeStruct((R,D),jnp.bfloat16),jax.ShapeDtypeStruct(piece,jnp.bfloat16),jax.ShapeDtypeStruct((G,S,1,ns*n),jnp.int32),
                   jax.ShapeDtypeStruct((C//CC,T,HR,width),jnp.bfloat16),jax.ShapeDtypeStruct((S,T,HR,width),jnp.bfloat16)]+
                  [jax.ShapeDtypeStruct((G,3,n,PAIR),jnp.bfloat16)]*spg,
        scratch_shapes=[pltpu.VMEM((T,2,HR,width),jnp.bfloat16),dma((2,T-1,2)),dma((2,T-1,2)),dma((2,most,2)),dma((2,most,2)),pltpu.VMEM(piece,jnp.bfloat16),pltpu.VMEM((3,G,spg,n,PAIR),jnp.bfloat16),pltpu.VMEM((S,1,ns*n),jnp.int32),
                        dma((3,total)),dma((3,total)),dma((3,G-1)),dma((3,G-1)),dma((S-1+G-1,)),dma((S-1+G-1,)),dma((12+3*spg,)),
                        [pltpu.VMEM(a.shape,a.dtype) for a in (wq,wk,wv,wo,wu,wd,ids,x,gain,shift,qs,vs)],dma((12,))],
        compiler_params=pltpu.CompilerParams(collective_id=0,has_side_effects=True,vmem_limit_bytes=63<<20),
        name="project")(x,gain,shift,wq,wk,wv,qs,vs,ids,wo,wu,wd)


SUB=128

def feed_kernel(S,C,T,NC,NO,*refs):
    place=Place(S,C,T)
    CX=place.size["x"]; CC=place.CC
    spg=NO
    o_refs=refs[:spg]; o_ref=o_refs[-1]; refs=refs[spg-1:]
    wa_refs=refs[1:1+S]; wb_refs=refs[1+S:1+S+CX]
    (x_ref,teach_ref,keep_ref,scale_ref,vec_ref,wide_ref)=refs[1+S+CX:7+S+CX]
    (res_ref,mg_ref,inner_ref,second_ref,out_ref,midl_ref,hid_ref,unl_ref,sum_ref)=refs[7+S+CX:16+S+CX]
    g_refs=refs[16+S+CX:16+S+CX+spg]; refs=refs[spg-1:]
    (w2,rbuf,mix,inner,second,outl,midl,hid,unl,act,dact,tt,acc,middle,og,s1,s2,res,mg,gout,vacc,wacc,
     w_local,w_send,w_recv,a_send,a_recv,g_send,g_recv,misc,o_sem,s1b,s2b,buffers,load)=refs[17+S+CX:]
    loads=fetch((x_ref,teach_ref,keep_ref,scale_ref,vec_ref,wide_ref),buffers,load)
    x_ref,teach_ref,keep_ref,scale_ref,vec_ref,wide_ref=buffers
    R,D=x_ref.shape
    G,n=o_ref.shape[:2]
    HP=D//PAIR; SG=G//HP
    HR=w2.shape[-2]
    F=hid.shape[1]; cf=F//T; c2=D//T
    B=R//spg; sub=min(SUB,n)
    f32=jnp.float32; b16=jnp.bfloat16
    me=place.group
    s0,x0,c0=place.at["s"],place.at["x"],place.at["c"]
    DS=D//S
    ranges=((0,c2),(c2,c2+cf),(c2+cf,c2+2*cf))
    def pieces(r):
        lo,hi=ranges[r]
        out=[]
        for d in range(S):
            src=lax.rem(s0+S-d,S)
            for i in range(CX):
                out.append((wa_refs[d].at[i,:,:,lo:hi],w2.at[:,src,i,c0,0,:,lo:hi]))
        for d in range(CX):
            src=lax.rem(x0+CX-d,CX)
            for i in range(S):
                out.append((wb_refs[d].at[i,:,:,lo:hi],w2.at[:,i,src,c0,1,:,lo:hi]))
        return out
    local=[[pltpu.make_async_copy(a,b,w_local.at[r,i]) for i,(a,b) in enumerate(pieces(r))] for r in range(3)]
    for r in range(3):
        for c in local[r]: c.start()
    barrier=pltpu.get_barrier_semaphore()
    count=0
    for _,_,dev in place.group_peers():
        pl.semaphore_signal(barrier,inc=1,device_id=dev,device_id_type=MESH_ID); count+=1
    pl.semaphore_wait(barrier,count)
    own=[pltpu.make_async_copy(o_ref.at[me],rbuf.at[me,spg-1],misc.at[0])]
    own+=[pltpu.make_async_copy(o_refs[i],rbuf.at[:,i],misc.at[1+i]) for i in range(spg-1)]
    for c in own: c.start()
    rows_in=[remote(o_ref.at[other],rbuf.at[me,spg-1],a_send.at[k],a_recv.at[k],dev) for k,other,dev in place.group_peers()]
    for c in rows_in: c.start()
    far=[[remote(a,b,w_send.at[r,k,i],w_recv.at[r,k,i],dev) for k,_,dev in place.peers("c") for i,(a,b) in enumerate(pieces(r))] for r in range(3)]
    for r in range(3):
        for c in far[r]: c.start()
    def weights(r):
        for c in local[r]: c.wait()
        for c in far[r]: c.wait_recv()
    sum_ref[...]=jnp.zeros_like(sum_ref)
    vacc[...]=jnp.zeros_like(vacc); wacc[...]=jnp.zeros_like(wacc)
    def vec(i): return vec_ref[i:i+1,:]
    MIXG,MIXS,OUTS,SECG,SECS,DOWNS=range(6)
    def each(fn):
        def body(i,_):
            fn(pl.ds(pl.multiple_of(i*sub,sub),sub),i)
            return 0
        lax.fori_loop(0,B//sub,body,0)
    def fold(a):
        return jnp.sum(a.reshape(a.shape[0]//8,8,a.shape[1]),axis=0)
    def lanes(a):
        v=a[:,:PAIR]
        for j in range(1,a.shape[1]//PAIR): v=v+a[:,j*PAIR:(j+1)*PAIR]
        return v
    def flat(t,lo,hi,s=None):
        if s is None: return w2[t,:,:,:,:,:,lo:hi].reshape(D,hi-lo)
        return w2[t,s,:,:,:,:,lo:hi].reshape(DS,hi-lo)
    for c in loads: c.wait()
    weights(0)
    def block(b):
        r0=b*B
        def rows(i): return pl.ds(pl.multiple_of(r0+i*sub,sub),sub)
        def tokens(i): return pl.ds(pl.multiple_of(i//(n//sub)*(spg*n)+b*n+lax.rem(i,n//sub)*sub,sub),sub)
        whole=pl.ds(r0,B)
        if b<spg-1: own[1+b].wait()
        else:
            own[0].wait()
            for c in rows_in: c.wait_recv()
        for gg in range(SG):
            for h in range(HP):
                mix[gg*n:(gg+1)*n,h*PAIR:(h+1)*PAIR]=rbuf[gg*HP+h,b]
        def f1(q,i):
            h,_=norm_parts(mix[q,:].astype(f32))
            inner[rows(i),:]=(h*vec(MIXG)+vec(MIXS)).astype(b16)
        each(f1)
        acc[...]=jnp.zeros_like(acc)
        def att(t,_):
            a=inner[whole,pl.ds(pl.multiple_of(t*c2,128),c2)]
            for s in range(S):
                acc[:,s*DS:(s+1)*DS]+=_dot(a,flat(t,0,c2,s),1,1)
            return 0
        lax.fori_loop(0,T,att,0)
        def f2(q,i):
            m=x_ref[tokens(i),:]+(acc[q,:]+vec(OUTS))
            middle[q,:]=m
            h,_=norm_parts(m)
            second[rows(i),:]=(h*vec(SECG)+vec(SECS)).astype(b16)
        each(f2)
        if b==0: weights(1)
        s1[...]=jnp.zeros_like(s1); s2[...]=jnp.zeros_like(s2)
        def up(t,_):
            a=second[whole,:]
            w=cf//NC
            for j in range(NC):
                lane=slice(j*w,(j+1)*w)
                u=_dot(a,flat(t,c2+j*w,c2+(j+1)*w),1,0)+wide_ref[t,0:1,lane]
                u2=u*u
                th=jnp.tanh(0.7978845608028654*u*(1.0+0.044715*u2))
                half=0.5+0.5*th
                v=u*half
                act[t,:,lane]=v
                dact[t,:,lane]=half+(0.5*0.7978845608028654)*u*(1.0-th*th)*(1.0+(3*0.044715)*u2)
                s1[...]+=lanes(v); s2[...]+=lanes(v*v)
            return 0
        lax.fori_loop(0,T,up,0)
        def f3(q,i):
            m=jnp.sum(s1[q,:],axis=1,keepdims=True)/F
            v=jnp.sum(s2[q,:],axis=1,keepdims=True)/F-m*m
            s1[q,:]=jnp.broadcast_to(m,(sub,PAIR)); s2[q,:]=jnp.broadcast_to(lax.rsqrt(v+EPS),(sub,PAIR))
        each(f3)
        if b==0: weights(2)
        acc[...]=jnp.zeros_like(acc)
        def down(t,_):
            fcols=pl.ds(pl.multiple_of(t*cf,128),cf)
            def e(q,i):
                h=(act[t,q,:]-s1[q,0:1])*s2[q,0:1]
                act[t,q,:]=h
                hid[rows(i),fcols]=(h*wide_ref[t,1:2,:]+wide_ref[t,2:3,:]).astype(b16)
            each(e)
            a=hid[whole,fcols]
            for s in range(S):
                acc[:,s*DS:(s+1)*DS]+=_dot(a,flat(t,c2+cf,c2+2*cf,s),1,1)
            return 0
        lax.fori_loop(0,T,down,0)
        def f4(q,i):
            r=middle[q,:]+(acc[q,:]+vec(DOWNS))
            res[tokens(i),:]=r
            err=r-teach_ref[tokens(i),:]
            k=keep_ref[tokens(i),:]
            e=k*err
            vacc[6]+=fold(e*err)
            g=e*scale_ref[0:1,0:1]
            og[q,:]=g
            low_=g.astype(b16)
            outl[rows(i),:]=low_
            vacc[5]+=fold(low_.astype(f32))
        each(f4)
        def back1(t,_):
            a=outl[whole,:]
            w=cf//NC
            for j in range(NC):
                lane=slice(j*w,(j+1)*w)
                g=_dot(a,flat(t,c2+cf+j*w,c2+cf+(j+1)*w),1,0)
                h=act[t,:,lane]
                wacc[0,t,:,lane]+=fold(g*h); wacc[1,t,:,lane]+=fold(g)
                v=g*wide_ref[t,1:2,lane]
                tt[t,:,lane]=v
                s1b[...]+=lanes(v); s2b[...]+=lanes(v*h)
            return 0
        s1b[...]=jnp.zeros_like(s1b); s2b[...]=jnp.zeros_like(s2b)
        lax.fori_loop(0,T,back1,0)
        def f5(q,i):
            s1b[q,:]=jnp.broadcast_to(jnp.sum(s1b[q,:],axis=1,keepdims=True)/F,(sub,PAIR))
            s2b[q,:]=jnp.broadcast_to(jnp.sum(s2b[q,:],axis=1,keepdims=True)/F,(sub,PAIR))
        each(f5)
        acc[...]=jnp.zeros_like(acc)
        def back2(t,_):
            fcols=pl.ds(pl.multiple_of(t*cf,128),cf)
            def e(q,i):
                ag=s2[q,0:1]*(tt[t,q,:]-s1b[q,0:1]-act[t,q,:]*s2b[q,0:1])
                ul=(ag*dact[t,q,:]).astype(b16)
                unl[rows(i),fcols]=ul
                wacc[2,t]+=fold(ul.astype(f32))
            each(e)
            a=unl[whole,fcols]
            for s in range(S):
                acc[:,s*DS:(s+1)*DS]+=_dot(a,flat(t,c2,c2+cf,s),1,1)
            return 0
        lax.fori_loop(0,T,back2,0)
        def f6(q,i):
            h,r=norm_parts(middle[q,:])
            e=acc[q,:]
            vacc[3]+=fold(e*h); vacc[4]+=fold(e)
            m=og[q,:]+norm_back(e,h,r,vec(SECG))
            mg[tokens(i),:]=m
            ml=m.astype(b16)
            midl[rows(i),:]=ml
            vacc[2]+=fold(ml.astype(f32))
        each(f6)
        def back3(t,_):
            acc[:,pl.ds(pl.multiple_of(t*c2,128),c2)]=_dot(midl[whole,:],flat(t,0,c2),1,0)
            return 0
        lax.fori_loop(0,T,back3,0)
        def f7(q,i):
            h,r=norm_parts(mix[q,:].astype(f32))
            e=acc[q,:]
            vacc[0]+=fold(e*h); vacc[1]+=fold(e)
            mix[q,:]=norm_back(e,h,r,vec(MIXG)).astype(b16)
        each(f7)
        for gg in range(SG):
            for h in range(HP):
                gout[b,gg*HP+h]=mix[gg*n:(gg+1)*n,h*PAIR:(h+1)*PAIR]
        copies=[pltpu.make_async_copy(src.at[whole],dst.at[whole],o_sem.at[b,i]) for i,(src,dst) in enumerate(
            ((inner,inner_ref),(second,second_ref),(outl,out_ref),(midl,midl_ref),(hid,hid_ref),(unl,unl_ref)))]
        for gg in range(SG):
            part=pl.ds(gg*spg*n+b*n,n)
            copies+=[pltpu.make_async_copy(src.at[part],dst.at[part],o_sem.at[b,6+2*gg+i]) for i,(src,dst) in enumerate(((res,res_ref),(mg,mg_ref)))]
        if b<spg-1:
            copies.append(pltpu.make_async_copy(gout.at[b,me],g_refs[b].at[me],o_sem.at[b,6+2*SG]))
            far_g=[remote(gout.at[b,other],g_refs[b].at[me],g_send.at[b,k],g_recv.at[b,k],dev) for k,other,dev in place.group_peers()]
            for c in far_g: c.start()
            g_out.extend(far_g)
        else:
            copies.append(pltpu.make_async_copy(gout.at[b],g_refs[b],o_sem.at[b,6+2*SG]))
        for c in copies: c.start()
        return copies
    g_out=[]
    done=[]
    for b in range(spg): done+=block(b)
    for i in range(7):
        sum_ref[i:i+1,:]=jnp.sum(vacc[i],axis=0,keepdims=True)
    for i in range(3):
        for t in range(T):
            at=(i*F+t*cf)
            sum_ref[7+at//D:8+at//D,at%D:at%D+cf]=jnp.sum(wacc[i,t],axis=0,keepdims=True)
    for c in done: c.wait()
    for c in g_out: c.wait()
    for c in rows_in: c.wait_send()
    for r in range(3):
        for c in far[r]: c.wait_send()

def feed(S,C,T,o,wa,wb,x,teacher,keep,scale,vecs,wides):
    R,D=x.shape
    spg=len(o)
    G,n=o[0].shape[:2]
    rows=(G,spg,n,PAIR)
    CC=2 if C%2==0 else 1
    CX=C//CC
    HR,c2=wa[0].shape[-2:]
    cf=wides.shape[-1]; F=cf*T; B=R//spg; SG=G//(D//PAIR)
    b16,f32=jnp.bfloat16,jnp.float32
    vm=pl.BlockSpec(memory_space=pltpu.VMEM); anyspec=pl.BlockSpec(memory_space=pl.ANY)
    dma=pltpu.SemaphoreType.DMA
    V=lambda shape,dt=b16: pltpu.VMEM(shape,dt)
    NP=2*S*CX; NCC=max(CC-1,1)
    sums=7+3*F//D; sums+=-sums%8
    sds=jax.ShapeDtypeStruct
    return pl.pallas_call(functools.partial(feed_kernel,S,C,T,max(cf//512,1),spg),
        in_specs=[pl.BlockSpec(memory_space=pltpu.HBM)]*(spg+S+CX+6),
        out_specs=[anyspec]*8+[vm]+[anyspec]*spg,
        out_shape=[sds((R,D),f32),sds((R,D),f32)]+[sds((R,D),b16)]*4+[sds((R,F),b16)]*2+[sds((sums,D),f32)]+[sds((G,n,PAIR),b16)]*spg,
        scratch_shapes=[V((T,S,CX,CC,2,HR,c2)),V(rows),V((B,D)),V((R,D)),V((R,D)),V((R,D)),V((R,D)),V((R,F)),V((R,F)),
                        V((T,B,cf),f32),V((T,B,cf),f32),V((T,B,cf),f32),V((B,D),f32),V((B,D),f32),V((B,D),f32),V((B,PAIR),f32),V((B,PAIR),f32),
                        V((R,D),f32),V((R,D),f32),V((spg,G,n,PAIR)),V((7,8,D),f32),V((3,T,8,cf),f32),
                        dma((3,NP)),dma((3,NCC,NP)),dma((3,NCC,NP)),dma((G-1,)),dma((G-1,)),dma((spg,G-1)),dma((spg,G-1)),dma((spg,)),dma((spg,7+2*SG)),V((B,PAIR),f32),V((B,PAIR),f32),
                        [V(a.shape,a.dtype) for a in (x,teacher,keep,scale,vecs,wides)],dma((6,))],
        compiler_params=pltpu.CompilerParams(collective_id=3,has_side_effects=True,vmem_limit_bytes=63<<20),
        name="feed")(*o,*wa,*wb,x,teacher,keep,scale,vecs,wides)


def weight_grads_kernel(S,C,T,out_ref,second_ref,middle_ref,inner_ref,unit_ref,hidden_ref,g_ref,early_ref,*rest):
    CX0=C//(2 if C%2==0 else 1)
    NA=1+2*(S-1); NB=1+2*(CX0-1); TH=T//2
    pa_refs,pb_refs=rest[:NA],rest[NA:NA+NB]
    gin_ref,sum_ref,own,got,send,recv,local,a_send,a_recv,a_local,ev,ev_recs,v_send,v_recv,buffers,load=rest[NA+NB:]
    loads=fetch((early_ref,middle_ref,inner_ref,second_ref,unit_ref,out_ref,hidden_ref),(ev,)+tuple(buffers),load)
    middle_ref,inner_ref,second_ref,unit_ref,out_ref,hidden_ref=buffers
    place=Place(S,C,T)
    R,D=out_ref.shape
    CX=place.size["x"]; CC=place.CC
    HR,width=own.shape[-2:]
    c2=inner_ref.shape[1]//T; cf=unit_ref.shape[1]//T
    cc=place.at["c"]
    barrier=pltpu.get_barrier_semaphore()
    others=list(place.peers("c"))
    count=0
    for _,_,dev in place.group_peers():
        pl.semaphore_signal(barrier,inc=1,device_id=dev,device_id_type=MESH_ID); count+=1
    for _,_,dev in place.peers("s"):
        pl.semaphore_signal(barrier,inc=1,device_id=dev,device_id_type=MESH_ID); count+=1
    pl.semaphore_wait(barrier,count)
    me=place.group
    mine=pltpu.make_async_copy(g_ref.at[me],gin_ref.at[me],a_local.at[0]); mine.start()
    rows_in=[remote(g_ref.at[other],gin_ref.at[me],a_send.at[k],a_recv.at[k],dev) for k,other,dev in place.group_peers()]
    for c in rows_in: c.start()
    loads[0].wait()
    early=VectorSum(place,ev,ev_recs,v_send,v_recv)
    early.start("c")
    for c in loads[1:]: c.wait()
    plan=[(middle_ref,inner_ref,0,c2,c2),(second_ref,unit_ref,c2,cf,min(cf,512)),(out_ref,hidden_ref,c2+cf,cf,min(cf,512))]
    def swap(t):
        return [remote(own.at[t,:,:,other],got.at[t,k],send.at[t,k],recv.at[t,k],dev) for k,other,dev in others]
    def outs(t,act):
        def go(src,ref,sem,cond=None):
            if cond is None: act(pltpu.make_async_copy(src,ref,sem))
            else:
                @pl.when(cond)
                def _(): act(pltpu.make_async_copy(src,ref,sem))
        for d in range(S):
            src=got.at[t,0,lax.rem(place.at["s"]+d,S),:,0]
            if d==0: go(src,pa_refs[0].at[t],local.at[t,0])
            else:
                go(src,pa_refs[2*d-1].at[lax.rem(t,TH)],local.at[t,d],t<TH)
                go(src,pa_refs[2*d].at[lax.rem(t,TH)],local.at[t,d],t>=TH)
        for d in range(CX):
            src=got.at[t,0,:,lax.rem(place.at["x"]+d,CX),1]
            if d==0: go(src,pb_refs[0].at[t],local.at[t,S])
            else:
                go(src,pb_refs[2*d-1].at[lax.rem(t,TH)],local.at[t,S+d],t<TH)
                go(src,pb_refs[2*d].at[lax.rem(t,TH)],local.at[t,S+d],t>=TH)
    def settle(t):
        for c in swap(t): c.wait_recv()
        for s in range(S):
            for x in range(CX):
                total=own[t,s,x,cc].astype(jnp.float32)
                for k,_,_ in others:
                    total=total+got[t,k,s,x].astype(jnp.float32)
                got[t,0,s,x]=total.astype(jnp.bfloat16)
        outs(t,lambda c: c.start())
    def one(t,_):
        for left,right,base,cols,chunk in plan:
            for j in range(cols//chunk):
                y=_dot(left[...],right[:,pl.ds(pl.multiple_of(t*cols+j*chunk,128),chunk)],0,0)
                own[t,:,:,:,:,:,base+j*chunk:base+(j+1)*chunk]=y.astype(jnp.bfloat16).reshape(S,CX,CC,2,HR,chunk)
        for c in swap(t): c.start()
        @pl.when(t>0)
        def _(): settle(t-1)
        for i,(x,y) in enumerate(("cs","sx","xt")):
            if i+1<T:
                @pl.when(t==i+1)
                def _(): early.end(x); early.start(y)
        return 0
    lax.fori_loop(0,T,one,0)
    settle(T-1)
    for i,(x,y) in enumerate(("cs","sx","xt")):
        if i+1>=T: early.end(x); early.start(y)
    early.end("t")
    sum_ref[...]=ev[...]
    def finish(t,_):
        for c in swap(t): c.wait_send()
        outs(t,lambda c: c.wait())
        return 0
    lax.fori_loop(0,T,finish,0)
    mine.wait()
    for c in rows_in: c.wait()

def weight_grads(S,C,T,out_low,second_low,middle_low,inner_low,unit_low,hidden_low,g,early):
    R,D=out_low.shape
    CC=2 if C%2==0 else 1
    CX=C//CC; HR=D//(S*C*2); width=(D+2*unit_low.shape[1])//T
    hbm=pl.BlockSpec(memory_space=pltpu.HBM); anyspec=pl.BlockSpec(memory_space=pl.ANY)
    dma=pltpu.SemaphoreType.DMA
    return pl.pallas_call(functools.partial(weight_grads_kernel,S,C,T),
        in_specs=[hbm]*8,out_specs=[anyspec]*(2*S+2*CX-1)+[pl.BlockSpec(memory_space=pltpu.VMEM)],
        out_shape=[jax.ShapeDtypeStruct((T,CX,HR,width),jnp.bfloat16)]+[jax.ShapeDtypeStruct((T//2,CX,HR,width),jnp.bfloat16)]*(2*S-2)+
                  [jax.ShapeDtypeStruct((T,S,HR,width),jnp.bfloat16)]+[jax.ShapeDtypeStruct((T//2,S,HR,width),jnp.bfloat16)]*(2*CX-2)+[jax.ShapeDtypeStruct(g.shape,jnp.bfloat16),jax.ShapeDtypeStruct(early.shape,jnp.float32)],
        scratch_shapes=[pltpu.VMEM((T,S,CX,CC,2,HR,width),jnp.bfloat16),pltpu.VMEM((T,max(CC-1,1),S,CX,2,HR,width),jnp.bfloat16),
                        dma((T,max(CC-1,1))),dma((T,max(CC-1,1))),dma((T,S+CX)),dma((C*T-1,)),dma((C*T-1,)),dma((1,))]+vector_scratch({"t":T,"s":S,"x":CX,"c":CC},early.shape[0],D)+
                       [[pltpu.VMEM(a.shape,a.dtype) for a in (middle_low,inner_low,second_low,unit_low,out_low,hidden_low)],dma((7,))],
        compiler_params=pltpu.CompilerParams(collective_id=1,has_side_effects=True,vmem_limit_bytes=63<<20),
        name="weight_grads")(out_low,second_low,middle_low,inner_low,unit_low,hidden_low,g,early)


def finish_kernel(S,C,T,NO,*refs):
    d_refs=refs[:NO]
    finish_split(S,C,T,d_refs,*refs[NO:])

def finish_split(S,C,T,d_refs,low_ref,wide_ref,x_ref,mg_ref,gain_ref,*rest):
    CX0=C//(2 if C%2==0 else 1)
    NA=1+2*(S-1); NB=1+2*(CX0-1)
    ra_refs,rb_refs=rest[:NA],rest[NA:NA+NB]
    *rest,buffers,load=rest[NA+NB:]
    own_loads=fetch((low_ref,x_ref,mg_ref,gain_ref),buffers,load)
    finish_body(S,C,T,own_loads,d_refs,buffers[0],wide_ref,*buffers[1:],ra_refs,rb_refs,*rest)

def finish_body(S,C,T,own_loads,d_refs,low_ref,wide_ref,x_ref,mg_ref,gain_ref,ra_refs,rb_refs,
                  grad_ref,dq_ref,dk_ref,dv_ref,do_ref,du_ref,dd_ref,late_ref,
                  rbuf,wbuf,acc,gbuf,rc,ra2,rb2,ra3,rb3,gz,gzr,bz,bzr,z_send,z_recv,
                  xa,xb,ya,yb,za,zb,d2,
                  lv,lv_recs,v_send,v_recv,
                  a_send,a_recv,w_send,w_recv,g_send,g_recv,local):
    gz,gzr,bz,bzr=[list(r) for r in (gz,gzr,bz,bzr)]
    place=Place(S,C,T)
    R,D=low_ref.shape
    G,_,n=d_refs[0].shape[:3]
    spg=len(d_refs)
    HP=D//PAIR; SG=G//HP
    cols=wbuf.shape[-1]; hpt=cols//PAIR
    DR=wbuf.shape[-2]
    CX=place.size["x"]; CC=place.CC; TH=T//2
    t0,s0,x0,c0=place.at["t"],place.at["s"],place.at["x"],place.at["c"]
    me=place.group
    f32=jnp.float32; b16=jnp.bfloat16
    sent=[]
    def go(copies):
        for c in copies: c.start()
        sent.extend(copies)
        return copies
    def land(copies):
        for c in copies: c.wait_recv()
    steps=[1<<k for k in range(T.bit_length()-1)]
    def bit(k): return lax.rem(t0//steps[k],2)
    def trade(k,which,bufs,recs):
        other=t0+steps[k]-2*steps[k]*bit(k)
        return go([remote(bufs[k].at[:,1-bit(k)],recs[k],z_send.at[which,k],z_recv.at[which,k],{"tensor":other})])
    def settle(k,copies,bufs,recs):
        land(copies)
        v=bufs[k][:,bit(k)].astype(f32)+recs[k][...].astype(f32)
        if k+1<len(steps): bufs[k+1][...]=v.astype(b16).reshape(bufs[k+1].shape)
        return v
    gzs=[[r.at[w] for r in gz] for w in range(3)]; gzrs=[[r.at[w] for r in gzr] for w in range(3)]
    loads=[pltpu.make_async_copy(wide_ref,wbuf,local.at[3*spg])]
    def arrivals(refs,buf,base):
        out=[pltpu.make_async_copy(refs[0],buf.at[0],local.at[base])]
        for i,ref in enumerate(refs[1:]):
            out.append(pltpu.make_async_copy(ref,buf.at[1+i//2,i%2*TH:i%2*TH+TH],local.at[base+1+i]))
        return out
    loads+=arrivals(ra_refs,xa,3*spg+1)
    loads+=arrivals(rb_refs,xb,3*spg+1+len(ra_refs))
    for c in loads: c.start()
    greet(place)
    rows_in=[None]*3
    mine=[None]*3
    last=d_refs[-1]
    for w in (2,1,0):
        mine[w]=[pltpu.make_async_copy(last.at[me,w],rbuf.at[w,me,spg-1],local.at[w*spg])]
        mine[w]+=[pltpu.make_async_copy(d_refs[i].at[:,w],rbuf.at[w,:,i],local.at[w*spg+1+i]) for i in range(spg-1)]
        for c in mine[w]: c.start()
        rows_in[w]=go([remote(last.at[other,w],rbuf.at[w,me,spg-1],a_send.at[w,k],a_recv.at[w,k],dev) for k,other,dev in place.group_peers()])

    late=VectorSum(place,lv,lv_recs,v_send,v_recv)

    for c in loads[1:]: c.wait()
    c2=xa.shape[-1]
    cuts=[0,c2//256*128,c2]
    plane_a,plane_b=[],[]
    for h in range(2):
        lane=slice(cuts[h],cuts[h+1])
        def add_a(t,_):
            v=xa[0,t,:,:,lane].astype(f32)
            for i in range(1,S): v=v+xa[i,t,:,:,lane].astype(f32)
            ya[t,:,:,lane]=v.astype(b16)
            return 0
        lax.fori_loop(0,T,add_a,0)
        plane_a.append(go([remote(ya.at[:,other,:,lane],za.at[k,:,:,lane],w_send.at[0,h,k],w_recv.at[0,h,k],dev) for k,other,dev in place.peers("x")]))
        def add_b(t,_):
            v=xb[0,t,:,:,lane].astype(f32)
            for i in range(1,CX): v=v+xb[i,t,:,:,lane].astype(f32)
            yb[t,:,:,lane]=v.astype(b16)
            return 0
        lax.fori_loop(0,T,add_b,0)
        plane_b.append(go([remote(yb.at[:,other,:,lane],zb.at[k,:,:,lane],w_send.at[1,h,k],w_recv.at[1,h,k],dev) for k,other,dev in place.peers("s")]))
    loads[0].wait()
    for c in own_loads: c.wait()

    lv[...]=jnp.zeros_like(lv)
    def compute(w,first):
        for c in mine[w]: c.wait()
        land(rows_in[w])
        def one(t,_):
            d=jnp.concatenate([jnp.concatenate([rbuf[w,g*HP+t*hpt+j].reshape(spg*n,PAIR) for j in range(hpt)],axis=1) for g in range(SG)],axis=0)
            y=_dot(low_ref[...],d,0,0)
            gbuf[w,t]=y.astype(b16).reshape(S,CX,CC,DR,cols)
            z=_dot(d,wbuf[w,t].reshape(D,cols),1,1)
            if first:
                @pl.when(t==0)
                def _(): acc[...]=z
                @pl.when(t>0)
                def _(): acc[...]+=z
            else:
                acc[...]+=z
            if w!=1:
                lv[2+w//2:3+w//2,pl.ds(pl.multiple_of(t*cols,128),cols)]=jnp.sum(d.astype(f32),axis=0,keepdims=True)
            return 0
        lax.fori_loop(0,T,one,0)
        return go([remote(gbuf.at[w,:,:,:,other],rc.at[w,k],g_send.at[w,0,k],g_recv.at[w,0,k],dev) for k,other,dev in place.peers("c")])
    def after_core(w,copies):
        land(copies)
        for t in range(T):
            v=gbuf[w,t,:,:,c0].astype(f32)
            for k in range(CC-1): v=v+rc[w,k,t].astype(f32)
            rc[w,0,t]=v.astype(b16)
        a=go([remote(rc.at[w,0,0:TH,other],ra2.at[w,k],g_send.at[w,1,k],g_recv.at[w,1,k],dev) for k,other,dev in place.peers("s")])
        b=go([remote(rc.at[w,0,TH:T,:,other],rb2.at[w,k],g_send.at[w,2,k],g_recv.at[w,2,k],dev) for k,other,dev in place.peers("x")])
        return a,b
    def after_second(w,pair):
        land(pair[0])
        v=rc[w,0,0:TH,s0].astype(f32)
        for k in range(S-1): v=v+ra2[w,k].astype(f32)
        ra2[w,0]=v.astype(b16)
        a=go([remote(ra2.at[w,0,:,other],ra3.at[w,k],g_send.at[w,3,k],g_recv.at[w,3,k],dev) for k,other,dev in place.peers("x")])
        land(pair[1])
        v=rc[w,0,TH:T,:,x0].astype(f32)
        for k in range(CX-1): v=v+rb2[w,k].astype(f32)
        rb2[w,0]=v.astype(b16)
        b=go([remote(rb2.at[w,0,:,other],rb3.at[w,k],g_send.at[w,4,k],g_recv.at[w,4,k],dev) for k,other,dev in place.peers("s")])
        return a,b
    def after_third(w,pair):
        land(pair[0])
        v=ra2[w,0,:,x0].astype(f32)
        for k in range(CX-1): v=v+ra3[w,k].astype(f32)
        gz[0][w,0:T//4]=v.astype(b16).reshape(T//4,2,DR,cols)
        land(pair[1])
        v=rb2[w,0,:,s0].astype(f32)
        for k in range(S-1): v=v+rb3[w,k].astype(f32)
        gz[0][w,T//4:T//2]=v.astype(b16).reshape(T//4,2,DR,cols)
        return trade(0,w,gzs[w],gzrs[w])
    def onward(k,w,copies):
        settle(k-1,copies,gzs[w],gzrs[w])
        return trade(k,w,gzs[w],gzrs[w])
    def big_trade(k,h):
        lane=slice(cuts[h],cuts[h+1])
        other=t0+steps[k]-2*steps[k]*bit(k)
        return go([remote(bz[k].at[i,:,1-bit(k),:,lane],bzr[k].at[i,:,:,lane],z_send.at[3+2*h+i,k],z_recv.at[3+2*h+i,k],{"tensor":other}) for i in range(2)])
    def big_settle(k,h,copies):
        lane=slice(cuts[h],cuts[h+1])
        land(copies)
        for i in range(2):
            v=bz[k][i,:,bit(k),:,lane].astype(f32)+bzr[k][i,:,:,lane].astype(f32)
            if k+1<len(steps): bz[k+1][i,:,:,:,lane]=v.astype(b16).reshape(bz[k+1].shape[1:4]+(v.shape[-1],))
            else: d2[i*v.shape[1]:(i+1)*v.shape[1],lane]=v[0]
    def big_onward(k,h,copies):
        big_settle(k-1,h,copies)
        return big_trade(k,h)
    def big_first(h):
        lane=slice(cuts[h],cuts[h+1])
        land(plane_a[h])
        def add_a2(j,_):
            v=ya[pl.ds(2*j,2),x0,:,lane].astype(f32)
            for k in range(CX-1): v=v+za[k,pl.ds(2*j,2),:,lane].astype(f32)
            bz[0][0,j,:,:,lane]=v.astype(b16)
            return 0
        lax.fori_loop(0,T//2,add_a2,0)
        land(plane_b[h])
        def add_b2(j,_):
            v=yb[pl.ds(2*j,2),s0,:,lane].astype(f32)
            for k in range(S-1): v=v+zb[k,pl.ds(2*j,2),:,lane].astype(f32)
            bz[0][1,j,:,:,lane]=v.astype(b16)
            return 0
        lax.fori_loop(0,T//2,add_b2,0)
        return big_trade(0,h)
    end=len(steps)
    core_v=compute(2,True)
    two_v=after_core(2,core_v)
    core_k=compute(1,False)
    big=[big_first(0),None]
    three_v=after_second(2,two_v)
    two_k=after_core(1,core_k)
    core_q=compute(0,False)
    big[1]=big_first(1)
    z_v=after_third(2,three_v)
    three_k=after_second(1,two_k)
    two_q=after_core(0,core_q)
    big[0]=big_onward(1,0,big[0])
    step=min(64,R)
    def back(i,carry):
        rows=pl.ds(pl.multiple_of(i*step,step),step)
        h,r=norm_parts(x_ref[rows,:])
        e=acc[rows,:]
        grad_ref[rows,:]=mg_ref[rows,:]+norm_back(e,h,r,gain_ref[...])
        return carry[0]+jnp.sum(e*h,axis=0,keepdims=True),carry[1]+jnp.sum(e,axis=0,keepdims=True)
    zero=jnp.zeros((1,D),f32)
    ga,sa=lax.fori_loop(0,R//step,back,(zero,zero))
    lv[0:1,:]=ga; lv[1:2,:]=sa
    late.start("c")
    three_q=after_second(0,two_q)
    z_k=after_third(1,three_k)
    z_v=onward(1,2,z_v)
    late.end("c"); late.start("s")
    z_q=after_third(0,three_q)
    big[1]=big_onward(1,1,big[1])
    z_k=onward(1,1,z_k)
    late.end("s"); late.start("x")
    z_q=onward(1,0,z_q)
    late.end("x"); late.start("t")
    for k in range(2,end):
        for h in range(2): big[h]=big_onward(k,h,big[h])
        z_v=onward(k,2,z_v); z_k=onward(k,1,z_k); z_q=onward(k,0,z_q)
    dv_ref[...]=settle(end-1,z_v,gzs[2],gzrs[2])[0]
    big_settle(end-1,0,big[0])
    dk_ref[...]=settle(end-1,z_k,gzs[1],gzrs[1])[0]
    dq_ref[...]=settle(end-1,z_q,gzs[0],gzrs[0])[0]
    big_settle(end-1,1,big[1])
    co=do_ref.shape[0]; cf=du_ref.shape[1]
    do_ref[...]=d2[:,:co].T
    du_ref[...]=d2[:,co:co+cf]
    dd_ref[...]=d2[:,co+cf:].T
    late.end("t"); late_ref[...]=lv[...]
    for c in sent: c.wait_send()

def finish(S,C,T,ds,first_low,wide,ra,rb,x,middle_grad,gain):
    R,D=x.shape
    G,_,n=ds[0].shape[:3]
    spg=len(ds)
    CC=2 if C%2==0 else 1
    CX=C//CC; TH=T//2
    DR,cols=wide.shape[-2:]
    HR,c2=ra[0].shape[-2:]
    b16,f32=jnp.bfloat16,jnp.float32
    vm=pl.BlockSpec(memory_space=pltpu.VMEM)
    dma=pltpu.SemaphoreType.DMA
    size={"t":T,"s":S,"x":CX,"c":CC}
    most=max(T,S,CX,CC)-1
    NL=8; co=D//T; cf=(c2-co)//2
    V=lambda shape,dt=b16: pltpu.VMEM(shape,dt)
    halves=[T>>(k+1) for k in range(T.bit_length()-1)]
    scratch=[V((3,G,spg,n,PAIR)),V(wide.shape),V((R,D),f32),V((3,T,S,CX,CC,DR,cols)),V((3,max(CC-1,1),T,S,CX,DR,cols)),
             V((3,max(S-1,1),TH,CX,DR,cols)),V((3,max(CX-1,1),TH,S,DR,cols)),V((3,max(CX-1,1),TH,DR,cols)),V((3,max(S-1,1),TH,DR,cols)),
             [V((3,h,2,DR,cols)) for h in halves],[V((3,h,DR,cols)) for h in halves],
             [V((2,h,2,HR,c2)) for h in halves],[V((2,h,HR,c2)) for h in halves],
             dma((7,len(halves))),dma((7,len(halves))),
             V((S,)+ra[0].shape),V((CX,)+rb[0].shape),V((T,CX,HR,c2)),V((T,S,HR,c2)),V((max(CX-1,1),T,HR,c2)),V((max(S-1,1),T,HR,c2)),
             V((2*HR,c2),f32)]+vector_scratch(size,NL,D)+[
             dma((3,G-1)),dma((3,G-1)),dma((2,2,most)),dma((2,2,most)),dma((3,6,most)),dma((3,6,most)),dma((3*spg+1+len(ra)+len(rb),)),
             [V((R,D)),V((R,D),f32),V((R,D),f32),V((1,D),f32)],dma((4,))]
    hbm=pl.BlockSpec(memory_space=pltpu.HBM)
    sds=jax.ShapeDtypeStruct
    return pl.pallas_call(functools.partial(finish_kernel,S,C,T,spg),
        in_specs=[hbm]*(spg+5+len(ra)+len(rb)),
        out_specs=[vm]*8,
        out_shape=[sds((R,D),f32)]+[sds((DR,cols),f32)]*3+[sds((co,2*HR),f32),sds((2*HR,cf),f32),sds((cf,2*HR),f32),sds((NL,D),f32)],
        scratch_shapes=scratch,
        compiler_params=pltpu.CompilerParams(collective_id=2,has_side_effects=True,vmem_limit_bytes=63<<20),
        name="finish")(*ds,first_low,wide,x,middle_grad,gain,*ra,*rb)


def shards(inputs,teacher,segments,pad_mask,query_weight,key_weight,value_weight,output_weight,up_weight,down_weight,
           first_gain,first_shift,query_shift,value_shift,mixed_gain,mixed_shift,output_shift,second_gain,second_shift,
           up_shift,hidden_gain,hidden_shift,down_shift):
    S,C,T=lax.axis_size("shard"),lax.axis_size("context"),lax.axis_size("tensor")
    CC=2 if C%2==0 else 1
    CX=C//CC
    G=C*T
    ns,n,D=inputs.shape
    R=ns*n
    HP=D//PAIR
    SG=G//HP
    spg=ns//SG
    token_total=S*C*T*R
    me_s=lax.axis_index("shard")
    me_g=lax.axis_index("context")*T+lax.axis_index("tensor")
    c1=query_weight.shape[1]; c2=output_weight.shape[0]; cf=up_weight.shape[1]
    F=cf*T
    x=inputs.reshape(R,D)
    first_low,wide,ids_all,pa,pb,*rows_out=project(S,C,T,x,first_gain[None],first_shift[None],query_weight,key_weight,value_weight,query_shift[None],value_shift[None],
                                             segments.reshape(1,R),output_weight,up_weight,down_weight,ns,n)
    def over_shard(a,d):
        return lax.ppermute(a,"shard",[(i,(i+d)%S) for i in range(S)]) if d else a
    def over_x(a,d):
        return lax.ppermute(a,"context",[(i*CC+j,((i+d)%CX)*CC+j) for i in range(CX) for j in range(CC)]) if d else a
    wa=[over_shard(pa,d) for d in range(S)]
    wb=[over_x(pb,d) for d in range(CX)]
    ids_all=ids_all.reshape(G,S,ns,n)
    valid_count=jnp.sum((ids_all!=(2048//60+1)).astype(jnp.float32))
    ids_mine=lax.dynamic_index_in_dim(ids_all,me_s,1,keepdims=False)
    ids_mine=lax.dynamic_slice_in_dim(ids_mine,(me_g//HP)*spg,spg,1).transpose(1,0,2).reshape(spg,G*n)
    edges=[bounds(ids_mine[i],BLOCK,BLOCK) for i in range(spg)]
    cols=[ids_mine[i][:,None] for i in range(spg)]
    def trade(a):
        return lax.all_to_all(a,("context","tensor"),0,0,tiled=True)
    qkv=[rows_out[0]]+[trade(a) for a in rows_out[1:]]
    mixed=[attend_fwd(qkv[i],ids_mine[i],cols[i],edges[i]) for i in range(spg)]
    arrived=[trade(mixed[i][0]) for i in range(spg-1)]+[mixed[-1][0]]
    keep=pad_mask.reshape(R,1).astype(jnp.float32)
    scale=jnp.full((1,PAIR),token_total/valid_count)
    vecs=jnp.stack([mixed_gain,mixed_shift,output_shift,second_gain,second_shift,down_shift,down_shift,down_shift])
    wides=jnp.stack([up_shift.reshape(T,cf),hidden_gain.reshape(T,cf),hidden_shift.reshape(T,cf)],axis=1)
    result,middle_grad,inner_low,second_low,out_low,middle_low,hidden_low,unit_low,early,*gs=feed(
        S,C,T,arrived,wa,wb,x,teacher.reshape(R,D),keep,scale,vecs,wides)
    *outs,last_g,early=weight_grads(S,C,T,out_low,second_low,middle_low,inner_low,unit_low,hidden_low,gs[-1],early)
    gs=list(lax.optimization_barrier(tuple(gs[:-1])+(last_g,)))
    NA=1+2*(S-1)
    hops=[over_shard(outs[1+i],1+i//2) for i in range(2*(S-1))],[over_x(outs[NA+1+i],1+i//2) for i in range(2*(CX-1))]
    ds=[attend_bwd(qkv[i],gs[i],mixed[i][0],mixed[i][1],ids_mine[i],cols[i],edges[i]) for i in range(spg)]
    if spg>1:
        ds[0],(first_a,first_b)=lax.optimization_barrier((ds[0],(hops[0][0::2],hops[1][0::2])))
        hops[0][0::2],hops[1][0::2]=first_a,first_b
    ra,rb=[outs[0]]+hops[0],[outs[NA]]+hops[1]
    ds=[trade(a) for a in ds[:-1]]+[ds[-1]]
    input_grad,*grads,late=finish(S,C,T,ds,first_low,wide,ra,rb,x,middle_grad,first_gain[None])
    B=F//D
    vectors=(late[0],late[1],late[2],late[3],early[0],early[1],early[2],early[3],early[4],early[7+2*B:7+3*B].reshape(F),
             early[7:7+B].reshape(F),early[7+B:7+2*B].reshape(F),early[5])
    loss=jnp.sum(early[6])
    return (result.reshape(ns,n,D),loss/valid_count,input_grad.reshape(ns,n,D))+tuple(grads)+vectors


def solution(mesh):
    rows=P("shard",("context","tensor"),None)
    ids=P("shard",("context","tensor"))
    wide=P(("shard","context"),"tensor")
    tall=P("tensor",("shard","context"))
    weights=(wide,wide,wide,tall,wide,tall)
    return jax.shard_map(shards,mesh=mesh,in_specs=(rows,rows,ids,ids)+weights+(P(),)*13,
                         out_specs=(rows,P(),rows)+weights+(P(),)*13,check_vma=False)
```

```python
import functools

import jax
import jax.numpy as jnp
from jax import lax
from jax.experimental import pallas as pl
from jax.experimental.pallas import tpu as pltpu
from jax.sharding import PartitionSpec as P


NEG=-1e30
BLOCK=512
def _dot(a,b,ca,cb):
    return lax.dot_general(a,b,(((ca,),(cb,)),((),())),preferred_element_type=jnp.float32)

def half_masks(rows):
    lane=lax.broadcasted_iota(jnp.int32,(rows,128),1)
    return lane<64

def fwd_kernel(lo_ref,hi_ref,q_ref,k_ref,v_ref,col_ref,row_ref,o_ref,lse_ref,vt_ref,acc_ref,m_ref):
    i=pl.program_id(0)
    bq=acc_ref.shape[2]; bk=vt_ref.shape[3]; n=k_ref.shape[2]; per=bk//n
    upper=lax.broadcasted_iota(jnp.int32,(128,1),0)<64
    @pl.when(i==0)
    def _():
        def turn(j,_):
            vt=v_ref[pl.ds(j*per,per),0].reshape(bk,128).astype(jnp.float32).T
            vt_ref[0,j]=jnp.where(upper,vt,1.0).astype(jnp.bfloat16)
            vt_ref[1,j]=jnp.where(upper,1.0,vt).astype(jnp.bfloat16)
            return 0
        lax.fori_loop(0,vt_ref.shape[1],turn,0)
    left=half_masks(bq)
    q=q_ref[...].reshape(bq,128)*jnp.bfloat16(0.125)
    zero=jnp.zeros_like(q)
    qs=(jnp.where(left,q,zero),jnp.where(left,zero,q))
    ids_q=row_ref[i]
    acc_ref[...]=jnp.zeros_like(acc_ref)
    m_ref[...]=jnp.full_like(m_ref,NEG)
    def step(j,_):
        k=k_ref[pl.ds(j*per,per),0].reshape(bk,128)
        same=col_ref[pl.ds(pl.multiple_of(j*bk,bk),bk),:]==ids_q
        for h in range(2):
            sc=jnp.where(same,_dot(k,qs[h],1,1),NEG)
            old=m_ref[h:h+1,:]
            top=jnp.maximum(old,jnp.max(sc,axis=0,keepdims=True))
            e=jnp.exp(sc-top).astype(jnp.bfloat16)
            m_ref[h:h+1,:]=top
            acc_ref[h]=acc_ref[h]*jnp.exp(old-top)+_dot(vt_ref[h,j],e,1,0)
        return 0
    lax.fori_loop(lo_ref[i],hi_ref[i],step,0)
    t0=acc_ref[0,64:65,:]; t1=acc_ref[1,0:1,:]
    o=jnp.where(upper,acc_ref[0]/t0,acc_ref[1]/t1).T
    o_ref[...]=o.astype(jnp.bfloat16).reshape(o_ref.shape)
    lse_ref[0,0:1,:]=m_ref[0:1,:]+jnp.log(t0)
    lse_ref[0,1:2,:]=m_ref[1:2,:]+jnp.log(t1)

def bounds(ids,bq,bk):
    first=ids[::bq]; last=ids[bq-1::bq]
    start=jnp.sum((ids[None,:]<first[:,None]).astype(jnp.int32),axis=1)
    end=jnp.sum((ids[None,:]<=last[:,None]).astype(jnp.int32),axis=1)
    return start//bk,(end+bk-1)//bk

def attend_fwd(qkv,ids,col,edges,bq=BLOCK,bk=BLOCK):
    G,_,n,_=qkv.shape; L=G*n
    row=ids.reshape(L//bq,1,bq)
    part=lambda w: pl.BlockSpec((G,1,n,128),lambda i,*_: (0,w,0,0))
    ospec=pl.BlockSpec((bq//n,n,128),lambda i,*_:(i,0,0))
    return pl.pallas_call(fwd_kernel,
        grid_spec=pltpu.PrefetchScalarGridSpec(num_scalar_prefetch=2,grid=(L//bq,),
            in_specs=[pl.BlockSpec((bq//n,1,n,128),lambda i,*_:(i,0,0,0)),part(1),part(2),pl.BlockSpec((L,1),lambda i,*_:(0,0)),
                      pl.BlockSpec((L//bq,1,bq),lambda i,*_:(0,0,0))],
            out_specs=[ospec,pl.BlockSpec((1,2,bq),lambda i,*_:(i,0,0))],
            scratch_shapes=[pltpu.VMEM((2,L//bk,128,bk),jnp.bfloat16),pltpu.VMEM((2,128,bq),jnp.float32),pltpu.VMEM((2,bq),jnp.float32)]),
        out_shape=[jax.ShapeDtypeStruct((G,n,128),jnp.bfloat16),jax.ShapeDtypeStruct((L//bq,2,bq),jnp.float32)],
        compiler_params=pltpu.CompilerParams(dimension_semantics=("arbitrary",),vmem_limit_bytes=63<<20),
        cost_estimate=pl.CostEstimate(flops=4*L*1024*128*2,bytes_accessed=8*L*256,transcendentals=2*L*1024),
        name="attend_fwd")(*edges,qkv,qkv,qkv,col,row)

def bwd_kernel(lo_ref,hi_ref,q_ref,k_ref,v_ref,g_ref,o_ref,lse_ref,col_ref,row_ref,d_ref,dqa,dka,dva):
    i=pl.program_id(0)
    bq=dqa.shape[1]; bk=BLOCK; n=k_ref.shape[2]; per=bk//n
    @pl.when(i==0)
    def _():
        dka[...]=jnp.zeros_like(dka); dva[...]=jnp.zeros_like(dva)
    left=half_masks(bq)
    q=q_ref[...].reshape(bq,128)*jnp.bfloat16(0.125)
    g=g_ref[...].reshape(bq,128)
    zero=jnp.zeros_like(q)
    qs=(jnp.where(left,q,zero),jnp.where(left,zero,q))
    gs=(jnp.where(left,g,zero),jnp.where(left,zero,g))
    d_t=(g.astype(jnp.float32)*o_ref[...].reshape(bq,128).astype(jnp.float32)).T
    lses=(lse_ref[0,0:1,:],lse_ref[0,1:2,:])
    ds=(jnp.sum(d_t[:64],axis=0,keepdims=True),jnp.sum(d_t[64:],axis=0,keepdims=True))
    ids_q=row_ref[i]
    dqa[...]=jnp.zeros_like(dqa)
    def step(j,_):
        k=k_ref[pl.ds(j*per,per),0].reshape(bk,128)
        v=v_ref[pl.ds(j*per,per),0].reshape(bk,128)
        rows=pl.ds(pl.multiple_of(j*bk,bk),bk)
        same=col_ref[rows,:]==ids_q
        dk=dka[rows,:]; dv=dva[rows,:]
        for h in range(2):
            st=_dot(k,qs[h],1,1)
            p=jnp.exp(jnp.where(same,st,NEG)-lses[h])
            dp=_dot(v,gs[h],1,1)
            d=(p*(dp-ds[h])).astype(jnp.bfloat16)
            dv=dv+_dot(p.astype(jnp.bfloat16),gs[h],1,0)
            dk=dk+_dot(d,qs[h],1,0)
            dqa[h]+=_dot(d,k,0,0)
        dka[rows,:]=dk; dva[rows,:]=dv
        return 0
    lax.fori_loop(lo_ref[i],hi_ref[i],step,0)
    d_ref[pl.ds(i*(bq//n),bq//n),0]=(jnp.where(left,dqa[0],dqa[1])*0.125).astype(jnp.bfloat16).reshape(bq//n,n,128)
    @pl.when(i==pl.num_programs(0)-1)
    def _():
        d_ref[:,1]=dka[...].astype(jnp.bfloat16).reshape(d_ref.shape[0],n,128)
        d_ref[:,2]=dva[...].astype(jnp.bfloat16).reshape(d_ref.shape[0],n,128)

def attend_bwd(qkv,g,o,lse,ids,col,edges,bq=BLOCK):
    bk=BLOCK
    G,_,n,_=qkv.shape; L=G*n
    row=ids.reshape(L//bq,1,bq)
    part=lambda w: pl.BlockSpec((G,1,n,128),lambda i,*_: (0,w,0,0))
    ospec=pl.BlockSpec((bq//n,n,128),lambda i,*_:(i,0,0))
    return pl.pallas_call(bwd_kernel,
        grid_spec=pltpu.PrefetchScalarGridSpec(num_scalar_prefetch=2,grid=(L//bq,),
            in_specs=[pl.BlockSpec((bq//n,1,n,128),lambda i,*_:(i,0,0,0)),part(1),part(2),ospec,
                      ospec,pl.BlockSpec((1,2,bq),lambda i,*_:(i,0,0)),pl.BlockSpec((L,1),lambda i,*_:(0,0)),pl.BlockSpec((L//bq,1,bq),lambda i,*_:(0,0,0))],
            out_specs=pl.BlockSpec((G,3,n,128),lambda i,*_:(0,0,0,0)),
            scratch_shapes=[pltpu.VMEM((2,bq,128),jnp.float32)]+[pltpu.VMEM((L,128),jnp.float32)]*2),
        out_shape=jax.ShapeDtypeStruct((G,3,n,128),jnp.bfloat16),
        compiler_params=pltpu.CompilerParams(dimension_semantics=("arbitrary",),vmem_limit_bytes=63<<20),
        cost_estimate=pl.CostEstimate(flops=1000000,bytes_accessed=1000000,transcendentals=0),
        name="attend_bwd")(*edges,qkv,qkv,qkv,g,o,lse,col,row)


EPS=1e-5
PAIR=128

def norm_parts(v):
    m=jnp.mean(v,axis=-1,keepdims=True)
    s=jnp.mean(v*v,axis=-1,keepdims=True)-m*m
    r=lax.rsqrt(s+EPS)
    return (v-m)*r,r

def norm_back(e,h,r,gain):
    t=e*gain
    return r*(t-jnp.mean(t,axis=-1,keepdims=True)-h*jnp.mean(t*h,axis=-1,keepdims=True))


MESH_ID=pl.DeviceIdType.MESH

class Place:
    def __init__(self,S,C,T):
        self.CC=2 if C%2==0 else 1
        self.size={"t":T,"s":S,"x":C//self.CC,"c":self.CC}
        c=lax.axis_index("context")
        self.at={"t":lax.axis_index("tensor"),"s":lax.axis_index("shard"),"x":c//self.CC,"c":lax.rem(c,self.CC)}
        self.group=c*T+self.at["t"]
        self.T=T; self.G=C*T
    def peers(self,axis):
        m=self.size[axis]
        for d in range(1,m):
            other=lax.rem(self.at[axis]+d,m)
            if axis=="t": yield d-1,other,{"tensor":other}
            elif axis=="s": yield d-1,other,{"shard":other}
            elif axis=="x": yield d-1,other,{"context":other*self.CC+self.at["c"]}
            else: yield d-1,other,{"context":self.at["x"]*self.CC+other}
    def group_peers(self):
        for d in range(1,self.G):
            other=lax.rem(self.group+d,self.G)
            yield d-1,other,{"context":other//self.T,"tensor":lax.rem(other,self.T)}

def upper_rows(rows):
    return max(rows*5//8//16*16,16)

def slots(size,order):
    base,total={},0
    for a in order:
        base[a]=total; total+=size[a]-1
    return base,total

def greet(place):
    barrier=pltpu.get_barrier_semaphore()
    count=0
    for _,_,dev in place.group_peers():
        pl.semaphore_signal(barrier,inc=1,device_id=dev,device_id_type=MESH_ID); count+=1
    for _,_,dev in place.peers("s"):
        pl.semaphore_signal(barrier,inc=1,device_id=dev,device_id_type=MESH_ID); count+=1
    pl.semaphore_wait(barrier,count)

class VectorSum:
    order="csxt"
    def __init__(self,place,cur,recs,send,recv):
        self.place,self.cur,self.send,self.recv=place,cur,send,recv
        self.recs=dict(zip(self.order,recs))
        self.base,_=slots(place.size,self.order)
    def copies(self,axis):
        at=self.place.at[axis]
        return [remote(self.cur,self.recs[axis].at[at],self.send.at[self.base[axis]+k],self.recv.at[self.base[axis]+k],dev)
                for k,_,dev in self.place.peers(axis)]
    def start(self,axis):
        self.recs[axis][self.place.at[axis]]=self.cur[...]
        for c in self.copies(axis): c.start()
    def end(self,axis):
        for c in self.copies(axis): c.wait()
        rec=self.recs[axis]
        total=rec[0]
        for i in range(1,self.place.size[axis]): total=total+rec[i]
        self.cur[...]=total

def vector_scratch(size,rows,D):
    _,total=slots(size,VectorSum.order)
    dma=pltpu.SemaphoreType.DMA
    return [pltpu.VMEM((rows,D),jnp.float32),[pltpu.VMEM((size[a],rows,D),jnp.float32) for a in VectorSum.order],dma((total,)),dma((total,))]

def remote(src,dst,send,recv,dev):
    return pltpu.make_async_remote_copy(src_ref=src,dst_ref=dst,send_sem=send,recv_sem=recv,device_id=dev,device_id_type=MESH_ID)

def fetch(sources,buffers,sem):
    copies=[pltpu.make_async_copy(a,b,sem.at[i]) for i,(a,b) in enumerate(zip(sources,buffers))]
    for c in copies: c.start()
    return copies

def project_kernel(S,C,T,x_ref,gain_ref,shift_ref,wq_ref,wk_ref,wv_ref,qs_ref,vs_ref,ids_ref,wo_ref,wu_ref,wd_ref,
                   low_ref,wide_ref,allids_ref,pa_ref,pb_ref,*rest):
    spg=len(rest)-17
    rows_refs=rest[:spg]
    *scratch,buffers,load=rest[spg:]
    loads=fetch((wq_ref,wk_ref,wv_ref,wo_ref,wu_ref,wd_ref,ids_ref,x_ref,gain_ref,shift_ref,qs_ref,vs_ref),buffers,load)
    wq_ref,wk_ref,wv_ref,wo_ref,wu_ref,wd_ref,ids_ref,x_ref,gain_ref,shift_ref,qs_ref,vs_ref=buffers
    project_body(S,C,T,loads,x_ref,gain_ref,shift_ref,wq_ref,wk_ref,wv_ref,(qs_ref,None,vs_ref),ids_ref,wo_ref,wu_ref,wd_ref,
                 low_ref,wide_ref,allids_ref,pa_ref,pb_ref,rows_refs,*scratch)

def project_body(S,C,T,loads,x_ref,gain_ref,shift_ref,wq_ref,wk_ref,wv_ref,bias_refs,ids_ref,wo_ref,wu_ref,wd_ref,
                   low_ref,wide_ref,allids_ref,pa_ref,pb_ref,rows_refs,
                   zbuf,z_send,z_recv,p_send,p_recv,wbuf,obuf,idbuf,ag_send,ag_recv,a_send,a_recv,i_send,i_recv,local):
    place=Place(S,C,T)
    R,D=low_ref.shape
    G,_,n=rows_refs[0].shape[:3]
    spg=len(rows_refs)
    HP=D//PAIR; SG=G//HP
    cols=wbuf.shape[-1]; hpt=cols//PAIR
    me=place.group
    order="tsxc"
    base,total=slots(place.size,order)
    own=[place.at[a] for a in order]
    for c in loads[:6]: c.wait()
    for w,ref in enumerate((wq_ref,wk_ref,wv_ref)):
        wbuf[w,own[0],own[1],own[2],own[3]]=ref[...].astype(jnp.bfloat16)
    t0=place.at["t"]
    HA=upper_rows(zbuf.shape[1])
    c0=wo_ref.shape[0]; cf=wu_ref.shape[1]
    zbuf[t0,:,0:c0]=wo_ref[...].T.astype(jnp.bfloat16)
    zbuf[t0,:,c0:c0+cf]=wu_ref[...].astype(jnp.bfloat16)
    zbuf[t0,:,c0+cf:]=wd_ref[...].T.astype(jnp.bfloat16)
    cuts=[0,(c0+cf)//128*128,c0+2*cf]
    def hop(way,h,piece,j):
        to=t0+1 if way==0 else t0-1
        lane=slice(cuts[j],cuts[j+1])
        return remote(zbuf.at[piece,:,lane],zbuf.at[piece,:,lane],z_send.at[way,h-1,j],z_recv.at[way,h-1,j],{"tensor":lax.rem(to+T,T)})
    def line_start(j):
        @pl.when(t0<T-1)
        def _(): hop(0,1,t0,j).start()
        @pl.when(t0>0)
        def _(): hop(1,1,t0,j).start()
    def line_pass(h,j):
        @pl.when(t0>=h)
        def _():
            hop(0,h,lax.rem(t0-h+T,T),j).wait_recv()
            @pl.when(t0<T-1)
            def _(): hop(0,h+1,lax.rem(t0-h+T,T),j).start()
        @pl.when(t0+h<=T-1)
        def _():
            hop(1,h,lax.rem(t0+h,T),j).wait_recv()
            @pl.when(t0>0)
            def _(): hop(1,h+1,lax.rem(t0+h,T),j).start()
    def line_end():
        for j in range(2):
            for h in range(1,T):
                @pl.when((t0<T-1)&(t0>=h-1))
                def _(): hop(0,h,lax.rem(t0-h+1+T,T),j).wait_send()
                @pl.when((t0>0)&(t0+h-1<=T-1))
                def _(): hop(1,h,lax.rem(t0+h-1,T),j).wait_send()
    def plane(j):
        lane=slice(cuts[j],cuts[j+1])
        x0,s0=place.at["x"],place.at["s"]
        out=[pltpu.make_async_copy(zbuf.at[:,0:HA,lane],pa_ref.at[x0,:,:,lane],local.at[8+2*j]),
             pltpu.make_async_copy(zbuf.at[:,HA:,lane],pb_ref.at[s0,:,:,lane],local.at[9+2*j])]
        for k,_,dev in place.peers("x"):
            c=remote(zbuf.at[:,0:HA,lane],pa_ref.at[x0,:,:,lane],p_send.at[0,k,j],p_recv.at[0,k,j],dev); sent.append(c); out.append(c)
        for k,_,dev in place.peers("s"):
            c=remote(zbuf.at[:,HA:,lane],pb_ref.at[s0,:,:,lane],p_send.at[1,k,j],p_recv.at[1,k,j],dev); sent.append(c); out.append(c)
        for c in out: c.start()
        return out
    greet(place)
    stages={2:"tsxc",1:"txsc",0:"txsc"}
    sent=[]
    copies={}
    def start(w,r):
        done=stages[w][:r]; axis=stages[w][r]
        idx=tuple(slice(None) if a in done else place.at[a] for a in order)
        copies[w,r]=[]
        for k,_,dev in place.peers(axis):
            c=remote(wbuf.at[(w,)+idx],wbuf.at[(w,)+idx],ag_send.at[w,base[axis]+k],ag_recv.at[w,base[axis]+k],dev)
            c.start(); copies[w,r].append(c); sent.append(c)
    def arrive(w,r):
        for c in copies[w,r]: c.wait_recv()
    for w in (2,1,0): start(w,0)
    line_start(0); line_start(1)
    loads[6].wait()
    ids_own=pltpu.make_async_copy(ids_ref,idbuf.at[place.at["s"]],local.at[0]); ids_own.start()
    id_first=[]
    for k,_,dev in place.peers("s"):
        c=remote(ids_ref,idbuf.at[place.at["s"]],i_send.at[k],i_recv.at[k],dev); c.start(); id_first.append(c); sent.append(c)
    for c in loads[7:]: c.wait()
    step=min(64,R)
    def norm(i,_):
        rows=pl.ds(pl.multiple_of(i*step,step),step)
        h,_r=norm_parts(x_ref[rows,:])
        low_ref[rows,:]=(h*gain_ref[...]+shift_ref[...]).astype(jnp.bfloat16)
        return 0
    lax.fori_loop(0,R//step,norm,0)
    def spread_ids():
        ids_own.wait()
        for c in id_first: c.wait_recv()
        out=[]
        mine=pltpu.make_async_copy(idbuf,allids_ref.at[me],local.at[1]); mine.start(); out.append(mine)
        for k,_,dev in place.group_peers():
            c=remote(idbuf,allids_ref.at[me],i_send.at[S-1+k],i_recv.at[S-1+k],dev); c.start(); sent.append(c); out.append(c)
        return out
    late=[]
    def compute(w):
        def one(t,_):
            y=_dot(low_ref[...],wbuf[w,t].reshape(D,cols),1,0)
            if bias_refs[w] is not None: y=y+bias_refs[w][:,pl.ds(pl.multiple_of(t*cols,128),cols)]
            y=y.astype(jnp.bfloat16)
            for g in range(SG):
                for j in range(hpt):
                    obuf[w,g*HP+t*hpt+j]=y[g*spg*n:(g+1)*spg*n,j*PAIR:(j+1)*PAIR].reshape(spg,n,PAIR)
            return 0
        lax.fori_loop(0,T,one,0)
        mine=pltpu.make_async_copy(obuf.at[w,me,0],rows_refs[0].at[me,w],local.at[2+w]); mine.start(); late.append(mine)
        for k,other,dev in place.group_peers():
            c=remote(obuf.at[w,other,0],rows_refs[0].at[me,w],a_send.at[w,k],a_recv.at[w,k],dev)
            c.start(); sent.append(c); late.append(c)
        for i in range(1,spg):
            c=pltpu.make_async_copy(obuf.at[w,:,i],rows_refs[i].at[:,w],local.at[12+w*spg+i]); c.start(); late.append(c)
        keep=pltpu.make_async_copy(wbuf.at[w],wide_ref.at[w],local.at[5+w]); keep.start(); late.append(keep)
    arrive(2,0); start(2,1)
    arrive(1,0); start(1,1)
    ids_out=spread_ids()
    arrive(2,1); start(2,2)
    arrive(0,0); start(0,1)
    arrive(1,1); start(1,2)
    line_pass(1,0)
    arrive(2,2); start(2,3)
    line_pass(1,1)
    arrive(2,3); compute(2)
    arrive(1,2); start(1,3)
    if T>2: line_pass(2,0)
    arrive(0,1); start(0,2)
    arrive(1,3); compute(1)
    if T>2: line_pass(2,1)
    for h in range(3,T): line_pass(h,0)
    ids_out=ids_out+plane(0)
    arrive(0,2); start(0,3)
    for h in range(3,T): line_pass(h,1)
    ids_out=ids_out+plane(1)
    arrive(0,3); compute(0)
    for c in late+ids_out:
        if any(c is o for o in sent): c.wait_recv()
        else: c.wait()
    for c in sent: c.wait_send()
    line_end()

def project(S,C,T,x,gain,shift,wq,wk,wv,qs,vs,ids,wo,wu,wd,ns,n):
    R,D=x.shape
    G=C*T; HP=D//PAIR; spg=ns*HP//G
    DR,cols=wq.shape
    CC=2 if C%2==0 else 1
    piece=(3,T,S,C//CC,CC,DR,cols)
    HA=upper_rows(DR); width=wo.shape[0]+2*wu.shape[1]; most=max(S,C//CC)-1
    _,total=slots({"t":T,"s":S,"x":C//CC,"c":CC},"tsxc")
    vm=pl.BlockSpec(memory_space=pltpu.VMEM); anyspec=pl.BlockSpec(memory_space=pl.ANY)
    dma=pltpu.SemaphoreType.DMA
    return pl.pallas_call(functools.partial(project_kernel,S,C,T),
        in_specs=[pl.BlockSpec(memory_space=pltpu.HBM)]*12,
        out_specs=[vm]+[anyspec]*(4+spg),
        out_shape=[jax.ShapeDtypeStruct((R,D),jnp.bfloat16),jax.ShapeDtypeStruct(piece,jnp.bfloat16),jax.ShapeDtypeStruct((G,S,1,ns*n),jnp.int32),
                   jax.ShapeDtypeStruct((C//CC,T,HA,width),jnp.bfloat16),jax.ShapeDtypeStruct((S,T,DR-HA,width),jnp.bfloat16)]+
                  [jax.ShapeDtypeStruct((G,3,n,PAIR),jnp.bfloat16)]*spg,
        scratch_shapes=[pltpu.VMEM((T,DR,width),jnp.bfloat16),dma((2,T-1,2)),dma((2,T-1,2)),dma((2,most,2)),dma((2,most,2)),pltpu.VMEM(piece,jnp.bfloat16),pltpu.VMEM((3,G,spg,n,PAIR),jnp.bfloat16),pltpu.VMEM((S,1,ns*n),jnp.int32),
                        dma((3,total)),dma((3,total)),dma((3,G-1)),dma((3,G-1)),dma((S-1+G-1,)),dma((S-1+G-1,)),dma((12+3*spg,)),
                        [pltpu.VMEM(a.shape,a.dtype) for a in (wq,wk,wv,wo,wu,wd,ids,x,gain,shift,qs,vs)],dma((12,))],
        compiler_params=pltpu.CompilerParams(collective_id=0,has_side_effects=True,vmem_limit_bytes=63<<20),
        name="project")(x,gain,shift,wq,wk,wv,qs,vs,ids,wo,wu,wd)


def feed_kernel(S,C,T,NC,NO,*refs):
    place=Place(S,C,T)
    CX=place.size["x"]; CC=place.CC
    spg=NO
    o_refs=refs[:spg]; o_ref=o_refs[-1]; refs=refs[spg-1:]
    wa_refs=refs[1:1+S]; wb_refs=refs[1+S:1+S+CX]
    (x_ref,teach_ref,ids_ref,mask_ref),vec_refs,wide_refs=refs[1+S+CX:5+S+CX],refs[5+S+CX:11+S+CX],refs[11+S+CX:14+S+CX]
    refs=refs[7:]
    (mid_ref,res_ref,mg_ref,inner_ref,second_ref,out_ref,midl_ref,hid_ref,unl_ref,sum_ref)=refs[7+S+CX:17+S+CX]
    g_refs=refs[17+S+CX:17+S+CX+spg]; refs=refs[1:]; refs=refs[spg-1:]
    (w2,rbuf,mix,inner,second,outl,midl,hid,unl,act,dact,tt,acc,middle,og,s1,s2,res,mg,gout,vacc,wacc,
     w_local,w_send,w_recv,a_send,a_recv,g_send,g_recv,misc,o_sem,s1b,s2b,buffers,load)=refs[17+S+CX:]
    loads=fetch((x_ref,teach_ref,ids_ref,mask_ref)+tuple(vec_refs)+tuple(wide_refs),buffers,load)
    x_ref,teach_ref,ids_ref,mask_ref=buffers[:4]
    vec_refs,wide_refs=buffers[4:10],buffers[10:]
    R,D=x_ref.shape
    G,n=o_ref.shape[:2]
    HP=D//PAIR; SG=G//HP
    HA=upper_rows(w2.shape[-2])
    F=hid.shape[1]; cf=F//T; c2=D//T
    B=R//spg; sub=n
    f32=jnp.float32; b16=jnp.bfloat16
    me=place.group
    s0,x0,c0=place.at["s"],place.at["x"],place.at["c"]
    DS=D//S
    ranges=((0,c2),(c2,c2+cf),(c2+cf,c2+2*cf))
    def pieces(r):
        lo,hi=ranges[r]
        out=[]
        for d in range(S):
            src=lax.rem(s0+S-d,S)
            for i in range(CX):
                out.append((wa_refs[d].at[i,:,:,lo:hi],w2.at[:,src,i,c0,0:HA,lo:hi]))
        for d in range(CX):
            src=lax.rem(x0+CX-d,CX)
            for i in range(S):
                out.append((wb_refs[d].at[i,:,:,lo:hi],w2.at[:,i,src,c0,HA:,lo:hi]))
        return out
    local=[[pltpu.make_async_copy(a,b,w_local.at[r,i]) for i,(a,b) in enumerate(pieces(r))] for r in range(3)]
    for r in range(3):
        for c in local[r]: c.start()
    barrier=pltpu.get_barrier_semaphore()
    count=0
    for _,_,dev in place.group_peers():
        pl.semaphore_signal(barrier,inc=1,device_id=dev,device_id_type=MESH_ID); count+=1
    pl.semaphore_wait(barrier,count)
    own=[pltpu.make_async_copy(o_ref.at[me],rbuf.at[me,spg-1],misc.at[0])]
    own+=[pltpu.make_async_copy(o_refs[i],rbuf.at[:,i],misc.at[1+i]) for i in range(spg-1)]
    for c in own: c.start()
    rows_in=[remote(o_ref.at[other],rbuf.at[me,spg-1],a_send.at[k],a_recv.at[k],dev) for k,other,dev in place.group_peers()]
    for c in rows_in: c.start()
    far=[[remote(a,b,w_send.at[r,k,i],w_recv.at[r,k,i],dev) for k,_,dev in place.peers("c") for i,(a,b) in enumerate(pieces(r))] for r in range(3)]
    for r in range(3):
        for c in far[r]: c.start()
    def weights(r):
        for c in local[r]: c.wait()
        for c in far[r]: c.wait_recv()
    vacc[...]=jnp.zeros_like(vacc); wacc[...]=jnp.zeros_like(wacc)
    def vec(i): return vec_refs[i][...]
    def wide(i,t,lo,size): return wide_refs[i][:,pl.ds(pl.multiple_of(t*cf+lo,128),size)]
    MIXG,MIXS,OUTS,SECG,SECS,DOWNS=range(6)
    def each(fn):
        def body(i,_):
            fn(pl.ds(pl.multiple_of(i*sub,sub),sub),i)
            return 0
        lax.fori_loop(0,B//sub,body,0)
    def fold(a):
        return jnp.sum(a.reshape(a.shape[0]//8,8,a.shape[1]),axis=0)
    def lanes(a):
        v=a[:,:PAIR]
        for j in range(1,a.shape[1]//PAIR): v=v+a[:,j*PAIR:(j+1)*PAIR]
        return v
    def flat(t,lo,hi,s=None):
        if s is None: return w2[t,:,:,:,:,lo:hi].reshape(D,hi-lo)
        return w2[t,s,:,:,:,lo:hi].reshape(DS,hi-lo)
    for c in loads: c.wait()
    count=jnp.sum((ids_ref[...]!=2048//60+1).astype(f32))
    scale=R*S*C*T/jnp.full((1,1),count)
    sum_ref[...]=jnp.zeros_like(sum_ref)
    sum_ref[sum_ref.shape[0]-1:,:]=jnp.full((1,D),count)
    weights(0)
    def block(b):
        r0=b*B
        def rows(i): return pl.ds(pl.multiple_of(r0+i*sub,sub),sub)
        def tokens(i): return pl.ds(pl.multiple_of(i//(n//sub)*(spg*n)+b*n+lax.rem(i,n//sub)*sub,sub),sub)
        whole=pl.ds(r0,B)
        if b<spg-1: own[1+b].wait()
        else:
            own[0].wait()
            for c in rows_in: c.wait_recv()
        for gg in range(SG):
            for h in range(HP):
                mix[gg*n:(gg+1)*n,h*PAIR:(h+1)*PAIR]=rbuf[gg*HP+h,b]
        def f1(q,i):
            h,_=norm_parts(mix[q,:].astype(f32))
            inner[rows(i),:]=(h*vec(MIXG)+vec(MIXS)).astype(b16)
        each(f1)
        acc[...]=jnp.zeros_like(acc)
        def att(t,_):
            a=inner[whole,pl.ds(pl.multiple_of(t*c2,128),c2)]
            for s in range(S):
                acc[:,s*DS:(s+1)*DS]+=_dot(a,flat(t,0,c2,s),1,1)
            return 0
        lax.fori_loop(0,T,att,0)
        def f2(q,i):
            m=x_ref[tokens(i),:]+(acc[q,:]+vec(OUTS))
            middle[q,:]=m
            x_ref[tokens(i),:]=m
            h,_=norm_parts(m)
            second[rows(i),:]=(h*vec(SECG)+vec(SECS)).astype(b16)
        each(f2)
        if b==0: weights(1)
        s1[...]=jnp.zeros_like(s1); s2[...]=jnp.zeros_like(s2)
        def up(t,_):
            a=second[whole,:]
            w=cf//NC
            for j in range(NC):
                lane=slice(j*w,(j+1)*w)
                u=_dot(a,flat(t,c2+j*w,c2+(j+1)*w),1,0)+wide(0,t,j*w,w)
                u2=u*u
                th=jnp.tanh(0.7978845608028654*u*(1.0+0.044715*u2))
                half=0.5+0.5*th
                v=u*half
                act[t,:,lane]=v
                dact[t,:,lane]=half+(0.5*0.7978845608028654)*u*(1.0-th*th)*(1.0+(3*0.044715)*u2)
                s1[...]+=lanes(v); s2[...]+=lanes(v*v)
            return 0
        lax.fori_loop(0,T,up,0)
        def f3(q,i):
            m=jnp.sum(s1[q,:],axis=1,keepdims=True)/F
            v=jnp.sum(s2[q,:],axis=1,keepdims=True)/F-m*m
            s1[q,:]=jnp.broadcast_to(m,(sub,PAIR)); s2[q,:]=jnp.broadcast_to(lax.rsqrt(v+EPS),(sub,PAIR))
        each(f3)
        if b==0: weights(2)
        acc[...]=jnp.zeros_like(acc)
        def down(t,_):
            fcols=pl.ds(pl.multiple_of(t*cf,128),cf)
            def e(q,i):
                h=(act[t,q,:]-s1[q,0:1])*s2[q,0:1]
                act[t,q,:]=h
                hid[rows(i),fcols]=(h*wide(1,t,0,cf)+wide(2,t,0,cf)).astype(b16)
            each(e)
            a=hid[whole,fcols]
            for s in range(S):
                acc[:,s*DS:(s+1)*DS]+=_dot(a,flat(t,c2+cf,c2+2*cf,s),1,1)
            return 0
        lax.fori_loop(0,T,down,0)
        def f4(q,i):
            branch=acc[q,:]+vec(DOWNS)
            res[tokens(i),:]=branch
            err=middle[q,:]+branch-teach_ref[tokens(i),:]
            k=jnp.broadcast_to(mask_ref[pl.ds(i*spg+b,1),:].astype(f32),(sub,sub)).T[:,0:1]
            e=k*err
            vacc[6]+=fold(e*err)
            g=e*scale
            og[q,:]=g
            low_=g.astype(b16)
            outl[rows(i),:]=low_
            vacc[5]+=fold(low_.astype(f32))
        each(f4)
        def back1(t,_):
            a=outl[whole,:]
            w=cf//NC
            for j in range(NC):
                lane=slice(j*w,(j+1)*w)
                g=_dot(a,flat(t,c2+cf+j*w,c2+cf+(j+1)*w),1,0)
                h=act[t,:,lane]
                wacc[0,t,:,lane]+=fold(g*h); wacc[1,t,:,lane]+=fold(g)
                v=g*wide(1,t,j*w,w)
                tt[t,:,lane]=v
                s1b[...]+=lanes(v); s2b[...]+=lanes(v*h)
            return 0
        s1b[...]=jnp.zeros_like(s1b); s2b[...]=jnp.zeros_like(s2b)
        lax.fori_loop(0,T,back1,0)
        def f5(q,i):
            s1b[q,:]=jnp.broadcast_to(jnp.sum(s1b[q,:],axis=1,keepdims=True)/F,(sub,PAIR))
            s2b[q,:]=jnp.broadcast_to(jnp.sum(s2b[q,:],axis=1,keepdims=True)/F,(sub,PAIR))
        each(f5)
        acc[...]=jnp.zeros_like(acc)
        def back2(t,_):
            fcols=pl.ds(pl.multiple_of(t*cf,128),cf)
            def e(q,i):
                ag=s2[q,0:1]*(tt[t,q,:]-s1b[q,0:1]-act[t,q,:]*s2b[q,0:1])
                ul=(ag*dact[t,q,:]).astype(b16)
                unl[rows(i),fcols]=ul
                wacc[2,t]+=fold(ul.astype(f32))
            each(e)
            a=unl[whole,fcols]
            for s in range(S):
                acc[:,s*DS:(s+1)*DS]+=_dot(a,flat(t,c2,c2+cf,s),1,1)
            return 0
        lax.fori_loop(0,T,back2,0)
        def f6(q,i):
            h,r=norm_parts(middle[q,:])
            e=acc[q,:]
            vacc[3]+=fold(e*h); vacc[4]+=fold(e)
            m=og[q,:]+norm_back(e,h,r,vec(SECG))
            mg[tokens(i),:]=m
            ml=m.astype(b16)
            midl[rows(i),:]=ml
            vacc[2]+=fold(ml.astype(f32))
        each(f6)
        def back3(t,_):
            acc[:,pl.ds(pl.multiple_of(t*c2,128),c2)]=_dot(midl[whole,:],flat(t,0,c2),1,0)
            return 0
        lax.fori_loop(0,T,back3,0)
        def f7(q,i):
            h,r=norm_parts(mix[q,:].astype(f32))
            e=acc[q,:]
            vacc[0]+=fold(e*h); vacc[1]+=fold(e)
            mix[q,:]=norm_back(e,h,r,vec(MIXG)).astype(b16)
        each(f7)
        for gg in range(SG):
            for h in range(HP):
                gout[b,gg*HP+h]=mix[gg*n:(gg+1)*n,h*PAIR:(h+1)*PAIR]
        copies=[pltpu.make_async_copy(src.at[whole],dst.at[whole],o_sem.at[b,i]) for i,(src,dst) in enumerate(
            ((inner,inner_ref),(second,second_ref),(outl,out_ref),(midl,midl_ref),(hid,hid_ref),(unl,unl_ref)))]
        for gg in range(SG):
            part=pl.ds(gg*spg*n+b*n,n)
            copies+=[pltpu.make_async_copy(src.at[part],dst.at[part],o_sem.at[b,6+3*gg+i]) for i,(src,dst) in enumerate(((x_ref,mid_ref),(res,res_ref),(mg,mg_ref)))]
        if b<spg-1:
            copies.append(pltpu.make_async_copy(gout.at[b,me],g_refs[b].at[me],o_sem.at[b,6+3*SG]))
            far_g=[remote(gout.at[b,other],g_refs[b].at[me],g_send.at[b,k],g_recv.at[b,k],dev) for k,other,dev in place.group_peers()]
            for c in far_g: c.start()
            g_out.extend(far_g)
        else:
            copies.append(pltpu.make_async_copy(gout.at[b],g_refs[b],o_sem.at[b,6+3*SG]))
        for c in copies: c.start()
        return copies
    g_out=[]
    done=[]
    for b in range(spg): done+=block(b)
    for i in range(7):
        sum_ref[i:i+1,:]=jnp.sum(vacc[i],axis=0,keepdims=True)
    for i in range(3):
        for t in range(T):
            at=(i*F+t*cf)
            sum_ref[7+at//D:8+at//D,at%D:at%D+cf]=jnp.sum(wacc[i,t],axis=0,keepdims=True)
    for c in done: c.wait()
    for c in g_out: c.wait()
    for c in rows_in: c.wait_send()
    for r in range(3):
        for c in far[r]: c.wait_send()

def feed(S,C,T,o,wa,wb,x,teacher,ids,mask,vecs,wides):
    plain=(x,teacher,ids,mask)+tuple(vecs)+tuple(wides)
    R,D=x.shape
    spg=len(o)
    G,n=o[0].shape[:2]
    rows=(G,spg,n,PAIR)
    CC=2 if C%2==0 else 1
    CX=C//CC
    DR,c2=wa[0].shape[-2]+wb[0].shape[-2],wa[0].shape[-1]
    F=wides[0].shape[-1]; cf=F//T; B=R//spg; SG=G//(D//PAIR)
    b16,f32=jnp.bfloat16,jnp.float32
    vm=pl.BlockSpec(memory_space=pltpu.VMEM); anyspec=pl.BlockSpec(memory_space=pl.ANY)
    dma=pltpu.SemaphoreType.DMA
    V=lambda shape,dt=b16: pltpu.VMEM(shape,dt)
    NP=2*S*CX; NCC=max(CC-1,1)
    sums=8+3*F//D; sums+=-sums%8
    sds=jax.ShapeDtypeStruct
    return pl.pallas_call(functools.partial(feed_kernel,S,C,T,max(cf//512,1),spg),
        in_specs=[pl.BlockSpec(memory_space=pltpu.HBM)]*(spg+S+CX+len(plain)),
        out_specs=[anyspec]*9+[vm]+[anyspec]*spg,
        out_shape=[sds((R,D),f32)]*3+[sds((R,D),b16)]*4+[sds((R,F),b16)]*2+[sds((sums,D),f32)]+[sds((G,n,PAIR),b16)]*spg,
        scratch_shapes=[V((T,S,CX,CC,DR,c2)),V(rows),V((B,D)),V((R,D)),V((R,D)),V((R,D)),V((R,D)),V((R,F)),V((R,F)),
                        V((T,B,cf),f32),V((T,B,cf),f32),V((T,B,cf),f32),V((B,D),f32),V((B,D),f32),V((B,D),f32),V((B,PAIR),f32),V((B,PAIR),f32),
                        V((R,D),f32),V((R,D),f32),V((spg,G,n,PAIR)),V((7,8,D),f32),V((3,T,8,cf),f32),
                        dma((3,NP)),dma((3,NCC,NP)),dma((3,NCC,NP)),dma((G-1,)),dma((G-1,)),dma((spg,G-1)),dma((spg,G-1)),dma((spg,)),dma((spg,7+3*SG)),V((B,PAIR),f32),V((B,PAIR),f32),
                        [V(a.shape,a.dtype) for a in plain],dma((len(plain),))],
        compiler_params=pltpu.CompilerParams(collective_id=3,has_side_effects=True,vmem_limit_bytes=63<<20),
        name="feed")(*o,*wa,*wb,*plain)


def weight_grads_kernel(S,C,T,out_ref,second_ref,middle_ref,inner_ref,unit_ref,hidden_ref,g_ref,early_ref,*rest):
    CX0=C//(2 if C%2==0 else 1)
    NA=1+2*(S-1); NB=1+2*(CX0-1); TH=T//2
    pa_refs,pb_refs=rest[:NA],rest[NA:NA+NB]
    gin_ref,sum_ref,own,got,send,recv,local,a_send,a_recv,a_local,ev,ev_recs,v_send,v_recv,buffers,load=rest[NA+NB:]
    loads=fetch((early_ref,middle_ref,inner_ref,second_ref,unit_ref,out_ref,hidden_ref),(ev,)+tuple(buffers),load)
    middle_ref,inner_ref,second_ref,unit_ref,out_ref,hidden_ref=buffers
    place=Place(S,C,T)
    R,D=out_ref.shape
    CX=place.size["x"]; CC=place.CC
    HR,width=own.shape[-2:]
    c2=inner_ref.shape[1]//T; cf=unit_ref.shape[1]//T
    cc=place.at["c"]
    barrier=pltpu.get_barrier_semaphore()
    others=list(place.peers("c"))
    count=0
    for _,_,dev in place.group_peers():
        pl.semaphore_signal(barrier,inc=1,device_id=dev,device_id_type=MESH_ID); count+=1
    for _,_,dev in place.peers("s"):
        pl.semaphore_signal(barrier,inc=1,device_id=dev,device_id_type=MESH_ID); count+=1
    pl.semaphore_wait(barrier,count)
    me=place.group
    mine=pltpu.make_async_copy(g_ref.at[me],gin_ref.at[me],a_local.at[0]); mine.start()
    rows_in=[remote(g_ref.at[other],gin_ref.at[me],a_send.at[k],a_recv.at[k],dev) for k,other,dev in place.group_peers()]
    for c in rows_in: c.start()
    loads[0].wait()
    early=VectorSum(place,ev,ev_recs,v_send,v_recv)
    early.start("c")
    for c in loads[1:]: c.wait()
    plan=[(middle_ref,inner_ref,0,c2,c2),(second_ref,unit_ref,c2,cf,min(cf,512)),(out_ref,hidden_ref,c2+cf,cf,min(cf,512))]
    def swap(t):
        return [remote(own.at[t,:,:,other],got.at[t,k],send.at[t,k],recv.at[t,k],dev) for k,other,dev in others]
    def outs(t,act):
        def go(src,ref,sem,cond=None):
            if cond is None: act(pltpu.make_async_copy(src,ref,sem))
            else:
                @pl.when(cond)
                def _(): act(pltpu.make_async_copy(src,ref,sem))
        for d in range(S):
            src=got.at[t,0,lax.rem(place.at["s"]+d,S),:,0]
            if d==0: go(src,pa_refs[0].at[t],local.at[t,0])
            else:
                go(src,pa_refs[2*d-1].at[lax.rem(t,TH)],local.at[t,d],t<TH)
                go(src,pa_refs[2*d].at[lax.rem(t,TH)],local.at[t,d],t>=TH)
        for d in range(CX):
            src=got.at[t,0,:,lax.rem(place.at["x"]+d,CX),1]
            if d==0: go(src,pb_refs[0].at[t],local.at[t,S])
            else:
                go(src,pb_refs[2*d-1].at[lax.rem(t,TH)],local.at[t,S+d],t<TH)
                go(src,pb_refs[2*d].at[lax.rem(t,TH)],local.at[t,S+d],t>=TH)
    def settle(t):
        for c in swap(t): c.wait_recv()
        for s in range(S):
            for x in range(CX):
                total=own[t,s,x,cc].astype(jnp.float32)
                for k,_,_ in others:
                    total=total+got[t,k,s,x].astype(jnp.float32)
                got[t,0,s,x]=total.astype(jnp.bfloat16)
        outs(t,lambda c: c.start())
    def one(t,_):
        for left,right,base,cols,chunk in plan:
            for j in range(cols//chunk):
                y=_dot(left[...],right[:,pl.ds(pl.multiple_of(t*cols+j*chunk,128),chunk)],0,0)
                own[t,:,:,:,:,:,base+j*chunk:base+(j+1)*chunk]=y.astype(jnp.bfloat16).reshape(S,CX,CC,2,HR,chunk)
        for c in swap(t): c.start()
        @pl.when(t>0)
        def _(): settle(t-1)
        for i,(x,y) in enumerate(("cs","sx","xt")):
            if i+1<T:
                @pl.when(t==i+1)
                def _(): early.end(x); early.start(y)
        return 0
    lax.fori_loop(0,T,one,0)
    settle(T-1)
    for i,(x,y) in enumerate(("cs","sx","xt")):
        if i+1>=T: early.end(x); early.start(y)
    early.end("t")
    sum_ref[...]=ev[...]
    def finish(t,_):
        for c in swap(t): c.wait_send()
        outs(t,lambda c: c.wait())
        return 0
    lax.fori_loop(0,T,finish,0)
    mine.wait()
    for c in rows_in: c.wait()

def weight_grads(S,C,T,out_low,second_low,middle_low,inner_low,unit_low,hidden_low,g,early):
    R,D=out_low.shape
    CC=2 if C%2==0 else 1
    CX=C//CC; HR=D//(S*C*2); width=(D+2*unit_low.shape[1])//T
    hbm=pl.BlockSpec(memory_space=pltpu.HBM); anyspec=pl.BlockSpec(memory_space=pl.ANY)
    dma=pltpu.SemaphoreType.DMA
    return pl.pallas_call(functools.partial(weight_grads_kernel,S,C,T),
        in_specs=[hbm]*8,out_specs=[anyspec]*(2*S+2*CX-1)+[pl.BlockSpec(memory_space=pltpu.VMEM)],
        out_shape=[jax.ShapeDtypeStruct((T,CX,HR,width),jnp.bfloat16)]+[jax.ShapeDtypeStruct((T//2,CX,HR,width),jnp.bfloat16)]*(2*S-2)+
                  [jax.ShapeDtypeStruct((T,S,HR,width),jnp.bfloat16)]+[jax.ShapeDtypeStruct((T//2,S,HR,width),jnp.bfloat16)]*(2*CX-2)+[jax.ShapeDtypeStruct(g.shape,jnp.bfloat16),jax.ShapeDtypeStruct(early.shape,jnp.float32)],
        scratch_shapes=[pltpu.VMEM((T,S,CX,CC,2,HR,width),jnp.bfloat16),pltpu.VMEM((T,max(CC-1,1),S,CX,2,HR,width),jnp.bfloat16),
                        dma((T,max(CC-1,1))),dma((T,max(CC-1,1))),dma((T,S+CX)),dma((C*T-1,)),dma((C*T-1,)),dma((1,))]+vector_scratch({"t":T,"s":S,"x":CX,"c":CC},early.shape[0],D)+
                       [[pltpu.VMEM(a.shape,a.dtype) for a in (middle_low,inner_low,second_low,unit_low,out_low,hidden_low)],dma((7,))],
        compiler_params=pltpu.CompilerParams(collective_id=1,has_side_effects=True,vmem_limit_bytes=63<<20),
        name="weight_grads")(out_low,second_low,middle_low,inner_low,unit_low,hidden_low,g,early)


CHUNKS=2

def finish_kernel(S,C,T,NO,*refs):
    d_refs=refs[:NO]
    finish_split(S,C,T,d_refs,*refs[NO:])

def finish_split(S,C,T,d_refs,low_ref,wide_ref,x_ref,mg_ref,gain_ref,*rest):
    CX0=C//(2 if C%2==0 else 1)
    NA=1+2*(S-1); NB=1+2*(CX0-1)
    ra_refs,rb_refs=rest[:NA],rest[NA:NA+NB]
    *rest,buffers,load=rest[NA+NB:]
    own_loads=fetch((low_ref,x_ref,mg_ref,gain_ref),buffers,load)
    finish_body(S,C,T,own_loads,d_refs,buffers[0],wide_ref,*buffers[1:],ra_refs,rb_refs,*rest)

def finish_body(S,C,T,own_loads,d_refs,low_ref,wide_ref,x_ref,mg_ref,gain_ref,ra_refs,rb_refs,
                  grad_ref,dq_ref,dk_ref,dv_ref,do_ref,du_ref,dd_ref,late_ref,
                  rbuf,wbuf,acc,gbuf,rc,ra2,rb2,ra3,rb3,gz,gzr,bz,bzr,z_send,z_recv,
                  xa,xb,ya,yb,za,zb,d2,
                  lv,lv_recs,v_send,v_recv,
                  a_send,a_recv,w_send,w_recv,g_send,g_recv,local):
    gz,gzr,bz,bzr=[list(r) for r in (gz,gzr,bz,bzr)]
    place=Place(S,C,T)
    R,D=low_ref.shape
    G,_,n=d_refs[0].shape[:3]
    spg=len(d_refs)
    HP=D//PAIR; SG=G//HP
    cols=wbuf.shape[-1]; hpt=cols//PAIR
    DR=wbuf.shape[-2]
    CX=place.size["x"]; CC=place.CC; TH=T//2
    t0,s0,x0,c0=place.at["t"],place.at["s"],place.at["x"],place.at["c"]
    me=place.group
    f32=jnp.float32; b16=jnp.bfloat16
    sent=[]
    def go(copies):
        for c in copies: c.start()
        sent.extend(copies)
        return copies
    def land(copies):
        for c in copies: c.wait_recv()
    steps=[1<<k for k in range(T.bit_length()-1)]
    def bit(k): return lax.rem(t0//steps[k],2)
    def trade(k,which,bufs,recs):
        other=t0+steps[k]-2*steps[k]*bit(k)
        return go([remote(bufs[k].at[:,1-bit(k)],recs[k],z_send.at[which,k],z_recv.at[which,k],{"tensor":other})])
    def settle(k,copies,bufs,recs):
        land(copies)
        v=bufs[k][:,bit(k)].astype(f32)+recs[k][...].astype(f32)
        if k+1<len(steps): bufs[k+1][...]=v.astype(b16).reshape(bufs[k+1].shape)
        return v
    gzs=[[r.at[w] for r in gz] for w in range(3)]; gzrs=[[r.at[w] for r in gzr] for w in range(3)]
    loads=[pltpu.make_async_copy(wide_ref,wbuf,local.at[3*spg])]
    def arrivals(refs,buf,base):
        out=[pltpu.make_async_copy(refs[0],buf.at[0],local.at[base])]
        for i,ref in enumerate(refs[1:]):
            out.append(pltpu.make_async_copy(ref,buf.at[1+i//2,i%2*TH:i%2*TH+TH],local.at[base+1+i]))
        return out
    loads+=arrivals(ra_refs,xa,3*spg+1)
    loads+=arrivals(rb_refs,xb,3*spg+1+len(ra_refs))
    for c in loads: c.start()
    greet(place)
    rows_in=[None]*3
    mine=[None]*3
    last=d_refs[-1]
    for w in (2,1,0):
        mine[w]=[pltpu.make_async_copy(last.at[me,w],rbuf.at[w,me,spg-1],local.at[w*spg])]
        mine[w]+=[pltpu.make_async_copy(d_refs[i].at[:,w],rbuf.at[w,:,i],local.at[w*spg+1+i]) for i in range(spg-1)]
        for c in mine[w]: c.start()
        rows_in[w]=go([remote(last.at[other,w],rbuf.at[w,me,spg-1],a_send.at[w,k],a_recv.at[w,k],dev) for k,other,dev in place.group_peers()])

    late=VectorSum(place,lv,lv_recs,v_send,v_recv)

    for c in loads[1:]: c.wait()
    c2=xa.shape[-1]
    cuts=[c2*h//(128*CHUNKS)*128 for h in range(CHUNKS)]+[c2]
    plane_a,plane_b=[],[]
    for h in range(CHUNKS):
        lane=slice(cuts[h],cuts[h+1])
        def add_a(t,_):
            v=xa[0,t,:,:,lane].astype(f32)
            for i in range(1,S): v=v+xa[i,t,:,:,lane].astype(f32)
            ya[t,:,:,lane]=v.astype(b16)
            return 0
        lax.fori_loop(0,T,add_a,0)
        plane_a.append(go([remote(ya.at[:,other,:,lane],za.at[k,:,:,lane],w_send.at[0,h,k],w_recv.at[0,h,k],dev) for k,other,dev in place.peers("x")]))
        def add_b(t,_):
            v=xb[0,t,:,:,lane].astype(f32)
            for i in range(1,CX): v=v+xb[i,t,:,:,lane].astype(f32)
            yb[t,:,:,lane]=v.astype(b16)
            return 0
        lax.fori_loop(0,T,add_b,0)
        plane_b.append(go([remote(yb.at[:,other,:,lane],zb.at[k,:,:,lane],w_send.at[1,h,k],w_recv.at[1,h,k],dev) for k,other,dev in place.peers("s")]))
    loads[0].wait()
    for c in own_loads: c.wait()

    lv[...]=jnp.zeros_like(lv)
    def compute(w,first):
        for c in mine[w]: c.wait()
        land(rows_in[w])
        def one(t,_):
            d=jnp.concatenate([jnp.concatenate([rbuf[w,g*HP+t*hpt+j].reshape(spg*n,PAIR) for j in range(hpt)],axis=1) for g in range(SG)],axis=0)
            y=_dot(low_ref[...],d,0,0)
            gbuf[w,t]=y.astype(b16).reshape(S,CX,CC,DR,cols)
            z=_dot(d,wbuf[w,t].reshape(D,cols),1,1)
            if first:
                @pl.when(t==0)
                def _(): acc[...]=z
                @pl.when(t>0)
                def _(): acc[...]+=z
            else:
                acc[...]+=z
            if w!=1:
                lv[2+w//2:3+w//2,pl.ds(pl.multiple_of(t*cols,128),cols)]=jnp.sum(d.astype(f32),axis=0,keepdims=True)
            return 0
        lax.fori_loop(0,T,one,0)
        return go([remote(gbuf.at[w,:,:,:,other],rc.at[w,k],g_send.at[w,0,k],g_recv.at[w,0,k],dev) for k,other,dev in place.peers("c")])
    def after_core(w,copies):
        land(copies)
        for t in range(T):
            v=gbuf[w,t,:,:,c0].astype(f32)
            for k in range(CC-1): v=v+rc[w,k,t].astype(f32)
            rc[w,0,t]=v.astype(b16)
        a=go([remote(rc.at[w,0,0:TH,other],ra2.at[w,k],g_send.at[w,1,k],g_recv.at[w,1,k],dev) for k,other,dev in place.peers("s")])
        b=go([remote(rc.at[w,0,TH:T,:,other],rb2.at[w,k],g_send.at[w,2,k],g_recv.at[w,2,k],dev) for k,other,dev in place.peers("x")])
        return a,b
    def after_second(w,pair):
        land(pair[0])
        v=rc[w,0,0:TH,s0].astype(f32)
        for k in range(S-1): v=v+ra2[w,k].astype(f32)
        ra2[w,0]=v.astype(b16)
        a=go([remote(ra2.at[w,0,:,other],ra3.at[w,k],g_send.at[w,3,k],g_recv.at[w,3,k],dev) for k,other,dev in place.peers("x")])
        land(pair[1])
        v=rc[w,0,TH:T,:,x0].astype(f32)
        for k in range(CX-1): v=v+rb2[w,k].astype(f32)
        rb2[w,0]=v.astype(b16)
        b=go([remote(rb2.at[w,0,:,other],rb3.at[w,k],g_send.at[w,4,k],g_recv.at[w,4,k],dev) for k,other,dev in place.peers("s")])
        return a,b
    def after_third(w,pair):
        land(pair[0])
        v=ra2[w,0,:,x0].astype(f32)
        for k in range(CX-1): v=v+ra3[w,k].astype(f32)
        gz[0][w,0:T//4]=v.astype(b16).reshape(T//4,2,DR,cols)
        land(pair[1])
        v=rb2[w,0,:,s0].astype(f32)
        for k in range(S-1): v=v+rb3[w,k].astype(f32)
        gz[0][w,T//4:T//2]=v.astype(b16).reshape(T//4,2,DR,cols)
        return trade(0,w,gzs[w],gzrs[w])
    def onward(k,w,copies):
        settle(k-1,copies,gzs[w],gzrs[w])
        return trade(k,w,gzs[w],gzrs[w])
    def big_trade(k,h):
        lane=slice(cuts[h],cuts[h+1])
        other=t0+steps[k]-2*steps[k]*bit(k)
        return go([remote(bz[k].at[i,:,1-bit(k),:,lane],bzr[k].at[i,:,:,lane],z_send.at[3+2*h+i,k],z_recv.at[3+2*h+i,k],{"tensor":other}) for i in range(2)])
    def big_settle(k,h,copies):
        lane=slice(cuts[h],cuts[h+1])
        land(copies)
        for i in range(2):
            v=bz[k][i,:,bit(k),:,lane].astype(f32)+bzr[k][i,:,:,lane].astype(f32)
            if k+1<len(steps): bz[k+1][i,:,:,:,lane]=v.astype(b16).reshape(bz[k+1].shape[1:4]+(v.shape[-1],))
            else: d2[i*v.shape[1]:(i+1)*v.shape[1],lane]=v[0]
    def big_onward(k,h,copies):
        big_settle(k-1,h,copies)
        return big_trade(k,h)
    def big_first(h):
        lane=slice(cuts[h],cuts[h+1])
        land(plane_a[h])
        def add_a2(j,_):
            v=ya[pl.ds(2*j,2),x0,:,lane].astype(f32)
            for k in range(CX-1): v=v+za[k,pl.ds(2*j,2),:,lane].astype(f32)
            bz[0][0,j,:,:,lane]=v.astype(b16)
            return 0
        lax.fori_loop(0,T//2,add_a2,0)
        land(plane_b[h])
        def add_b2(j,_):
            v=yb[pl.ds(2*j,2),s0,:,lane].astype(f32)
            for k in range(S-1): v=v+zb[k,pl.ds(2*j,2),:,lane].astype(f32)
            bz[0][1,j,:,:,lane]=v.astype(b16)
            return 0
        lax.fori_loop(0,T//2,add_b2,0)
        return big_trade(0,h)
    end=len(steps)
    big=[None]*CHUNKS
    core_v=compute(2,True)
    big[0]=big_first(0)
    two_v=after_core(2,core_v)
    core_k=compute(1,False)
    big[1]=big_first(1)
    three_v=after_second(2,two_v)
    two_k=after_core(1,core_k)
    for h in range(2,CHUNKS): big[h]=big_first(h)
    core_q=compute(0,False)
    big[0]=big_onward(1,0,big[0])
    z_v=after_third(2,three_v)
    three_k=after_second(1,two_k)
    two_q=after_core(0,core_q)
    big[1]=big_onward(1,1,big[1])
    step=min(64,R)
    def back(i,carry):
        rows=pl.ds(pl.multiple_of(i*step,step),step)
        h,r=norm_parts(x_ref[rows,:])
        e=acc[rows,:]
        grad_ref[rows,:]=mg_ref[rows,:]+norm_back(e,h,r,gain_ref[...])
        return carry[0]+jnp.sum(e*h,axis=0,keepdims=True),carry[1]+jnp.sum(e,axis=0,keepdims=True)
    zero=jnp.zeros((1,D),f32)
    ga,sa=lax.fori_loop(0,R//step,back,(zero,zero))
    lv[0:1,:]=ga; lv[1:2,:]=sa
    late.start("c")
    three_q=after_second(0,two_q)
    z_k=after_third(1,three_k)
    z_v=onward(1,2,z_v)
    late.end("c"); late.start("s")
    z_q=after_third(0,three_q)
    for h in range(2,CHUNKS): big[h]=big_onward(1,h,big[h])
    z_k=onward(1,1,z_k)
    late.end("s"); late.start("x")
    z_q=onward(1,0,z_q)
    late.end("x"); late.start("t")
    for k in range(2,end):
        for h in range(CHUNKS): big[h]=big_onward(k,h,big[h])
        z_v=onward(k,2,z_v); z_k=onward(k,1,z_k); z_q=onward(k,0,z_q)
    dv_ref[...]=settle(end-1,z_v,gzs[2],gzrs[2])[0]
    big_settle(end-1,0,big[0])
    dk_ref[...]=settle(end-1,z_k,gzs[1],gzrs[1])[0]
    dq_ref[...]=settle(end-1,z_q,gzs[0],gzrs[0])[0]
    for h in range(1,CHUNKS): big_settle(end-1,h,big[h])
    co=do_ref.shape[0]; cf=du_ref.shape[1]
    do_ref[...]=d2[:,:co].T
    du_ref[...]=d2[:,co:co+cf]
    dd_ref[...]=d2[:,co+cf:].T
    late.end("t"); late_ref[...]=lv[...]
    for c in sent: c.wait_send()

def finish(S,C,T,ds,first_low,wide,ra,rb,x,middle_grad,gain):
    R,D=x.shape
    G,_,n=ds[0].shape[:3]
    spg=len(ds)
    CC=2 if C%2==0 else 1
    CX=C//CC; TH=T//2
    DR,cols=wide.shape[-2:]
    HR,c2=ra[0].shape[-2:]
    b16,f32=jnp.bfloat16,jnp.float32
    vm=pl.BlockSpec(memory_space=pltpu.VMEM)
    dma=pltpu.SemaphoreType.DMA
    size={"t":T,"s":S,"x":CX,"c":CC}
    most=max(T,S,CX,CC)-1
    NL=8; co=D//T; cf=(c2-co)//2
    V=lambda shape,dt=b16: pltpu.VMEM(shape,dt)
    halves=[T>>(k+1) for k in range(T.bit_length()-1)]
    scratch=[V((3,G,spg,n,PAIR)),V(wide.shape),V((R,D),f32),V((3,T,S,CX,CC,DR,cols)),V((3,max(CC-1,1),T,S,CX,DR,cols)),
             V((3,max(S-1,1),TH,CX,DR,cols)),V((3,max(CX-1,1),TH,S,DR,cols)),V((3,max(CX-1,1),TH,DR,cols)),V((3,max(S-1,1),TH,DR,cols)),
             [V((3,h,2,DR,cols)) for h in halves],[V((3,h,DR,cols)) for h in halves],
             [V((2,h,2,HR,c2)) for h in halves],[V((2,h,HR,c2)) for h in halves],
             dma((3+2*CHUNKS,len(halves))),dma((3+2*CHUNKS,len(halves))),
             V((S,)+ra[0].shape),V((CX,)+rb[0].shape),V((T,CX,HR,c2)),V((T,S,HR,c2)),V((max(CX-1,1),T,HR,c2)),V((max(S-1,1),T,HR,c2)),
             V((2*HR,c2),f32)]+vector_scratch(size,NL,D)+[
             dma((3,G-1)),dma((3,G-1)),dma((2,CHUNKS,most)),dma((2,CHUNKS,most)),dma((3,6,most)),dma((3,6,most)),dma((3*spg+1+len(ra)+len(rb),)),
             [V((R,D)),V((R,D),f32),V((R,D),f32),V((1,D),f32)],dma((4,))]
    hbm=pl.BlockSpec(memory_space=pltpu.HBM)
    sds=jax.ShapeDtypeStruct
    return pl.pallas_call(functools.partial(finish_kernel,S,C,T,spg),
        in_specs=[hbm]*(spg+5+len(ra)+len(rb)),
        out_specs=[vm]*8,
        out_shape=[sds((R,D),f32)]+[sds((DR,cols),f32)]*3+[sds((co,2*HR),f32),sds((2*HR,cf),f32),sds((cf,2*HR),f32),sds((NL,D),f32)],
        scratch_shapes=scratch,
        compiler_params=pltpu.CompilerParams(collective_id=2,has_side_effects=True,vmem_limit_bytes=63<<20),
        name="finish")(*ds,first_low,wide,x,middle_grad,gain,*ra,*rb)


def shards(inputs,teacher,segments,pad_mask,query_weight,key_weight,value_weight,output_weight,up_weight,down_weight,
           first_gain,first_shift,query_shift,value_shift,mixed_gain,mixed_shift,output_shift,second_gain,second_shift,
           up_shift,hidden_gain,hidden_shift,down_shift):
    S,C,T=lax.axis_size("shard"),lax.axis_size("context"),lax.axis_size("tensor")
    CC=2 if C%2==0 else 1
    CX=C//CC
    G=C*T
    ns,n,D=inputs.shape
    R=ns*n
    HP=D//PAIR
    SG=G//HP
    spg=ns//SG
    me_s=lax.axis_index("shard")
    me_g=lax.axis_index("context")*T+lax.axis_index("tensor")
    c1=query_weight.shape[1]; c2=output_weight.shape[0]; cf=up_weight.shape[1]
    F=cf*T
    x=inputs.reshape(R,D)
    first_low,wide,ids_all,pa,pb,*rows_out=project(S,C,T,x,first_gain[None],first_shift[None],query_weight,key_weight,value_weight,query_shift[None],value_shift[None],
                                             segments.reshape(1,R),output_weight,up_weight,down_weight,ns,n)
    def over_shard(a,d):
        return lax.ppermute(a,"shard",[(i,(i+d)%S) for i in range(S)]) if d else a
    def over_x(a,d):
        return lax.ppermute(a,"context",[(i*CC+j,((i+d)%CX)*CC+j) for i in range(CX) for j in range(CC)]) if d else a
    wa=[over_shard(pa,d) for d in range(S)]
    wb=[over_x(pb,d) for d in range(CX)]
    ids_flat=ids_all
    ids_all=ids_all.reshape(G,S,ns,n)
    ids_mine=lax.dynamic_index_in_dim(ids_all,me_s,1,keepdims=False)
    ids_mine=lax.dynamic_slice_in_dim(ids_mine,(me_g//HP)*spg,spg,1).transpose(1,0,2).reshape(spg,G*n)
    edges=[bounds(ids_mine[i],BLOCK,BLOCK) for i in range(spg)]
    cols=[ids_mine[i][:,None] for i in range(spg)]
    def trade(a):
        return lax.all_to_all(a,("context","tensor"),0,0,tiled=True)
    qkv=[rows_out[0]]+[trade(a) for a in rows_out[1:]]
    mixed=[attend_fwd(qkv[i],ids_mine[i],cols[i],edges[i]) for i in range(spg)]
    arrived=[trade(mixed[i][0]) for i in range(spg-1)]+[mixed[-1][0]]
    vecs=[a[None] for a in (mixed_gain,mixed_shift,output_shift,second_gain,second_shift,down_shift)]
    wides=[a[None] for a in (up_shift,hidden_gain,hidden_shift)]
    middle,branch,middle_grad,inner_low,second_low,out_low,middle_low,hidden_low,unit_low,early,*gs=feed(
        S,C,T,arrived,wa,wb,x,teacher.reshape(R,D),ids_flat,pad_mask,vecs,wides)
    *outs,last_g,early=weight_grads(S,C,T,out_low,second_low,middle_low,inner_low,unit_low,hidden_low,gs[-1],early)
    gs=list(lax.optimization_barrier(tuple(gs[:-1])+(last_g,)))
    NA=1+2*(S-1)
    hops=[over_shard(outs[1+i],1+i//2) for i in range(2*(S-1))],[over_x(outs[NA+1+i],1+i//2) for i in range(2*(CX-1))]
    ds=[attend_bwd(qkv[i],gs[i],mixed[i][0],mixed[i][1],ids_mine[i],cols[i],edges[i]) for i in range(spg)]
    if spg>1:
        ds[0],(first_a,first_b)=lax.optimization_barrier((ds[0],(hops[0][0::2],hops[1][0::2])))
        hops[0][0::2],hops[1][0::2]=first_a,first_b
    ra,rb=[outs[0]]+hops[0],[outs[NA]]+hops[1]
    ds=[trade(a) for a in ds[:-1]]+[ds[-1]]
    result,middle_grad=lax.optimization_barrier((middle+branch,middle_grad))
    input_grad,*grads,late=finish(S,C,T,ds,first_low,wide,ra,rb,x,middle_grad,first_gain[None])
    B=F//D
    vectors=(late[0],late[1],late[2],late[3],early[0],early[1],early[2],early[3],early[4],early[7+2*B:7+3*B].reshape(F),
             early[7:7+B].reshape(F),early[7+B:7+2*B].reshape(F),early[5])
    loss=jnp.sum(early[6])/(early[-1,0]/(S*C*T))
    return (result.reshape(ns,n,D),loss,input_grad.reshape(ns,n,D))+tuple(grads)+vectors


def solution(mesh):
    rows=P("shard",("context","tensor"),None)
    ids=P("shard",("context","tensor"))
    wide=P(("shard","context"),"tensor")
    tall=P("tensor",("shard","context"))
    weights=(wide,wide,wide,tall,wide,tall)
    return jax.shard_map(shards,mesh=mesh,in_specs=(rows,rows,ids,ids)+weights+(P(),)*13,
                         out_specs=(rows,P(),rows)+weights+(P(),)*13,check_vma=False)
```

```python
import functools

import jax
import jax.numpy as jnp
from jax import lax
from jax.experimental import pallas as pl
from jax.experimental.pallas import tpu as pltpu
from jax.sharding import PartitionSpec as P


NEG=-1e30
BLOCK=512
def _dot(a,b,ca,cb):
    return lax.dot_general(a,b,(((ca,),(cb,)),((),())),preferred_element_type=jnp.float32)

def half_masks(rows):
    lane=lax.broadcasted_iota(jnp.int32,(rows,128),1)
    return lane<64

def fwd_kernel(lo_ref,hi_ref,q_ref,k_ref,v_ref,col_ref,row_ref,o_ref,lse_ref,vt_ref,acc_ref,m_ref):
    i=pl.program_id(0)
    bq=acc_ref.shape[2]; bk=vt_ref.shape[3]; n=k_ref.shape[2]; per=bk//n
    upper=lax.broadcasted_iota(jnp.int32,(128,1),0)<64
    @pl.when(i==0)
    def _():
        def turn(j,_):
            vt=v_ref[pl.ds(j*per,per),0].reshape(bk,128).astype(jnp.float32).T
            vt_ref[0,j]=jnp.where(upper,vt,1.0).astype(jnp.bfloat16)
            vt_ref[1,j]=jnp.where(upper,1.0,vt).astype(jnp.bfloat16)
            return 0
        lax.fori_loop(0,vt_ref.shape[1],turn,0)
    left=half_masks(bq)
    q=q_ref[...].reshape(bq,128)*jnp.bfloat16(0.125)
    zero=jnp.zeros_like(q)
    qs=(jnp.where(left,q,zero),jnp.where(left,zero,q))
    ids_q=row_ref[i]
    acc_ref[...]=jnp.zeros_like(acc_ref)
    m_ref[...]=jnp.full_like(m_ref,NEG)
    def step(j,_):
        k=k_ref[pl.ds(j*per,per),0].reshape(bk,128)
        same=col_ref[pl.ds(pl.multiple_of(j*bk,bk),bk),:]==ids_q
        for h in range(2):
            sc=jnp.where(same,_dot(k,qs[h],1,1),NEG)
            old=m_ref[h:h+1,:]
            top=jnp.maximum(old,jnp.max(sc,axis=0,keepdims=True))
            e=jnp.exp(sc-top).astype(jnp.bfloat16)
            m_ref[h:h+1,:]=top
            acc_ref[h]=acc_ref[h]*jnp.exp(old-top)+_dot(vt_ref[h,j],e,1,0)
        return 0
    lax.fori_loop(lo_ref[i],hi_ref[i],step,0)
    t0=acc_ref[0,64:65,:]; t1=acc_ref[1,0:1,:]
    o=jnp.where(upper,acc_ref[0]/t0,acc_ref[1]/t1).T
    o_ref[...]=o.astype(jnp.bfloat16).reshape(o_ref.shape)
    lse_ref[0,0:1,:]=m_ref[0:1,:]+jnp.log(t0)
    lse_ref[0,1:2,:]=m_ref[1:2,:]+jnp.log(t1)

def bounds(ids,bq,bk):
    first=ids[::bq]; last=ids[bq-1::bq]
    start=jnp.sum((ids[None,:]<first[:,None]).astype(jnp.int32),axis=1)
    end=jnp.sum((ids[None,:]<=last[:,None]).astype(jnp.int32),axis=1)
    return start//bk,(end+bk-1)//bk

def attend_fwd(qkv,ids,col,edges,bq=BLOCK,bk=BLOCK):
    G,_,n,_=qkv.shape; L=G*n
    row=ids.reshape(L//bq,1,bq)
    part=lambda w: pl.BlockSpec((G,1,n,128),lambda i,*_: (0,w,0,0))
    ospec=pl.BlockSpec((bq//n,n,128),lambda i,*_:(i,0,0))
    return pl.pallas_call(fwd_kernel,
        grid_spec=pltpu.PrefetchScalarGridSpec(num_scalar_prefetch=2,grid=(L//bq,),
            in_specs=[pl.BlockSpec((bq//n,1,n,128),lambda i,*_:(i,0,0,0)),part(1),part(2),pl.BlockSpec((L,1),lambda i,*_:(0,0)),
                      pl.BlockSpec((L//bq,1,bq),lambda i,*_:(0,0,0))],
            out_specs=[ospec,pl.BlockSpec((1,2,bq),lambda i,*_:(i,0,0))],
            scratch_shapes=[pltpu.VMEM((2,L//bk,128,bk),jnp.bfloat16),pltpu.VMEM((2,128,bq),jnp.float32),pltpu.VMEM((2,bq),jnp.float32)]),
        out_shape=[jax.ShapeDtypeStruct((G,n,128),jnp.bfloat16),jax.ShapeDtypeStruct((L//bq,2,bq),jnp.float32)],
        compiler_params=pltpu.CompilerParams(dimension_semantics=("arbitrary",),vmem_limit_bytes=63<<20),
        cost_estimate=pl.CostEstimate(flops=4*L*1024*128*2,bytes_accessed=8*L*256,transcendentals=2*L*1024),
        name="attend_fwd")(*edges,qkv,qkv,qkv,col,row)

def bwd_kernel(lo_ref,hi_ref,q_ref,k_ref,v_ref,g_ref,o_ref,lse_ref,col_ref,row_ref,d_ref,dqa,dka,dva):
    i=pl.program_id(0)
    bq=dqa.shape[1]; bk=BLOCK; n=k_ref.shape[2]; per=bk//n
    @pl.when(i==0)
    def _():
        dka[...]=jnp.zeros_like(dka); dva[...]=jnp.zeros_like(dva)
    left=half_masks(bq)
    q=q_ref[...].reshape(bq,128)*jnp.bfloat16(0.125)
    g=g_ref[...].reshape(bq,128)
    zero=jnp.zeros_like(q)
    qs=(jnp.where(left,q,zero),jnp.where(left,zero,q))
    gs=(jnp.where(left,g,zero),jnp.where(left,zero,g))
    d_t=(g.astype(jnp.float32)*o_ref[...].reshape(bq,128).astype(jnp.float32)).T
    lses=(lse_ref[0,0:1,:],lse_ref[0,1:2,:])
    ds=(jnp.sum(d_t[:64],axis=0,keepdims=True),jnp.sum(d_t[64:],axis=0,keepdims=True))
    ids_q=row_ref[i]
    dqa[...]=jnp.zeros_like(dqa)
    def step(j,_):
        k=k_ref[pl.ds(j*per,per),0].reshape(bk,128)
        v=v_ref[pl.ds(j*per,per),0].reshape(bk,128)
        rows=pl.ds(pl.multiple_of(j*bk,bk),bk)
        same=col_ref[rows,:]==ids_q
        dk=dka[rows,:]; dv=dva[rows,:]
        for h in range(2):
            st=_dot(k,qs[h],1,1)
            p=jnp.exp(jnp.where(same,st,NEG)-lses[h])
            dp=_dot(v,gs[h],1,1)
            d=(p*(dp-ds[h])).astype(jnp.bfloat16)
            dv=dv+_dot(p.astype(jnp.bfloat16),gs[h],1,0)
            dk=dk+_dot(d,qs[h],1,0)
            dqa[h]+=_dot(d,k,0,0)
        dka[rows,:]=dk; dva[rows,:]=dv
        return 0
    lax.fori_loop(lo_ref[i],hi_ref[i],step,0)
    d_ref[pl.ds(i*(bq//n),bq//n),0]=(jnp.where(left,dqa[0],dqa[1])*0.125).astype(jnp.bfloat16).reshape(bq//n,n,128)
    @pl.when(i==pl.num_programs(0)-1)
    def _():
        d_ref[:,1]=dka[...].astype(jnp.bfloat16).reshape(d_ref.shape[0],n,128)
        d_ref[:,2]=dva[...].astype(jnp.bfloat16).reshape(d_ref.shape[0],n,128)

def attend_bwd(qkv,g,o,lse,ids,col,edges,bq=BLOCK):
    bk=BLOCK
    G,_,n,_=qkv.shape; L=G*n
    row=ids.reshape(L//bq,1,bq)
    part=lambda w: pl.BlockSpec((G,1,n,128),lambda i,*_: (0,w,0,0))
    ospec=pl.BlockSpec((bq//n,n,128),lambda i,*_:(i,0,0))
    return pl.pallas_call(bwd_kernel,
        grid_spec=pltpu.PrefetchScalarGridSpec(num_scalar_prefetch=2,grid=(L//bq,),
            in_specs=[pl.BlockSpec((bq//n,1,n,128),lambda i,*_:(i,0,0,0)),part(1),part(2),ospec,
                      ospec,pl.BlockSpec((1,2,bq),lambda i,*_:(i,0,0)),pl.BlockSpec((L,1),lambda i,*_:(0,0)),pl.BlockSpec((L//bq,1,bq),lambda i,*_:(0,0,0))],
            out_specs=pl.BlockSpec((G,3,n,128),lambda i,*_:(0,0,0,0)),
            scratch_shapes=[pltpu.VMEM((2,bq,128),jnp.float32)]+[pltpu.VMEM((L,128),jnp.float32)]*2),
        out_shape=jax.ShapeDtypeStruct((G,3,n,128),jnp.bfloat16),
        compiler_params=pltpu.CompilerParams(dimension_semantics=("arbitrary",),vmem_limit_bytes=63<<20),
        cost_estimate=pl.CostEstimate(flops=1000000,bytes_accessed=1000000,transcendentals=0),
        name="attend_bwd")(*edges,qkv,qkv,qkv,g,o,lse,col,row)


EPS=1e-5
PAIR=128

def norm_parts(v):
    m=jnp.mean(v,axis=-1,keepdims=True)
    s=jnp.mean(v*v,axis=-1,keepdims=True)-m*m
    r=lax.rsqrt(s+EPS)
    return (v-m)*r,r

def norm_back(e,h,r,gain):
    t=e*gain
    return r*(t-jnp.mean(t,axis=-1,keepdims=True)-h*jnp.mean(t*h,axis=-1,keepdims=True))


LINES=3
MESH_ID=pl.DeviceIdType.MESH

class Place:
    def __init__(self,S,C,T):
        self.CC=2 if C%2==0 else 1
        self.size={"t":T,"s":S,"x":C//self.CC,"c":self.CC}
        c=lax.axis_index("context")
        self.at={"t":lax.axis_index("tensor"),"s":lax.axis_index("shard"),"x":c//self.CC,"c":lax.rem(c,self.CC)}
        self.group=c*T+self.at["t"]
        self.T=T; self.G=C*T
    def peers(self,axis):
        m=self.size[axis]
        for d in range(1,m):
            other=lax.rem(self.at[axis]+d,m)
            if axis=="t": yield d-1,other,{"tensor":other}
            elif axis=="s": yield d-1,other,{"shard":other}
            elif axis=="x": yield d-1,other,{"context":other*self.CC+self.at["c"]}
            else: yield d-1,other,{"context":self.at["x"]*self.CC+other}
    def group_peers(self):
        for d in range(1,self.G):
            other=lax.rem(self.group+d,self.G)
            yield d-1,other,{"context":other//self.T,"tensor":lax.rem(other,self.T)}

def upper_rows(rows):
    return max(rows*5//8//16*16,16)

def slots(size,order):
    base,total={},0
    for a in order:
        base[a]=total; total+=size[a]-1
    return base,total

def greet(place):
    barrier=pltpu.get_barrier_semaphore()
    count=0
    for _,_,dev in place.group_peers():
        pl.semaphore_signal(barrier,inc=1,device_id=dev,device_id_type=MESH_ID); count+=1
    for _,_,dev in place.peers("s"):
        pl.semaphore_signal(barrier,inc=1,device_id=dev,device_id_type=MESH_ID); count+=1
    pl.semaphore_wait(barrier,count)

class VectorSum:
    order="csxt"
    def __init__(self,place,cur,recs,send,recv):
        self.place,self.cur,self.send,self.recv=place,cur,send,recv
        self.recs=dict(zip(self.order,recs))
        self.base,_=slots(place.size,self.order)
    def copies(self,axis):
        at=self.place.at[axis]
        return [remote(self.cur,self.recs[axis].at[at],self.send.at[self.base[axis]+k],self.recv.at[self.base[axis]+k],dev)
                for k,_,dev in self.place.peers(axis)]
    def start(self,axis):
        self.recs[axis][self.place.at[axis]]=self.cur[...]
        for c in self.copies(axis): c.start()
    def end(self,axis):
        for c in self.copies(axis): c.wait()
        rec=self.recs[axis]
        total=rec[0]
        for i in range(1,self.place.size[axis]): total=total+rec[i]
        self.cur[...]=total

def vector_scratch(size,rows,D):
    _,total=slots(size,VectorSum.order)
    dma=pltpu.SemaphoreType.DMA
    return [pltpu.VMEM((rows,D),jnp.float32),[pltpu.VMEM((size[a],rows,D),jnp.float32) for a in VectorSum.order],dma((total,)),dma((total,))]

def remote(src,dst,send,recv,dev):
    return pltpu.make_async_remote_copy(src_ref=src,dst_ref=dst,send_sem=send,recv_sem=recv,device_id=dev,device_id_type=MESH_ID)

def fetch(sources,buffers,sem):
    copies=[pltpu.make_async_copy(a,b,sem.at[i]) for i,(a,b) in enumerate(zip(sources,buffers))]
    for c in copies: c.start()
    return copies

def project_kernel(S,C,T,x_ref,gain_ref,shift_ref,wq_ref,wk_ref,wv_ref,qs_ref,vs_ref,ids_ref,wo_ref,wu_ref,wd_ref,
                   low_ref,wide_ref,allids_ref,pa_ref,pb_ref,*rest):
    spg=len(rest)-17
    rows_refs=rest[:spg]
    *scratch,buffers,load=rest[spg:]
    loads=fetch((wq_ref,wk_ref,wv_ref,wo_ref,wu_ref,wd_ref,ids_ref,x_ref,gain_ref,shift_ref,qs_ref,vs_ref),buffers,load)
    wq_ref,wk_ref,wv_ref,wo_ref,wu_ref,wd_ref,ids_ref,x_ref,gain_ref,shift_ref,qs_ref,vs_ref=buffers
    project_body(S,C,T,loads,x_ref,gain_ref,shift_ref,wq_ref,wk_ref,wv_ref,(qs_ref,None,vs_ref),ids_ref,wo_ref,wu_ref,wd_ref,
                 low_ref,wide_ref,allids_ref,pa_ref,pb_ref,rows_refs,*scratch)

def project_body(S,C,T,loads,x_ref,gain_ref,shift_ref,wq_ref,wk_ref,wv_ref,bias_refs,ids_ref,wo_ref,wu_ref,wd_ref,
                   low_ref,wide_ref,allids_ref,pa_ref,pb_ref,rows_refs,
                   zbuf,z_send,z_recv,p_send,p_recv,wbuf,obuf,idbuf,ag_send,ag_recv,a_send,a_recv,i_send,i_recv,local):
    place=Place(S,C,T)
    R,D=low_ref.shape
    G,_,n=rows_refs[0].shape[:3]
    spg=len(rows_refs)
    HP=D//PAIR; SG=G//HP
    cols=wbuf.shape[-1]; hpt=cols//PAIR
    me=place.group
    order="tsxc"
    base,total=slots(place.size,order)
    own=[place.at[a] for a in order]
    for c in loads[:6]: c.wait()
    for w,ref in enumerate((wq_ref,wk_ref,wv_ref)):
        wbuf[w,own[0],own[1],own[2],own[3]]=ref[...].astype(jnp.bfloat16)
    t0=place.at["t"]
    HA=upper_rows(zbuf.shape[1])
    c0=wo_ref.shape[0]; cf=wu_ref.shape[1]
    zbuf[t0,:,0:c0]=wo_ref[...].T.astype(jnp.bfloat16)
    zbuf[t0,:,c0:c0+cf]=wu_ref[...].astype(jnp.bfloat16)
    zbuf[t0,:,c0+cf:]=wd_ref[...].T.astype(jnp.bfloat16)
    wide=c0+2*cf
    cuts=[wide*j//(128*LINES)*128 for j in range(LINES)]+[wide]
    def hop(way,h,piece,j):
        to=t0+1 if way==0 else t0-1
        lane=slice(cuts[j],cuts[j+1])
        return remote(zbuf.at[piece,:,lane],zbuf.at[piece,:,lane],z_send.at[way,h-1,j],z_recv.at[way,h-1,j],{"tensor":lax.rem(to+T,T)})
    def line_start(j):
        @pl.when(t0<T-1)
        def _(): hop(0,1,t0,j).start()
        @pl.when(t0>0)
        def _(): hop(1,1,t0,j).start()
    def line_pass(h,j):
        @pl.when(t0>=h)
        def _():
            hop(0,h,lax.rem(t0-h+T,T),j).wait_recv()
            @pl.when(t0<T-1)
            def _(): hop(0,h+1,lax.rem(t0-h+T,T),j).start()
        @pl.when(t0+h<=T-1)
        def _():
            hop(1,h,lax.rem(t0+h,T),j).wait_recv()
            @pl.when(t0>0)
            def _(): hop(1,h+1,lax.rem(t0+h,T),j).start()
    def line_end():
        for j in range(LINES):
            for h in range(1,T):
                @pl.when((t0<T-1)&(t0>=h-1))
                def _(): hop(0,h,lax.rem(t0-h+1+T,T),j).wait_send()
                @pl.when((t0>0)&(t0+h-1<=T-1))
                def _(): hop(1,h,lax.rem(t0+h-1,T),j).wait_send()
    def plane(j):
        lane=slice(cuts[j],cuts[j+1])
        x0,s0=place.at["x"],place.at["s"]
        out=[pltpu.make_async_copy(zbuf.at[:,0:HA,lane],pa_ref.at[x0,:,:,lane],local.at[8+2*j]),
             pltpu.make_async_copy(zbuf.at[:,HA:,lane],pb_ref.at[s0,:,:,lane],local.at[9+2*j])]
        for k,_,dev in place.peers("x"):
            c=remote(zbuf.at[:,0:HA,lane],pa_ref.at[x0,:,:,lane],p_send.at[0,k,j],p_recv.at[0,k,j],dev); sent.append(c); out.append(c)
        for k,_,dev in place.peers("s"):
            c=remote(zbuf.at[:,HA:,lane],pb_ref.at[s0,:,:,lane],p_send.at[1,k,j],p_recv.at[1,k,j],dev); sent.append(c); out.append(c)
        for c in out: c.start()
        return out
    greet(place)
    stages={2:"tsxc",1:"txsc",0:"txsc"}
    sent=[]
    copies={}
    def start(w,r):
        done=stages[w][:r]; axis=stages[w][r]
        idx=tuple(slice(None) if a in done else place.at[a] for a in order)
        copies[w,r]=[]
        for k,_,dev in place.peers(axis):
            c=remote(wbuf.at[(w,)+idx],wbuf.at[(w,)+idx],ag_send.at[w,base[axis]+k],ag_recv.at[w,base[axis]+k],dev)
            c.start(); copies[w,r].append(c); sent.append(c)
    def arrive(w,r):
        for c in copies[w,r]: c.wait_recv()
    for w in (2,1,0): start(w,0)
    for j in range(LINES): line_start(j)
    loads[6].wait()
    ids_own=pltpu.make_async_copy(ids_ref,idbuf.at[place.at["s"]],local.at[0]); ids_own.start()
    id_first=[]
    for k,_,dev in place.peers("s"):
        c=remote(ids_ref,idbuf.at[place.at["s"]],i_send.at[k],i_recv.at[k],dev); c.start(); id_first.append(c); sent.append(c)
    for c in loads[7:]: c.wait()
    step=min(64,R)
    def norm(i,_):
        rows=pl.ds(pl.multiple_of(i*step,step),step)
        h,_r=norm_parts(x_ref[rows,:])
        low_ref[rows,:]=(h*gain_ref[...]+shift_ref[...]).astype(jnp.bfloat16)
        return 0
    lax.fori_loop(0,R//step,norm,0)
    def spread_ids():
        ids_own.wait()
        for c in id_first: c.wait_recv()
        out=[]
        mine=pltpu.make_async_copy(idbuf,allids_ref.at[me],local.at[1]); mine.start(); out.append(mine)
        for k,_,dev in place.group_peers():
            c=remote(idbuf,allids_ref.at[me],i_send.at[S-1+k],i_recv.at[S-1+k],dev); c.start(); sent.append(c); out.append(c)
        return out
    late=[]
    def compute(w):
        def one(t,_):
            y=_dot(low_ref[...],wbuf[w,t].reshape(D,cols),1,0)
            if bias_refs[w] is not None: y=y+bias_refs[w][:,pl.ds(pl.multiple_of(t*cols,128),cols)]
            y=y.astype(jnp.bfloat16)
            for g in range(SG):
                for j in range(hpt):
                    obuf[w,g*HP+t*hpt+j]=y[g*spg*n:(g+1)*spg*n,j*PAIR:(j+1)*PAIR].reshape(spg,n,PAIR)
            return 0
        lax.fori_loop(0,T,one,0)
        mine=pltpu.make_async_copy(obuf.at[w,me,0],rows_refs[0].at[me,w],local.at[2+w]); mine.start(); late.append(mine)
        for k,other,dev in place.group_peers():
            c=remote(obuf.at[w,other,0],rows_refs[0].at[me,w],a_send.at[w,k],a_recv.at[w,k],dev)
            c.start(); sent.append(c); late.append(c)
        for i in range(1,spg):
            c=pltpu.make_async_copy(obuf.at[w,:,i],rows_refs[i].at[:,w],local.at[8+2*LINES+w*spg+i]); c.start(); late.append(c)
        keep=pltpu.make_async_copy(wbuf.at[w],wide_ref.at[w],local.at[5+w]); keep.start(); late.append(keep)
    arrive(2,0); start(2,1)
    arrive(1,0); start(1,1)
    ids_out=spread_ids()
    arrive(2,1); start(2,2)
    arrive(0,0); start(0,1)
    arrive(1,1); start(1,2)
    line_pass(1,0)
    arrive(2,2); start(2,3)
    for j in range(1,LINES): line_pass(1,j)
    arrive(2,3); compute(2)
    arrive(1,2); start(1,3)
    line_pass(2,0)
    arrive(0,1); start(0,2)
    arrive(1,3); compute(1)
    for j in range(1,LINES): line_pass(2,j)
    for h in range(3,T): line_pass(h,0)
    ids_out=ids_out+plane(0)
    arrive(0,2); start(0,3)
    for j in range(1,LINES):
        for h in range(3,T): line_pass(h,j)
        ids_out=ids_out+plane(j)
    arrive(0,3); compute(0)
    for c in late+ids_out:
        if any(c is o for o in sent): c.wait_recv()
        else: c.wait()
    for c in sent: c.wait_send()
    line_end()

def project(S,C,T,x,gain,shift,wq,wk,wv,qs,vs,ids,wo,wu,wd,ns,n):
    R,D=x.shape
    G=C*T; HP=D//PAIR; spg=ns*HP//G
    DR,cols=wq.shape
    CC=2 if C%2==0 else 1
    piece=(3,T,S,C//CC,CC,DR,cols)
    HA=upper_rows(DR); width=wo.shape[0]+2*wu.shape[1]; most=max(S,C//CC)-1
    _,total=slots({"t":T,"s":S,"x":C//CC,"c":CC},"tsxc")
    vm=pl.BlockSpec(memory_space=pltpu.VMEM); anyspec=pl.BlockSpec(memory_space=pl.ANY)
    dma=pltpu.SemaphoreType.DMA
    return pl.pallas_call(functools.partial(project_kernel,S,C,T),
        in_specs=[pl.BlockSpec(memory_space=pltpu.HBM)]*12,
        out_specs=[vm]+[anyspec]*(4+spg),
        out_shape=[jax.ShapeDtypeStruct((R,D),jnp.bfloat16),jax.ShapeDtypeStruct(piece,jnp.bfloat16),jax.ShapeDtypeStruct((G,S,1,ns*n),jnp.int32),
                   jax.ShapeDtypeStruct((C//CC,T,HA,width),jnp.bfloat16),jax.ShapeDtypeStruct((S,T,DR-HA,width),jnp.bfloat16)]+
                  [jax.ShapeDtypeStruct((G,3,n,PAIR),jnp.bfloat16)]*spg,
        scratch_shapes=[pltpu.VMEM((T,DR,width),jnp.bfloat16),dma((2,T-1,LINES)),dma((2,T-1,LINES)),dma((2,most,LINES)),dma((2,most,LINES)),pltpu.VMEM(piece,jnp.bfloat16),pltpu.VMEM((3,G,spg,n,PAIR),jnp.bfloat16),pltpu.VMEM((S,1,ns*n),jnp.int32),
                        dma((3,total)),dma((3,total)),dma((3,G-1)),dma((3,G-1)),dma((S-1+G-1,)),dma((S-1+G-1,)),dma((8+2*LINES+3*spg,)),
                        [pltpu.VMEM(a.shape,a.dtype) for a in (wq,wk,wv,wo,wu,wd,ids,x,gain,shift,qs,vs)],dma((12,))],
        compiler_params=pltpu.CompilerParams(collective_id=0,has_side_effects=True,vmem_limit_bytes=63<<20),
        name="project")(x,gain,shift,wq,wk,wv,qs,vs,ids,wo,wu,wd)


def feed_kernel(S,C,T,NC,NO,*refs):
    place=Place(S,C,T)
    CX=place.size["x"]; CC=place.CC
    spg=NO
    o_refs=refs[:spg]; o_ref=o_refs[-1]; refs=refs[spg-1:]
    wa_refs=refs[1:1+S]; wb_refs=refs[1+S:1+S+CX]
    (x_ref,teach_ref,ids_ref,mask_ref),vec_refs,wide_refs=refs[1+S+CX:5+S+CX],refs[5+S+CX:11+S+CX],refs[11+S+CX:14+S+CX]
    refs=refs[7:]
    (mid_ref,res_ref,mg_ref,inner_ref,second_ref,out_ref,midl_ref,hid_ref,unl_ref,sum_ref)=refs[7+S+CX:17+S+CX]
    g_refs=refs[17+S+CX:17+S+CX+spg]; refs=refs[1:]; refs=refs[spg-1:]
    (w2,rbuf,mix,inner,second,outl,midl,hid,unl,act,dact,tt,acc,middle,og,s1,s2,res,mg,gout,vacc,wacc,
     w_local,w_send,w_recv,a_send,a_recv,g_send,g_recv,misc,o_sem,s1b,s2b,buffers,load)=refs[17+S+CX:]
    loads=fetch((x_ref,teach_ref,ids_ref,mask_ref)+tuple(vec_refs)+tuple(wide_refs),buffers,load)
    x_ref,teach_ref,ids_ref,mask_ref=buffers[:4]
    vec_refs,wide_refs=buffers[4:10],buffers[10:]
    R,D=x_ref.shape
    G,n=o_ref.shape[:2]
    HP=D//PAIR; SG=G//HP
    HA=upper_rows(w2.shape[-2])
    F=hid.shape[1]; cf=F//T; c2=D//T
    B=R//spg; sub=n
    f32=jnp.float32; b16=jnp.bfloat16
    me=place.group
    s0,x0,c0=place.at["s"],place.at["x"],place.at["c"]
    DS=D//S
    ranges=((0,c2),(c2,c2+cf),(c2+cf,c2+2*cf))
    def pieces(r):
        lo,hi=ranges[r]
        out=[]
        for d in range(S):
            src=lax.rem(s0+S-d,S)
            for i in range(CX):
                out.append((wa_refs[d].at[i,:,:,lo:hi],w2.at[:,src,i,c0,0:HA,lo:hi]))
        for d in range(CX):
            src=lax.rem(x0+CX-d,CX)
            for i in range(S):
                out.append((wb_refs[d].at[i,:,:,lo:hi],w2.at[:,i,src,c0,HA:,lo:hi]))
        return out
    local=[[pltpu.make_async_copy(a,b,w_local.at[r,i]) for i,(a,b) in enumerate(pieces(r))] for r in range(3)]
    for r in range(3):
        for c in local[r]: c.start()
    barrier=pltpu.get_barrier_semaphore()
    count=0
    for _,_,dev in place.group_peers():
        pl.semaphore_signal(barrier,inc=1,device_id=dev,device_id_type=MESH_ID); count+=1
    pl.semaphore_wait(barrier,count)
    own=[pltpu.make_async_copy(o_ref.at[me],rbuf.at[me,spg-1],misc.at[0])]
    own+=[pltpu.make_async_copy(o_refs[i],rbuf.at[:,i],misc.at[1+i]) for i in range(spg-1)]
    for c in own: c.start()
    rows_in=[remote(o_ref.at[other],rbuf.at[me,spg-1],a_send.at[k],a_recv.at[k],dev) for k,other,dev in place.group_peers()]
    for c in rows_in: c.start()
    far=[[remote(a,b,w_send.at[r,k,i],w_recv.at[r,k,i],dev) for k,_,dev in place.peers("c") for i,(a,b) in enumerate(pieces(r))] for r in range(3)]
    for r in range(3):
        for c in far[r]: c.start()
    def weights(r):
        for c in local[r]: c.wait()
        for c in far[r]: c.wait_recv()
    vacc[...]=jnp.zeros_like(vacc); wacc[...]=jnp.zeros_like(wacc)
    def vec(i): return vec_refs[i][...]
    def wide(i,t,lo,size): return wide_refs[i][:,pl.ds(pl.multiple_of(t*cf+lo,128),size)]
    MIXG,MIXS,OUTS,SECG,SECS,DOWNS=range(6)
    def each(fn):
        def body(i,_):
            fn(pl.ds(pl.multiple_of(i*sub,sub),sub),i)
            return 0
        lax.fori_loop(0,B//sub,body,0)
    def fold(a):
        return jnp.sum(a.reshape(a.shape[0]//8,8,a.shape[1]),axis=0)
    def lanes(a):
        v=a[:,:PAIR]
        for j in range(1,a.shape[1]//PAIR): v=v+a[:,j*PAIR:(j+1)*PAIR]
        return v
    def flat(t,lo,hi,s=None):
        if s is None: return w2[t,:,:,:,:,lo:hi].reshape(D,hi-lo)
        return w2[t,s,:,:,:,lo:hi].reshape(DS,hi-lo)
    for c in loads: c.wait()
    count=jnp.sum((ids_ref[...]!=2048//60+1).astype(f32))
    scale=R*S*C*T/jnp.full((1,1),count)
    sum_ref[...]=jnp.zeros_like(sum_ref)
    sum_ref[sum_ref.shape[0]-1:,:]=jnp.full((1,D),count)
    weights(0)
    def block(b):
        r0=b*B
        def rows(i): return pl.ds(pl.multiple_of(r0+i*sub,sub),sub)
        def tokens(i): return pl.ds(pl.multiple_of(i//(n//sub)*(spg*n)+b*n+lax.rem(i,n//sub)*sub,sub),sub)
        whole=pl.ds(r0,B)
        if b<spg-1: own[1+b].wait()
        else:
            own[0].wait()
            for c in rows_in: c.wait_recv()
        for gg in range(SG):
            for h in range(HP):
                mix[gg*n:(gg+1)*n,h*PAIR:(h+1)*PAIR]=rbuf[gg*HP+h,b]
        def f1(q,i):
            h,_=norm_parts(mix[q,:].astype(f32))
            inner[rows(i),:]=(h*vec(MIXG)+vec(MIXS)).astype(b16)
        each(f1)
        acc[...]=jnp.zeros_like(acc)
        def att(t,_):
            a=inner[whole,pl.ds(pl.multiple_of(t*c2,128),c2)]
            for s in range(S):
                acc[:,s*DS:(s+1)*DS]+=_dot(a,flat(t,0,c2,s),1,1)
            return 0
        lax.fori_loop(0,T,att,0)
        def f2(q,i):
            m=x_ref[tokens(i),:]+(acc[q,:]+vec(OUTS))
            middle[q,:]=m
            x_ref[tokens(i),:]=m
            h,_=norm_parts(m)
            second[rows(i),:]=(h*vec(SECG)+vec(SECS)).astype(b16)
        each(f2)
        if b==0: weights(1)
        s1[...]=jnp.zeros_like(s1); s2[...]=jnp.zeros_like(s2)
        def up(t,_):
            a=second[whole,:]
            w=cf//NC
            for j in range(NC):
                lane=slice(j*w,(j+1)*w)
                u=_dot(a,flat(t,c2+j*w,c2+(j+1)*w),1,0)+wide(0,t,j*w,w)
                u2=u*u
                th=jnp.tanh(0.7978845608028654*u*(1.0+0.044715*u2))
                half=0.5+0.5*th
                v=u*half
                act[t,:,lane]=v
                dact[t,:,lane]=half+(0.5*0.7978845608028654)*u*(1.0-th*th)*(1.0+(3*0.044715)*u2)
                s1[...]+=lanes(v); s2[...]+=lanes(v*v)
            return 0
        lax.fori_loop(0,T,up,0)
        def f3(q,i):
            m=jnp.sum(s1[q,:],axis=1,keepdims=True)/F
            v=jnp.sum(s2[q,:],axis=1,keepdims=True)/F-m*m
            s1[q,:]=jnp.broadcast_to(m,(sub,PAIR)); s2[q,:]=jnp.broadcast_to(lax.rsqrt(v+EPS),(sub,PAIR))
        each(f3)
        if b==0: weights(2)
        acc[...]=jnp.zeros_like(acc)
        def down(t,_):
            fcols=pl.ds(pl.multiple_of(t*cf,128),cf)
            def e(q,i):
                h=(act[t,q,:]-s1[q,0:1])*s2[q,0:1]
                act[t,q,:]=h
                hid[rows(i),fcols]=(h*wide(1,t,0,cf)+wide(2,t,0,cf)).astype(b16)
            each(e)
            a=hid[whole,fcols]
            for s in range(S):
                acc[:,s*DS:(s+1)*DS]+=_dot(a,flat(t,c2+cf,c2+2*cf,s),1,1)
            return 0
        lax.fori_loop(0,T,down,0)
        def f4(q,i):
            branch=acc[q,:]+vec(DOWNS)
            res[tokens(i),:]=branch
            err=middle[q,:]+branch-teach_ref[tokens(i),:]
            k=jnp.broadcast_to(mask_ref[pl.ds(i*spg+b,1),:].astype(f32),(sub,sub)).T[:,0:1]
            e=k*err
            vacc[6]+=fold(e*err)
            g=e*scale
            og[q,:]=g
            low_=g.astype(b16)
            outl[rows(i),:]=low_
            vacc[5]+=fold(low_.astype(f32))
        each(f4)
        def back1(t,_):
            a=outl[whole,:]
            w=cf//NC
            for j in range(NC):
                lane=slice(j*w,(j+1)*w)
                g=_dot(a,flat(t,c2+cf+j*w,c2+cf+(j+1)*w),1,0)
                h=act[t,:,lane]
                wacc[0,t,:,lane]+=fold(g*h); wacc[1,t,:,lane]+=fold(g)
                v=g*wide(1,t,j*w,w)
                tt[t,:,lane]=v
                s1b[...]+=lanes(v); s2b[...]+=lanes(v*h)
            return 0
        s1b[...]=jnp.zeros_like(s1b); s2b[...]=jnp.zeros_like(s2b)
        lax.fori_loop(0,T,back1,0)
        def f5(q,i):
            s1b[q,:]=jnp.broadcast_to(jnp.sum(s1b[q,:],axis=1,keepdims=True)/F,(sub,PAIR))
            s2b[q,:]=jnp.broadcast_to(jnp.sum(s2b[q,:],axis=1,keepdims=True)/F,(sub,PAIR))
        each(f5)
        acc[...]=jnp.zeros_like(acc)
        def back2(t,_):
            fcols=pl.ds(pl.multiple_of(t*cf,128),cf)
            def e(q,i):
                ag=s2[q,0:1]*(tt[t,q,:]-s1b[q,0:1]-act[t,q,:]*s2b[q,0:1])
                ul=(ag*dact[t,q,:]).astype(b16)
                unl[rows(i),fcols]=ul
                wacc[2,t]+=fold(ul.astype(f32))
            each(e)
            a=unl[whole,fcols]
            for s in range(S):
                acc[:,s*DS:(s+1)*DS]+=_dot(a,flat(t,c2,c2+cf,s),1,1)
            return 0
        lax.fori_loop(0,T,back2,0)
        def f6(q,i):
            h,r=norm_parts(middle[q,:])
            e=acc[q,:]
            vacc[3]+=fold(e*h); vacc[4]+=fold(e)
            m=og[q,:]+norm_back(e,h,r,vec(SECG))
            mg[tokens(i),:]=m
            ml=m.astype(b16)
            midl[rows(i),:]=ml
            vacc[2]+=fold(ml.astype(f32))
        each(f6)
        def back3(t,_):
            acc[:,pl.ds(pl.multiple_of(t*c2,128),c2)]=_dot(midl[whole,:],flat(t,0,c2),1,0)
            return 0
        lax.fori_loop(0,T,back3,0)
        def f7(q,i):
            h,r=norm_parts(mix[q,:].astype(f32))
            e=acc[q,:]
            vacc[0]+=fold(e*h); vacc[1]+=fold(e)
            mix[q,:]=norm_back(e,h,r,vec(MIXG)).astype(b16)
        each(f7)
        for gg in range(SG):
            for h in range(HP):
                gout[b,gg*HP+h]=mix[gg*n:(gg+1)*n,h*PAIR:(h+1)*PAIR]
        copies=[pltpu.make_async_copy(src.at[whole],dst.at[whole],o_sem.at[b,i]) for i,(src,dst) in enumerate(
            ((inner,inner_ref),(second,second_ref),(outl,out_ref),(midl,midl_ref),(hid,hid_ref),(unl,unl_ref)))]
        for gg in range(SG):
            part=pl.ds(gg*spg*n+b*n,n)
            copies+=[pltpu.make_async_copy(src.at[part],dst.at[part],o_sem.at[b,6+3*gg+i]) for i,(src,dst) in enumerate(((x_ref,mid_ref),(res,res_ref),(mg,mg_ref)))]
        if b<spg-1:
            copies.append(pltpu.make_async_copy(gout.at[b,me],g_refs[b].at[me],o_sem.at[b,6+3*SG]))
            far_g=[remote(gout.at[b,other],g_refs[b].at[me],g_send.at[b,k],g_recv.at[b,k],dev) for k,other,dev in place.group_peers()]
            for c in far_g: c.start()
            g_out.extend(far_g)
        else:
            copies.append(pltpu.make_async_copy(gout.at[b],g_refs[b],o_sem.at[b,6+3*SG]))
        for c in copies: c.start()
        return copies
    g_out=[]
    done=[]
    for b in range(spg): done+=block(b)
    for i in range(7):
        sum_ref[i:i+1,:]=jnp.sum(vacc[i],axis=0,keepdims=True)
    for i in range(3):
        for t in range(T):
            at=(i*F+t*cf)
            sum_ref[7+at//D:8+at//D,at%D:at%D+cf]=jnp.sum(wacc[i,t],axis=0,keepdims=True)
    for c in done: c.wait()
    for c in g_out: c.wait()
    for c in rows_in: c.wait_send()
    for r in range(3):
        for c in far[r]: c.wait_send()

def feed(S,C,T,o,wa,wb,x,teacher,ids,mask,vecs,wides):
    plain=(x,teacher,ids,mask)+tuple(vecs)+tuple(wides)
    R,D=x.shape
    spg=len(o)
    G,n=o[0].shape[:2]
    rows=(G,spg,n,PAIR)
    CC=2 if C%2==0 else 1
    CX=C//CC
    DR,c2=wa[0].shape[-2]+wb[0].shape[-2],wa[0].shape[-1]
    F=wides[0].shape[-1]; cf=F//T; B=R//spg; SG=G//(D//PAIR)
    b16,f32=jnp.bfloat16,jnp.float32
    vm=pl.BlockSpec(memory_space=pltpu.VMEM); anyspec=pl.BlockSpec(memory_space=pl.ANY)
    dma=pltpu.SemaphoreType.DMA
    V=lambda shape,dt=b16: pltpu.VMEM(shape,dt)
    NP=2*S*CX; NCC=max(CC-1,1)
    sums=8+3*F//D; sums+=-sums%8
    sds=jax.ShapeDtypeStruct
    return pl.pallas_call(functools.partial(feed_kernel,S,C,T,max(cf//512,1),spg),
        in_specs=[pl.BlockSpec(memory_space=pltpu.HBM)]*(spg+S+CX+len(plain)),
        out_specs=[anyspec]*9+[vm]+[anyspec]*spg,
        out_shape=[sds((R,D),f32)]*3+[sds((R,D),b16)]*4+[sds((R,F),b16)]*2+[sds((sums,D),f32)]+[sds((G,n,PAIR),b16)]*spg,
        scratch_shapes=[V((T,S,CX,CC,DR,c2)),V(rows),V((B,D)),V((R,D)),V((R,D)),V((R,D)),V((R,D)),V((R,F)),V((R,F)),
                        V((T,B,cf),f32),V((T,B,cf),f32),V((T,B,cf),f32),V((B,D),f32),V((B,D),f32),V((B,D),f32),V((B,PAIR),f32),V((B,PAIR),f32),
                        V((R,D),f32),V((R,D),f32),V((spg,G,n,PAIR)),V((7,8,D),f32),V((3,T,8,cf),f32),
                        dma((3,NP)),dma((3,NCC,NP)),dma((3,NCC,NP)),dma((G-1,)),dma((G-1,)),dma((spg,G-1)),dma((spg,G-1)),dma((spg,)),dma((spg,7+3*SG)),V((B,PAIR),f32),V((B,PAIR),f32),
                        [V(a.shape,a.dtype) for a in plain],dma((len(plain),))],
        compiler_params=pltpu.CompilerParams(collective_id=3,has_side_effects=True,vmem_limit_bytes=63<<20),
        name="feed")(*o,*wa,*wb,*plain)


def weight_grads_kernel(S,C,T,out_ref,second_ref,middle_ref,inner_ref,unit_ref,hidden_ref,g_ref,early_ref,*rest):
    CX0=C//(2 if C%2==0 else 1)
    NA=1+2*(S-1); NB=1+2*(CX0-1); TH=T//2
    pa_refs,pb_refs=rest[:NA],rest[NA:NA+NB]
    gin_ref,sum_ref,own,got,send,recv,local,a_send,a_recv,a_local,ev,ev_recs,v_send,v_recv,buffers,load=rest[NA+NB:]
    loads=fetch((early_ref,middle_ref,inner_ref,second_ref,unit_ref,out_ref,hidden_ref),(ev,)+tuple(buffers),load)
    middle_ref,inner_ref,second_ref,unit_ref,out_ref,hidden_ref=buffers
    place=Place(S,C,T)
    R,D=out_ref.shape
    CX=place.size["x"]; CC=place.CC
    HR,width=own.shape[-2:]
    c2=inner_ref.shape[1]//T; cf=unit_ref.shape[1]//T
    cc=place.at["c"]
    barrier=pltpu.get_barrier_semaphore()
    others=list(place.peers("c"))
    count=0
    for _,_,dev in place.group_peers():
        pl.semaphore_signal(barrier,inc=1,device_id=dev,device_id_type=MESH_ID); count+=1
    for _,_,dev in place.peers("s"):
        pl.semaphore_signal(barrier,inc=1,device_id=dev,device_id_type=MESH_ID); count+=1
    pl.semaphore_wait(barrier,count)
    me=place.group
    mine=pltpu.make_async_copy(g_ref.at[me],gin_ref.at[me],a_local.at[0]); mine.start()
    rows_in=[remote(g_ref.at[other],gin_ref.at[me],a_send.at[k],a_recv.at[k],dev) for k,other,dev in place.group_peers()]
    for c in rows_in: c.start()
    loads[0].wait()
    early=VectorSum(place,ev,ev_recs,v_send,v_recv)
    early.start("c")
    for c in loads[1:]: c.wait()
    plan=[(middle_ref,inner_ref,0,c2,c2),(second_ref,unit_ref,c2,cf,min(cf,512)),(out_ref,hidden_ref,c2+cf,cf,min(cf,512))]
    cut=[0,c2+cf,c2+2*cf]
    def swap(t,j):
        lane=slice(cut[j],cut[j+1])
        return [remote(own.at[t,:,:,other,:,:,lane],got.at[t,k,:,:,:,:,lane],send.at[t,k,j],recv.at[t,k,j],dev) for k,other,dev in others]
    def outs(t,act):
        def go(src,ref,sem,cond=None):
            if cond is None: act(pltpu.make_async_copy(src,ref,sem))
            else:
                @pl.when(cond)
                def _(): act(pltpu.make_async_copy(src,ref,sem))
        for d in range(S):
            src=got.at[t,0,lax.rem(place.at["s"]+d,S),:,0]
            if d==0: go(src,pa_refs[0].at[t],local.at[t,0])
            else:
                go(src,pa_refs[2*d-1].at[lax.rem(t,TH)],local.at[t,d],t<TH)
                go(src,pa_refs[2*d].at[lax.rem(t,TH)],local.at[t,d],t>=TH)
        for d in range(CX):
            src=got.at[t,0,:,lax.rem(place.at["x"]+d,CX),1]
            if d==0: go(src,pb_refs[0].at[t],local.at[t,S])
            else:
                go(src,pb_refs[2*d-1].at[lax.rem(t,TH)],local.at[t,S+d],t<TH)
                go(src,pb_refs[2*d].at[lax.rem(t,TH)],local.at[t,S+d],t>=TH)
    def settle(t):
        for j in range(2):
            lane=slice(cut[j],cut[j+1])
            for c in swap(t,j): c.wait_recv()
            for s in range(S):
                for x in range(CX):
                    total=own[t,s,x,cc,:,:,lane].astype(jnp.float32)
                    for k,_,_ in others:
                        total=total+got[t,k,s,x,:,:,lane].astype(jnp.float32)
                    got[t,0,s,x,:,:,lane]=total.astype(jnp.bfloat16)
        outs(t,lambda c: c.start())
    def one(t,_):
        for i,(left,right,base,cols,chunk) in enumerate(plan):
            for j in range(cols//chunk):
                y=_dot(left[...],right[:,pl.ds(pl.multiple_of(t*cols+j*chunk,128),chunk)],0,0)
                own[t,:,:,:,:,:,base+j*chunk:base+(j+1)*chunk]=y.astype(jnp.bfloat16).reshape(S,CX,CC,2,HR,chunk)
            if i>0:
                for c in swap(t,i-1): c.start()
        @pl.when(t>0)
        def _(): settle(t-1)
        for i,(x,y) in enumerate(("cs","sx","xt")):
            if i+1<T:
                @pl.when(t==i+1)
                def _(): early.end(x); early.start(y)
        return 0
    lax.fori_loop(0,T,one,0)
    settle(T-1)
    for i,(x,y) in enumerate(("cs","sx","xt")):
        if i+1>=T: early.end(x); early.start(y)
    early.end("t")
    sum_ref[...]=ev[...]
    def finish(t,_):
        for j in range(2):
            for c in swap(t,j): c.wait_send()
        outs(t,lambda c: c.wait())
        return 0
    lax.fori_loop(0,T,finish,0)
    mine.wait()
    for c in rows_in: c.wait()

def weight_grads(S,C,T,out_low,second_low,middle_low,inner_low,unit_low,hidden_low,g,early):
    R,D=out_low.shape
    CC=2 if C%2==0 else 1
    CX=C//CC; HR=D//(S*C*2); width=(D+2*unit_low.shape[1])//T
    hbm=pl.BlockSpec(memory_space=pltpu.HBM); anyspec=pl.BlockSpec(memory_space=pl.ANY)
    dma=pltpu.SemaphoreType.DMA
    return pl.pallas_call(functools.partial(weight_grads_kernel,S,C,T),
        in_specs=[hbm]*8,out_specs=[anyspec]*(2*S+2*CX-1)+[pl.BlockSpec(memory_space=pltpu.VMEM)],
        out_shape=[jax.ShapeDtypeStruct((T,CX,HR,width),jnp.bfloat16)]+[jax.ShapeDtypeStruct((T//2,CX,HR,width),jnp.bfloat16)]*(2*S-2)+
                  [jax.ShapeDtypeStruct((T,S,HR,width),jnp.bfloat16)]+[jax.ShapeDtypeStruct((T//2,S,HR,width),jnp.bfloat16)]*(2*CX-2)+[jax.ShapeDtypeStruct(g.shape,jnp.bfloat16),jax.ShapeDtypeStruct(early.shape,jnp.float32)],
        scratch_shapes=[pltpu.VMEM((T,S,CX,CC,2,HR,width),jnp.bfloat16),pltpu.VMEM((T,max(CC-1,1),S,CX,2,HR,width),jnp.bfloat16),
                        dma((T,max(CC-1,1),2)),dma((T,max(CC-1,1),2)),dma((T,S+CX)),dma((C*T-1,)),dma((C*T-1,)),dma((1,))]+vector_scratch({"t":T,"s":S,"x":CX,"c":CC},early.shape[0],D)+
                       [[pltpu.VMEM(a.shape,a.dtype) for a in (middle_low,inner_low,second_low,unit_low,out_low,hidden_low)],dma((7,))],
        compiler_params=pltpu.CompilerParams(collective_id=1,has_side_effects=True,vmem_limit_bytes=63<<20),
        name="weight_grads")(out_low,second_low,middle_low,inner_low,unit_low,hidden_low,g,early)


CHUNKS=2

def finish_kernel(S,C,T,NO,*refs):
    d_refs=refs[:NO]
    finish_split(S,C,T,d_refs,*refs[NO:])

def finish_split(S,C,T,d_refs,low_ref,wide_ref,x_ref,mg_ref,gain_ref,*rest):
    CX0=C//(2 if C%2==0 else 1)
    NA=1+2*(S-1); NB=1+2*(CX0-1)
    ra_refs,rb_refs=rest[:NA],rest[NA:NA+NB]
    *rest,buffers,load=rest[NA+NB:]
    own=(low_ref,x_ref,mg_ref,gain_ref)
    finish_body(S,C,T,lambda: fetch(own,buffers,load),d_refs,buffers[0],wide_ref,*buffers[1:],ra_refs,rb_refs,*rest)

def finish_body(S,C,T,fetch_own,d_refs,low_ref,wide_ref,x_ref,mg_ref,gain_ref,ra_refs,rb_refs,
                  grad_ref,dq_ref,dk_ref,dv_ref,do_ref,du_ref,dd_ref,late_ref,
                  rbuf,wbuf,acc,gbuf,rc,ra2,rb2,ra3,rb3,gz,gzr,bz,bzr,z_send,z_recv,
                  xa,xb,ya,yb,za,zb,d2,
                  lv,lv_recs,v_send,v_recv,
                  a_send,a_recv,w_send,w_recv,g_send,g_recv,local):
    gz,gzr,bz,bzr=[list(r) for r in (gz,gzr,bz,bzr)]
    place=Place(S,C,T)
    R,D=low_ref.shape
    G,_,n=d_refs[0].shape[:3]
    spg=len(d_refs)
    HP=D//PAIR; SG=G//HP
    cols=wbuf.shape[-1]; hpt=cols//PAIR
    DR=wbuf.shape[-2]
    CX=place.size["x"]; CC=place.CC; TH=T//2
    t0,s0,x0,c0=place.at["t"],place.at["s"],place.at["x"],place.at["c"]
    me=place.group
    f32=jnp.float32; b16=jnp.bfloat16
    sent=[]
    def go(copies):
        for c in copies: c.start()
        sent.extend(copies)
        return copies
    def land(copies):
        for c in copies: c.wait_recv()
    steps=[1<<k for k in range(T.bit_length()-1)]
    def bit(k): return lax.rem(t0//steps[k],2)
    def trade(k,which,bufs,recs):
        other=t0+steps[k]-2*steps[k]*bit(k)
        return go([remote(bufs[k].at[:,1-bit(k)],recs[k],z_send.at[which,k],z_recv.at[which,k],{"tensor":other})])
    def settle(k,copies,bufs,recs):
        land(copies)
        v=bufs[k][:,bit(k)].astype(f32)+recs[k][...].astype(f32)
        if k+1<len(steps): bufs[k+1][...]=v.astype(b16).reshape(bufs[k+1].shape)
        return v
    gzs=[[r.at[w] for r in gz] for w in range(3)]; gzrs=[[r.at[w] for r in gzr] for w in range(3)]
    loads=[pltpu.make_async_copy(wide_ref,wbuf,local.at[3*spg])]
    def arrivals(refs,buf,base):
        out=[pltpu.make_async_copy(refs[0],buf.at[0],local.at[base])]
        for i,ref in enumerate(refs[1:]):
            out.append(pltpu.make_async_copy(ref,buf.at[1+i//2,i%2*TH:i%2*TH+TH],local.at[base+1+i]))
        return out
    loads+=arrivals(ra_refs,xa,3*spg+1)
    loads+=arrivals(rb_refs,xb,3*spg+1+len(ra_refs))
    for c in loads[1:]: c.start()
    greet(place)
    rows_in=[None]*3
    mine=[None]*3
    last=d_refs[-1]
    for w in (2,1,0):
        mine[w]=[pltpu.make_async_copy(last.at[me,w],rbuf.at[w,me,spg-1],local.at[w*spg])]
        mine[w]+=[pltpu.make_async_copy(d_refs[i].at[:,w],rbuf.at[w,:,i],local.at[w*spg+1+i]) for i in range(spg-1)]
        for c in mine[w]: c.start()
        rows_in[w]=go([remote(last.at[other,w],rbuf.at[w,me,spg-1],a_send.at[w,k],a_recv.at[w,k],dev) for k,other,dev in place.group_peers()])

    late=VectorSum(place,lv,lv_recs,v_send,v_recv)

    loads[0].start()
    own_loads=fetch_own()
    for c in loads[1:]: c.wait()
    c2=xa.shape[-1]
    cuts=[c2*h//(128*CHUNKS)*128 for h in range(CHUNKS)]+[c2]
    plane_a,plane_b=[],[]
    for h in range(CHUNKS):
        lane=slice(cuts[h],cuts[h+1])
        def add_a(t,_):
            v=xa[0,t,:,:,lane].astype(f32)
            for i in range(1,S): v=v+xa[i,t,:,:,lane].astype(f32)
            ya[t,:,:,lane]=v.astype(b16)
            return 0
        lax.fori_loop(0,T,add_a,0)
        plane_a.append(go([remote(ya.at[:,other,:,lane],za.at[k,:,:,lane],w_send.at[0,h,k],w_recv.at[0,h,k],dev) for k,other,dev in place.peers("x")]))
        def add_b(t,_):
            v=xb[0,t,:,:,lane].astype(f32)
            for i in range(1,CX): v=v+xb[i,t,:,:,lane].astype(f32)
            yb[t,:,:,lane]=v.astype(b16)
            return 0
        lax.fori_loop(0,T,add_b,0)
        plane_b.append(go([remote(yb.at[:,other,:,lane],zb.at[k,:,:,lane],w_send.at[1,h,k],w_recv.at[1,h,k],dev) for k,other,dev in place.peers("s")]))
    loads[0].wait()
    for c in own_loads: c.wait()

    lv[...]=jnp.zeros_like(lv)
    def compute(w,first):
        for c in mine[w]: c.wait()
        land(rows_in[w])
        def one(t,_):
            d=jnp.concatenate([jnp.concatenate([rbuf[w,g*HP+t*hpt+j].reshape(spg*n,PAIR) for j in range(hpt)],axis=1) for g in range(SG)],axis=0)
            y=_dot(low_ref[...],d,0,0)
            gbuf[w,t]=y.astype(b16).reshape(S,CX,CC,DR,cols)
            z=_dot(d,wbuf[w,t].reshape(D,cols),1,1)
            if first:
                @pl.when(t==0)
                def _(): acc[...]=z
                @pl.when(t>0)
                def _(): acc[...]+=z
            else:
                acc[...]+=z
            if w!=1:
                lv[2+w//2:3+w//2,pl.ds(pl.multiple_of(t*cols,128),cols)]=jnp.sum(d.astype(f32),axis=0,keepdims=True)
            return 0
        lax.fori_loop(0,T,one,0)
        return go([remote(gbuf.at[w,:,:,:,other],rc.at[w,k],g_send.at[w,0,k],g_recv.at[w,0,k],dev) for k,other,dev in place.peers("c")])
    def after_core(w,copies):
        land(copies)
        for t in range(T):
            v=gbuf[w,t,:,:,c0].astype(f32)
            for k in range(CC-1): v=v+rc[w,k,t].astype(f32)
            rc[w,0,t]=v.astype(b16)
        a=go([remote(rc.at[w,0,0:TH,other],ra2.at[w,k],g_send.at[w,1,k],g_recv.at[w,1,k],dev) for k,other,dev in place.peers("s")])
        b=go([remote(rc.at[w,0,TH:T,:,other],rb2.at[w,k],g_send.at[w,2,k],g_recv.at[w,2,k],dev) for k,other,dev in place.peers("x")])
        return a,b
    def after_second(w,pair):
        land(pair[0])
        v=rc[w,0,0:TH,s0].astype(f32)
        for k in range(S-1): v=v+ra2[w,k].astype(f32)
        ra2[w,0]=v.astype(b16)
        a=go([remote(ra2.at[w,0,:,other],ra3.at[w,k],g_send.at[w,3,k],g_recv.at[w,3,k],dev) for k,other,dev in place.peers("x")])
        land(pair[1])
        v=rc[w,0,TH:T,:,x0].astype(f32)
        for k in range(CX-1): v=v+rb2[w,k].astype(f32)
        rb2[w,0]=v.astype(b16)
        b=go([remote(rb2.at[w,0,:,other],rb3.at[w,k],g_send.at[w,4,k],g_recv.at[w,4,k],dev) for k,other,dev in place.peers("s")])
        return a,b
    def after_third(w,pair):
        land(pair[0])
        v=ra2[w,0,:,x0].astype(f32)
        for k in range(CX-1): v=v+ra3[w,k].astype(f32)
        gz[0][w,0:T//4]=v.astype(b16).reshape(T//4,2,DR,cols)
        land(pair[1])
        v=rb2[w,0,:,s0].astype(f32)
        for k in range(S-1): v=v+rb3[w,k].astype(f32)
        gz[0][w,T//4:T//2]=v.astype(b16).reshape(T//4,2,DR,cols)
        return trade(0,w,gzs[w],gzrs[w])
    def onward(k,w,copies):
        settle(k-1,copies,gzs[w],gzrs[w])
        return trade(k,w,gzs[w],gzrs[w])
    def big_trade(k,h):
        lane=slice(cuts[h],cuts[h+1])
        other=t0+steps[k]-2*steps[k]*bit(k)
        return go([remote(bz[k].at[i,:,1-bit(k),:,lane],bzr[k].at[i,:,:,lane],z_send.at[3+2*h+i,k],z_recv.at[3+2*h+i,k],{"tensor":other}) for i in range(2)])
    def big_settle(k,h,copies):
        lane=slice(cuts[h],cuts[h+1])
        land(copies)
        for i in range(2):
            v=bz[k][i,:,bit(k),:,lane].astype(f32)+bzr[k][i,:,:,lane].astype(f32)
            if k+1<len(steps): bz[k+1][i,:,:,:,lane]=v.astype(b16).reshape(bz[k+1].shape[1:4]+(v.shape[-1],))
            else: d2[i*v.shape[1]:(i+1)*v.shape[1],lane]=v[0]
    def big_onward(k,h,copies):
        big_settle(k-1,h,copies)
        return big_trade(k,h)
    def big_first(h):
        lane=slice(cuts[h],cuts[h+1])
        land(plane_a[h])
        def add_a2(j,_):
            v=ya[pl.ds(2*j,2),x0,:,lane].astype(f32)
            for k in range(CX-1): v=v+za[k,pl.ds(2*j,2),:,lane].astype(f32)
            bz[0][0,j,:,:,lane]=v.astype(b16)
            return 0
        lax.fori_loop(0,T//2,add_a2,0)
        land(plane_b[h])
        def add_b2(j,_):
            v=yb[pl.ds(2*j,2),s0,:,lane].astype(f32)
            for k in range(S-1): v=v+zb[k,pl.ds(2*j,2),:,lane].astype(f32)
            bz[0][1,j,:,:,lane]=v.astype(b16)
            return 0
        lax.fori_loop(0,T//2,add_b2,0)
        return big_trade(0,h)
    end=len(steps)
    big=[None]*CHUNKS
    core_v=compute(2,True)
    big[0]=big_first(0)
    two_v=after_core(2,core_v)
    for h in range(1,CHUNKS): big[h]=big_first(h)
    core_k=compute(1,False)
    three_v=after_second(2,two_v)
    big[0]=big_onward(1,0,big[0])
    two_k=after_core(1,core_k)
    core_q=compute(0,False)
    z_v=after_third(2,three_v)
    three_k=after_second(1,two_k)
    two_q=after_core(0,core_q)
    big[1]=big_onward(1,1,big[1])
    step=min(64,R)
    def back(i,carry):
        rows=pl.ds(pl.multiple_of(i*step,step),step)
        h,r=norm_parts(x_ref[rows,:])
        e=acc[rows,:]
        grad_ref[rows,:]=mg_ref[rows,:]+norm_back(e,h,r,gain_ref[...])
        return carry[0]+jnp.sum(e*h,axis=0,keepdims=True),carry[1]+jnp.sum(e,axis=0,keepdims=True)
    zero=jnp.zeros((1,D),f32)
    ga,sa=lax.fori_loop(0,R//step,back,(zero,zero))
    lv[0:1,:]=ga; lv[1:2,:]=sa
    late.start("c")
    three_q=after_second(0,two_q)
    z_k=after_third(1,three_k)
    z_v=onward(1,2,z_v)
    late.end("c"); late.start("s")
    z_q=after_third(0,three_q)
    for h in range(2,CHUNKS): big[h]=big_onward(1,h,big[h])
    z_k=onward(1,1,z_k)
    late.end("s"); late.start("x")
    z_q=onward(1,0,z_q)
    late.end("x"); late.start("t")
    for k in range(2,end):
        for h in range(CHUNKS): big[h]=big_onward(k,h,big[h])
        z_v=onward(k,2,z_v); z_k=onward(k,1,z_k); z_q=onward(k,0,z_q)
    dv_ref[...]=settle(end-1,z_v,gzs[2],gzrs[2])[0]
    big_settle(end-1,0,big[0])
    dk_ref[...]=settle(end-1,z_k,gzs[1],gzrs[1])[0]
    dq_ref[...]=settle(end-1,z_q,gzs[0],gzrs[0])[0]
    for h in range(1,CHUNKS): big_settle(end-1,h,big[h])
    co=do_ref.shape[0]; cf=du_ref.shape[1]
    do_ref[...]=d2[:,:co].T
    du_ref[...]=d2[:,co:co+cf]
    dd_ref[...]=d2[:,co+cf:].T
    late.end("t"); late_ref[...]=lv[...]
    for c in sent: c.wait_send()

def finish(S,C,T,ds,first_low,wide,ra,rb,x,middle_grad,gain):
    R,D=x.shape
    G,_,n=ds[0].shape[:3]
    spg=len(ds)
    CC=2 if C%2==0 else 1
    CX=C//CC; TH=T//2
    DR,cols=wide.shape[-2:]
    HR,c2=ra[0].shape[-2:]
    b16,f32=jnp.bfloat16,jnp.float32
    vm=pl.BlockSpec(memory_space=pltpu.VMEM)
    dma=pltpu.SemaphoreType.DMA
    size={"t":T,"s":S,"x":CX,"c":CC}
    most=max(T,S,CX,CC)-1
    NL=8; co=D//T; cf=(c2-co)//2
    V=lambda shape,dt=b16: pltpu.VMEM(shape,dt)
    halves=[T>>(k+1) for k in range(T.bit_length()-1)]
    scratch=[V((3,G,spg,n,PAIR)),V(wide.shape),V((R,D),f32),V((3,T,S,CX,CC,DR,cols)),V((3,max(CC-1,1),T,S,CX,DR,cols)),
             V((3,max(S-1,1),TH,CX,DR,cols)),V((3,max(CX-1,1),TH,S,DR,cols)),V((3,max(CX-1,1),TH,DR,cols)),V((3,max(S-1,1),TH,DR,cols)),
             [V((3,h,2,DR,cols)) for h in halves],[V((3,h,DR,cols)) for h in halves],
             [V((2,h,2,HR,c2)) for h in halves],[V((2,h,HR,c2)) for h in halves],
             dma((3+2*CHUNKS,len(halves))),dma((3+2*CHUNKS,len(halves))),
             V((S,)+ra[0].shape),V((CX,)+rb[0].shape),V((T,CX,HR,c2)),V((T,S,HR,c2)),V((max(CX-1,1),T,HR,c2)),V((max(S-1,1),T,HR,c2)),
             V((2*HR,c2),f32)]+vector_scratch(size,NL,D)+[
             dma((3,G-1)),dma((3,G-1)),dma((2,CHUNKS,most)),dma((2,CHUNKS,most)),dma((3,6,most)),dma((3,6,most)),dma((3*spg+1+len(ra)+len(rb),)),
             [V((R,D)),V((R,D),f32),V((R,D),f32),V((1,D),f32)],dma((4,))]
    hbm=pl.BlockSpec(memory_space=pltpu.HBM)
    sds=jax.ShapeDtypeStruct
    return pl.pallas_call(functools.partial(finish_kernel,S,C,T,spg),
        in_specs=[hbm]*(spg+5+len(ra)+len(rb)),
        out_specs=[vm]*8,
        out_shape=[sds((R,D),f32)]+[sds((DR,cols),f32)]*3+[sds((co,2*HR),f32),sds((2*HR,cf),f32),sds((cf,2*HR),f32),sds((NL,D),f32)],
        scratch_shapes=scratch,
        compiler_params=pltpu.CompilerParams(collective_id=2,has_side_effects=True,vmem_limit_bytes=63<<20),
        name="finish")(*ds,first_low,wide,x,middle_grad,gain,*ra,*rb)


def shards(inputs,teacher,segments,pad_mask,query_weight,key_weight,value_weight,output_weight,up_weight,down_weight,
           first_gain,first_shift,query_shift,value_shift,mixed_gain,mixed_shift,output_shift,second_gain,second_shift,
           up_shift,hidden_gain,hidden_shift,down_shift):
    S,C,T=lax.axis_size("shard"),lax.axis_size("context"),lax.axis_size("tensor")
    CC=2 if C%2==0 else 1
    CX=C//CC
    G=C*T
    ns,n,D=inputs.shape
    R=ns*n
    HP=D//PAIR
    SG=G//HP
    spg=ns//SG
    me_s=lax.axis_index("shard")
    me_g=lax.axis_index("context")*T+lax.axis_index("tensor")
    c1=query_weight.shape[1]; c2=output_weight.shape[0]; cf=up_weight.shape[1]
    F=cf*T
    x=inputs.reshape(R,D)
    first_low,wide,ids_all,pa,pb,*rows_out=project(S,C,T,x,first_gain[None],first_shift[None],query_weight,key_weight,value_weight,query_shift[None],value_shift[None],
                                             segments.reshape(1,R),output_weight,up_weight,down_weight,ns,n)
    def over_shard(a,d):
        return lax.ppermute(a,"shard",[(i,(i+d)%S) for i in range(S)]) if d else a
    def over_x(a,d):
        return lax.ppermute(a,"context",[(i*CC+j,((i+d)%CX)*CC+j) for i in range(CX) for j in range(CC)]) if d else a
    wa=[over_shard(pa,d) for d in range(S)]
    wb=[over_x(pb,d) for d in range(CX)]
    ids_flat=ids_all
    ids_all=ids_all.reshape(G,S,ns,n)
    ids_mine=lax.dynamic_index_in_dim(ids_all,me_s,1,keepdims=False)
    ids_mine=lax.dynamic_slice_in_dim(ids_mine,(me_g//HP)*spg,spg,1).transpose(1,0,2).reshape(spg,G*n)
    edges=[bounds(ids_mine[i],BLOCK,BLOCK) for i in range(spg)]
    cols=[ids_mine[i][:,None] for i in range(spg)]
    def trade(a):
        return lax.all_to_all(a,("context","tensor"),0,0,tiled=True)
    qkv=[rows_out[0]]+[trade(a) for a in rows_out[1:]]
    mixed=[attend_fwd(qkv[i],ids_mine[i],cols[i],edges[i]) for i in range(spg)]
    arrived=[trade(mixed[i][0]) for i in range(spg-1)]+[mixed[-1][0]]
    vecs=[a[None] for a in (mixed_gain,mixed_shift,output_shift,second_gain,second_shift,down_shift)]
    wides=[a[None] for a in (up_shift,hidden_gain,hidden_shift)]
    middle,branch,middle_grad,inner_low,second_low,out_low,middle_low,hidden_low,unit_low,early,*gs=feed(
        S,C,T,arrived,wa,wb,x,teacher.reshape(R,D),ids_flat,pad_mask,vecs,wides)
    *outs,last_g,early=weight_grads(S,C,T,out_low,second_low,middle_low,inner_low,unit_low,hidden_low,gs[-1],early)
    gs=list(lax.optimization_barrier(tuple(gs[:-1])+(last_g,)))
    NA=1+2*(S-1)
    hops=[over_shard(outs[1+i],1+i//2) for i in range(2*(S-1))],[over_x(outs[NA+1+i],1+i//2) for i in range(2*(CX-1))]
    ds=[attend_bwd(qkv[i],gs[i],mixed[i][0],mixed[i][1],ids_mine[i],cols[i],edges[i]) for i in range(spg)]
    if spg>1:
        ds[0],(first_a,first_b)=lax.optimization_barrier((ds[0],(hops[0][0::2],hops[1][0::2])))
        hops[0][0::2],hops[1][0::2]=first_a,first_b
    ra,rb=[outs[0]]+hops[0],[outs[NA]]+hops[1]
    ds=[trade(a) for a in ds[:-1]]+[ds[-1]]
    result,middle_grad=lax.optimization_barrier((middle+branch,middle_grad))
    input_grad,*grads,late=finish(S,C,T,ds,first_low,wide,ra,rb,x,middle_grad,first_gain[None])
    B=F//D
    vectors=(late[0],late[1],late[2],late[3],early[0],early[1],early[2],early[3],early[4],early[7+2*B:7+3*B].reshape(F),
             early[7:7+B].reshape(F),early[7+B:7+2*B].reshape(F),early[5])
    loss=jnp.sum(early[6])/(early[-1,0]/(S*C*T))
    return (result.reshape(ns,n,D),loss,input_grad.reshape(ns,n,D))+tuple(grads)+vectors


def solution(mesh):
    rows=P("shard",("context","tensor"),None)
    ids=P("shard",("context","tensor"))
    wide=P(("shard","context"),"tensor")
    tall=P("tensor",("shard","context"))
    weights=(wide,wide,wide,tall,wide,tall)
    return jax.shard_map(shards,mesh=mesh,in_specs=(rows,rows,ids,ids)+weights+(P(),)*13,
                         out_specs=(rows,P(),rows)+weights+(P(),)*13,check_vma=False)
```

```python
import functools

import jax
import jax.numpy as jnp
from jax import lax
from jax.experimental import pallas as pl
from jax.experimental.pallas import tpu as pltpu
from jax.sharding import PartitionSpec as P


NEG=-1e30
BLOCK=512
def _dot(a,b,ca,cb):
    return lax.dot_general(a,b,(((ca,),(cb,)),((),())),preferred_element_type=jnp.float32)

def half_masks(rows):
    lane=lax.broadcasted_iota(jnp.int32,(rows,128),1)
    return lane<64

def fwd_kernel(lo_ref,hi_ref,q_ref,k_ref,v_ref,col_ref,row_ref,o_ref,lse_ref,vt_ref,acc_ref,m_ref):
    i=pl.program_id(0)
    bq=acc_ref.shape[2]; bk=vt_ref.shape[3]; n=k_ref.shape[2]; per=bk//n
    upper=lax.broadcasted_iota(jnp.int32,(128,1),0)<64
    @pl.when(i==0)
    def _():
        def turn(j,_):
            vt=v_ref[pl.ds(j*per,per),0].reshape(bk,128).astype(jnp.float32).T
            vt_ref[0,j]=jnp.where(upper,vt,1.0).astype(jnp.bfloat16)
            vt_ref[1,j]=jnp.where(upper,1.0,vt).astype(jnp.bfloat16)
            return 0
        lax.fori_loop(0,vt_ref.shape[1],turn,0)
    left=half_masks(bq)
    q=q_ref[...].reshape(bq,128)*jnp.bfloat16(0.125)
    zero=jnp.zeros_like(q)
    qs=(jnp.where(left,q,zero),jnp.where(left,zero,q))
    ids_q=row_ref[i]
    acc_ref[...]=jnp.zeros_like(acc_ref)
    m_ref[...]=jnp.full_like(m_ref,NEG)
    def step(j,_):
        k=k_ref[pl.ds(j*per,per),0].reshape(bk,128)
        same=col_ref[pl.ds(pl.multiple_of(j*bk,bk),bk),:]==ids_q
        for h in range(2):
            sc=jnp.where(same,_dot(k,qs[h],1,1),NEG)
            old=m_ref[h:h+1,:]
            top=jnp.maximum(old,jnp.max(sc,axis=0,keepdims=True))
            e=jnp.exp(sc-top).astype(jnp.bfloat16)
            m_ref[h:h+1,:]=top
            acc_ref[h]=acc_ref[h]*jnp.exp(old-top)+_dot(vt_ref[h,j],e,1,0)
        return 0
    lax.fori_loop(lo_ref[i],hi_ref[i],step,0)
    t0=acc_ref[0,64:65,:]; t1=acc_ref[1,0:1,:]
    o=jnp.where(upper,acc_ref[0]/t0,acc_ref[1]/t1).T
    o_ref[...]=o.astype(jnp.bfloat16).reshape(o_ref.shape)
    lse_ref[0,0:1,:]=m_ref[0:1,:]+jnp.log(t0)
    lse_ref[0,1:2,:]=m_ref[1:2,:]+jnp.log(t1)

def bounds(ids,bq,bk):
    first=ids[::bq]; last=ids[bq-1::bq]
    start=jnp.sum((ids[None,:]<first[:,None]).astype(jnp.int32),axis=1)
    end=jnp.sum((ids[None,:]<=last[:,None]).astype(jnp.int32),axis=1)
    return start//bk,(end+bk-1)//bk

def attend_fwd(qkv,ids,col,edges,bq=BLOCK,bk=BLOCK):
    G,_,n,_=qkv.shape; L=G*n
    row=ids.reshape(L//bq,1,bq)
    part=lambda w: pl.BlockSpec((G,1,n,128),lambda i,*_: (0,w,0,0))
    ospec=pl.BlockSpec((bq//n,n,128),lambda i,*_:(i,0,0))
    return pl.pallas_call(fwd_kernel,
        grid_spec=pltpu.PrefetchScalarGridSpec(num_scalar_prefetch=2,grid=(L//bq,),
            in_specs=[pl.BlockSpec((bq//n,1,n,128),lambda i,*_:(i,0,0,0)),part(1),part(2),pl.BlockSpec((L,1),lambda i,*_:(0,0)),
                      pl.BlockSpec((L//bq,1,bq),lambda i,*_:(0,0,0))],
            out_specs=[ospec,pl.BlockSpec((1,2,bq),lambda i,*_:(i,0,0))],
            scratch_shapes=[pltpu.VMEM((2,L//bk,128,bk),jnp.bfloat16),pltpu.VMEM((2,128,bq),jnp.float32),pltpu.VMEM((2,bq),jnp.float32)]),
        out_shape=[jax.ShapeDtypeStruct((G,n,128),jnp.bfloat16),jax.ShapeDtypeStruct((L//bq,2,bq),jnp.float32)],
        compiler_params=pltpu.CompilerParams(dimension_semantics=("arbitrary",),vmem_limit_bytes=63<<20),
        cost_estimate=pl.CostEstimate(flops=4*L*1024*128*2,bytes_accessed=8*L*256,transcendentals=2*L*1024),
        name="attend_fwd")(*edges,qkv,qkv,qkv,col,row)

def bwd_kernel(lo_ref,hi_ref,q_ref,k_ref,v_ref,g_ref,o_ref,lse_ref,col_ref,row_ref,d_ref,dqa,dka,dva):
    i=pl.program_id(0)
    bq=dqa.shape[1]; bk=BLOCK; n=k_ref.shape[2]; per=bk//n
    @pl.when(i==0)
    def _():
        dka[...]=jnp.zeros_like(dka); dva[...]=jnp.zeros_like(dva)
    left=half_masks(bq)
    q=q_ref[...].reshape(bq,128)*jnp.bfloat16(0.125)
    g=g_ref[...].reshape(bq,128)
    zero=jnp.zeros_like(q)
    qs=(jnp.where(left,q,zero),jnp.where(left,zero,q))
    gs=(jnp.where(left,g,zero),jnp.where(left,zero,g))
    d_t=(g.astype(jnp.float32)*o_ref[...].reshape(bq,128).astype(jnp.float32)).T
    lses=(lse_ref[0,0:1,:],lse_ref[0,1:2,:])
    ds=(jnp.sum(d_t[:64],axis=0,keepdims=True),jnp.sum(d_t[64:],axis=0,keepdims=True))
    ids_q=row_ref[i]
    dqa[...]=jnp.zeros_like(dqa)
    def step(j,_):
        k=k_ref[pl.ds(j*per,per),0].reshape(bk,128)
        v=v_ref[pl.ds(j*per,per),0].reshape(bk,128)
        rows=pl.ds(pl.multiple_of(j*bk,bk),bk)
        same=col_ref[rows,:]==ids_q
        dk=dka[rows,:]; dv=dva[rows,:]
        for h in range(2):
            st=_dot(k,qs[h],1,1)
            p=jnp.exp(jnp.where(same,st,NEG)-lses[h])
            dp=_dot(v,gs[h],1,1)
            d=(p*(dp-ds[h])).astype(jnp.bfloat16)
            dv=dv+_dot(p.astype(jnp.bfloat16),gs[h],1,0)
            dk=dk+_dot(d,qs[h],1,0)
            dqa[h]+=_dot(d,k,0,0)
        dka[rows,:]=dk; dva[rows,:]=dv
        return 0
    lax.fori_loop(lo_ref[i],hi_ref[i],step,0)
    d_ref[pl.ds(i*(bq//n),bq//n),0]=(jnp.where(left,dqa[0],dqa[1])*0.125).astype(jnp.bfloat16).reshape(bq//n,n,128)
    @pl.when(i==pl.num_programs(0)-1)
    def _():
        d_ref[:,1]=dka[...].astype(jnp.bfloat16).reshape(d_ref.shape[0],n,128)
        d_ref[:,2]=dva[...].astype(jnp.bfloat16).reshape(d_ref.shape[0],n,128)

def attend_bwd(qkv,g,o,lse,ids,col,edges,bq=BLOCK):
    bk=BLOCK
    G,_,n,_=qkv.shape; L=G*n
    row=ids.reshape(L//bq,1,bq)
    part=lambda w: pl.BlockSpec((G,1,n,128),lambda i,*_: (0,w,0,0))
    ospec=pl.BlockSpec((bq//n,n,128),lambda i,*_:(i,0,0))
    return pl.pallas_call(bwd_kernel,
        grid_spec=pltpu.PrefetchScalarGridSpec(num_scalar_prefetch=2,grid=(L//bq,),
            in_specs=[pl.BlockSpec((bq//n,1,n,128),lambda i,*_:(i,0,0,0)),part(1),part(2),ospec,
                      ospec,pl.BlockSpec((1,2,bq),lambda i,*_:(i,0,0)),pl.BlockSpec((L,1),lambda i,*_:(0,0)),pl.BlockSpec((L//bq,1,bq),lambda i,*_:(0,0,0))],
            out_specs=pl.BlockSpec((G,3,n,128),lambda i,*_:(0,0,0,0)),
            scratch_shapes=[pltpu.VMEM((2,bq,128),jnp.float32)]+[pltpu.VMEM((L,128),jnp.float32)]*2),
        out_shape=jax.ShapeDtypeStruct((G,3,n,128),jnp.bfloat16),
        compiler_params=pltpu.CompilerParams(dimension_semantics=("arbitrary",),vmem_limit_bytes=63<<20),
        cost_estimate=pl.CostEstimate(flops=1000000,bytes_accessed=1000000,transcendentals=0),
        name="attend_bwd")(*edges,qkv,qkv,qkv,g,o,lse,col,row)


EPS=1e-5
PAIR=128

def norm_parts(v):
    m=jnp.mean(v,axis=-1,keepdims=True)
    s=jnp.mean(v*v,axis=-1,keepdims=True)-m*m
    r=lax.rsqrt(s+EPS)
    return (v-m)*r,r

def norm_back(e,h,r,gain):
    t=e*gain
    return r*(t-jnp.mean(t,axis=-1,keepdims=True)-h*jnp.mean(t*h,axis=-1,keepdims=True))


LINES=3
MESH_ID=pl.DeviceIdType.MESH

class Place:
    def __init__(self,S,C,T):
        self.CC=2 if C%2==0 else 1
        self.size={"t":T,"s":S,"x":C//self.CC,"c":self.CC}
        c=lax.axis_index("context")
        self.at={"t":lax.axis_index("tensor"),"s":lax.axis_index("shard"),"x":c//self.CC,"c":lax.rem(c,self.CC)}
        self.group=c*T+self.at["t"]
        self.T=T; self.G=C*T
    def peers(self,axis):
        m=self.size[axis]
        for d in range(1,m):
            other=lax.rem(self.at[axis]+d,m)
            if axis=="t": yield d-1,other,{"tensor":other}
            elif axis=="s": yield d-1,other,{"shard":other}
            elif axis=="x": yield d-1,other,{"context":other*self.CC+self.at["c"]}
            else: yield d-1,other,{"context":self.at["x"]*self.CC+other}
    def group_peers(self):
        for d in range(1,self.G):
            other=lax.rem(self.group+d,self.G)
            yield d-1,other,{"context":other//self.T,"tensor":lax.rem(other,self.T)}

def upper_rows(rows):
    return max(rows*5//8//16*16,16)

def slots(size,order):
    base,total={},0
    for a in order:
        base[a]=total; total+=size[a]-1
    return base,total

def greet(place):
    barrier=pltpu.get_barrier_semaphore()
    count=0
    for _,_,dev in place.group_peers():
        pl.semaphore_signal(barrier,inc=1,device_id=dev,device_id_type=MESH_ID); count+=1
    for _,_,dev in place.peers("s"):
        pl.semaphore_signal(barrier,inc=1,device_id=dev,device_id_type=MESH_ID); count+=1
    pl.semaphore_wait(barrier,count)

class VectorSum:
    order="csxt"
    def __init__(self,place,cur,recs,send,recv):
        self.place,self.cur,self.send,self.recv=place,cur,send,recv
        self.recs=dict(zip(self.order,recs))
        self.base,_=slots(place.size,self.order)
    def copies(self,axis):
        at=self.place.at[axis]
        return [remote(self.cur,self.recs[axis].at[at],self.send.at[self.base[axis]+k],self.recv.at[self.base[axis]+k],dev)
                for k,_,dev in self.place.peers(axis)]
    def start(self,axis):
        self.recs[axis][self.place.at[axis]]=self.cur[...]
        for c in self.copies(axis): c.start()
    def end(self,axis):
        for c in self.copies(axis): c.wait()
        rec=self.recs[axis]
        total=rec[0]
        for i in range(1,self.place.size[axis]): total=total+rec[i]
        self.cur[...]=total

def vector_scratch(size,rows,D):
    _,total=slots(size,VectorSum.order)
    dma=pltpu.SemaphoreType.DMA
    return [pltpu.VMEM((rows,D),jnp.float32),[pltpu.VMEM((size[a],rows,D),jnp.float32) for a in VectorSum.order],dma((total,)),dma((total,))]

def remote(src,dst,send,recv,dev):
    return pltpu.make_async_remote_copy(src_ref=src,dst_ref=dst,send_sem=send,recv_sem=recv,device_id=dev,device_id_type=MESH_ID)

def fetch(sources,buffers,sem):
    copies=[pltpu.make_async_copy(a,b,sem.at[i]) for i,(a,b) in enumerate(zip(sources,buffers))]
    for c in copies: c.start()
    return copies

def project_kernel(S,C,T,x_ref,gain_ref,shift_ref,wq_ref,wk_ref,wv_ref,qs_ref,vs_ref,ids_ref,wo_ref,wu_ref,wd_ref,
                   low_ref,wide_ref,allids_ref,pa_ref,pb_ref,*rest):
    spg=len(rest)-17
    rows_refs=rest[:spg]
    *scratch,buffers,load=rest[spg:]
    loads=fetch((wq_ref,wk_ref,wv_ref,wo_ref,wu_ref,wd_ref,ids_ref,x_ref,gain_ref,shift_ref,qs_ref,vs_ref),buffers,load)
    wq_ref,wk_ref,wv_ref,wo_ref,wu_ref,wd_ref,ids_ref,x_ref,gain_ref,shift_ref,qs_ref,vs_ref=buffers
    project_body(S,C,T,loads,x_ref,gain_ref,shift_ref,wq_ref,wk_ref,wv_ref,(qs_ref,None,vs_ref),ids_ref,wo_ref,wu_ref,wd_ref,
                 low_ref,wide_ref,allids_ref,pa_ref,pb_ref,rows_refs,*scratch)

def project_body(S,C,T,loads,x_ref,gain_ref,shift_ref,wq_ref,wk_ref,wv_ref,bias_refs,ids_ref,wo_ref,wu_ref,wd_ref,
                   low_ref,wide_ref,allids_ref,pa_ref,pb_ref,rows_refs,
                   zbuf,z_send,z_recv,p_send,p_recv,wbuf,obuf,idbuf,ag_send,ag_recv,a_send,a_recv,i_send,i_recv,local):
    place=Place(S,C,T)
    R,D=low_ref.shape
    G,_,n=rows_refs[0].shape[:3]
    spg=len(rows_refs)
    HP=D//PAIR; SG=G//HP
    cols=wbuf.shape[-1]; hpt=cols//PAIR
    me=place.group
    order="tsxc"
    base,total=slots(place.size,order)
    own=[place.at[a] for a in order]
    for c in loads[:6]: c.wait()
    for w,ref in enumerate((wq_ref,wk_ref,wv_ref)):
        wbuf[w,own[0],own[1],own[2],own[3]]=ref[...].astype(jnp.bfloat16)
    t0=place.at["t"]
    HA=upper_rows(zbuf.shape[1])
    c0=wo_ref.shape[0]; cf=wu_ref.shape[1]
    zbuf[t0,:,0:c0]=wo_ref[...].T.astype(jnp.bfloat16)
    zbuf[t0,:,c0:c0+cf]=wu_ref[...].astype(jnp.bfloat16)
    zbuf[t0,:,c0+cf:]=wd_ref[...].T.astype(jnp.bfloat16)
    wide=c0+2*cf
    cuts=[wide*j//(128*LINES)*128 for j in range(LINES)]+[wide]
    def hop(way,h,piece,j):
        to=t0+1 if way==0 else t0-1
        lane=slice(cuts[j],cuts[j+1])
        return remote(zbuf.at[piece,:,lane],zbuf.at[piece,:,lane],z_send.at[way,h-1,j],z_recv.at[way,h-1,j],{"tensor":lax.rem(to+T,T)})
    def line_start(j):
        @pl.when(t0<T-1)
        def _(): hop(0,1,t0,j).start()
        @pl.when(t0>0)
        def _(): hop(1,1,t0,j).start()
    def line_pass(h,j):
        @pl.when(t0>=h)
        def _():
            hop(0,h,lax.rem(t0-h+T,T),j).wait_recv()
            @pl.when(t0<T-1)
            def _(): hop(0,h+1,lax.rem(t0-h+T,T),j).start()
        @pl.when(t0+h<=T-1)
        def _():
            hop(1,h,lax.rem(t0+h,T),j).wait_recv()
            @pl.when(t0>0)
            def _(): hop(1,h+1,lax.rem(t0+h,T),j).start()
    def line_end():
        for j in range(LINES):
            for h in range(1,T):
                @pl.when((t0<T-1)&(t0>=h-1))
                def _(): hop(0,h,lax.rem(t0-h+1+T,T),j).wait_send()
                @pl.when((t0>0)&(t0+h-1<=T-1))
                def _(): hop(1,h,lax.rem(t0+h-1,T),j).wait_send()
    def plane(j):
        lane=slice(cuts[j],cuts[j+1])
        x0,s0=place.at["x"],place.at["s"]
        out=[pltpu.make_async_copy(zbuf.at[:,0:HA,lane],pa_ref.at[x0,:,:,lane],local.at[8+2*j]),
             pltpu.make_async_copy(zbuf.at[:,HA:,lane],pb_ref.at[s0,:,:,lane],local.at[9+2*j])]
        for k,_,dev in place.peers("x"):
            c=remote(zbuf.at[:,0:HA,lane],pa_ref.at[x0,:,:,lane],p_send.at[0,k,j],p_recv.at[0,k,j],dev); sent.append(c); out.append(c)
        for k,_,dev in place.peers("s"):
            c=remote(zbuf.at[:,HA:,lane],pb_ref.at[s0,:,:,lane],p_send.at[1,k,j],p_recv.at[1,k,j],dev); sent.append(c); out.append(c)
        for c in out: c.start()
        return out
    greet(place)
    stages={2:"tsxc",1:"txsc",0:"txsc"}
    sent=[]
    copies={}
    def start(w,r):
        done=stages[w][:r]; axis=stages[w][r]
        idx=tuple(slice(None) if a in done else place.at[a] for a in order)
        copies[w,r]=[]
        for k,_,dev in place.peers(axis):
            c=remote(wbuf.at[(w,)+idx],wbuf.at[(w,)+idx],ag_send.at[w,base[axis]+k],ag_recv.at[w,base[axis]+k],dev)
            c.start(); copies[w,r].append(c); sent.append(c)
    def arrive(w,r):
        for c in copies[w,r]: c.wait_recv()
    for w in (2,1,0): start(w,0)
    for j in range(LINES): line_start(j)
    loads[6].wait()
    ids_own=pltpu.make_async_copy(ids_ref,idbuf.at[place.at["s"]],local.at[0]); ids_own.start()
    id_first=[]
    for k,_,dev in place.peers("s"):
        c=remote(ids_ref,idbuf.at[place.at["s"]],i_send.at[k],i_recv.at[k],dev); c.start(); id_first.append(c); sent.append(c)
    for c in loads[7:]: c.wait()
    step=min(64,R)
    def norm(i,_):
        rows=pl.ds(pl.multiple_of(i*step,step),step)
        h,_r=norm_parts(x_ref[rows,:])
        low_ref[rows,:]=(h*gain_ref[...]+shift_ref[...]).astype(jnp.bfloat16)
        return 0
    lax.fori_loop(0,R//step,norm,0)
    def spread_ids():
        ids_own.wait()
        for c in id_first: c.wait_recv()
        out=[]
        mine=pltpu.make_async_copy(idbuf,allids_ref.at[me],local.at[1]); mine.start(); out.append(mine)
        for k,_,dev in place.group_peers():
            c=remote(idbuf,allids_ref.at[me],i_send.at[S-1+k],i_recv.at[S-1+k],dev); c.start(); sent.append(c); out.append(c)
        return out
    late=[]
    def compute(w):
        def one(t,_):
            y=_dot(low_ref[...],wbuf[w,t].reshape(D,cols),1,0)
            if bias_refs[w] is not None: y=y+bias_refs[w][:,pl.ds(pl.multiple_of(t*cols,128),cols)]
            y=y.astype(jnp.bfloat16)
            for g in range(SG):
                for j in range(hpt):
                    obuf[w,g*HP+t*hpt+j]=y[g*spg*n:(g+1)*spg*n,j*PAIR:(j+1)*PAIR].reshape(spg,n,PAIR)
            return 0
        lax.fori_loop(0,T,one,0)
        mine=pltpu.make_async_copy(obuf.at[w,me,0],rows_refs[0].at[me,w],local.at[2+w]); mine.start(); late.append(mine)
        for k,other,dev in place.group_peers():
            c=remote(obuf.at[w,other,0],rows_refs[0].at[me,w],a_send.at[w,k],a_recv.at[w,k],dev)
            c.start(); sent.append(c); late.append(c)
        for i in range(1,spg):
            c=pltpu.make_async_copy(obuf.at[w,:,i],rows_refs[i].at[:,w],local.at[8+2*LINES+w*spg+i]); c.start(); late.append(c)
        keep=pltpu.make_async_copy(wbuf.at[w],wide_ref.at[w],local.at[5+w]); keep.start(); late.append(keep)
    arrive(2,0); start(2,1)
    arrive(1,0); start(1,1)
    ids_out=spread_ids()
    arrive(2,1); start(2,2)
    arrive(0,0); start(0,1)
    arrive(1,1); start(1,2)
    line_pass(1,0)
    arrive(2,2); start(2,3)
    for j in range(1,LINES): line_pass(1,j)
    arrive(2,3); compute(2)
    arrive(1,2); start(1,3)
    line_pass(2,0)
    arrive(0,1); start(0,2)
    arrive(1,3); compute(1)
    for j in range(1,LINES): line_pass(2,j)
    for h in range(3,T): line_pass(h,0)
    ids_out=ids_out+plane(0)
    arrive(0,2); start(0,3)
    for j in range(1,LINES):
        for h in range(3,T): line_pass(h,j)
        ids_out=ids_out+plane(j)
    arrive(0,3); compute(0)
    for c in late+ids_out:
        if any(c is o for o in sent): c.wait_recv()
        else: c.wait()
    for c in sent: c.wait_send()
    line_end()

def project(S,C,T,x,gain,shift,wq,wk,wv,qs,vs,ids,wo,wu,wd,ns,n):
    R,D=x.shape
    G=C*T; HP=D//PAIR; spg=ns*HP//G
    DR,cols=wq.shape
    CC=2 if C%2==0 else 1
    piece=(3,T,S,C//CC,CC,DR,cols)
    HA=upper_rows(DR); width=wo.shape[0]+2*wu.shape[1]; most=max(S,C//CC)-1
    _,total=slots({"t":T,"s":S,"x":C//CC,"c":CC},"tsxc")
    vm=pl.BlockSpec(memory_space=pltpu.VMEM); anyspec=pl.BlockSpec(memory_space=pl.ANY)
    dma=pltpu.SemaphoreType.DMA
    return pl.pallas_call(functools.partial(project_kernel,S,C,T),
        in_specs=[pl.BlockSpec(memory_space=pltpu.HBM)]*12,
        out_specs=[vm]+[anyspec]*(4+spg),
        out_shape=[jax.ShapeDtypeStruct((R,D),jnp.bfloat16),jax.ShapeDtypeStruct(piece,jnp.bfloat16),jax.ShapeDtypeStruct((G,S,1,ns*n),jnp.int32),
                   jax.ShapeDtypeStruct((C//CC,T,HA,width),jnp.bfloat16),jax.ShapeDtypeStruct((S,T,DR-HA,width),jnp.bfloat16)]+
                  [jax.ShapeDtypeStruct((G,3,n,PAIR),jnp.bfloat16)]*spg,
        scratch_shapes=[pltpu.VMEM((T,DR,width),jnp.bfloat16),dma((2,T-1,LINES)),dma((2,T-1,LINES)),dma((2,most,LINES)),dma((2,most,LINES)),pltpu.VMEM(piece,jnp.bfloat16),pltpu.VMEM((3,G,spg,n,PAIR),jnp.bfloat16),pltpu.VMEM((S,1,ns*n),jnp.int32),
                        dma((3,total)),dma((3,total)),dma((3,G-1)),dma((3,G-1)),dma((S-1+G-1,)),dma((S-1+G-1,)),dma((8+2*LINES+3*spg,)),
                        [pltpu.VMEM(a.shape,a.dtype) for a in (wq,wk,wv,wo,wu,wd,ids,x,gain,shift,qs,vs)],dma((12,))],
        compiler_params=pltpu.CompilerParams(collective_id=0,has_side_effects=True,vmem_limit_bytes=63<<20),
        name="project")(x,gain,shift,wq,wk,wv,qs,vs,ids,wo,wu,wd)


def feed_kernel(S,C,T,NC,NO,*refs):
    place=Place(S,C,T)
    CX=place.size["x"]; CC=place.CC
    spg=NO
    o_refs=refs[:spg]; o_ref=o_refs[-1]; refs=refs[spg-1:]
    wa_refs=refs[1:1+S]; wb_refs=refs[1+S:1+S+CX]
    (x_ref,teach_ref,ids_ref,mask_ref),vec_refs,wide_refs=refs[1+S+CX:5+S+CX],refs[5+S+CX:11+S+CX],refs[11+S+CX:14+S+CX]
    refs=refs[7:]
    (mid_ref,res_ref,mg_ref,inner_ref,second_ref,out_ref,midl_ref,hid_ref,unl_ref,sum_ref)=refs[7+S+CX:17+S+CX]
    g_refs=refs[17+S+CX:17+S+CX+spg]; refs=refs[1:]; refs=refs[spg-1:]
    (w2,rbuf,mix,inner,second,outl,midl,hid,unl,act,dact,tt,acc,middle,og,s1,s2,res,mg,gout,vacc,wacc,
     w_local,w_send,w_recv,a_send,a_recv,g_send,g_recv,misc,o_sem,s1b,s2b,buffers,load)=refs[17+S+CX:]
    loads=fetch((x_ref,teach_ref,ids_ref,mask_ref)+tuple(vec_refs)+tuple(wide_refs),buffers,load)
    x_ref,teach_ref,ids_ref,mask_ref=buffers[:4]
    vec_refs,wide_refs=buffers[4:10],buffers[10:]
    R,D=x_ref.shape
    G,n=o_ref.shape[:2]
    HP=D//PAIR; SG=G//HP
    HA=upper_rows(w2.shape[-2])
    F=hid.shape[1]; cf=F//T; c2=D//T
    B=R//spg; sub=n
    f32=jnp.float32; b16=jnp.bfloat16
    me=place.group
    s0,x0,c0=place.at["s"],place.at["x"],place.at["c"]
    DS=D//S
    ranges=((0,c2),(c2,c2+cf),(c2+cf,c2+2*cf))
    def pieces(r):
        lo,hi=ranges[r]
        out=[]
        for d in range(S):
            src=lax.rem(s0+S-d,S)
            for i in range(CX):
                out.append((wa_refs[d].at[i,:,:,lo:hi],w2.at[:,src,i,c0,0:HA,lo:hi]))
        for d in range(CX):
            src=lax.rem(x0+CX-d,CX)
            for i in range(S):
                out.append((wb_refs[d].at[i,:,:,lo:hi],w2.at[:,i,src,c0,HA:,lo:hi]))
        return out
    local=[[pltpu.make_async_copy(a,b,w_local.at[r,i]) for i,(a,b) in enumerate(pieces(r))] for r in range(3)]
    for r in range(3):
        for c in local[r]: c.start()
    barrier=pltpu.get_barrier_semaphore()
    count=0
    for _,_,dev in place.group_peers():
        pl.semaphore_signal(barrier,inc=1,device_id=dev,device_id_type=MESH_ID); count+=1
    pl.semaphore_wait(barrier,count)
    own=[pltpu.make_async_copy(o_ref.at[me],rbuf.at[me,spg-1],misc.at[0])]
    own+=[pltpu.make_async_copy(o_refs[i],rbuf.at[:,i],misc.at[1+i]) for i in range(spg-1)]
    for c in own: c.start()
    rows_in=[remote(o_ref.at[other],rbuf.at[me,spg-1],a_send.at[k],a_recv.at[k],dev) for k,other,dev in place.group_peers()]
    for c in rows_in: c.start()
    far=[[remote(a,b,w_send.at[r,k,i],w_recv.at[r,k,i],dev) for k,_,dev in place.peers("c") for i,(a,b) in enumerate(pieces(r))] for r in range(3)]
    for r in range(3):
        for c in far[r]: c.start()
    def weights(r):
        for c in local[r]: c.wait()
        for c in far[r]: c.wait_recv()
    vacc[...]=jnp.zeros_like(vacc); wacc[...]=jnp.zeros_like(wacc)
    def vec(i): return vec_refs[i][...]
    def wide(i,t,lo,size): return wide_refs[i][:,pl.ds(pl.multiple_of(t*cf+lo,128),size)]
    MIXG,MIXS,OUTS,SECG,SECS,DOWNS=range(6)
    def each(fn):
        def body(i,_):
            fn(pl.ds(pl.multiple_of(i*sub,sub),sub),i)
            return 0
        lax.fori_loop(0,B//sub,body,0)
    def fold(a):
        return jnp.sum(a.reshape(a.shape[0]//8,8,a.shape[1]),axis=0)
    def lanes(a):
        v=a[:,:PAIR]
        for j in range(1,a.shape[1]//PAIR): v=v+a[:,j*PAIR:(j+1)*PAIR]
        return v
    def flat(t,lo,hi,s=None):
        if s is None: return w2[t,:,:,:,:,lo:hi].reshape(D,hi-lo)
        return w2[t,s,:,:,:,lo:hi].reshape(DS,hi-lo)
    for c in loads: c.wait()
    count=jnp.sum((ids_ref[...]!=2048//60+1).astype(f32))
    scale=R*S*C*T/jnp.full((1,1),count)
    sum_ref[...]=jnp.zeros_like(sum_ref)
    sum_ref[sum_ref.shape[0]-1:,:]=jnp.full((1,D),count)
    weights(0)
    def block(b):
        r0=b*B
        def rows(i): return pl.ds(pl.multiple_of(r0+i*sub,sub),sub)
        def tokens(i): return pl.ds(pl.multiple_of(i//(n//sub)*(spg*n)+b*n+lax.rem(i,n//sub)*sub,sub),sub)
        whole=pl.ds(r0,B)
        if b<spg-1: own[1+b].wait()
        else:
            own[0].wait()
            for c in rows_in: c.wait_recv()
        for gg in range(SG):
            for h in range(HP):
                mix[gg*n:(gg+1)*n,h*PAIR:(h+1)*PAIR]=rbuf[gg*HP+h,b]
        def f1(q,i):
            h,_=norm_parts(mix[q,:].astype(f32))
            inner[rows(i),:]=(h*vec(MIXG)+vec(MIXS)).astype(b16)
        each(f1)
        acc[...]=jnp.zeros_like(acc)
        def att(t,_):
            a=inner[whole,pl.ds(pl.multiple_of(t*c2,128),c2)]
            for s in range(S):
                acc[:,s*DS:(s+1)*DS]+=_dot(a,flat(t,0,c2,s),1,1)
            return 0
        lax.fori_loop(0,T,att,0)
        def f2(q,i):
            m=x_ref[tokens(i),:]+(acc[q,:]+vec(OUTS))
            middle[q,:]=m
            x_ref[tokens(i),:]=m
            h,_=norm_parts(m)
            second[rows(i),:]=(h*vec(SECG)+vec(SECS)).astype(b16)
        each(f2)
        if b==0: weights(1)
        s1[...]=jnp.zeros_like(s1); s2[...]=jnp.zeros_like(s2)
        def up(t,_):
            a=second[whole,:]
            w=cf//NC
            for j in range(NC):
                lane=slice(j*w,(j+1)*w)
                u=_dot(a,flat(t,c2+j*w,c2+(j+1)*w),1,0)+wide(0,t,j*w,w)
                u2=u*u
                th=jnp.tanh(0.7978845608028654*u*(1.0+0.044715*u2))
                half=0.5+0.5*th
                v=u*half
                act[t,:,lane]=v
                dact[t,:,lane]=half+(0.5*0.7978845608028654)*u*(1.0-th*th)*(1.0+(3*0.044715)*u2)
                s1[...]+=lanes(v); s2[...]+=lanes(v*v)
            return 0
        lax.fori_loop(0,T,up,0,unroll=2)
        def f3(q,i):
            m=jnp.sum(s1[q,:],axis=1,keepdims=True)/F
            v=jnp.sum(s2[q,:],axis=1,keepdims=True)/F-m*m
            s1[q,:]=jnp.broadcast_to(m,(sub,PAIR)); s2[q,:]=jnp.broadcast_to(lax.rsqrt(v+EPS),(sub,PAIR))
        each(f3)
        if b==0: weights(2)
        acc[...]=jnp.zeros_like(acc)
        def down(t,_):
            fcols=pl.ds(pl.multiple_of(t*cf,128),cf)
            def e(q,i):
                h=(act[t,q,:]-s1[q,0:1])*s2[q,0:1]
                act[t,q,:]=h
                hid[rows(i),fcols]=(h*wide(1,t,0,cf)+wide(2,t,0,cf)).astype(b16)
            each(e)
            a=hid[whole,fcols]
            for s in range(S):
                acc[:,s*DS:(s+1)*DS]+=_dot(a,flat(t,c2+cf,c2+2*cf,s),1,1)
            return 0
        lax.fori_loop(0,T,down,0,unroll=2)
        def f4(q,i):
            branch=acc[q,:]+vec(DOWNS)
            res[tokens(i),:]=branch
            err=middle[q,:]+branch-teach_ref[tokens(i),:]
            k=jnp.broadcast_to(mask_ref[pl.ds(i*spg+b,1),:].astype(f32),(sub,sub)).T[:,0:1]
            e=k*err
            vacc[6]+=fold(e*err)
            g=e*scale
            og[q,:]=g
            low_=g.astype(b16)
            outl[rows(i),:]=low_
            vacc[5]+=fold(low_.astype(f32))
        each(f4)
        def back1(t,_):
            a=outl[whole,:]
            w=cf//NC
            for j in range(NC):
                lane=slice(j*w,(j+1)*w)
                g=_dot(a,flat(t,c2+cf+j*w,c2+cf+(j+1)*w),1,0)
                h=act[t,:,lane]
                wacc[0,t,:,lane]+=fold(g*h); wacc[1,t,:,lane]+=fold(g)
                v=g*wide(1,t,j*w,w)
                tt[t,:,lane]=v
                s1b[...]+=lanes(v); s2b[...]+=lanes(v*h)
            return 0
        s1b[...]=jnp.zeros_like(s1b); s2b[...]=jnp.zeros_like(s2b)
        lax.fori_loop(0,T,back1,0,unroll=2)
        def f5(q,i):
            s1b[q,:]=jnp.broadcast_to(jnp.sum(s1b[q,:],axis=1,keepdims=True)/F,(sub,PAIR))
            s2b[q,:]=jnp.broadcast_to(jnp.sum(s2b[q,:],axis=1,keepdims=True)/F,(sub,PAIR))
        each(f5)
        acc[...]=jnp.zeros_like(acc)
        def back2(t,_):
            fcols=pl.ds(pl.multiple_of(t*cf,128),cf)
            def e(q,i):
                ag=s2[q,0:1]*(tt[t,q,:]-s1b[q,0:1]-act[t,q,:]*s2b[q,0:1])
                ul=(ag*dact[t,q,:]).astype(b16)
                unl[rows(i),fcols]=ul
                wacc[2,t]+=fold(ul.astype(f32))
            each(e)
            a=unl[whole,fcols]
            for s in range(S):
                acc[:,s*DS:(s+1)*DS]+=_dot(a,flat(t,c2,c2+cf,s),1,1)
            return 0
        lax.fori_loop(0,T,back2,0,unroll=2)
        def f6(q,i):
            h,r=norm_parts(middle[q,:])
            e=acc[q,:]
            vacc[3]+=fold(e*h); vacc[4]+=fold(e)
            m=og[q,:]+norm_back(e,h,r,vec(SECG))
            mg[tokens(i),:]=m
            ml=m.astype(b16)
            midl[rows(i),:]=ml
            vacc[2]+=fold(ml.astype(f32))
        each(f6)
        def back3(t,_):
            acc[:,pl.ds(pl.multiple_of(t*c2,128),c2)]=_dot(midl[whole,:],flat(t,0,c2),1,0)
            return 0
        lax.fori_loop(0,T,back3,0)
        def f7(q,i):
            h,r=norm_parts(mix[q,:].astype(f32))
            e=acc[q,:]
            vacc[0]+=fold(e*h); vacc[1]+=fold(e)
            mix[q,:]=norm_back(e,h,r,vec(MIXG)).astype(b16)
        each(f7)
        for gg in range(SG):
            for h in range(HP):
                gout[b,gg*HP+h]=mix[gg*n:(gg+1)*n,h*PAIR:(h+1)*PAIR]
        copies=[pltpu.make_async_copy(src.at[whole],dst.at[whole],o_sem.at[b,i]) for i,(src,dst) in enumerate(
            ((inner,inner_ref),(second,second_ref),(outl,out_ref),(midl,midl_ref),(hid,hid_ref),(unl,unl_ref)))]
        for gg in range(SG):
            part=pl.ds(gg*spg*n+b*n,n)
            copies+=[pltpu.make_async_copy(src.at[part],dst.at[part],o_sem.at[b,6+3*gg+i]) for i,(src,dst) in enumerate(((x_ref,mid_ref),(res,res_ref),(mg,mg_ref)))]
        if b<spg-1:
            copies.append(pltpu.make_async_copy(gout.at[b,me],g_refs[b].at[me],o_sem.at[b,6+3*SG]))
            far_g=[remote(gout.at[b,other],g_refs[b].at[me],g_send.at[b,k],g_recv.at[b,k],dev) for k,other,dev in place.group_peers()]
            for c in far_g: c.start()
            g_out.extend(far_g)
        else:
            copies.append(pltpu.make_async_copy(gout.at[b],g_refs[b],o_sem.at[b,6+3*SG]))
        for c in copies: c.start()
        return copies
    g_out=[]
    done=[]
    for b in range(spg): done+=block(b)
    for i in range(7):
        sum_ref[i:i+1,:]=jnp.sum(vacc[i],axis=0,keepdims=True)
    for i in range(3):
        for t in range(T):
            at=(i*F+t*cf)
            sum_ref[7+at//D:8+at//D,at%D:at%D+cf]=jnp.sum(wacc[i,t],axis=0,keepdims=True)
    for c in done: c.wait()
    for c in g_out: c.wait()
    for c in rows_in: c.wait_send()
    for r in range(3):
        for c in far[r]: c.wait_send()

def feed(S,C,T,o,wa,wb,x,teacher,ids,mask,vecs,wides):
    plain=(x,teacher,ids,mask)+tuple(vecs)+tuple(wides)
    R,D=x.shape
    spg=len(o)
    G,n=o[0].shape[:2]
    rows=(G,spg,n,PAIR)
    CC=2 if C%2==0 else 1
    CX=C//CC
    DR,c2=wa[0].shape[-2]+wb[0].shape[-2],wa[0].shape[-1]
    F=wides[0].shape[-1]; cf=F//T; B=R//spg; SG=G//(D//PAIR)
    b16,f32=jnp.bfloat16,jnp.float32
    vm=pl.BlockSpec(memory_space=pltpu.VMEM); anyspec=pl.BlockSpec(memory_space=pl.ANY)
    dma=pltpu.SemaphoreType.DMA
    V=lambda shape,dt=b16: pltpu.VMEM(shape,dt)
    NP=2*S*CX; NCC=max(CC-1,1)
    sums=8+3*F//D; sums+=-sums%8
    sds=jax.ShapeDtypeStruct
    return pl.pallas_call(functools.partial(feed_kernel,S,C,T,max(cf//512,1),spg),
        in_specs=[pl.BlockSpec(memory_space=pltpu.HBM)]*(spg+S+CX+len(plain)),
        out_specs=[anyspec]*9+[vm]+[anyspec]*spg,
        out_shape=[sds((R,D),f32)]*3+[sds((R,D),b16)]*4+[sds((R,F),b16)]*2+[sds((sums,D),f32)]+[sds((G,n,PAIR),b16)]*spg,
        scratch_shapes=[V((T,S,CX,CC,DR,c2)),V(rows),V((B,D)),V((R,D)),V((R,D)),V((R,D)),V((R,D)),V((R,F)),V((R,F)),
                        V((T,B,cf),f32),V((T,B,cf),f32),V((T,B,cf),f32),V((B,D),f32),V((B,D),f32),V((B,D),f32),V((B,PAIR),f32),V((B,PAIR),f32),
                        V((R,D),f32),V((R,D),f32),V((spg,G,n,PAIR)),V((7,8,D),f32),V((3,T,8,cf),f32),
                        dma((3,NP)),dma((3,NCC,NP)),dma((3,NCC,NP)),dma((G-1,)),dma((G-1,)),dma((spg,G-1)),dma((spg,G-1)),dma((spg,)),dma((spg,7+3*SG)),V((B,PAIR),f32),V((B,PAIR),f32),
                        [V(a.shape,a.dtype) for a in plain],dma((len(plain),))],
        compiler_params=pltpu.CompilerParams(collective_id=3,has_side_effects=True,vmem_limit_bytes=63<<20),
        name="feed")(*o,*wa,*wb,*plain)


def weight_grads_kernel(S,C,T,out_ref,second_ref,middle_ref,inner_ref,unit_ref,hidden_ref,g_ref,early_ref,*rest):
    CX0=C//(2 if C%2==0 else 1)
    NA=1+2*(S-1); NB=1+2*(CX0-1); TH=T//2
    pa_refs,pb_refs=rest[:NA],rest[NA:NA+NB]
    gin_ref,sum_ref,own,got,send,recv,local,a_send,a_recv,a_local,ev,ev_recs,v_send,v_recv,buffers,load=rest[NA+NB:]
    loads=fetch((early_ref,middle_ref,inner_ref,second_ref,unit_ref,out_ref,hidden_ref),(ev,)+tuple(buffers),load)
    middle_ref,inner_ref,second_ref,unit_ref,out_ref,hidden_ref=buffers
    place=Place(S,C,T)
    R,D=out_ref.shape
    CX=place.size["x"]; CC=place.CC
    HR,width=own.shape[-2:]
    c2=inner_ref.shape[1]//T; cf=unit_ref.shape[1]//T
    cc=place.at["c"]
    barrier=pltpu.get_barrier_semaphore()
    others=list(place.peers("c"))
    count=0
    for _,_,dev in place.group_peers():
        pl.semaphore_signal(barrier,inc=1,device_id=dev,device_id_type=MESH_ID); count+=1
    for _,_,dev in place.peers("s"):
        pl.semaphore_signal(barrier,inc=1,device_id=dev,device_id_type=MESH_ID); count+=1
    pl.semaphore_wait(barrier,count)
    me=place.group
    mine=pltpu.make_async_copy(g_ref.at[me],gin_ref.at[me],a_local.at[0]); mine.start()
    rows_in=[remote(g_ref.at[other],gin_ref.at[me],a_send.at[k],a_recv.at[k],dev) for k,other,dev in place.group_peers()]
    for c in rows_in: c.start()
    loads[0].wait()
    early=VectorSum(place,ev,ev_recs,v_send,v_recv)
    early.start("c")
    for c in loads[1:]: c.wait()
    plan=[(middle_ref,inner_ref,0,c2,c2),(second_ref,unit_ref,c2,cf,min(cf,512)),(out_ref,hidden_ref,c2+cf,cf,min(cf,512))]
    cut=[0,c2+cf,c2+2*cf]
    def swap(t,j):
        lane=slice(cut[j],cut[j+1])
        return [remote(own.at[t,:,:,other,:,:,lane],got.at[t,k,:,:,:,:,lane],send.at[t,k,j],recv.at[t,k,j],dev) for k,other,dev in others]
    def outs(t,act):
        def go(src,ref,sem,cond=None):
            if cond is None: act(pltpu.make_async_copy(src,ref,sem))
            else:
                @pl.when(cond)
                def _(): act(pltpu.make_async_copy(src,ref,sem))
        for d in range(S):
            src=got.at[t,0,lax.rem(place.at["s"]+d,S),:,0]
            if d==0: go(src,pa_refs[0].at[t],local.at[t,0])
            else:
                go(src,pa_refs[2*d-1].at[lax.rem(t,TH)],local.at[t,d],t<TH)
                go(src,pa_refs[2*d].at[lax.rem(t,TH)],local.at[t,d],t>=TH)
        for d in range(CX):
            src=got.at[t,0,:,lax.rem(place.at["x"]+d,CX),1]
            if d==0: go(src,pb_refs[0].at[t],local.at[t,S])
            else:
                go(src,pb_refs[2*d-1].at[lax.rem(t,TH)],local.at[t,S+d],t<TH)
                go(src,pb_refs[2*d].at[lax.rem(t,TH)],local.at[t,S+d],t>=TH)
    def settle(t):
        for j in range(2):
            lane=slice(cut[j],cut[j+1])
            for c in swap(t,j): c.wait_recv()
            for s in range(S):
                for x in range(CX):
                    total=own[t,s,x,cc,:,:,lane].astype(jnp.float32)
                    for k,_,_ in others:
                        total=total+got[t,k,s,x,:,:,lane].astype(jnp.float32)
                    got[t,0,s,x,:,:,lane]=total.astype(jnp.bfloat16)
        outs(t,lambda c: c.start())
    def one(t,_):
        for i,(left,right,base,cols,chunk) in enumerate(plan):
            for j in range(cols//chunk):
                y=_dot(left[...],right[:,pl.ds(pl.multiple_of(t*cols+j*chunk,128),chunk)],0,0)
                own[t,:,:,:,:,:,base+j*chunk:base+(j+1)*chunk]=y.astype(jnp.bfloat16).reshape(S,CX,CC,2,HR,chunk)
            if i>0:
                for c in swap(t,i-1): c.start()
        @pl.when(t>0)
        def _(): settle(t-1)
        for i,(x,y) in enumerate(("cs","sx","xt")):
            if i+1<T:
                @pl.when(t==i+1)
                def _(): early.end(x); early.start(y)
        return 0
    lax.fori_loop(0,T,one,0)
    settle(T-1)
    for i,(x,y) in enumerate(("cs","sx","xt")):
        if i+1>=T: early.end(x); early.start(y)
    early.end("t")
    sum_ref[...]=ev[...]
    def finish(t,_):
        for j in range(2):
            for c in swap(t,j): c.wait_send()
        outs(t,lambda c: c.wait())
        return 0
    lax.fori_loop(0,T,finish,0)
    mine.wait()
    for c in rows_in: c.wait()

def weight_grads(S,C,T,out_low,second_low,middle_low,inner_low,unit_low,hidden_low,g,early):
    R,D=out_low.shape
    CC=2 if C%2==0 else 1
    CX=C//CC; HR=D//(S*C*2); width=(D+2*unit_low.shape[1])//T
    hbm=pl.BlockSpec(memory_space=pltpu.HBM); anyspec=pl.BlockSpec(memory_space=pl.ANY)
    dma=pltpu.SemaphoreType.DMA
    return pl.pallas_call(functools.partial(weight_grads_kernel,S,C,T),
        in_specs=[hbm]*8,out_specs=[anyspec]*(2*S+2*CX-1)+[pl.BlockSpec(memory_space=pltpu.VMEM)],
        out_shape=[jax.ShapeDtypeStruct((T,CX,HR,width),jnp.bfloat16)]+[jax.ShapeDtypeStruct((T//2,CX,HR,width),jnp.bfloat16)]*(2*S-2)+
                  [jax.ShapeDtypeStruct((T,S,HR,width),jnp.bfloat16)]+[jax.ShapeDtypeStruct((T//2,S,HR,width),jnp.bfloat16)]*(2*CX-2)+[jax.ShapeDtypeStruct(g.shape,jnp.bfloat16),jax.ShapeDtypeStruct(early.shape,jnp.float32)],
        scratch_shapes=[pltpu.VMEM((T,S,CX,CC,2,HR,width),jnp.bfloat16),pltpu.VMEM((T,max(CC-1,1),S,CX,2,HR,width),jnp.bfloat16),
                        dma((T,max(CC-1,1),2)),dma((T,max(CC-1,1),2)),dma((T,S+CX)),dma((C*T-1,)),dma((C*T-1,)),dma((1,))]+vector_scratch({"t":T,"s":S,"x":CX,"c":CC},early.shape[0],D)+
                       [[pltpu.VMEM(a.shape,a.dtype) for a in (middle_low,inner_low,second_low,unit_low,out_low,hidden_low)],dma((7,))],
        compiler_params=pltpu.CompilerParams(collective_id=1,has_side_effects=True,vmem_limit_bytes=63<<20),
        name="weight_grads")(out_low,second_low,middle_low,inner_low,unit_low,hidden_low,g,early)


CHUNKS=2

def finish_kernel(S,C,T,NO,*refs):
    d_refs=refs[:NO]
    finish_split(S,C,T,d_refs,*refs[NO:])

def finish_split(S,C,T,d_refs,low_ref,wide_ref,x_ref,mg_ref,gain_ref,*rest):
    CX0=C//(2 if C%2==0 else 1)
    NA=1+2*(S-1); NB=1+2*(CX0-1)
    ra_refs,rb_refs=rest[:NA],rest[NA:NA+NB]
    *rest,buffers,load=rest[NA+NB:]
    own=(low_ref,x_ref,mg_ref,gain_ref)
    finish_body(S,C,T,lambda: fetch(own,buffers,load),d_refs,buffers[0],wide_ref,*buffers[1:],ra_refs,rb_refs,*rest)

def finish_body(S,C,T,fetch_own,d_refs,low_ref,wide_ref,x_ref,mg_ref,gain_ref,ra_refs,rb_refs,
                  grad_ref,dq_ref,dk_ref,dv_ref,do_ref,du_ref,dd_ref,late_ref,
                  rbuf,wbuf,acc,gbuf,rc,ra2,rb2,ra3,rb3,gz,gzr,bz,bzr,z_send,z_recv,
                  xa,xb,ya,yb,za,zb,d2,
                  lv,lv_recs,v_send,v_recv,
                  a_send,a_recv,w_send,w_recv,g_send,g_recv,local):
    gz,gzr,bz,bzr=[list(r) for r in (gz,gzr,bz,bzr)]
    place=Place(S,C,T)
    R,D=low_ref.shape
    G,_,n=d_refs[0].shape[:3]
    spg=len(d_refs)
    HP=D//PAIR; SG=G//HP
    cols=wbuf.shape[-1]; hpt=cols//PAIR
    DR=wbuf.shape[-2]
    CX=place.size["x"]; CC=place.CC; TH=T//2
    t0,s0,x0,c0=place.at["t"],place.at["s"],place.at["x"],place.at["c"]
    me=place.group
    f32=jnp.float32; b16=jnp.bfloat16
    sent=[]
    def go(copies):
        for c in copies: c.start()
        sent.extend(copies)
        return copies
    def land(copies):
        for c in copies: c.wait_recv()
    steps=[1<<k for k in range(T.bit_length()-1)]
    def bit(k): return lax.rem(t0//steps[k],2)
    def trade(k,which,bufs,recs):
        other=t0+steps[k]-2*steps[k]*bit(k)
        return go([remote(bufs[k].at[:,1-bit(k)],recs[k],z_send.at[which,k],z_recv.at[which,k],{"tensor":other})])
    def settle(k,copies,bufs,recs):
        land(copies)
        v=bufs[k][:,bit(k)].astype(f32)+recs[k][...].astype(f32)
        if k+1<len(steps): bufs[k+1][...]=v.astype(b16).reshape(bufs[k+1].shape)
        return v
    gzs=[[r.at[w] for r in gz] for w in range(3)]; gzrs=[[r.at[w] for r in gzr] for w in range(3)]
    loads=[pltpu.make_async_copy(wide_ref,wbuf,local.at[3*spg])]
    def arrivals(refs,buf,base):
        out=[pltpu.make_async_copy(refs[0],buf.at[0],local.at[base])]
        for i,ref in enumerate(refs[1:]):
            out.append(pltpu.make_async_copy(ref,buf.at[1+i//2,i%2*TH:i%2*TH+TH],local.at[base+1+i]))
        return out
    loads+=arrivals(ra_refs,xa,3*spg+1)
    loads+=arrivals(rb_refs,xb,3*spg+1+len(ra_refs))
    for c in loads[1:]: c.start()
    greet(place)
    rows_in=[None]*3
    mine=[None]*3
    last=d_refs[-1]
    for w in (2,1,0):
        mine[w]=[pltpu.make_async_copy(last.at[me,w],rbuf.at[w,me,spg-1],local.at[w*spg])]
        mine[w]+=[pltpu.make_async_copy(d_refs[i].at[:,w],rbuf.at[w,:,i],local.at[w*spg+1+i]) for i in range(spg-1)]
        for c in mine[w]: c.start()
        rows_in[w]=go([remote(last.at[other,w],rbuf.at[w,me,spg-1],a_send.at[w,k],a_recv.at[w,k],dev) for k,other,dev in place.group_peers()])

    late=VectorSum(place,lv,lv_recs,v_send,v_recv)

    loads[0].start()
    own_loads=fetch_own()
    for c in loads[1:]: c.wait()
    c2=xa.shape[-1]
    cuts=[c2*h//(128*CHUNKS)*128 for h in range(CHUNKS)]+[c2]
    plane_a,plane_b=[],[]
    for h in range(CHUNKS):
        lane=slice(cuts[h],cuts[h+1])
        def add_a(t,_):
            v=xa[0,t,:,:,lane].astype(f32)
            for i in range(1,S): v=v+xa[i,t,:,:,lane].astype(f32)
            ya[t,:,:,lane]=v.astype(b16)
            return 0
        lax.fori_loop(0,T,add_a,0)
        plane_a.append(go([remote(ya.at[:,other,:,lane],za.at[k,:,:,lane],w_send.at[0,h,k],w_recv.at[0,h,k],dev) for k,other,dev in place.peers("x")]))
        def add_b(t,_):
            v=xb[0,t,:,:,lane].astype(f32)
            for i in range(1,CX): v=v+xb[i,t,:,:,lane].astype(f32)
            yb[t,:,:,lane]=v.astype(b16)
            return 0
        lax.fori_loop(0,T,add_b,0)
        plane_b.append(go([remote(yb.at[:,other,:,lane],zb.at[k,:,:,lane],w_send.at[1,h,k],w_recv.at[1,h,k],dev) for k,other,dev in place.peers("s")]))
    loads[0].wait()
    for c in own_loads: c.wait()

    lv[...]=jnp.zeros_like(lv)
    def compute(w,first):
        for c in mine[w]: c.wait()
        land(rows_in[w])
        def one(t,_):
            d=jnp.concatenate([jnp.concatenate([rbuf[w,g*HP+t*hpt+j].reshape(spg*n,PAIR) for j in range(hpt)],axis=1) for g in range(SG)],axis=0)
            y=_dot(low_ref[...],d,0,0)
            gbuf[w,t]=y.astype(b16).reshape(S,CX,CC,DR,cols)
            z=_dot(d,wbuf[w,t].reshape(D,cols),1,1)
            if first:
                @pl.when(t==0)
                def _(): acc[...]=z
                @pl.when(t>0)
                def _(): acc[...]+=z
            else:
                acc[...]+=z
            if w!=1:
                lv[2+w//2:3+w//2,pl.ds(pl.multiple_of(t*cols,128),cols)]=jnp.sum(d.astype(f32),axis=0,keepdims=True)
            return 0
        lax.fori_loop(0,T,one,0)
        return go([remote(gbuf.at[w,:,:,:,other],rc.at[w,k],g_send.at[w,0,k],g_recv.at[w,0,k],dev) for k,other,dev in place.peers("c")])
    def after_core(w,copies):
        land(copies)
        for t in range(T):
            v=gbuf[w,t,:,:,c0].astype(f32)
            for k in range(CC-1): v=v+rc[w,k,t].astype(f32)
            rc[w,0,t]=v.astype(b16)
        a=go([remote(rc.at[w,0,0:TH,other],ra2.at[w,k],g_send.at[w,1,k],g_recv.at[w,1,k],dev) for k,other,dev in place.peers("s")])
        b=go([remote(rc.at[w,0,TH:T,:,other],rb2.at[w,k],g_send.at[w,2,k],g_recv.at[w,2,k],dev) for k,other,dev in place.peers("x")])
        return a,b
    def after_second(w,pair):
        land(pair[0])
        v=rc[w,0,0:TH,s0].astype(f32)
        for k in range(S-1): v=v+ra2[w,k].astype(f32)
        ra2[w,0]=v.astype(b16)
        a=go([remote(ra2.at[w,0,:,other],ra3.at[w,k],g_send.at[w,3,k],g_recv.at[w,3,k],dev) for k,other,dev in place.peers("x")])
        land(pair[1])
        v=rc[w,0,TH:T,:,x0].astype(f32)
        for k in range(CX-1): v=v+rb2[w,k].astype(f32)
        rb2[w,0]=v.astype(b16)
        b=go([remote(rb2.at[w,0,:,other],rb3.at[w,k],g_send.at[w,4,k],g_recv.at[w,4,k],dev) for k,other,dev in place.peers("s")])
        return a,b
    def after_third(w,pair):
        land(pair[0])
        v=ra2[w,0,:,x0].astype(f32)
        for k in range(CX-1): v=v+ra3[w,k].astype(f32)
        gz[0][w,0:T//4]=v.astype(b16).reshape(T//4,2,DR,cols)
        land(pair[1])
        v=rb2[w,0,:,s0].astype(f32)
        for k in range(S-1): v=v+rb3[w,k].astype(f32)
        gz[0][w,T//4:T//2]=v.astype(b16).reshape(T//4,2,DR,cols)
        return trade(0,w,gzs[w],gzrs[w])
    def onward(k,w,copies):
        settle(k-1,copies,gzs[w],gzrs[w])
        return trade(k,w,gzs[w],gzrs[w])
    def big_trade(k,h):
        lane=slice(cuts[h],cuts[h+1])
        other=t0+steps[k]-2*steps[k]*bit(k)
        return go([remote(bz[k].at[i,:,1-bit(k),:,lane],bzr[k].at[i,:,:,lane],z_send.at[3+2*h+i,k],z_recv.at[3+2*h+i,k],{"tensor":other}) for i in range(2)])
    def big_settle(k,h,copies):
        lane=slice(cuts[h],cuts[h+1])
        land(copies)
        for i in range(2):
            v=bz[k][i,:,bit(k),:,lane].astype(f32)+bzr[k][i,:,:,lane].astype(f32)
            if k+1<len(steps): bz[k+1][i,:,:,:,lane]=v.astype(b16).reshape(bz[k+1].shape[1:4]+(v.shape[-1],))
            else: d2[i*v.shape[1]:(i+1)*v.shape[1],lane]=v[0]
    def big_onward(k,h,copies):
        big_settle(k-1,h,copies)
        return big_trade(k,h)
    def big_first(h):
        lane=slice(cuts[h],cuts[h+1])
        land(plane_a[h])
        def add_a2(j,_):
            v=ya[pl.ds(2*j,2),x0,:,lane].astype(f32)
            for k in range(CX-1): v=v+za[k,pl.ds(2*j,2),:,lane].astype(f32)
            bz[0][0,j,:,:,lane]=v.astype(b16)
            return 0
        lax.fori_loop(0,T//2,add_a2,0)
        land(plane_b[h])
        def add_b2(j,_):
            v=yb[pl.ds(2*j,2),s0,:,lane].astype(f32)
            for k in range(S-1): v=v+zb[k,pl.ds(2*j,2),:,lane].astype(f32)
            bz[0][1,j,:,:,lane]=v.astype(b16)
            return 0
        lax.fori_loop(0,T//2,add_b2,0)
        return big_trade(0,h)
    end=len(steps)
    big=[None]*CHUNKS
    core_v=compute(2,True)
    big[0]=big_first(0)
    two_v=after_core(2,core_v)
    for h in range(1,CHUNKS): big[h]=big_first(h)
    core_k=compute(1,False)
    three_v=after_second(2,two_v)
    big[0]=big_onward(1,0,big[0])
    two_k=after_core(1,core_k)
    core_q=compute(0,False)
    z_v=after_third(2,three_v)
    three_k=after_second(1,two_k)
    two_q=after_core(0,core_q)
    big[1]=big_onward(1,1,big[1])
    step=min(64,R)
    def back(i,carry):
        rows=pl.ds(pl.multiple_of(i*step,step),step)
        h,r=norm_parts(x_ref[rows,:])
        e=acc[rows,:]
        grad_ref[rows,:]=mg_ref[rows,:]+norm_back(e,h,r,gain_ref[...])
        return carry[0]+jnp.sum(e*h,axis=0,keepdims=True),carry[1]+jnp.sum(e,axis=0,keepdims=True)
    zero=jnp.zeros((1,D),f32)
    ga,sa=lax.fori_loop(0,R//step,back,(zero,zero))
    lv[0:1,:]=ga; lv[1:2,:]=sa
    late.start("c")
    three_q=after_second(0,two_q)
    z_k=after_third(1,three_k)
    z_v=onward(1,2,z_v)
    late.end("c"); late.start("s")
    z_q=after_third(0,three_q)
    for h in range(2,CHUNKS): big[h]=big_onward(1,h,big[h])
    z_k=onward(1,1,z_k)
    late.end("s"); late.start("x")
    z_q=onward(1,0,z_q)
    late.end("x"); late.start("t")
    for k in range(2,end):
        for h in range(CHUNKS): big[h]=big_onward(k,h,big[h])
        z_v=onward(k,2,z_v); z_k=onward(k,1,z_k); z_q=onward(k,0,z_q)
    dv_ref[...]=settle(end-1,z_v,gzs[2],gzrs[2])[0]
    big_settle(end-1,0,big[0])
    dk_ref[...]=settle(end-1,z_k,gzs[1],gzrs[1])[0]
    dq_ref[...]=settle(end-1,z_q,gzs[0],gzrs[0])[0]
    for h in range(1,CHUNKS): big_settle(end-1,h,big[h])
    co=do_ref.shape[0]; cf=du_ref.shape[1]
    do_ref[...]=d2[:,:co].T
    du_ref[...]=d2[:,co:co+cf]
    dd_ref[...]=d2[:,co+cf:].T
    late.end("t"); late_ref[...]=lv[...]
    for c in sent: c.wait_send()

def finish(S,C,T,ds,first_low,wide,ra,rb,x,middle_grad,gain):
    R,D=x.shape
    G,_,n=ds[0].shape[:3]
    spg=len(ds)
    CC=2 if C%2==0 else 1
    CX=C//CC; TH=T//2
    DR,cols=wide.shape[-2:]
    HR,c2=ra[0].shape[-2:]
    b16,f32=jnp.bfloat16,jnp.float32
    vm=pl.BlockSpec(memory_space=pltpu.VMEM)
    dma=pltpu.SemaphoreType.DMA
    size={"t":T,"s":S,"x":CX,"c":CC}
    most=max(T,S,CX,CC)-1
    NL=8; co=D//T; cf=(c2-co)//2
    V=lambda shape,dt=b16: pltpu.VMEM(shape,dt)
    halves=[T>>(k+1) for k in range(T.bit_length()-1)]
    scratch=[V((3,G,spg,n,PAIR)),V(wide.shape),V((R,D),f32),V((3,T,S,CX,CC,DR,cols)),V((3,max(CC-1,1),T,S,CX,DR,cols)),
             V((3,max(S-1,1),TH,CX,DR,cols)),V((3,max(CX-1,1),TH,S,DR,cols)),V((3,max(CX-1,1),TH,DR,cols)),V((3,max(S-1,1),TH,DR,cols)),
             [V((3,h,2,DR,cols)) for h in halves],[V((3,h,DR,cols)) for h in halves],
             [V((2,h,2,HR,c2)) for h in halves],[V((2,h,HR,c2)) for h in halves],
             dma((3+2*CHUNKS,len(halves))),dma((3+2*CHUNKS,len(halves))),
             V((S,)+ra[0].shape),V((CX,)+rb[0].shape),V((T,CX,HR,c2)),V((T,S,HR,c2)),V((max(CX-1,1),T,HR,c2)),V((max(S-1,1),T,HR,c2)),
             V((2*HR,c2),f32)]+vector_scratch(size,NL,D)+[
             dma((3,G-1)),dma((3,G-1)),dma((2,CHUNKS,most)),dma((2,CHUNKS,most)),dma((3,6,most)),dma((3,6,most)),dma((3*spg+1+len(ra)+len(rb),)),
             [V((R,D)),V((R,D),f32),V((R,D),f32),V((1,D),f32)],dma((4,))]
    hbm=pl.BlockSpec(memory_space=pltpu.HBM)
    sds=jax.ShapeDtypeStruct
    return pl.pallas_call(functools.partial(finish_kernel,S,C,T,spg),
        in_specs=[hbm]*(spg+5+len(ra)+len(rb)),
        out_specs=[vm]*8,
        out_shape=[sds((R,D),f32)]+[sds((DR,cols),f32)]*3+[sds((co,2*HR),f32),sds((2*HR,cf),f32),sds((cf,2*HR),f32),sds((NL,D),f32)],
        scratch_shapes=scratch,
        compiler_params=pltpu.CompilerParams(collective_id=2,has_side_effects=True,vmem_limit_bytes=63<<20),
        name="finish")(*ds,first_low,wide,x,middle_grad,gain,*ra,*rb)


def shards(inputs,teacher,segments,pad_mask,query_weight,key_weight,value_weight,output_weight,up_weight,down_weight,
           first_gain,first_shift,query_shift,value_shift,mixed_gain,mixed_shift,output_shift,second_gain,second_shift,
           up_shift,hidden_gain,hidden_shift,down_shift):
    S,C,T=lax.axis_size("shard"),lax.axis_size("context"),lax.axis_size("tensor")
    CC=2 if C%2==0 else 1
    CX=C//CC
    G=C*T
    ns,n,D=inputs.shape
    R=ns*n
    HP=D//PAIR
    SG=G//HP
    spg=ns//SG
    me_s=lax.axis_index("shard")
    me_g=lax.axis_index("context")*T+lax.axis_index("tensor")
    c1=query_weight.shape[1]; c2=output_weight.shape[0]; cf=up_weight.shape[1]
    F=cf*T
    x=inputs.reshape(R,D)
    first_low,wide,ids_all,pa,pb,*rows_out=project(S,C,T,x,first_gain[None],first_shift[None],query_weight,key_weight,value_weight,query_shift[None],value_shift[None],
                                             segments.reshape(1,R),output_weight,up_weight,down_weight,ns,n)
    def over_shard(a,d):
        return lax.ppermute(a,"shard",[(i,(i+d)%S) for i in range(S)]) if d else a
    def over_x(a,d):
        return lax.ppermute(a,"context",[(i*CC+j,((i+d)%CX)*CC+j) for i in range(CX) for j in range(CC)]) if d else a
    wa=[over_shard(pa,d) for d in range(S)]
    wb=[over_x(pb,d) for d in range(CX)]
    ids_flat=ids_all
    ids_all=ids_all.reshape(G,S,ns,n)
    ids_mine=lax.dynamic_index_in_dim(ids_all,me_s,1,keepdims=False)
    ids_mine=lax.dynamic_slice_in_dim(ids_mine,(me_g//HP)*spg,spg,1).transpose(1,0,2).reshape(spg,G*n)
    edges=[bounds(ids_mine[i],BLOCK,BLOCK) for i in range(spg)]
    cols=[ids_mine[i][:,None] for i in range(spg)]
    def trade(a):
        return lax.all_to_all(a,("context","tensor"),0,0,tiled=True)
    qkv=[rows_out[0]]+[trade(a) for a in rows_out[1:]]
    mixed=[attend_fwd(qkv[i],ids_mine[i],cols[i],edges[i]) for i in range(spg)]
    arrived=[trade(mixed[i][0]) for i in range(spg-1)]+[mixed[-1][0]]
    vecs=[a[None] for a in (mixed_gain,mixed_shift,output_shift,second_gain,second_shift,down_shift)]
    wides=[a[None] for a in (up_shift,hidden_gain,hidden_shift)]
    middle,branch,middle_grad,inner_low,second_low,out_low,middle_low,hidden_low,unit_low,early,*gs=feed(
        S,C,T,arrived,wa,wb,x,teacher.reshape(R,D),ids_flat,pad_mask,vecs,wides)
    *outs,last_g,early=weight_grads(S,C,T,out_low,second_low,middle_low,inner_low,unit_low,hidden_low,gs[-1],early)
    gs=list(lax.optimization_barrier(tuple(gs[:-1])+(last_g,)))
    NA=1+2*(S-1)
    hops=[over_shard(outs[1+i],1+i//2) for i in range(2*(S-1))],[over_x(outs[NA+1+i],1+i//2) for i in range(2*(CX-1))]
    ds=[attend_bwd(qkv[i],gs[i],mixed[i][0],mixed[i][1],ids_mine[i],cols[i],edges[i]) for i in range(spg)]
    if spg>1:
        ds[0],(first_a,first_b)=lax.optimization_barrier((ds[0],(hops[0][0::2],hops[1][0::2])))
        hops[0][0::2],hops[1][0::2]=first_a,first_b
    ra,rb=[outs[0]]+hops[0],[outs[NA]]+hops[1]
    ds=[trade(a) for a in ds[:-1]]+[ds[-1]]
    result,middle_grad=lax.optimization_barrier((middle+branch,middle_grad))
    input_grad,*grads,late=finish(S,C,T,ds,first_low,wide,ra,rb,x,middle_grad,first_gain[None])
    B=F//D
    vectors=(late[0],late[1],late[2],late[3],early[0],early[1],early[2],early[3],early[4],early[7+2*B:7+3*B].reshape(F),
             early[7:7+B].reshape(F),early[7+B:7+2*B].reshape(F),early[5])
    loss=jnp.sum(early[6])/(early[-1,0]/(S*C*T))
    return (result.reshape(ns,n,D),loss,input_grad.reshape(ns,n,D))+tuple(grads)+vectors


def solution(mesh):
    rows=P("shard",("context","tensor"),None)
    ids=P("shard",("context","tensor"))
    wide=P(("shard","context"),"tensor")
    tall=P("tensor",("shard","context"))
    weights=(wide,wide,wide,tall,wide,tall)
    return jax.shard_map(shards,mesh=mesh,in_specs=(rows,rows,ids,ids)+weights+(P(),)*13,
                         out_specs=(rows,P(),rows)+weights+(P(),)*13,check_vma=False)
```
